32 devices in a mesh: dp: 16 (over z, y, core), seq: 2 (over x).
Axes of the slice: x: 2, y: 2, z: 4, core: 2. Of those that a mesh axis runs over, the one named last changes fastest.
Arguments:
- tokens: bfloat16 [4096, 2048], P(('dp', 'seq')), may hold values from -6 to 6
- cotangent: bfloat16 [4096, 2048], P(('dp', 'seq')), may hold values from -6 to 6
- w_qkv: bfloat16 [2048, 5120], P(('dp', 'seq')), may hold values from -0.125 to 0.125
- w_out: bfloat16 [4096, 2048], P(('dp', 'seq')), may hold values from -0.75 to 0.75
- w_router: bfloat16 [2048, 32], P(('dp', 'seq')), may hold values from -0.0625 to 0.0625
- norm_gains: bfloat16 [4352], P(('dp', 'seq')), may hold values from 0.5 to 1.5
- w_expert: bfloat16 [32, 2048, 2304], P(('dp', 'seq')), may hold values from -0.21875 to 0.21875
- lengths: int32 [16, 4], P('dp'), may hold values from 1 to 192, 256 in all within a row
- deal: int32 [16, 256], P('dp'), may hold values from 0 to 255, each once within a row
- routes: int32 [16, 256, 8], P('dp'), may hold values from 0 to 31, all different within a row
Outputs:
- layer_out: bfloat16 [4096, 2048], P(('dp', 'seq'))
- grad_tokens: bfloat16 [4096, 2048], P(('dp', 'seq'))
- grad_qkv: float32 [2048, 5120], P(('dp', 'seq'))
- grad_out: float32 [4096, 2048], P(('dp', 'seq'))
- grad_router: float32 [2048, 32], P(('dp', 'seq'))
- grad_gains: float32 [4352], P(('dp', 'seq'))
- grad_expert: float32 [32, 2048, 2304], P(('dp', 'seq'))
The draws below stay inside these ranges and needn't reach their ends.
Inputs may be any that keep to these rules, and one draw needn't show every extreme that they name: `lengths`: each group's entries sum to 256; the last counts padding positions. `deal`: each group's row holds every position once. `routes`: each token names 8 different experts.
All inputs are finite; a program needn't handle non-finite values.
Results may differ from the reference program's by a relative error of at most 0.015.
Values may be sent and summed in bfloat16 or wider, within the bound.
No kernel may reach another device: no remote copies, remote signals or barrier semaphores. Data moves between devices by JAX's collectives and lax.ppermute only.
A program may use at most 256 MiB of HBM per device.

```python
import math
import jax
import jax.numpy as jnp
import numpy as np
from jax import lax

D = 2048
HEADS = 32
KV_HEADS = 4
HEAD_DIM = 128
FF = 768
TOPK = 8
NSEG = 4
TOK_DEV = 128
EXPERTS = 32
ROW = 256
TOKENS = 4096
QDIM = 4096
KVDIM = 512
QKVDIM = 5120
GAINS = 4352
CAP = 32
N_DP = 16
DEVICES = 32


def strengthened(array, stream_key, source, target, blocks, factor):
    def block_of(dim):
        return (jnp.arange(array.shape[dim]) // (array.shape[dim] // blocks)).reshape((-1,) + (1,) * (array.ndim - 1 - dim))

    first = jax.random.permutation(stream_key, blocks)[block_of(target)]
    far = (block_of(target) + blocks // 2) % blocks
    return jnp.where((block_of(source) == first) | (block_of(source) == far), factor * array, array)


def block_levels(rng, shape, cuts, least, top_value):
    def one(axis_at, blocks):
        steps = jax.random.uniform(jax.random.fold_in(jax.random.fold_in(rng, 6), axis_at), (blocks,), jnp.float32, least / len(cuts), top_value / len(cuts))
        return jnp.repeat(jnp.exp(steps), shape[axis_at] // blocks).reshape((-1,) + (1,) * (len(shape) - axis_at - 1))

    level = one(*cuts[0])
    for cut in cuts[1:]:
        level = level * one(*cut)
    return level


def distinct(stream_key, rows, number_of, top, lift):
    ranking = jax.random.permutation(jax.random.fold_in(stream_key, 1), number_of)
    favour = ranking
    for power in range(3):
        favour = favour * favour // number_of
    favour = favour * lift // number_of
    lots = jax.random.randint(jax.random.fold_in(stream_key, 2), (rows, number_of), 0, 4096) + favour
    fixed_rows = jax.random.permutation(jax.random.fold_in(stream_key, 3), rows)[jnp.arange(number_of) % rows]
    lots = jnp.where(jnp.arange(rows)[:, None] == fixed_rows[None, :], 1 << 14, lots)
    score = lots * number_of + jnp.arange(number_of)
    return lax.top_k(score.astype(jnp.int32), top)[1].astype(jnp.int32)


def split_up(amount, total, reach, skew):
    weights = [(1 << 20) // math.isqrt(grade ** skew) + 1 for grade in range(2, amount + 1)]
    surplus, holding = total - reach - (amount - 1), [1] * (amount - 1)
    while surplus > 0:
        free = [i for i in range(amount - 1) if holding[i] < reach]
        whole, budget = sum([weights[i] for i in free]), surplus
        for i in free:
            more = min(reach - holding[i], max(1, budget * weights[i] // whole), surplus)
            holding[i] = holding[i] + more
            surplus = surplus - more
    return np.array([reach] + holding)


def ragged(rng, number_of, total, bound, slope):
    if number_of == 2:
        one = jax.random.randint(rng, (), max(1, total - bound), min(bound, total - 1) + 1)
        return jnp.stack([one, total - one])
    tallies = jnp.asarray(split_up(number_of, total, bound, slope), jnp.int32)
    couples = (number_of - 1) // 2
    donor, taker = tallies[1:1 + 2 * couples:2], tallies[2:2 + 2 * couples:2]
    room = jnp.minimum(donor - 1, bound - taker)
    shifted = jax.random.randint(jax.random.fold_in(rng, 1), (couples,), 0, 1 << 20) % (room + 1)
    tallies = tallies.at[1:1 + 2 * couples:2].set(donor - shifted).at[2:2 + 2 * couples:2].set(taker + shifted)
    return tallies[jax.random.permutation(jax.random.fold_in(rng, 2), number_of)]


def normal_values(rng, extent, deviation, limit, cuts=(), kind=jnp.bfloat16):
    values = deviation * jax.random.normal(rng, extent, jnp.float32)
    if cuts:
        values = values * block_levels(rng, extent, cuts, -0.22, 0.18)
    return jnp.clip(values, -limit, limit).astype(kind)


def bell_draw_with(own_key, extent, scale, limit, cuts, heavy, held_as=jnp.bfloat16):
    entries = scale * jax.random.normal(own_key, extent, jnp.float32)
    if cuts:
        entries = entries * block_levels(own_key, extent, cuts, -0.22, 0.18)
    return jnp.clip(strengthened(entries, jax.random.fold_in(own_key, 3), *heavy), -limit, limit).astype(held_as)


def setup_inputs(seed: int = 0) -> dict:
    keys = jax.random.split(jax.random.key(seed), 11)
    tokens = bell_draw_with(keys[0], (TOKENS, D), 1.0, 6.0, ((0, 32),), (0, 1, 32, 2.75))
    cotangent = normal_values(keys[1], (TOKENS, D), 1.0, 6.0, ((0, 32),))
    w_qkv = normal_values(keys[2], (D, QKVDIM), D ** -0.5, 0.125, ((0, 32),))
    w_out = normal_values(keys[3], (QDIM, D), (QDIM // 64) ** -0.5, 0.75, ((0, 32),))
    w_router = normal_values(keys[4], (D, EXPERTS), (4 * D) ** -0.5, 0.0625, ((0, 32),))
    norm_gains = jnp.clip(1.0 + 0.1 * jax.random.normal(keys[5], (GAINS,), jnp.float32), 0.5, 1.5).astype(jnp.bfloat16)
    w_expert = normal_values(keys[6], (EXPERTS, D, 3 * FF), FF ** -0.5, 0.21875, ((0, 32),))
    lengths = jax.vmap(lambda own: ragged(own, NSEG, ROW, ROW * 3 // 4, 2))(jax.random.split(keys[7], N_DP)).reshape((N_DP, NSEG)).astype(jnp.int32)
    deal = jax.vmap(lambda own: jax.random.permutation(own, ROW))(jax.random.split(keys[8], N_DP)).reshape((N_DP, ROW)).astype(jnp.int32)
    routes = distinct(keys[9], N_DP * ROW, EXPERTS, TOPK, 0).reshape((N_DP, ROW, TOPK))
    return {"tokens": tokens, "cotangent": cotangent, "w_qkv": w_qkv, "w_out": w_out, "w_router": w_router, "norm_gains": norm_gains, "w_expert": w_expert, "lengths": lengths, "deal": deal, "routes": routes}


EPS = 1e-06
THETA = 1000000.0
HIGHEST = lax.Precision.HIGHEST

@jax.custom_vjp
def low(v):
    return lax.optimization_barrier(v.astype(jnp.bfloat16)).astype(jnp.float32)

@jax.custom_vjp
def low_back(v):
    return v

def low_keep(v):
    return (low(v), None)

def low_pass(kept, grad):
    return (grad,)

def back_keep(v):
    return (v, None)

def back_low(kept, grad):
    return (low(grad),)
low.defvjp(low_keep, low_pass)
low_back.defvjp(back_keep, back_low)

def rounded(values):
    return low(low_back(values))

def rms_norm(values, scales):
    return values * lax.rsqrt(lax.optimization_barrier(jnp.mean(values * values, axis=-1, keepdims=True)) + EPS) * scales

def rotary(values, cosine, sine_part):
    half_width = values.shape[-1] // 2
    front_part = values[..., :half_width]
    back_part = values[..., half_width:]
    cos_wide = cosine[..., None, :]
    sin_wide = sine_part[..., None, :]
    return jnp.concatenate([front_part * cos_wide - back_part * sin_wide, back_part * cos_wide + front_part * sin_wide], axis=-1)

def tables(positions, head_width):
    half_width = head_width // 2
    inverse = THETA ** (-(jnp.arange(half_width, dtype=jnp.float32) * 2.0 / head_width))
    angles = positions.astype(jnp.float32)[..., None] * inverse
    return (jnp.cos(angles), jnp.sin(angles))

def positions_of(lengths):
    end_points = jnp.cumsum(lengths, axis=1).astype(jnp.int32)
    starts = end_points - lengths
    indices = jnp.arange(ROW, dtype=jnp.int32)
    segment = lax.optimization_barrier(jnp.sum((indices[None, :, None] >= end_points[:, None, :]).astype(jnp.int32), axis=2)).astype(jnp.int32)
    picked = segment[:, :, None] == jnp.arange(NSEG, dtype=jnp.int32)[None, None, :]
    offset = lax.optimization_barrier(jnp.sum(jnp.where(picked, starts[:, None, :], 0), axis=2)).astype(jnp.int32)
    return (segment, indices[None, :] - offset)

def place_pairs(experts, usable):
    onehot = ((experts[..., None] == jnp.arange(EXPERTS, dtype=jnp.int32)) & usable[..., None]).astype(jnp.int32)
    before = jnp.cumsum(onehot, axis=1).astype(jnp.int32) - onehot
    place_rank = lax.optimization_barrier(jnp.sum(before * onehot, axis=2)).astype(jnp.int32)
    kept_pair = usable & (place_rank < CAP)
    return jnp.where(kept_pair, experts * CAP + place_rank, EXPERTS * CAP).astype(jnp.int32)

def attend(pieces):
    queries, key_rows, value_rows, segment, position = pieces
    grouped = queries.reshape(ROW, KV_HEADS, HEADS // KV_HEADS, HEAD_DIM)
    scores = jnp.einsum('qkgd,skd->kgqs', grouped, key_rows, precision=HIGHEST) * HEAD_DIM ** (-0.5)
    scores = low_back(scores)
    allowed = (segment[:, None] == segment[None, :]) & (position[None, :] <= position[:, None])
    scores = jnp.where(allowed, scores, -1e+30)
    prob_full = jax.nn.softmax(scores, axis=-1)
    mixed_heads = jnp.einsum('kgqs,skd->qkgd', low(prob_full), value_rows, precision=HIGHEST)
    return mixed_heads.reshape(ROW, QDIM)

def expert(pieces):
    rows_in, weight = pieces
    gate_up = low_back(jnp.dot(rows_in, weight[:, :2 * FF], preferred_element_type=jnp.float32, precision=HIGHEST))
    active = low(jax.nn.silu(gate_up[:, :FF]) * gate_up[:, FF:])
    result = jnp.dot(active, weight[:, 2 * FF:].T, preferred_element_type=jnp.float32, precision=HIGHEST)
    return rounded(result)

def reference(tokens, cotangent, w_qkv, w_out, w_router, norm_gains, w_expert, lengths, deal, routes):
    pair_count = TOK_DEV * TOPK
    slot_count = EXPERTS * CAP
    segment, position = positions_of(lengths)
    group_ids = jnp.arange(N_DP, dtype=jnp.int32)[:, None]
    row_ids = jnp.broadcast_to(jnp.arange(ROW, dtype=jnp.int32)[None, :], (N_DP, ROW))
    inverse = jnp.zeros((N_DP, ROW), jnp.int32).at[group_ids, deal].set(row_ids)
    seg_dealt = jnp.take_along_axis(segment, deal, axis=1)
    pos_dealt = jnp.take_along_axis(position, deal, axis=1)
    route_dealt = jnp.take_along_axis(routes, deal[:, :, None], axis=1)
    usable = jnp.broadcast_to((seg_dealt != NSEG - 1)[:, :, None], (N_DP, ROW, TOPK)).reshape(DEVICES, pair_count)
    pair_slot = place_pairs(route_dealt.reshape(DEVICES, pair_count), usable)
    device_ids = jnp.arange(DEVICES, dtype=jnp.int32)[:, None]
    pair_ids = jnp.broadcast_to(jnp.arange(pair_count, dtype=jnp.int32)[None, :], (DEVICES, pair_count))
    slot_pair = jnp.full((DEVICES, slot_count + 1), pair_count, jnp.int32).at[device_ids, pair_slot].set(pair_ids)[:, :slot_count]
    slot_token = (slot_pair // TOPK).astype(jnp.int32)
    cosine, sine_part = tables(pos_dealt, HEAD_DIM)

    def forward(inputs, qkv_weight, out_weight, router_weight, gains, expert_weight):
        gain_attn = gains[:D]
        gain_ffn = gains[D:2 * D]
        gain_query = gains[2 * D:2 * D + HEAD_DIM]
        gain_key = gains[2 * D + HEAD_DIM:]
        dealt_in = jnp.take_along_axis(inputs, deal[:, :, None], axis=1)
        normed = low(rms_norm(dealt_in, gain_attn))
        projected = low_back(jnp.einsum('grd,de->gre', normed, qkv_weight, precision=HIGHEST))
        query_raw = projected[:, :, :QDIM].reshape(N_DP, ROW, HEADS, HEAD_DIM)
        key_raw = projected[:, :, QDIM:QDIM + KVDIM].reshape(N_DP, ROW, KV_HEADS, HEAD_DIM)
        value_rows = low(projected[:, :, QDIM + KVDIM:].reshape(N_DP, ROW, KV_HEADS, HEAD_DIM))
        queries = rounded(rotary(rms_norm(query_raw, gain_query), cosine, sine_part))
        key_rows = rounded(rotary(rms_norm(key_raw, gain_key), cosine, sine_part))
        mixed = rounded(lax.map(jax.checkpoint(attend), (queries, key_rows, value_rows, seg_dealt, pos_dealt)))
        residual = dealt_in + low_back(jnp.einsum('grq,qd->grd', mixed, out_weight, precision=HIGHEST))
        hidden = low(rms_norm(residual, gain_ffn))
        logits = low_back(jnp.einsum('grd,de->gre', hidden, router_weight, precision=HIGHEST))
        gate_probs = jax.nn.softmax(jnp.take_along_axis(logits, route_dealt, axis=2), axis=-1)
        per_device = jnp.concatenate([hidden.reshape(DEVICES, TOK_DEV, D), jnp.zeros((DEVICES, 1, D), jnp.float32)], axis=1)
        dispatched = low_back(jnp.take_along_axis(per_device, slot_token[:, :, None], axis=1))
        by_expert = dispatched.reshape(DEVICES, EXPERTS, CAP, D).transpose(1, 0, 2, 3).reshape(EXPERTS, DEVICES * CAP, D)
        expert_out = lax.map(jax.checkpoint(expert), (by_expert, expert_weight))
        by_source = expert_out.reshape(EXPERTS, DEVICES, CAP, D).transpose(1, 0, 2, 3).reshape(DEVICES, slot_count, D)
        padded = jnp.concatenate([by_source, jnp.zeros((DEVICES, 1, D), jnp.float32)], axis=1)
        pair_out = jnp.take_along_axis(padded, pair_slot[:, :, None], axis=1).reshape(N_DP, ROW, TOPK, D)
        final_rows = residual + lax.optimization_barrier(jnp.sum(gate_probs[..., None] * pair_out, axis=2))
        return jnp.take_along_axis(final_rows, inverse[:, :, None], axis=1)
    inputs = tokens.astype(jnp.float32).reshape(N_DP, ROW, D)
    layer_out, pullback = jax.vjp(forward, inputs, w_qkv.astype(jnp.float32), w_out.astype(jnp.float32), w_router.astype(jnp.float32), norm_gains.astype(jnp.float32), w_expert.astype(jnp.float32))
    grad_list = pullback(cotangent.astype(jnp.float32).reshape(N_DP, ROW, D))
    return (layer_out.reshape(TOKENS, D).astype(jnp.bfloat16), grad_list[0].reshape(TOKENS, D).astype(jnp.bfloat16), grad_list[1], grad_list[2], grad_list[3], grad_list[4], grad_list[5])
```

```python
import jax
import jax.numpy as jnp
from jax import lax
from jax.sharding import Mesh
from jax.sharding import PartitionSpec as P

D = 2048
HEADS = 32
KV_HEADS = 4
HEAD_DIM = 128
FF = 768
TOPK = 8
NSEG = 4
TOK_DEV = 128
ROW = 256
QDIM = 4096
KVDIM = 512
NEAR = 2
CORES = 2
LANES = 128

EPS = 1e-06
THETA = 1000000.0
BF = jnp.bfloat16
F32 = jnp.float32

FAR_AXIS = "far"
NEAR_AXIS = "near"
CORE_AXIS = "core"
SEQ_AXIS = "seq"
HEAD_AXES = (NEAR_AXIS, SEQ_AXIS)
ALL_AXES = (FAR_AXIS, NEAR_AXIS, CORE_AXIS, SEQ_AXIS)
DP_AXES = (FAR_AXIS, NEAR_AXIS, CORE_AXIS)


def rms_norm(values, scales):
    return values * lax.rsqrt(jnp.mean(values * values, axis=-1, keepdims=True) + EPS) * scales


def rotary(values, cosine, sine_part):
    half_width = values.shape[-1] // 2
    front_part = values[..., :half_width]
    back_part = values[..., half_width:]
    cos_wide = cosine[..., None, :]
    sin_wide = sine_part[..., None, :]
    return jnp.concatenate(
        [
            front_part * cos_wide - back_part * sin_wide,
            back_part * cos_wide + front_part * sin_wide,
        ],
        axis=-1,
    )


def tables(positions, head_width):
    half_width = head_width // 2
    inverse = THETA ** (-(jnp.arange(half_width, dtype=F32) * 2.0 / head_width))
    angles = positions.astype(F32)[..., None] * inverse
    return (jnp.cos(angles), jnp.sin(angles))


def dot(left, right, dims):
    return lax.dot_general(left, right, (dims, ((), ())), preferred_element_type=F32)


def mm(left, right):
    return dot(left, right, ((1,), (0,)))


def mm_nt(left, right):
    return dot(left, right, ((1,), (1,)))


def mm_tn(left, right):
    return dot(left, right, ((0,), (0,)))


def swap(value, axis):
    return lax.ppermute(value, axis, [(0, 1), (1, 0)])


def pair_order(own, other, axis):
    first = lax.axis_index(axis) == 0
    return (jnp.where(first, own, other), jnp.where(first, other, own))


def exchange(value, axes):
    return lax.all_to_all(value, axes, split_axis=0, concat_axis=0, tiled=True)


def ring_gather(chunk, axis, count):
    here = lax.axis_index(axis)
    zeros = (0,) * chunk.ndim
    full = jnp.zeros((count,) + chunk.shape, chunk.dtype)
    full = lax.dynamic_update_slice(full, chunk[None], (here,) + zeros)
    for step in range(1, count):
        chunk = lax.ppermute(chunk, axis, [(i, (i + 1) % count) for i in range(count)])
        full = lax.dynamic_update_slice(full, chunk[None], (lax.rem(here + count - step, count),) + zeros)
    return full


def shards(tokens, cotangent, w_qkv, w_out, w_router, norm_gains, w_expert, lengths, deal, routes):
    far_count = lax.axis_size(FAR_AXIS)
    device_count = far_count * NEAR * CORES * 2
    experts_all = w_router.shape[1]
    capacity = TOK_DEV * TOPK // experts_all
    slot_count = experts_all * capacity
    seq_index = lax.axis_index(SEQ_AXIS)
    near_index = lax.axis_index(NEAR_AXIS)
    core_index = lax.axis_index(CORE_AXIS)
    per_group = HEADS // KV_HEADS
    qcols = per_group * HEAD_DIM
    width = qcols + 2 * HEAD_DIM
    qkv_rows = w_qkv.shape[0]
    out_rows = w_out.shape[0]
    gain_rows = norm_gains.shape[0]
    score_scale = HEAD_DIM ** (-0.5)

    router_size = qkv_rows * experts_all
    small_size = router_size + gain_rows
    small_rows = -(-small_size // (8 * LANES)) * 8
    small = jnp.concatenate([w_router.reshape(router_size), norm_gains])
    small = jnp.pad(small, (0, small_rows * LANES - small_size)).reshape(1, small_rows, LANES)
    small_all = exchange(
        jnp.broadcast_to(small, (device_count, small_rows, LANES)), ALL_AXES
    ).reshape(device_count, small_rows * LANES)
    router_full = small_all[:, :router_size].reshape(D, experts_all)
    gains_float = small_all[:, router_size:small_size].reshape(-1).astype(F32)
    gain_attn = gains_float[:D]
    gain_ffn = gains_float[D : 2 * D]
    gain_query = gains_float[2 * D : 2 * D + HEAD_DIM]
    gain_key = gains_float[2 * D + HEAD_DIM :]

    tokens_pair = jnp.concatenate(pair_order(tokens, swap(tokens, SEQ_AXIS), SEQ_AXIS), axis=0)
    tokens_both = jnp.stack(pair_order(tokens_pair, swap(tokens_pair, NEAR_AXIS), NEAR_AXIS))
    table = jnp.concatenate([deal, jnp.pad(lengths, ((0, 0), (0, LANES - NSEG)))], axis=1)
    table_both = jnp.concatenate(pair_order(table, swap(table, NEAR_AXIS), NEAR_AXIS), axis=0)
    deal_both = table_both[:, :ROW]
    ends = jnp.cumsum(table_both[:, ROW : ROW + NSEG], axis=1)
    starts = ends - table_both[:, ROW : ROW + NSEG]
    seg_both = jnp.sum((deal_both[:, :, None] >= ends[:, None, :]).astype(jnp.int32), axis=2)
    picked = seg_both[:, :, None] == jnp.arange(NSEG, dtype=jnp.int32)[None, None, :]
    pos_both = deal_both - jnp.sum(jnp.where(picked, starts[:, None, :], 0), axis=2)
    dealt_hot = (deal_both[:, :, None] == jnp.arange(ROW, dtype=jnp.int32)[None, None, :]).astype(BF)
    hot_mine = lax.dynamic_index_in_dim(dealt_hot, near_index, 0, keepdims=False)
    hot_half = lax.dynamic_slice_in_dim(hot_mine, seq_index * TOK_DEV, TOK_DEV, axis=0)
    back_half = lax.dynamic_slice_in_dim(hot_mine, seq_index * TOK_DEV, TOK_DEV, axis=1)
    seg_mine = lax.dynamic_slice_in_dim(
        lax.dynamic_index_in_dim(seg_both, near_index, 0, keepdims=False), seq_index * TOK_DEV, TOK_DEV
    )

    expert_ids = jnp.arange(experts_all, dtype=jnp.int32)
    chosen_rows = jnp.sum(
        (routes[0][:, :, None] == expert_ids[None, None, :]).astype(jnp.int32), axis=1
    ).astype(BF)
    chosen = mm(hot_half, chosen_rows)
    live = jnp.where((seg_mine != NSEG - 1)[:, None], chosen, 0.0)
    steps = jnp.arange(TOK_DEV, dtype=jnp.int32)
    earlier = (steps[None, :] < steps[:, None]).astype(BF)
    place = mm(earlier, live.astype(BF))
    place = jnp.where(live > 0.5, place, -1.0).astype(jnp.int32)
    slot_hot = place.T[:, None, :] == jnp.arange(capacity, dtype=jnp.int32)[None, :, None]
    slot_low = slot_hot.astype(BF).reshape(slot_count, TOK_DEV)

    cot_pair = jnp.concatenate(pair_order(cotangent, swap(cotangent, SEQ_AXIS), SEQ_AXIS), axis=0)
    cot_low = mm(hot_half, cot_pair).astype(BF)
    cot_rows = cot_low.astype(F32)
    cot_sent = mm(slot_low, cot_low).astype(BF).reshape(experts_all, capacity, D)
    cot_back = exchange(cot_sent, ALL_AXES).reshape(slot_count, D)

    wide = jnp.concatenate(
        [
            w_qkv[:, :QDIM].reshape(qkv_rows, KV_HEADS, qcols),
            w_qkv[:, QDIM : QDIM + KVDIM].reshape(qkv_rows, KV_HEADS, HEAD_DIM),
            w_qkv[:, QDIM + KVDIM :].reshape(qkv_rows, KV_HEADS, HEAD_DIM),
        ],
        axis=2,
    ).transpose(1, 0, 2)
    core_rows = KV_HEADS * qkv_rows
    qkv_own = ring_gather(exchange(wide, HEAD_AXES).reshape(core_rows, width), FAR_AXIS, far_count)
    qkv_own = qkv_own.reshape(far_count * core_rows, width)
    qkv_other = swap(qkv_own, CORE_AXIS)

    def split_core(values):
        parts = values.reshape(values.shape[0], far_count * NEAR, CORES, 2 * qkv_rows)
        own = jnp.where(core_index == 0, parts[:, :, 0], parts[:, :, 1])
        other = jnp.where(core_index == 0, parts[:, :, 1], parts[:, :, 0])
        return (own.reshape(values.shape[0], D // 2), other.reshape(values.shape[0], D // 2))

    def join_core(own, other):
        shape = (own.shape[0], far_count * NEAR, 2 * qkv_rows)
        return jnp.stack(
            pair_order(own.reshape(shape), other.reshape(shape), CORE_AXIS), axis=2
        ).reshape(own.shape[0], D)

    out_slabs = ring_gather(w_out, FAR_AXIS, far_count).reshape(
        KV_HEADS, far_count // KV_HEADS * out_rows, D
    )
    out_mates = exchange(out_slabs, HEAD_AXES).reshape(NEAR, 2, far_count // KV_HEADS, out_rows, D)
    out_own = out_mates.transpose(2, 0, 1, 3, 4).reshape(qcols // 2, D)
    out_other = swap(out_own, CORE_AXIS)
    far_part = far_count // KV_HEADS

    def split_heads(values):
        parts = values.reshape(values.shape[0], far_part * NEAR, CORES, 2 * out_rows)
        own = jnp.where(core_index == 0, parts[:, :, 0], parts[:, :, 1])
        other = jnp.where(core_index == 0, parts[:, :, 1], parts[:, :, 0])
        return (own.reshape(values.shape[0], qcols // 2), other.reshape(values.shape[0], qcols // 2))

    def join_heads(own, other):
        shape = (own.shape[0], far_part * NEAR, 2 * out_rows)
        return jnp.stack(
            pair_order(own.reshape(shape), other.reshape(shape), CORE_AXIS), axis=2
        ).reshape(own.shape[0], qcols)

    x_both = lax.dot_general(
        dealt_hot, tokens_both, (((2,), (1,)), ((0,), (0,))), preferred_element_type=F32
    )
    x_rows = lax.dynamic_slice(
        x_both, (near_index, seq_index * TOK_DEV, 0), (1, TOK_DEV, D)
    )[0]
    normed_low = rms_norm(x_both.reshape(2 * ROW, D), gain_attn).astype(BF)
    normed_own, normed_other = split_core(normed_low)
    projected = mm(normed_own, qkv_own) + mm(normed_other, qkv_other)
    cosine, sine_part = tables(pos_both.reshape(2 * ROW), HEAD_DIM)

    def head_piece(proj_qk, scale_query, scale_key):
        query_raw = proj_qk[:, :qcols].reshape(2 * ROW, per_group, HEAD_DIM)
        key_raw = proj_qk[:, qcols:].reshape(2 * ROW, 1, HEAD_DIM)
        return (
            rotary(rms_norm(query_raw, scale_query), cosine, sine_part),
            rotary(rms_norm(key_raw, scale_key), cosine, sine_part),
        )

    (queries, key_rot), head_back = jax.vjp(
        head_piece, projected[:, : qcols + HEAD_DIM], gain_query, gain_key
    )
    query_heads = queries.astype(BF).reshape(2, ROW, per_group, HEAD_DIM)
    key_heads = key_rot.astype(BF).reshape(2, ROW, HEAD_DIM)
    value_heads = projected[:, qcols + HEAD_DIM :].astype(BF).reshape(2, ROW, HEAD_DIM)
    allowed = (seg_both[:, :, None] == seg_both[:, None, :]) & (
        pos_both[:, None, :] <= pos_both[:, :, None]
    )
    scores = (
        jnp.einsum("bqgd,bsd->bgqs", query_heads, key_heads, preferred_element_type=F32) * score_scale
    )
    scores = jnp.where(allowed[:, None], scores, -1e30)
    prob_full = jax.nn.softmax(scores, axis=-1)
    prob_low = prob_full.astype(BF)
    mixed_heads = jnp.einsum("bgqs,bsd->bqgd", prob_low, value_heads, preferred_element_type=F32)
    mixed_low = mixed_heads.astype(BF).reshape(2 * ROW, qcols)
    mixed_own, mixed_other = split_heads(mixed_low)
    out_partial = mm(mixed_own, out_own) + mm(mixed_other, out_other)
    out_parts = exchange(out_partial.astype(BF).reshape(4, TOK_DEV, D), HEAD_AXES)
    residual = x_rows + jnp.sum(out_parts.astype(F32), axis=0)

    normed_two, ffn_back = jax.vjp(rms_norm, residual, gain_ffn)
    ffn_in = normed_two.astype(BF)
    send_rows = mm(slot_low, ffn_in).astype(BF).reshape(experts_all, capacity, D)
    in_flat = exchange(send_rows, ALL_AXES).reshape(slot_count, D)
    logits = mm(ffn_in, router_full)
    logits = jnp.where(chosen > 0.5, logits, -1e30)
    gate_probs = jax.nn.softmax(logits, axis=-1)
    gate_probs = jnp.where(chosen > 0.5, gate_probs, 0.0)
    slot_gate = jnp.sum(jnp.where(slot_hot, gate_probs.T[:, None, :], 0.0), axis=2)
    gate_back = exchange(slot_gate[:, None, :], ALL_AXES).reshape(slot_count, 1)

    expert_weight = w_expert[0]
    gate_up = mm(in_flat, expert_weight[:, : 2 * FF])
    gate_pre = gate_up[:, :FF]
    up_pre = gate_up[:, FF:]
    sig_gate = jax.nn.sigmoid(gate_pre)
    silu_val = gate_pre * sig_gate
    active = (silu_val * up_pre).astype(BF)
    expert_out = mm_nt(active, expert_weight[:, 2 * FF :]).astype(BF)
    cot_float = cot_back.astype(F32)
    slot_dot = jnp.sum(cot_float * expert_out.astype(F32), axis=1)
    dot_back = exchange(slot_dot.reshape(device_count, 1, capacity), ALL_AXES).reshape(
        experts_all, capacity
    )
    grad_flat = (gate_back * cot_float).astype(BF)
    act_grad = mm(grad_flat, expert_weight[:, 2 * FF :])
    silu_slope = sig_gate * (1.0 + gate_pre * (1.0 - sig_gate))
    gu_grad = jnp.concatenate([act_grad * up_pre * silu_slope, act_grad * silu_val], axis=1).astype(BF)
    in_grad = mm_nt(gu_grad, expert_weight[:, : 2 * FF]).astype(BF)
    pair_grads = exchange(in_grad.reshape(device_count, capacity, D), ALL_AXES).reshape(slot_count, D)
    returned = exchange(expert_out.reshape(device_count, capacity, D), ALL_AXES).reshape(slot_count, D)
    grad_expert = jnp.concatenate([mm_tn(in_flat, gu_grad), mm_tn(grad_flat, active)], axis=1)[None]

    gate_grad = jnp.sum(jnp.where(slot_hot, dot_back[:, :, None], 0.0), axis=1).T
    mean_term = jnp.sum(gate_probs * gate_grad, axis=1, keepdims=True)
    logit_grad = (gate_probs * (gate_grad - mean_term)).astype(BF)
    router_grad = mm_tn(ffn_in, logit_grad)
    ffn_in_grad = mm_tn(slot_low, pair_grads) + mm_nt(logit_grad, router_full)
    resid_part, gain_ffn_grad = ffn_back(ffn_in_grad)
    resid_low = (cot_rows + resid_part).astype(BF)
    resid_pair = jnp.concatenate(pair_order(resid_low, swap(resid_low, SEQ_AXIS), SEQ_AXIS), axis=0)
    resid_both = jnp.concatenate(
        pair_order(resid_pair, swap(resid_pair, NEAR_AXIS), NEAR_AXIS), axis=0
    )

    gate_slots = jnp.where(slot_hot, gate_probs.T[:, None, :], 0.0).reshape(slot_count, TOK_DEV)
    gate_high = gate_slots.astype(BF)
    gate_rest = (gate_slots - gate_high.astype(F32)).astype(BF)
    final_rows = (residual + mm_tn(gate_high, returned) + mm_tn(gate_rest, returned)).astype(BF)
    final_pair = jnp.concatenate(
        pair_order(final_rows, swap(final_rows, SEQ_AXIS), SEQ_AXIS), axis=0
    )
    layer_out = mm_tn(back_half, final_pair).astype(BF)

    mixed_grad = join_heads(mm_nt(resid_both, out_own), mm_nt(resid_both, out_other)).astype(BF)
    grad_heads = mixed_grad.reshape(2, ROW, per_group, HEAD_DIM)
    out_grad = mm_tn(mixed_own, resid_both) + swap(
        mm_tn(mixed_other, resid_both).astype(BF), CORE_AXIS
    ).astype(F32)
    out_grad = (
        out_grad.astype(BF)
        .reshape(far_part, NEAR * 2, out_rows, D)
        .transpose(1, 0, 2, 3)
        .reshape(NEAR * 2, far_part * out_rows, D)
    )
    out_grad = exchange(out_grad, HEAD_AXES).reshape(far_count, out_rows, D)
    out_share = jnp.sum(exchange(out_grad, FAR_AXIS).astype(F32), axis=0)

    value_grad = jnp.einsum("bgqs,bqgd->bsd", prob_low, grad_heads, preferred_element_type=F32)
    prob_grad = jnp.einsum("bqgd,bsd->bgqs", grad_heads, value_heads, preferred_element_type=F32)
    score_grad = (
        prob_full * (prob_grad - jnp.sum(prob_full * prob_grad, axis=-1, keepdims=True))
    ).astype(BF)
    query_grad = (
        jnp.einsum("bgqs,bsd->bqgd", score_grad, key_heads, preferred_element_type=F32) * score_scale
    )
    key_grad = (
        jnp.einsum("bgqs,bqgd->bsd", score_grad, query_heads, preferred_element_type=F32) * score_scale
    )
    qk_grad, query_gain_grad, key_gain_grad = head_back(
        (
            query_grad.reshape(2 * ROW, per_group, HEAD_DIM),
            key_grad.reshape(2 * ROW, 1, HEAD_DIM),
        )
    )
    proj_grad = jnp.concatenate([qk_grad, value_grad.reshape(2 * ROW, HEAD_DIM)], axis=1).astype(BF)
    back_grad = lax.dot_general(
        dealt_hot,
        proj_grad.reshape(2, ROW, width),
        (((1,), (1,)), ((0,), (0,))),
        preferred_element_type=F32,
    ).astype(BF).reshape(2 * ROW, width)
    normed_partial = jnp.concatenate(
        [mm_nt(back_grad, qkv_own), mm_nt(back_grad, qkv_other)], axis=1
    ).astype(BF)
    normed_parts = exchange(normed_partial.reshape(4, TOK_DEV, D), HEAD_AXES)
    normed_grad = jnp.sum(normed_parts.astype(F32), axis=0)
    normed_grad = join_core(normed_grad[:, : D // 2], normed_grad[:, D // 2 :])
    _, attn_back = jax.vjp(rms_norm, tokens.astype(F32), gain_attn)
    input_part, gain_attn_grad = attn_back(normed_grad)
    resid_group = lax.dynamic_slice_in_dim(resid_both, near_index * ROW, ROW, axis=0)
    grad_tokens = (mm_tn(back_half, resid_group) + input_part).astype(BF)

    qkv_grad = mm_tn(normed_own, proj_grad) + swap(
        mm_tn(normed_other, proj_grad).astype(BF), CORE_AXIS
    ).astype(F32)
    qkv_grad = exchange(qkv_grad.astype(BF).reshape(far_count, core_rows, width), FAR_AXIS)
    qkv_grad = jnp.sum(qkv_grad.astype(F32), axis=0).astype(BF).reshape(KV_HEADS, qkv_rows, width)
    qkv_grad = exchange(qkv_grad, HEAD_AXES).transpose(1, 0, 2).astype(F32)
    qkv_share = jnp.concatenate(
        [
            qkv_grad[:, :, :qcols].reshape(qkv_rows, QDIM),
            qkv_grad[:, :, qcols : qcols + HEAD_DIM].reshape(qkv_rows, KVDIM),
            qkv_grad[:, :, qcols + HEAD_DIM :].reshape(qkv_rows, KVDIM),
        ],
        axis=1,
    )

    gains_grad = jnp.concatenate([gain_attn_grad, gain_ffn_grad, query_gain_grad, key_gain_grad])
    small_grad = jnp.concatenate(
        [router_grad.reshape(device_count, router_size), gains_grad.reshape(device_count, gain_rows)],
        axis=1,
    )
    small_grad = jnp.pad(small_grad, ((0, 0), (0, small_rows * LANES - small_size)))
    small_share = jnp.sum(
        exchange(small_grad.reshape(device_count, small_rows, LANES), ALL_AXES), axis=0
    ).reshape(small_rows * LANES)
    router_share = small_share[:router_size].reshape(qkv_rows, experts_all)
    gains_share = small_share[router_size:small_size]
    return (layer_out, grad_tokens, qkv_share, out_share, router_share, gains_share, grad_expert)


def solution(mesh):
    shape = dict(mesh.shape)
    inner = Mesh(
        mesh.devices.reshape(shape["dp"] // (NEAR * CORES), NEAR, CORES, shape["seq"]), ALL_AXES
    )
    rows = P(ALL_AXES, None)
    in_specs = (
        rows,
        rows,
        rows,
        rows,
        rows,
        P(ALL_AXES),
        P(ALL_AXES, None, None),
        P(DP_AXES, None),
        P(DP_AXES, None),
        P(DP_AXES, None, None),
    )
    out_specs = (rows, rows, rows, rows, rows, P(ALL_AXES), P(ALL_AXES, None, None))
    return jax.shard_map(shards, mesh=inner, in_specs=in_specs, out_specs=out_specs, check_vma=False)
```

```python
import jax
import jax.numpy as jnp
from jax import lax
from jax.experimental import pallas as pl
from jax.experimental.pallas import tpu as pltpu
from jax.sharding import Mesh
from jax.sharding import PartitionSpec as P

D = 2048
HEADS = 32
KV_HEADS = 4
HEAD_DIM = 128
FF = 768
TOPK = 8
NSEG = 4
TOK_DEV = 128
ROW = 256
QDIM = 4096
KVDIM = 512
NEAR = 2
CORES = 2
LANES = 128

EPS = 1e-06
THETA = 1000000.0
BF = jnp.bfloat16
F32 = jnp.float32

FAR_AXIS = "far"
NEAR_AXIS = "near"
CORE_AXIS = "core"
SEQ_AXIS = "seq"
HEAD_AXES = (NEAR_AXIS, SEQ_AXIS)
ALL_AXES = (FAR_AXIS, NEAR_AXIS, CORE_AXIS, SEQ_AXIS)
DP_AXES = (FAR_AXIS, NEAR_AXIS, CORE_AXIS)


def rms_norm(values, scales):
    return values * lax.rsqrt(jnp.mean(values * values, axis=-1, keepdims=True) + EPS) * scales


def rotary(values, cosine, sine_part):
    half_width = values.shape[-1] // 2
    front_part = values[..., :half_width]
    back_part = values[..., half_width:]
    cos_wide = cosine[..., None, :]
    sin_wide = sine_part[..., None, :]
    return jnp.concatenate(
        [
            front_part * cos_wide - back_part * sin_wide,
            back_part * cos_wide + front_part * sin_wide,
        ],
        axis=-1,
    )


def tables(positions, head_width):
    half_width = head_width // 2
    inverse = THETA ** (-(jnp.arange(half_width, dtype=F32) * 2.0 / head_width))
    angles = positions.astype(F32)[..., None] * inverse
    return (jnp.cos(angles), jnp.sin(angles))


def dot(left, right, dims):
    return lax.dot_general(left, right, (dims, ((), ())), preferred_element_type=F32)


def mm(left, right):
    return dot(left, right, ((1,), (0,)))


def mm_nt(left, right):
    return dot(left, right, ((1,), (1,)))


def mm_tn(left, right):
    return dot(left, right, ((0,), (0,)))


def swap(value, axis):
    return lax.ppermute(value, axis, [(0, 1), (1, 0)])


def pair_order(own, other, axis):
    first = lax.axis_index(axis) == 0
    return (jnp.where(first, own, other), jnp.where(first, other, own))


def exchange(value, axes):
    return lax.all_to_all(value, axes, split_axis=0, concat_axis=0, tiled=True)


def quad_index():
    return lax.axis_index(NEAR_AXIS) * 2 + lax.axis_index(SEQ_AXIS)


def quad_send(parts, step):
    block = lax.dynamic_index_in_dim(parts, lax.bitwise_xor(quad_index(), step), 0, keepdims=False)
    return lax.ppermute(block, HEAD_AXES, [(i, i ^ step) for i in range(4)])


def quad_order(found):
    low = pair_order(found[0], found[1], SEQ_AXIS)
    high = pair_order(found[2], found[3], SEQ_AXIS)
    rows = [pair_order(low[k], high[k], NEAR_AXIS) for k in range(2)]
    return jnp.stack([rows[0][0], rows[1][0], rows[0][1], rows[1][1]])


def quad_gather(value):
    found = [value] + [
        lax.ppermute(value, HEAD_AXES, [(i, i ^ step) for i in range(4)]) for step in range(1, 4)
    ]
    return quad_order(found)


def quad_swap(parts):
    own = lax.dynamic_index_in_dim(parts, quad_index(), 0, keepdims=False)
    return quad_order([own] + [quad_send(parts, step) for step in range(1, 4)])


def quad_sum(parts):
    total = lax.dynamic_index_in_dim(parts, quad_index(), 0, keepdims=False).astype(F32)
    for step in range(1, 4):
        total = total + quad_send(parts, step).astype(F32)
    return total


def far_sum(parts, count):
    here = lax.axis_index(FAR_AXIS)
    total = lax.dynamic_index_in_dim(parts, here, 0, keepdims=False).astype(F32)
    for step in range(1, count):
        block = lax.dynamic_index_in_dim(parts, lax.rem(here + step, count), 0, keepdims=False)
        block = lax.ppermute(block, FAR_AXIS, [(i, (i + step) % count) for i in range(count)])
        total = total + block.astype(F32)
    return total


def ring_gather(chunk, axis, count):
    here = lax.axis_index(axis)
    zeros = (0,) * chunk.ndim
    full = jnp.zeros((count,) + chunk.shape, chunk.dtype)
    full = lax.dynamic_update_slice(full, chunk[None], (here,) + zeros)
    for step in range(1, count):
        chunk = lax.ppermute(chunk, axis, [(i, (i + 1) % count) for i in range(count)])
        full = lax.dynamic_update_slice(full, chunk[None], (lax.rem(here + count - step, count),) + zeros)
    return full


def expert_grad_kernel(in_ref, gu_ref, grad_ref, active_ref, out_ref):
    column = pl.program_id(1)

    @pl.when(column < 2)
    def _():
        out_ref[...] = mm_tn(in_ref[...], gu_ref[...])

    @pl.when(column == 2)
    def _():
        out_ref[...] = mm_tn(grad_ref[...], active_ref[...])


def expert_grads(in_flat, gu_grad, grad_flat, active):
    rows = in_flat.shape[0]
    tile = 512
    return pl.pallas_call(
        expert_grad_kernel,
        grid=(D // tile, 3),
        in_specs=[
            pl.BlockSpec((rows, tile), lambda i, j: (0, i)),
            pl.BlockSpec((rows, FF), lambda i, j: (0, jnp.minimum(j, 1))),
            pl.BlockSpec((rows, tile), lambda i, j: (0, i)),
            pl.BlockSpec((rows, FF), lambda i, j: (0, 0)),
        ],
        out_specs=pl.BlockSpec((tile, FF), lambda i, j: (i, j)),
        out_shape=jax.ShapeDtypeStruct((D, 3 * FF), F32),
        compiler_params=pltpu.CompilerParams(vmem_limit_bytes=48 << 20),
        cost_estimate=pl.CostEstimate(
            flops=2 * rows * D * 3 * FF, bytes_accessed=rows * D * 4 + D * 3 * FF * 4, transcendentals=0
        ),
        name="expert_grads",
    )(in_flat, gu_grad, grad_flat, active)


def shards(tokens, cotangent, w_qkv, w_out, w_router, norm_gains, w_expert, lengths, deal, routes):
    far_count = lax.axis_size(FAR_AXIS)
    device_count = far_count * NEAR * CORES * 2
    experts_all = w_router.shape[1]
    capacity = TOK_DEV * TOPK // experts_all
    slot_count = experts_all * capacity
    seq_index = lax.axis_index(SEQ_AXIS)
    near_index = lax.axis_index(NEAR_AXIS)
    core_index = lax.axis_index(CORE_AXIS)
    per_group = HEADS // KV_HEADS
    qcols = per_group * HEAD_DIM
    width = qcols + 2 * HEAD_DIM
    qkv_rows = w_qkv.shape[0]
    out_rows = w_out.shape[0]
    gain_rows = norm_gains.shape[0]
    score_scale = HEAD_DIM ** (-0.5)

    tokens_both = quad_gather(tokens).reshape(2, ROW, D)
    table = jnp.concatenate([deal, jnp.pad(lengths, ((0, 0), (0, LANES - NSEG)))], axis=1)
    table_both = jnp.concatenate(pair_order(table, swap(table, NEAR_AXIS), NEAR_AXIS), axis=0)
    deal_both = table_both[:, :ROW]
    ends = jnp.cumsum(table_both[:, ROW : ROW + NSEG], axis=1)
    starts = ends - table_both[:, ROW : ROW + NSEG]
    seg_both = jnp.sum((deal_both[:, :, None] >= ends[:, None, :]).astype(jnp.int32), axis=2)
    picked = seg_both[:, :, None] == jnp.arange(NSEG, dtype=jnp.int32)[None, None, :]
    pos_both = deal_both - jnp.sum(jnp.where(picked, starts[:, None, :], 0), axis=2)
    dealt_hot = (deal_both[:, :, None] == jnp.arange(ROW, dtype=jnp.int32)[None, None, :]).astype(BF)
    hot_mine = lax.dynamic_index_in_dim(dealt_hot, near_index, 0, keepdims=False)
    hot_half = lax.dynamic_slice_in_dim(hot_mine, seq_index * TOK_DEV, TOK_DEV, axis=0)
    back_half = lax.dynamic_slice_in_dim(hot_mine, seq_index * TOK_DEV, TOK_DEV, axis=1)
    seg_mine = lax.dynamic_slice_in_dim(
        lax.dynamic_index_in_dim(seg_both, near_index, 0, keepdims=False), seq_index * TOK_DEV, TOK_DEV
    )

    expert_ids = jnp.arange(experts_all, dtype=jnp.int32)
    chosen_rows = jnp.sum(
        (routes[0][:, :, None] == expert_ids[None, None, :]).astype(jnp.int32), axis=1
    ).astype(BF)
    chosen = mm(hot_half, chosen_rows)
    live = jnp.where((seg_mine != NSEG - 1)[:, None], chosen, 0.0)
    steps = jnp.arange(TOK_DEV, dtype=jnp.int32)
    earlier = (steps[None, :] < steps[:, None]).astype(BF)
    place = mm(earlier, live.astype(BF))
    place = jnp.where(live > 0.5, place, -1.0).astype(jnp.int32)
    slot_hot = place.T[:, None, :] == jnp.arange(capacity, dtype=jnp.int32)[None, :, None]
    slot_low = slot_hot.astype(BF).reshape(slot_count, TOK_DEV)

    router_size = qkv_rows * experts_all
    small_size = router_size + gain_rows
    mask_size = capacity * experts_all
    small_rows = -(-(small_size + mask_size) // (8 * LANES)) * 8
    small = jnp.broadcast_to(
        jnp.concatenate([w_router.reshape(router_size), norm_gains]), (device_count, small_size)
    )
    slot_mask = mm(slot_low, chosen.astype(BF)).astype(BF).reshape(device_count, mask_size)
    small = jnp.concatenate([slot_mask, small], axis=1)
    small = jnp.pad(small, ((0, 0), (0, small_rows * LANES - small_size - mask_size)))
    small_all = exchange(small.reshape(device_count, small_rows, LANES), ALL_AXES).reshape(
        device_count, small_rows * LANES
    )
    mask_back = small_all[:, :mask_size].reshape(slot_count, experts_all)
    small_all = small_all[:, mask_size : mask_size + small_size]
    router_full = small_all[:, :router_size].reshape(D, experts_all)
    gains_float = small_all[:, router_size:].reshape(-1).astype(F32)
    gain_attn = gains_float[:D]
    gain_ffn = gains_float[D : 2 * D]
    gain_query = gains_float[2 * D : 2 * D + HEAD_DIM]
    gain_key = gains_float[2 * D + HEAD_DIM :]

    cot_pair = jnp.concatenate(pair_order(cotangent, swap(cotangent, SEQ_AXIS), SEQ_AXIS), axis=0)
    cot_low = mm(hot_half, cot_pair).astype(BF)
    cot_rows = cot_low.astype(F32)
    cot_sent = mm(slot_low, cot_low).astype(BF).reshape(experts_all, capacity, D)
    cot_back = exchange(cot_sent, ALL_AXES).reshape(slot_count, D)

    wide = jnp.concatenate(
        [
            w_qkv[:, :QDIM].reshape(qkv_rows, KV_HEADS, qcols),
            w_qkv[:, QDIM : QDIM + KVDIM].reshape(qkv_rows, KV_HEADS, HEAD_DIM),
            w_qkv[:, QDIM + KVDIM :].reshape(qkv_rows, KV_HEADS, HEAD_DIM),
        ],
        axis=2,
    ).transpose(1, 0, 2)
    core_rows = KV_HEADS * qkv_rows
    half_rows = 2 * qkv_rows
    qkv_own = ring_gather(quad_swap(wide).reshape(core_rows, width), FAR_AXIS, far_count)
    qkv_own = qkv_own.reshape(far_count * NEAR, half_rows, width)
    qkv_mine = jnp.stack(pair_order(qkv_own, swap(qkv_own, CORE_AXIS), CORE_AXIS), axis=1).reshape(
        D, width
    )

    out_slabs = ring_gather(w_out, FAR_AXIS, far_count).reshape(
        KV_HEADS, far_count // KV_HEADS * out_rows, D
    )
    far_part = far_count // KV_HEADS
    out_own = quad_swap(out_slabs).reshape(NEAR * 2, far_part, out_rows, D)
    out_own = out_own.transpose(1, 0, 2, 3).reshape(far_part * NEAR, 2 * out_rows, D)
    out_mine = jnp.stack(pair_order(out_own, swap(out_own, CORE_AXIS), CORE_AXIS), axis=1).reshape(
        qcols, D
    )

    x_both = lax.dot_general(
        dealt_hot, tokens_both, (((2,), (1,)), ((0,), (0,))), preferred_element_type=F32
    )
    x_rows = lax.dynamic_slice(
        x_both, (near_index, seq_index * TOK_DEV, 0), (1, TOK_DEV, D)
    )[0]
    normed_low = rms_norm(x_both.reshape(2 * ROW, D), gain_attn).astype(BF)
    projected = mm(normed_low, qkv_mine)
    cosine, sine_part = tables(pos_both.reshape(2 * ROW), HEAD_DIM)

    def head_piece(proj_qk, scale_query, scale_key):
        query_raw = proj_qk[:, :qcols].reshape(2 * ROW, per_group, HEAD_DIM)
        key_raw = proj_qk[:, qcols:].reshape(2 * ROW, 1, HEAD_DIM)
        return (
            rotary(rms_norm(query_raw, scale_query), cosine, sine_part),
            rotary(rms_norm(key_raw, scale_key), cosine, sine_part),
        )

    (queries, key_rot), head_back = jax.vjp(
        head_piece, projected[:, : qcols + HEAD_DIM], gain_query, gain_key
    )
    query_heads = queries.astype(BF).reshape(2, ROW, per_group, HEAD_DIM)
    key_heads = key_rot.astype(BF).reshape(2, ROW, HEAD_DIM)
    value_heads = projected[:, qcols + HEAD_DIM :].astype(BF).reshape(2, ROW, HEAD_DIM)
    allowed = (seg_both[:, :, None] == seg_both[:, None, :]) & (
        pos_both[:, None, :] <= pos_both[:, :, None]
    )
    scores = (
        jnp.einsum("bqgd,bsd->bgqs", query_heads, key_heads, preferred_element_type=F32) * score_scale
    )
    scores = jnp.where(allowed[:, None], scores, -1e30)
    prob_full = jax.nn.softmax(scores, axis=-1)
    prob_low = prob_full.astype(BF)
    mixed_heads = jnp.einsum("bgqs,bsd->bqgd", prob_low, value_heads, preferred_element_type=F32)
    mixed_low = mixed_heads.astype(BF).reshape(2 * ROW, qcols)
    out_partial = mm(mixed_low, out_mine).astype(BF)
    residual = x_rows + quad_sum(out_partial.reshape(4, TOK_DEV, D))
    residual, cot_back = lax.optimization_barrier((residual, cot_back))

    normed_two, ffn_back = jax.vjp(rms_norm, residual, gain_ffn)
    ffn_in = normed_two.astype(BF)
    send_rows = mm(slot_low, ffn_in).astype(BF).reshape(experts_all, capacity, D)
    in_flat = exchange(send_rows, ALL_AXES).reshape(slot_count, D)
    logits = mm(ffn_in, router_full)
    logits = jnp.where(chosen > 0.5, logits, -1e30)
    gate_probs = jax.nn.softmax(logits, axis=-1)
    gate_probs = jnp.where(chosen > 0.5, gate_probs, 0.0)
    expert_weight = w_expert[0]
    expert_here = (
        (lax.axis_index(FAR_AXIS) * NEAR + near_index) * CORES + core_index
    ) * 2 + seq_index
    slot_logits = jnp.where(mask_back > 0.5, mm(in_flat, router_full), -1e30)
    slot_probs = jnp.where(mask_back > 0.5, jax.nn.softmax(slot_logits, axis=-1), 0.0)
    gate_back = jnp.sum(jnp.where(expert_ids == expert_here, slot_probs, 0.0), axis=1, keepdims=True)
    gate_up = mm(in_flat, expert_weight[:, : 2 * FF])
    gate_pre = gate_up[:, :FF]
    up_pre = gate_up[:, FF:]
    sig_gate = jax.nn.sigmoid(gate_pre)
    silu_val = gate_pre * sig_gate
    active = (silu_val * up_pre).astype(BF)
    expert_out = mm_nt(active, expert_weight[:, 2 * FF :]).astype(BF)
    cot_float = cot_back.astype(F32)
    slot_dot = jnp.sum(cot_float * expert_out.astype(F32), axis=1)
    dot_back = exchange(slot_dot.reshape(device_count, 1, capacity), ALL_AXES).reshape(
        experts_all, capacity
    )
    grad_flat = (gate_back * cot_float).astype(BF)
    act_grad = mm(grad_flat, expert_weight[:, 2 * FF :])
    silu_slope = sig_gate * (1.0 + gate_pre * (1.0 - sig_gate))
    gu_grad = jnp.concatenate([act_grad * up_pre * silu_slope, act_grad * silu_val], axis=1).astype(BF)
    in_grad = mm_nt(gu_grad, expert_weight[:, : 2 * FF]).astype(BF)
    pair_grads = exchange(in_grad.reshape(device_count, capacity, D), ALL_AXES).reshape(slot_count, D)
    returned = exchange(expert_out.reshape(device_count, capacity, D), ALL_AXES).reshape(slot_count, D)
    grad_expert = expert_grads(in_flat, gu_grad, grad_flat, active)[None]

    gate_grad = jnp.sum(jnp.where(slot_hot, dot_back[:, :, None], 0.0), axis=1).T
    mean_term = jnp.sum(gate_probs * gate_grad, axis=1, keepdims=True)
    logit_grad = (gate_probs * (gate_grad - mean_term)).astype(BF)
    router_grad = mm_tn(ffn_in, logit_grad)
    ffn_in_grad = mm_tn(slot_low, pair_grads) + mm_nt(logit_grad, router_full)
    resid_part, gain_ffn_grad = ffn_back(ffn_in_grad)
    resid_low = (cot_rows + resid_part).astype(BF)
    resid_both = quad_gather(resid_low).reshape(2 * ROW, D)

    gate_slots = jnp.where(slot_hot, gate_probs.T[:, None, :], 0.0).reshape(slot_count, TOK_DEV)
    gate_high = gate_slots.astype(BF)
    gate_rest = (gate_slots - gate_high.astype(F32)).astype(BF)
    final_rows = (residual + mm_tn(gate_high, returned) + mm_tn(gate_rest, returned)).astype(BF)
    final_pair = jnp.concatenate(
        pair_order(final_rows, swap(final_rows, SEQ_AXIS), SEQ_AXIS), axis=0
    )
    layer_out = mm_tn(back_half, final_pair).astype(BF)

    def core_sum(values):
        own, other = pair_order(values[:, 0], values[:, 1], CORE_AXIS)
        return own.astype(F32) + swap(other, CORE_AXIS).astype(F32)

    mixed_grad = mm_nt(resid_both, out_mine).astype(BF)
    grad_heads = mixed_grad.reshape(2, ROW, per_group, HEAD_DIM)
    out_grad = mm_tn(mixed_low, resid_both).astype(BF)
    out_grad = core_sum(out_grad.reshape(far_part * NEAR, CORES, 2 * out_rows, D))
    out_grad = (
        out_grad.astype(BF)
        .reshape(far_part, NEAR * 2, out_rows, D)
        .transpose(1, 0, 2, 3)
        .reshape(NEAR * 2, far_part * out_rows, D)
    )
    out_grad = quad_swap(out_grad).reshape(far_count, out_rows, D)
    out_share = far_sum(out_grad, far_count)

    value_grad = jnp.einsum("bgqs,bqgd->bsd", prob_low, grad_heads, preferred_element_type=F32)
    prob_grad = jnp.einsum("bqgd,bsd->bgqs", grad_heads, value_heads, preferred_element_type=F32)
    score_grad = (
        prob_full * (prob_grad - jnp.sum(prob_full * prob_grad, axis=-1, keepdims=True))
    ).astype(BF)
    query_grad = (
        jnp.einsum("bgqs,bsd->bqgd", score_grad, key_heads, preferred_element_type=F32) * score_scale
    )
    key_grad = (
        jnp.einsum("bgqs,bqgd->bsd", score_grad, query_heads, preferred_element_type=F32) * score_scale
    )
    qk_grad, query_gain_grad, key_gain_grad = head_back(
        (
            query_grad.reshape(2 * ROW, per_group, HEAD_DIM),
            key_grad.reshape(2 * ROW, 1, HEAD_DIM),
        )
    )
    proj_grad = jnp.concatenate([qk_grad, value_grad.reshape(2 * ROW, HEAD_DIM)], axis=1).astype(BF)
    back_grad = lax.dot_general(
        dealt_hot,
        proj_grad.reshape(2, ROW, width),
        (((1,), (1,)), ((0,), (0,))),
        preferred_element_type=F32,
    ).astype(BF).reshape(2 * ROW, width)
    normed_partial = mm_nt(back_grad, qkv_mine).astype(BF)
    normed_grad = quad_sum(normed_partial.reshape(4, TOK_DEV, D))
    _, attn_back = jax.vjp(rms_norm, tokens.astype(F32), gain_attn)
    input_part, gain_attn_grad = attn_back(normed_grad)
    resid_group = lax.dynamic_slice_in_dim(resid_both, near_index * ROW, ROW, axis=0)
    grad_tokens = (mm_tn(back_half, resid_group) + input_part).astype(BF)

    qkv_grad = mm_tn(normed_low, proj_grad).astype(BF)
    qkv_grad = core_sum(qkv_grad.reshape(far_count * NEAR, CORES, half_rows, width))
    qkv_grad = far_sum(qkv_grad.astype(BF).reshape(far_count, core_rows, width), far_count)
    qkv_grad = quad_swap(qkv_grad.astype(BF).reshape(KV_HEADS, qkv_rows, width))
    qkv_grad = qkv_grad.transpose(1, 0, 2).astype(F32)
    qkv_share = jnp.concatenate(
        [
            qkv_grad[:, :, :qcols].reshape(qkv_rows, QDIM),
            qkv_grad[:, :, qcols : qcols + HEAD_DIM].reshape(qkv_rows, KVDIM),
            qkv_grad[:, :, qcols + HEAD_DIM :].reshape(qkv_rows, KVDIM),
        ],
        axis=1,
    )

    gains_grad = jnp.concatenate([gain_attn_grad, gain_ffn_grad, query_gain_grad, key_gain_grad])
    share_rows = -(-small_size // (8 * LANES)) * 8
    small_grad = jnp.concatenate(
        [router_grad.reshape(device_count, router_size), gains_grad.reshape(device_count, gain_rows)],
        axis=1,
    )
    small_grad = jnp.pad(small_grad, ((0, 0), (0, share_rows * LANES - small_size)))
    small_share = jnp.sum(
        exchange(small_grad.reshape(device_count, share_rows, LANES), ALL_AXES), axis=0
    ).reshape(share_rows * LANES)
    router_share = small_share[:router_size].reshape(qkv_rows, experts_all)
    gains_share = small_share[router_size:small_size]
    return (layer_out, grad_tokens, qkv_share, out_share, router_share, gains_share, grad_expert)


def solution(mesh):
    shape = dict(mesh.shape)
    inner = Mesh(
        mesh.devices.reshape(shape["dp"] // (NEAR * CORES), NEAR, CORES, shape["seq"]), ALL_AXES
    )
    rows = P(ALL_AXES, None)
    in_specs = (
        rows,
        rows,
        rows,
        rows,
        rows,
        P(ALL_AXES),
        P(ALL_AXES, None, None),
        P(DP_AXES, None),
        P(DP_AXES, None),
        P(DP_AXES, None, None),
    )
    out_specs = (rows, rows, rows, rows, rows, P(ALL_AXES), P(ALL_AXES, None, None))
    return jax.shard_map(shards, mesh=inner, in_specs=in_specs, out_specs=out_specs, check_vma=False)
```

```python
import functools

import jax
import jax.numpy as jnp
from jax import lax
from jax.experimental import pallas as pl
from jax.experimental.pallas import tpu as pltpu
from jax.sharding import Mesh
from jax.sharding import PartitionSpec as P

D = 2048
HEADS = 32
KV_HEADS = 4
HEAD_DIM = 128
FF = 768
TOPK = 8
NSEG = 4
TOK_DEV = 128
ROW = 256
QDIM = 4096
KVDIM = 512
NEAR = 2
CORES = 2
LANES = 128

EPS = 1e-06
THETA = 1000000.0
BF = jnp.bfloat16
F32 = jnp.float32

FAR_AXIS = "far"
NEAR_AXIS = "near"
CORE_AXIS = "core"
SEQ_AXIS = "seq"
HEAD_AXES = (NEAR_AXIS, SEQ_AXIS)
ALL_AXES = (FAR_AXIS, NEAR_AXIS, CORE_AXIS, SEQ_AXIS)
DP_AXES = (FAR_AXIS, NEAR_AXIS, CORE_AXIS)


def rms_norm(values, scales):
    return values * lax.rsqrt(jnp.mean(values * values, axis=-1, keepdims=True) + EPS) * scales


def rotary(values, cosine, sine_part):
    half_width = values.shape[-1] // 2
    front_part = values[..., :half_width]
    back_part = values[..., half_width:]
    cos_wide = cosine[..., None, :]
    sin_wide = sine_part[..., None, :]
    return jnp.concatenate(
        [
            front_part * cos_wide - back_part * sin_wide,
            back_part * cos_wide + front_part * sin_wide,
        ],
        axis=-1,
    )


def tables(positions, head_width):
    half_width = head_width // 2
    inverse = THETA ** (-(jnp.arange(half_width, dtype=F32) * 2.0 / head_width))
    angles = positions.astype(F32)[..., None] * inverse
    return (jnp.cos(angles), jnp.sin(angles))


def dot(left, right, dims):
    return lax.dot_general(left, right, (dims, ((), ())), preferred_element_type=F32)


def mm(left, right):
    return dot(left, right, ((1,), (0,)))


def mm_nt(left, right):
    return dot(left, right, ((1,), (1,)))


def mm_tn(left, right):
    return dot(left, right, ((0,), (0,)))


def swap(value, axis):
    return lax.ppermute(value, axis, [(0, 1), (1, 0)])


def pair_order(own, other, axis):
    first = lax.axis_index(axis) == 0
    return (jnp.where(first, own, other), jnp.where(first, other, own))


def exchange(value, axes):
    return lax.all_to_all(value, axes, split_axis=0, concat_axis=0, tiled=True)


def quad_index():
    return lax.axis_index(NEAR_AXIS) * 2 + lax.axis_index(SEQ_AXIS)


def quad_send(parts, step):
    block = lax.dynamic_index_in_dim(parts, lax.bitwise_xor(quad_index(), step), 0, keepdims=False)
    return lax.ppermute(block, HEAD_AXES, [(i, i ^ step) for i in range(4)])


def quad_order(found):
    low = pair_order(found[0], found[1], SEQ_AXIS)
    high = pair_order(found[2], found[3], SEQ_AXIS)
    rows = [pair_order(low[k], high[k], NEAR_AXIS) for k in range(2)]
    return jnp.stack([rows[0][0], rows[1][0], rows[0][1], rows[1][1]])


def quad_gather(value):
    found = [value] + [
        lax.ppermute(value, HEAD_AXES, [(i, i ^ step) for i in range(4)]) for step in range(1, 4)
    ]
    return quad_order(found)


def quad_swap(parts):
    own = lax.dynamic_index_in_dim(parts, quad_index(), 0, keepdims=False)
    return quad_order([own] + [quad_send(parts, step) for step in range(1, 4)])


def quad_sum(parts):
    total = lax.dynamic_index_in_dim(parts, quad_index(), 0, keepdims=False).astype(F32)
    for step in range(1, 4):
        total = total + quad_send(parts, step).astype(F32)
    return total


def far_sum(parts, count):
    here = lax.axis_index(FAR_AXIS)
    total = lax.dynamic_index_in_dim(parts, here, 0, keepdims=False).astype(F32)
    for step in range(1, count):
        block = lax.dynamic_index_in_dim(parts, lax.rem(here + step, count), 0, keepdims=False)
        block = lax.ppermute(block, FAR_AXIS, [(i, (i + step) % count) for i in range(count)])
        total = total + block.astype(F32)
    return total


def ring_gather(chunk, axis, count):
    here = lax.axis_index(axis)
    zeros = (0,) * chunk.ndim
    full = jnp.zeros((count,) + chunk.shape, chunk.dtype)
    full = lax.dynamic_update_slice(full, chunk[None], (here,) + zeros)
    for step in range(1, count):
        chunk = lax.ppermute(chunk, axis, [(i, (i + 1) % count) for i in range(count)])
        full = lax.dynamic_update_slice(full, chunk[None], (lax.rem(here + count - step, count),) + zeros)
    return full


def far_next(value, count):
    return lax.ppermute(value, FAR_AXIS, [(i, (i + 1) % count) for i in range(count)])


def quad_xor(value, step):
    return lax.ppermute(value, HEAD_AXES, [(i, i ^ step) for i in range(4)])


def slab_out(blocks):
    got = [blocks[0]] + [quad_xor(blocks[step], step) for step in range(1, 4)]
    keep = jnp.stack([part[0] for part in got])
    other = swap(jnp.stack([part[1] for part in got]), CORE_AXIS)
    return jnp.stack([keep, other])


def slab_back(blocks):
    other = swap(blocks[1], CORE_AXIS)
    parts = [jnp.stack([blocks[0, step], other[step]]) for step in range(4)]
    return jnp.stack([parts[0]] + [quad_xor(parts[step], step) for step in range(1, 4)])


def ring_reduce(parts, count):
    total = parts[1].astype(BF)
    for step in range(2, count):
        total = (far_next(total, count).astype(F32) + parts[step]).astype(BF)
    return far_next(total, count).astype(F32) + parts[0]


def expert_grad_kernel(count, *refs):
    in_refs, gu_refs = refs[:count], refs[count : 2 * count]
    grad_refs, active_refs = refs[2 * count : 3 * count], refs[3 * count : 4 * count]
    out_ref = refs[4 * count]
    column = pl.program_id(1)

    def total(lefts, rights):
        found = mm_tn(lefts[0][...], rights[0][...])
        for left, right in zip(lefts[1:], rights[1:]):
            found = found + mm_tn(left[...], right[...])
        out_ref[...] = found

    @pl.when(column < 2)
    def _():
        total(in_refs, gu_refs)

    @pl.when(column == 2)
    def _():
        total(grad_refs, active_refs)


def expert_grads(in_rows, gu_grads, grad_rows, actives):
    count = len(in_rows)
    rows = in_rows[0].shape[0]
    tile = 512
    tall = pl.BlockSpec((rows, tile), lambda i, j: (0, i))
    gate_up = pl.BlockSpec((rows, FF), lambda i, j: (0, jnp.minimum(j, 1)))
    whole = pl.BlockSpec((rows, FF), lambda i, j: (0, 0))
    total_rows = rows * count
    return pl.pallas_call(
        functools.partial(expert_grad_kernel, count),
        grid=(D // tile, 3),
        in_specs=[tall] * count + [gate_up] * count + [tall] * count + [whole] * count,
        out_specs=pl.BlockSpec((tile, FF), lambda i, j: (i, j)),
        out_shape=jax.ShapeDtypeStruct((D, 3 * FF), F32),
        compiler_params=pltpu.CompilerParams(vmem_limit_bytes=48 << 20),
        cost_estimate=pl.CostEstimate(
            flops=2 * total_rows * D * 3 * FF,
            bytes_accessed=total_rows * D * 4 + D * 3 * FF * 4,
            transcendentals=0,
        ),
        name="expert_grads",
    )(*in_rows, *gu_grads, *grad_rows, *actives)


def shards(tokens, cotangent, w_qkv, w_out, w_router, norm_gains, w_expert, lengths, deal, routes):
    far_count = lax.axis_size(FAR_AXIS)
    device_count = far_count * NEAR * CORES * 2
    experts_all = w_router.shape[1]
    capacity = TOK_DEV * TOPK // experts_all
    slot_count = experts_all * capacity
    seq_index = lax.axis_index(SEQ_AXIS)
    near_index = lax.axis_index(NEAR_AXIS)
    far_index = lax.axis_index(FAR_AXIS)
    core_index = lax.axis_index(CORE_AXIS)
    per_group = HEADS // KV_HEADS
    qcols = per_group * HEAD_DIM
    width = qcols + 2 * HEAD_DIM
    qkv_rows = w_qkv.shape[0]
    out_rows = w_out.shape[0]
    gain_rows = norm_gains.shape[0]
    score_scale = HEAD_DIM ** (-0.5)

    tokens_both = quad_gather(tokens).reshape(2, ROW, D)
    table = jnp.concatenate([deal, jnp.pad(lengths, ((0, 0), (0, LANES - NSEG)))], axis=1)
    table_both = jnp.concatenate(pair_order(table, swap(table, NEAR_AXIS), NEAR_AXIS), axis=0)
    deal_both = table_both[:, :ROW]
    ends = jnp.cumsum(table_both[:, ROW : ROW + NSEG], axis=1)
    starts = ends - table_both[:, ROW : ROW + NSEG]
    seg_both = jnp.sum((deal_both[:, :, None] >= ends[:, None, :]).astype(jnp.int32), axis=2)
    picked = seg_both[:, :, None] == jnp.arange(NSEG, dtype=jnp.int32)[None, None, :]
    pos_both = deal_both - jnp.sum(jnp.where(picked, starts[:, None, :], 0), axis=2)
    dealt_hot = (deal_both[:, :, None] == jnp.arange(ROW, dtype=jnp.int32)[None, None, :]).astype(BF)
    hot_mine = lax.dynamic_index_in_dim(dealt_hot, near_index, 0, keepdims=False)
    hot_half = lax.dynamic_slice_in_dim(hot_mine, seq_index * TOK_DEV, TOK_DEV, axis=0)
    back_half = lax.dynamic_slice_in_dim(hot_mine, seq_index * TOK_DEV, TOK_DEV, axis=1)
    seg_mine = lax.dynamic_slice_in_dim(
        lax.dynamic_index_in_dim(seg_both, near_index, 0, keepdims=False), seq_index * TOK_DEV, TOK_DEV
    )

    expert_ids = jnp.arange(experts_all, dtype=jnp.int32)
    chosen_rows = jnp.sum(
        (routes[0][:, :, None] == expert_ids[None, None, :]).astype(jnp.int32), axis=1
    ).astype(BF)
    chosen = mm(hot_half, chosen_rows)
    live = jnp.where((seg_mine != NSEG - 1)[:, None], chosen, 0.0)
    steps = jnp.arange(TOK_DEV, dtype=jnp.int32)
    earlier = (steps[None, :] < steps[:, None]).astype(BF)
    place = mm(earlier, live.astype(BF))
    place = jnp.where(live > 0.5, place, -1.0).astype(jnp.int32)
    slot_hot = place.T[:, None, :] == jnp.arange(capacity, dtype=jnp.int32)[None, :, None]
    slot_low = slot_hot.astype(BF).reshape(slot_count, TOK_DEV)

    slab = NEAR * CORES * 2
    slab_index = (near_index * CORES + core_index) * 2 + seq_index
    out_order = jnp.array([0, 2, 1, 3, 4, 6, 5, 7], jnp.int32)
    in_order = jnp.array([0, 1, 4, 5, 2, 3, 6, 7], jnp.int32)
    place_far = ring_gather(place.T.astype(BF), FAR_AXIS, far_count)
    place_slab = jnp.take(
        place_far, far_index * slab + lax.bitwise_xor(out_order, slab_index), axis=1
    ).astype(jnp.int32)
    chunk_slots = []
    for step in range(far_count):
        found = lax.dynamic_index_in_dim(
            place_slab, lax.rem(far_index + far_count - step, far_count), 0, keepdims=False
        )
        found = found[:, None, :] == jnp.arange(capacity, dtype=jnp.int32)[None, :, None]
        chunk_slots.append(found.astype(BF).reshape(slab * capacity, TOK_DEV))
    chunk_steps = jnp.arange(far_count, dtype=jnp.int32)
    source_ids = (
        lax.rem(far_index + far_count - chunk_steps, far_count)[:, None] * slab
        + lax.bitwise_xor(in_order, slab_index)[None, :]
    ).reshape(device_count)
    device_ids = jnp.arange(device_count, dtype=jnp.int32)
    found_at = jnp.sum(
        jnp.where(source_ids[None, :] == device_ids[:, None], device_ids[None, :], 0), axis=1
    )

    def to_blocks(rows):
        return rows.reshape(4, 2, rows.shape[0] // slab, rows.shape[1])


    router_size = qkv_rows * experts_all
    small_size = router_size + gain_rows
    mask_size = capacity * experts_all
    small_rows = -(-(small_size + mask_size) // (8 * LANES)) * 8
    small = jnp.broadcast_to(
        jnp.concatenate([w_router.reshape(router_size), norm_gains]), (device_count, small_size)
    )
    slot_mask = mm(slot_low, chosen.astype(BF)).astype(BF).reshape(device_count, mask_size)
    small = jnp.concatenate([slot_mask, small], axis=1)
    small = jnp.pad(small, ((0, 0), (0, small_rows * LANES - small_size - mask_size)))
    small_all = exchange(small.reshape(device_count, small_rows, LANES), ALL_AXES).reshape(
        device_count, small_rows * LANES
    )
    mask_back = jnp.take(small_all[:, :mask_size], source_ids, axis=0).reshape(
        far_count, slab * capacity, experts_all
    )
    small_all = small_all[:, mask_size : mask_size + small_size]
    router_full = small_all[:, :router_size].reshape(D, experts_all)
    gains_float = small_all[:, router_size:].reshape(-1).astype(F32)
    gain_attn = gains_float[:D]
    gain_ffn = gains_float[D : 2 * D]
    gain_query = gains_float[2 * D : 2 * D + HEAD_DIM]
    gain_key = gains_float[2 * D + HEAD_DIM :]

    cot_pair = jnp.concatenate(pair_order(cotangent, swap(cotangent, SEQ_AXIS), SEQ_AXIS), axis=0)
    cot_low = mm(hot_half, cot_pair).astype(BF)
    cot_rows = cot_low.astype(F32)
    wide = jnp.concatenate(
        [
            w_qkv[:, :QDIM].reshape(qkv_rows, KV_HEADS, qcols),
            w_qkv[:, QDIM : QDIM + KVDIM].reshape(qkv_rows, KV_HEADS, HEAD_DIM),
            w_qkv[:, QDIM + KVDIM :].reshape(qkv_rows, KV_HEADS, HEAD_DIM),
        ],
        axis=2,
    ).transpose(1, 0, 2)
    core_rows = KV_HEADS * qkv_rows
    half_rows = 2 * qkv_rows
    qkv_own = ring_gather(quad_swap(wide).reshape(core_rows, width), FAR_AXIS, far_count)
    qkv_own = qkv_own.reshape(far_count * NEAR, half_rows, width)
    qkv_mine = jnp.stack(pair_order(qkv_own, swap(qkv_own, CORE_AXIS), CORE_AXIS), axis=1).reshape(
        D, width
    )

    w_late, cot_late, _ = lax.optimization_barrier((w_out, cot_low, qkv_own))
    cot_far = [cot_late]
    for step in range(1, far_count):
        cot_far.append(far_next(cot_far[-1], far_count))
    cot_sent = jnp.stack(
        [to_blocks(mm(hot, rows).astype(BF)) for hot, rows in zip(chunk_slots, cot_far)], axis=2
    )
    cot_back = slab_out(cot_sent.reshape(4, 2, far_count * capacity, D)).reshape(
        slab, far_count, capacity, D
    )
    out_slabs = ring_gather(w_late, FAR_AXIS, far_count).reshape(
        KV_HEADS, far_count // KV_HEADS * out_rows, D
    )
    far_part = far_count // KV_HEADS
    out_own = quad_swap(out_slabs).reshape(NEAR * 2, far_part, out_rows, D)
    out_own = out_own.transpose(1, 0, 2, 3).reshape(far_part * NEAR, 2 * out_rows, D)
    out_mine = jnp.stack(pair_order(out_own, swap(out_own, CORE_AXIS), CORE_AXIS), axis=1).reshape(
        qcols, D
    )

    x_both = lax.dot_general(
        dealt_hot, tokens_both, (((2,), (1,)), ((0,), (0,))), preferred_element_type=F32
    )
    x_rows = lax.dynamic_slice(
        x_both, (near_index, seq_index * TOK_DEV, 0), (1, TOK_DEV, D)
    )[0]
    normed_low = rms_norm(x_both.reshape(2 * ROW, D), gain_attn).astype(BF)
    projected = mm(normed_low, qkv_mine)
    cosine, sine_part = tables(pos_both.reshape(2 * ROW), HEAD_DIM)

    def head_piece(proj_qk, scale_query, scale_key):
        query_raw = proj_qk[:, :qcols].reshape(2 * ROW, per_group, HEAD_DIM)
        key_raw = proj_qk[:, qcols:].reshape(2 * ROW, 1, HEAD_DIM)
        return (
            rotary(rms_norm(query_raw, scale_query), cosine, sine_part),
            rotary(rms_norm(key_raw, scale_key), cosine, sine_part),
        )

    (queries, key_rot), head_back = jax.vjp(
        head_piece, projected[:, : qcols + HEAD_DIM], gain_query, gain_key
    )
    query_heads = queries.astype(BF).reshape(2, ROW, per_group, HEAD_DIM)
    key_heads = key_rot.astype(BF).reshape(2, ROW, HEAD_DIM)
    value_heads = projected[:, qcols + HEAD_DIM :].astype(BF).reshape(2, ROW, HEAD_DIM)
    allowed = (seg_both[:, :, None] == seg_both[:, None, :]) & (
        pos_both[:, None, :] <= pos_both[:, :, None]
    )
    scores = (
        jnp.einsum("bqgd,bsd->bgqs", query_heads, key_heads, preferred_element_type=F32) * score_scale
    )
    scores = jnp.where(allowed[:, None], scores, -1e30)
    prob_full = jax.nn.softmax(scores, axis=-1)
    prob_low = prob_full.astype(BF)
    mixed_heads = jnp.einsum("bgqs,bsd->bqgd", prob_low, value_heads, preferred_element_type=F32)
    mixed_low = mixed_heads.astype(BF).reshape(2 * ROW, qcols)
    out_partial = mm(mixed_low, out_mine).astype(BF)
    residual = x_rows + quad_sum(out_partial.reshape(4, TOK_DEV, D))

    normed_two, ffn_back = jax.vjp(rms_norm, residual, gain_ffn)
    ffn_in = normed_two.astype(BF)
    ffn_in, cot_back = lax.optimization_barrier((ffn_in, cot_back))
    logits = mm(ffn_in, router_full)
    logits = jnp.where(chosen > 0.5, logits, -1e30)
    gate_probs = jax.nn.softmax(logits, axis=-1)
    gate_probs = jnp.where(chosen > 0.5, gate_probs, 0.0)

    expert_weight = w_expert[0]
    expert_here = far_index * slab + slab_index
    in_rows, gu_grads, grad_rows, actives, gated_outs, slot_dots, partials = ([] for _ in range(7))
    far_rows = ffn_in
    for step in range(far_count):
        hot = chunk_slots[step]
        in_chunk = slab_out(to_blocks(mm(hot, far_rows).astype(BF))).reshape(slab * capacity, D)
        if step < far_count - 1:
            far_rows = far_next(far_rows, far_count)
        mask = mask_back[step]
        slot_logits = jnp.where(mask > 0.5, mm(in_chunk, router_full), -1e30)
        slot_probs = jnp.where(mask > 0.5, jax.nn.softmax(slot_logits, axis=-1), 0.0)
        gate_slot = jnp.sum(
            jnp.where(expert_ids == expert_here, slot_probs, 0.0), axis=1, keepdims=True
        )
        gate_up = mm(in_chunk, expert_weight[:, : 2 * FF])
        gate_pre = gate_up[:, :FF]
        up_pre = gate_up[:, FF:]
        sig_gate = jax.nn.sigmoid(gate_pre)
        silu_val = gate_pre * sig_gate
        active = (silu_val * up_pre).astype(BF)
        expert_out = mm_nt(active, expert_weight[:, 2 * FF :]).astype(BF).astype(F32)
        cot_float = cot_back[:, step].reshape(slab * capacity, D).astype(F32)
        slot_dots.append(jnp.sum(cot_float * expert_out, axis=1))
        gated_outs.append((gate_slot * expert_out).astype(BF).reshape(2, 4, capacity, D))
        grad_chunk = (gate_slot * cot_float).astype(BF)
        act_grad = mm(grad_chunk, expert_weight[:, 2 * FF :])
        silu_slope = sig_gate * (1.0 + gate_pre * (1.0 - sig_gate))
        gu_grad = jnp.concatenate(
            [act_grad * up_pre * silu_slope, act_grad * silu_val], axis=1
        ).astype(BF)
        in_grad = mm_nt(gu_grad, expert_weight[:, : 2 * FF]).astype(BF)
        back = slab_back(in_grad.reshape(2, 4, capacity, D)).reshape(slab * capacity, D)
        partials.append(mm_tn(hot, back))
        in_rows.append(in_chunk)
        gu_grads.append(gu_grad)
        grad_rows.append(grad_chunk)
        actives.append(active)
    dot_sent = jnp.take(jnp.stack(slot_dots).reshape(device_count, capacity), found_at, axis=0)
    dot_back = exchange(dot_sent[:, None, :], ALL_AXES).reshape(experts_all, capacity)
    from_experts = ring_reduce(partials, far_count)
    grad_expert = expert_grads(in_rows, gu_grads, grad_rows, actives)[None]

    gate_grad = jnp.sum(jnp.where(slot_hot, dot_back[:, :, None], 0.0), axis=1).T
    mean_term = jnp.sum(gate_probs * gate_grad, axis=1, keepdims=True)
    logit_grad = (gate_probs * (gate_grad - mean_term)).astype(BF)
    router_grad = mm_tn(ffn_in, logit_grad)
    ffn_in_grad = from_experts + mm_nt(logit_grad, router_full)
    resid_part, gain_ffn_grad = ffn_back(ffn_in_grad)
    resid_low = (cot_rows + resid_part).astype(BF)

    gated_sent = jnp.stack(gated_outs, axis=2).reshape(2, 4, far_count * capacity, D)
    gated_sent, resid_low = lax.optimization_barrier((gated_sent, resid_low))
    gated_back = slab_back(gated_sent).reshape(slab, far_count, capacity, D)
    out_sum = ring_reduce(
        [
            mm_tn(hot, gated_back[:, step].reshape(slab * capacity, D))
            for step, hot in enumerate(chunk_slots)
        ],
        far_count,
    )
    final_rows = (residual + out_sum).astype(BF)
    final_pair = jnp.concatenate(
        pair_order(final_rows, swap(final_rows, SEQ_AXIS), SEQ_AXIS), axis=0
    )
    layer_out = mm_tn(back_half, final_pair).astype(BF)

    resid_both = quad_gather(resid_low).reshape(2 * ROW, D)

    def core_sum(values):
        own, other = pair_order(values[:, 0], values[:, 1], CORE_AXIS)
        return own.astype(F32) + swap(other, CORE_AXIS).astype(F32)

    mixed_grad = mm_nt(resid_both, out_mine).astype(BF)
    out_grad = mm_tn(mixed_low, resid_both).astype(BF)
    mixed_grad, out_grad = lax.optimization_barrier((mixed_grad, out_grad))
    grad_heads = mixed_grad.reshape(2, ROW, per_group, HEAD_DIM)
    out_grad = core_sum(out_grad.reshape(far_part * NEAR, CORES, 2 * out_rows, D))
    out_grad = (
        out_grad.astype(BF)
        .reshape(far_part, NEAR * 2, out_rows, D)
        .transpose(1, 0, 2, 3)
        .reshape(NEAR * 2, far_part * out_rows, D)
    )
    out_grad = quad_swap(out_grad).reshape(far_count, out_rows, D)
    out_share = far_sum(out_grad, far_count)

    value_grad = jnp.einsum("bgqs,bqgd->bsd", prob_low, grad_heads, preferred_element_type=F32)
    prob_grad = jnp.einsum("bqgd,bsd->bgqs", grad_heads, value_heads, preferred_element_type=F32)
    score_grad = (
        prob_full * (prob_grad - jnp.sum(prob_full * prob_grad, axis=-1, keepdims=True))
    ).astype(BF)
    query_grad = (
        jnp.einsum("bgqs,bsd->bqgd", score_grad, key_heads, preferred_element_type=F32) * score_scale
    )
    key_grad = (
        jnp.einsum("bgqs,bqgd->bsd", score_grad, query_heads, preferred_element_type=F32) * score_scale
    )
    qk_grad, query_gain_grad, key_gain_grad = head_back(
        (
            query_grad.reshape(2 * ROW, per_group, HEAD_DIM),
            key_grad.reshape(2 * ROW, 1, HEAD_DIM),
        )
    )
    proj_grad = jnp.concatenate([qk_grad, value_grad.reshape(2 * ROW, HEAD_DIM)], axis=1).astype(BF)
    back_grad = lax.dot_general(
        dealt_hot,
        proj_grad.reshape(2, ROW, width),
        (((1,), (1,)), ((0,), (0,))),
        preferred_element_type=F32,
    ).astype(BF).reshape(2 * ROW, width)
    normed_partial = mm_nt(back_grad, qkv_mine).astype(BF)
    normed_grad = quad_sum(normed_partial.reshape(4, TOK_DEV, D))
    _, attn_back = jax.vjp(rms_norm, tokens.astype(F32), gain_attn)
    input_part, gain_attn_grad = attn_back(normed_grad)
    resid_group = lax.dynamic_slice_in_dim(resid_both, near_index * ROW, ROW, axis=0)
    grad_tokens = (mm_tn(back_half, resid_group) + input_part).astype(BF)

    qkv_grad = mm_tn(normed_low, proj_grad).astype(BF)
    qkv_grad = core_sum(qkv_grad.reshape(far_count * NEAR, CORES, half_rows, width))
    qkv_grad = far_sum(qkv_grad.astype(BF).reshape(far_count, core_rows, width), far_count)
    qkv_grad = quad_swap(qkv_grad.astype(BF).reshape(KV_HEADS, qkv_rows, width))
    qkv_grad = qkv_grad.transpose(1, 0, 2).astype(F32)
    qkv_share = jnp.concatenate(
        [
            qkv_grad[:, :, :qcols].reshape(qkv_rows, QDIM),
            qkv_grad[:, :, qcols : qcols + HEAD_DIM].reshape(qkv_rows, KVDIM),
            qkv_grad[:, :, qcols + HEAD_DIM :].reshape(qkv_rows, KVDIM),
        ],
        axis=1,
    )

    gains_grad = jnp.concatenate([gain_attn_grad, gain_ffn_grad, query_gain_grad, key_gain_grad])
    share_rows = -(-small_size // (8 * LANES)) * 8
    small_grad = jnp.concatenate(
        [router_grad.reshape(device_count, router_size), gains_grad.reshape(device_count, gain_rows)],
        axis=1,
    )
    small_grad = jnp.pad(small_grad, ((0, 0), (0, share_rows * LANES - small_size)))
    small_share = jnp.sum(
        exchange(small_grad.reshape(device_count, share_rows, LANES), ALL_AXES), axis=0
    ).reshape(share_rows * LANES)
    router_share = small_share[:router_size].reshape(qkv_rows, experts_all)
    gains_share = small_share[router_size:small_size]
    return (layer_out, grad_tokens, qkv_share, out_share, router_share, gains_share, grad_expert)


def solution(mesh):
    shape = dict(mesh.shape)
    inner = Mesh(
        mesh.devices.reshape(shape["dp"] // (NEAR * CORES), NEAR, CORES, shape["seq"]), ALL_AXES
    )
    rows = P(ALL_AXES, None)
    in_specs = (
        rows,
        rows,
        rows,
        rows,
        rows,
        P(ALL_AXES),
        P(ALL_AXES, None, None),
        P(DP_AXES, None),
        P(DP_AXES, None),
        P(DP_AXES, None, None),
    )
    out_specs = (rows, rows, rows, rows, rows, P(ALL_AXES), P(ALL_AXES, None, None))
    return jax.shard_map(shards, mesh=inner, in_specs=in_specs, out_specs=out_specs, check_vma=False)
```

```python
import functools

import jax
import jax.numpy as jnp
from jax import lax
from jax.experimental import pallas as pl
from jax.experimental.pallas import tpu as pltpu
from jax.sharding import Mesh
from jax.sharding import PartitionSpec as P

D = 2048
HEADS = 32
KV_HEADS = 4
HEAD_DIM = 128
FF = 768
TOPK = 8
NSEG = 4
TOK_DEV = 128
ROW = 256
QDIM = 4096
KVDIM = 512
NEAR = 2
CORES = 2
LANES = 128

EPS = 1e-06
THETA = 1000000.0
BF = jnp.bfloat16
F32 = jnp.float32

FAR_AXIS = "far"
NEAR_AXIS = "near"
CORE_AXIS = "core"
SEQ_AXIS = "seq"
HEAD_AXES = (NEAR_AXIS, SEQ_AXIS)
ALL_AXES = (FAR_AXIS, NEAR_AXIS, CORE_AXIS, SEQ_AXIS)
DP_AXES = (FAR_AXIS, NEAR_AXIS, CORE_AXIS)


def rms_norm(values, scales):
    return values * lax.rsqrt(jnp.mean(values * values, axis=-1, keepdims=True) + EPS) * scales


def rotary(values, cosine, sine_part):
    half_width = values.shape[-1] // 2
    front_part = values[..., :half_width]
    back_part = values[..., half_width:]
    cos_wide = cosine[..., None, :]
    sin_wide = sine_part[..., None, :]
    return jnp.concatenate(
        [
            front_part * cos_wide - back_part * sin_wide,
            back_part * cos_wide + front_part * sin_wide,
        ],
        axis=-1,
    )


def tables(positions, head_width):
    half_width = head_width // 2
    inverse = THETA ** (-(jnp.arange(half_width, dtype=F32) * 2.0 / head_width))
    angles = positions.astype(F32)[..., None] * inverse
    return (jnp.cos(angles), jnp.sin(angles))


def dot(left, right, dims):
    return lax.dot_general(left, right, (dims, ((), ())), preferred_element_type=F32)


def mm(left, right):
    return dot(left, right, ((1,), (0,)))


def mm_nt(left, right):
    return dot(left, right, ((1,), (1,)))


def mm_tn(left, right):
    return dot(left, right, ((0,), (0,)))


def swap(value, axis):
    return lax.ppermute(value, axis, [(0, 1), (1, 0)])


def pair_order(own, other, axis):
    first = lax.axis_index(axis) == 0
    return (jnp.where(first, own, other), jnp.where(first, other, own))


def exchange(value, axes):
    return lax.all_to_all(value, axes, split_axis=0, concat_axis=0, tiled=True)


def quad_index():
    return lax.axis_index(NEAR_AXIS) * 2 + lax.axis_index(SEQ_AXIS)


def quad_send(parts, step):
    block = lax.dynamic_index_in_dim(parts, lax.bitwise_xor(quad_index(), step), 0, keepdims=False)
    return lax.ppermute(block, HEAD_AXES, [(i, i ^ step) for i in range(4)])


def quad_order(found):
    low = pair_order(found[0], found[1], SEQ_AXIS)
    high = pair_order(found[2], found[3], SEQ_AXIS)
    rows = [pair_order(low[k], high[k], NEAR_AXIS) for k in range(2)]
    return jnp.stack([rows[0][0], rows[1][0], rows[0][1], rows[1][1]])


def quad_gather(value):
    found = [value] + [
        lax.ppermute(value, HEAD_AXES, [(i, i ^ step) for i in range(4)]) for step in range(1, 4)
    ]
    return quad_order(found)


def quad_swap(parts):
    own = lax.dynamic_index_in_dim(parts, quad_index(), 0, keepdims=False)
    return quad_order([own] + [quad_send(parts, step) for step in range(1, 4)])


def quad_sum(parts):
    total = lax.dynamic_index_in_dim(parts, quad_index(), 0, keepdims=False).astype(F32)
    for step in range(1, 4):
        total = total + quad_send(parts, step).astype(F32)
    return total


def far_sum(parts, count):
    here = lax.axis_index(FAR_AXIS)
    total = lax.dynamic_index_in_dim(parts, here, 0, keepdims=False).astype(F32)
    for step in range(1, count):
        block = lax.dynamic_index_in_dim(parts, lax.rem(here + step, count), 0, keepdims=False)
        block = lax.ppermute(block, FAR_AXIS, [(i, (i + step) % count) for i in range(count)])
        total = total + block.astype(F32)
    return total


def far_all(value, count, first=None):
    ahead = count // 2
    found = [value] + [None] * (count - 1)
    found[1] = far_shift(value, 1, count)
    if count > 2:
        found[count - 1] = far_shift(value, -1, count)
    for step in range(2, ahead + 1):
        found[step] = far_shift(found[step - 1], 1, count)
    for step in range(count - 2, ahead, -1):
        found[step] = far_shift(found[step + 1], -1, count)
    return found


def far_stack(found):
    count = len(found)
    here = lax.axis_index(FAR_AXIS)
    zeros = (0,) * found[0].ndim
    full = jnp.zeros((count,) + found[0].shape, found[0].dtype)
    for step, chunk in enumerate(found):
        full = lax.dynamic_update_slice(full, chunk[None], (lax.rem(here + count - step, count),) + zeros)
    return full


def tie(*values):
    return lax.optimization_barrier(values)


def far_shift(value, step, count):
    return lax.ppermute(value, FAR_AXIS, [(i, (i + step) % count) for i in range(count)])


def far_next(value, count):
    return lax.ppermute(value, FAR_AXIS, [(i, (i + 1) % count) for i in range(count)])


def quad_xor(value, step):
    return lax.ppermute(value, HEAD_AXES, [(i, i ^ step) for i in range(4)])


def slab_out(blocks):
    got = [blocks[0]] + [quad_xor(blocks[step], step) for step in range(1, 4)]
    keep = jnp.stack([part[0] for part in got])
    other = swap(jnp.stack([part[1] for part in got]), CORE_AXIS)
    return jnp.stack([keep, other])


def slab_back(blocks):
    other = swap(blocks[1], CORE_AXIS)
    parts = [jnp.stack([blocks[0, step], other[step]]) for step in range(4)]
    return jnp.stack([parts[0]] + [quad_xor(parts[step], step) for step in range(1, 4)])


def expert_grad_kernel(count, *refs):
    in_refs, gu_refs = refs[:count], refs[count : 2 * count]
    grad_refs, active_refs = refs[2 * count : 3 * count], refs[3 * count : 4 * count]
    out_ref = refs[4 * count]
    column = pl.program_id(1)

    def total(lefts, rights):
        found = mm_tn(lefts[0][...], rights[0][...])
        for left, right in zip(lefts[1:], rights[1:]):
            found = found + mm_tn(left[...], right[...])
        out_ref[...] = found

    @pl.when(column < 2)
    def _():
        total(in_refs, gu_refs)

    @pl.when(column == 2)
    def _():
        total(grad_refs, active_refs)


def expert_grads(in_rows, gu_grads, grad_rows, actives):
    count = len(in_rows)
    rows = in_rows[0].shape[0]
    tile = 512
    tall = pl.BlockSpec((rows, tile), lambda i, j: (0, i))
    gate_up = pl.BlockSpec((rows, FF), lambda i, j: (0, jnp.minimum(j, 1)))
    whole = pl.BlockSpec((rows, FF), lambda i, j: (0, 0))
    total_rows = rows * count
    return pl.pallas_call(
        functools.partial(expert_grad_kernel, count),
        grid=(D // tile, 3),
        in_specs=[tall] * count + [gate_up] * count + [tall] * count + [whole] * count,
        out_specs=pl.BlockSpec((tile, FF), lambda i, j: (i, j)),
        out_shape=jax.ShapeDtypeStruct((D, 3 * FF), F32),
        compiler_params=pltpu.CompilerParams(vmem_limit_bytes=48 << 20),
        cost_estimate=pl.CostEstimate(
            flops=1 << 20,
            bytes_accessed=1 << 20,
            transcendentals=0,
        ),
        name="expert_grads",
    )(*in_rows, *gu_grads, *grad_rows, *actives)


def head_normed(raw, gain_ref):
    scale = lax.rsqrt(jnp.mean(raw * raw, axis=-1, keepdims=True) + EPS)
    normal = raw * scale
    return (normal, scale, normal * gain_ref[...])


def turned(values, cos_ref, sin_ref):
    return values * cos_ref[...] + pltpu.roll(values, HEAD_DIM // 2, 1) * sin_ref[...]


def turned_back(values, cos_ref, sin_ref):
    return values * cos_ref[...] + pltpu.roll(values * sin_ref[...], HEAD_DIM // 2, 1)


def head_probs(query, key, row_ref, start_ref, key_row_ref):
    scores = mm_nt(query, key) * HEAD_DIM ** (-0.5)
    allowed = (key_row_ref[0] <= row_ref[0]) & (key_row_ref[0] >= start_ref[0])
    scores = jnp.where(allowed, scores, -1e30)
    exped = jnp.exp(scores - jnp.max(scores, axis=-1, keepdims=True))
    return exped / jnp.sum(exped, axis=-1, keepdims=True)


def attend_kernel(
    query_ref, key_ref, value_ref, cos_ref, sin_ref, qgain_ref, kgain_ref,
    row_ref, start_ref, key_row_ref, mixed_ref, key_low, value_low,
):
    @pl.when(pl.program_id(1) == 0)
    def _():
        key_low[...] = turned(head_normed(key_ref[...], kgain_ref)[2], cos_ref, sin_ref).astype(BF)
        value_low[...] = value_ref[...].astype(BF)

    query = turned(head_normed(query_ref[...], qgain_ref)[2], cos_ref, sin_ref).astype(BF)
    probs = head_probs(query, key_low[...], row_ref, start_ref, key_row_ref)
    mixed_ref[...] = mm(probs.astype(BF), value_low[...]).astype(BF)


def attend_back_kernel(
    query_ref, key_ref, value_ref, cos_ref, sin_ref, qgain_ref, kgain_ref,
    row_ref, start_ref, key_row_ref, grad_ref,
    query_out, key_out, value_out, qgain_out, kgain_out,
    key_low, value_low, key_total, value_total,
):
    group, head = pl.program_id(0), pl.program_id(1)
    score_scale = HEAD_DIM ** (-0.5)

    @pl.when((group == 0) & (head == 0))
    def _():
        qgain_out[...] = jnp.zeros_like(qgain_out)
        kgain_out[...] = jnp.zeros_like(kgain_out)

    @pl.when(head == 0)
    def _():
        key_low[...] = turned(head_normed(key_ref[...], kgain_ref)[2], cos_ref, sin_ref).astype(BF)
        value_low[...] = value_ref[...].astype(BF)
        key_total[...] = jnp.zeros_like(key_total)
        value_total[...] = jnp.zeros_like(value_total)

    def raw_grad(grad, normal, scale, gain_ref, gain_out):
        grad = turned_back(grad, cos_ref, sin_ref)
        gain_out[...] += jnp.sum(grad * normal, axis=0, keepdims=True)
        grad = grad * gain_ref[...]
        return scale * (grad - normal * jnp.mean(normal * grad, axis=-1, keepdims=True))

    normal, scale, gained = head_normed(query_ref[...], qgain_ref)
    query = turned(gained, cos_ref, sin_ref).astype(BF)
    probs = head_probs(query, key_low[...], row_ref, start_ref, key_row_ref)
    grad = grad_ref[...]
    value_total[...] += mm_tn(probs.astype(BF), grad)
    prob_grad = mm_nt(grad, value_low[...])
    score_grad = (probs * (prob_grad - jnp.sum(probs * prob_grad, axis=-1, keepdims=True))).astype(BF)
    key_total[...] += mm_tn(score_grad, query) * score_scale
    query_grad = mm(score_grad, key_low[...]) * score_scale
    query_out[...] = raw_grad(query_grad, normal, scale, qgain_ref, qgain_out).astype(BF)

    @pl.when(head == pl.num_programs(1) - 1)
    def _():
        key_normal, key_scale, _ = head_normed(key_ref[...], kgain_ref)
        key_out[...] = raw_grad(key_total[...], key_normal, key_scale, kgain_ref, kgain_out).astype(BF)
        value_out[...] = value_total[...].astype(BF)


def attend_specs(heads):
    head = pl.BlockSpec((ROW, HEAD_DIM), lambda b, h: (b, h))
    whole = pl.BlockSpec((ROW, HEAD_DIM), lambda b, h: (b, 0))
    gain = pl.BlockSpec((1, HEAD_DIM), lambda b, h: (0, 0))
    column = pl.BlockSpec((1, ROW, 1), lambda b, h: (b, 0, 0))
    specs = [
        head,
        pl.BlockSpec((ROW, HEAD_DIM), lambda b, h: (b, heads)),
        pl.BlockSpec((ROW, HEAD_DIM), lambda b, h: (b, heads + 1)),
        whole, whole, gain, gain, column, column,
        pl.BlockSpec((1, 1, ROW), lambda b, h: (b, 0, 0)),
    ]
    return (specs, head, whole, gain)


def attend(projected, shared, heads):
    specs, head, _, _ = attend_specs(heads)
    rows = projected.shape[0]
    return pl.pallas_call(
        attend_kernel,
        grid=(rows // ROW, heads),
        in_specs=specs,
        out_specs=head,
        out_shape=jax.ShapeDtypeStruct((rows, heads * HEAD_DIM), BF),
        scratch_shapes=[pltpu.VMEM((ROW, HEAD_DIM), BF)] * 2,
        cost_estimate=pl.CostEstimate(flops=1 << 20, bytes_accessed=1 << 20, transcendentals=0),
        name="attend",
    )(projected, projected, projected, *shared)


def attend_back(projected, shared, grad, heads):
    specs, head, whole, gain = attend_specs(heads)
    rows = projected.shape[0]
    return pl.pallas_call(
        attend_back_kernel,
        grid=(rows // ROW, heads),
        in_specs=specs + [head],
        out_specs=[head, whole, whole, gain, gain],
        out_shape=[
            jax.ShapeDtypeStruct((rows, heads * HEAD_DIM), BF),
            jax.ShapeDtypeStruct((rows, HEAD_DIM), BF),
            jax.ShapeDtypeStruct((rows, HEAD_DIM), BF),
            jax.ShapeDtypeStruct((1, HEAD_DIM), F32),
            jax.ShapeDtypeStruct((1, HEAD_DIM), F32),
        ],
        scratch_shapes=[pltpu.VMEM((ROW, HEAD_DIM), BF)] * 2 + [pltpu.VMEM((ROW, HEAD_DIM), F32)] * 2,
        cost_estimate=pl.CostEstimate(flops=1 << 20, bytes_accessed=1 << 20, transcendentals=0),
        name="attend_back",
    )(projected, projected, projected, *shared, grad)


def shards(tokens, cotangent, w_qkv, w_out, w_router, norm_gains, w_expert, lengths, deal, routes):
    far_count = lax.axis_size(FAR_AXIS)
    device_count = far_count * NEAR * CORES * 2
    experts_all = w_router.shape[1]
    capacity = TOK_DEV * TOPK // experts_all
    slot_count = experts_all * capacity
    seq_index = lax.axis_index(SEQ_AXIS)
    near_index = lax.axis_index(NEAR_AXIS)
    far_index = lax.axis_index(FAR_AXIS)
    core_index = lax.axis_index(CORE_AXIS)
    per_group = HEADS // KV_HEADS
    qcols = per_group * HEAD_DIM
    width = qcols + 2 * HEAD_DIM
    qkv_rows = w_qkv.shape[0]
    out_rows = w_out.shape[0]
    gain_rows = norm_gains.shape[0]
    score_scale = HEAD_DIM ** (-0.5)

    wide = jnp.concatenate(
        [
            w_qkv[:, :QDIM].reshape(qkv_rows, KV_HEADS, qcols),
            w_qkv[:, QDIM : QDIM + KVDIM].reshape(qkv_rows, KV_HEADS, HEAD_DIM),
            w_qkv[:, QDIM + KVDIM :].reshape(qkv_rows, KV_HEADS, HEAD_DIM),
        ],
        axis=2,
    ).transpose(1, 0, 2)
    core_rows = KV_HEADS * qkv_rows
    half_rows = 2 * qkv_rows
    qkv_far = far_all(quad_swap(wide).reshape(core_rows, width), far_count)
    tokens, cotangent, qkv_far[1] = tie(tokens, cotangent, qkv_far[1])

    tokens_both = quad_gather(tokens).reshape(2, ROW, D)
    table = jnp.concatenate([deal, jnp.pad(lengths, ((0, 0), (0, LANES - NSEG)))], axis=1)
    table_both = jnp.concatenate(pair_order(table, swap(table, NEAR_AXIS), NEAR_AXIS), axis=0)
    deal_both = table_both[:, :ROW]
    ends = jnp.cumsum(table_both[:, ROW : ROW + NSEG], axis=1)
    starts = ends - table_both[:, ROW : ROW + NSEG]
    seg_both = jnp.sum((deal_both[:, :, None] >= ends[:, None, :]).astype(jnp.int32), axis=2)
    picked = seg_both[:, :, None] == jnp.arange(NSEG, dtype=jnp.int32)[None, None, :]
    pos_both = deal_both - jnp.sum(jnp.where(picked, starts[:, None, :], 0), axis=2)
    dealt_hot = (deal_both[:, :, None] == jnp.arange(ROW, dtype=jnp.int32)[None, None, :]).astype(BF)
    hot_mine = lax.dynamic_index_in_dim(dealt_hot, near_index, 0, keepdims=False)
    hot_half = lax.dynamic_slice_in_dim(hot_mine, seq_index * TOK_DEV, TOK_DEV, axis=0)
    back_half = lax.dynamic_slice_in_dim(hot_mine, seq_index * TOK_DEV, TOK_DEV, axis=1)
    seg_mine = lax.dynamic_slice_in_dim(
        lax.dynamic_index_in_dim(seg_both, near_index, 0, keepdims=False), seq_index * TOK_DEV, TOK_DEV
    )

    expert_ids = jnp.arange(experts_all, dtype=jnp.int32)
    chosen_rows = jnp.sum(
        (routes[0][:, :, None] == expert_ids[None, None, :]).astype(jnp.int32), axis=1
    ).astype(BF)
    chosen = mm(hot_half, chosen_rows)
    live = jnp.where((seg_mine != NSEG - 1)[:, None], chosen, 0.0)
    steps = jnp.arange(TOK_DEV, dtype=jnp.int32)
    earlier = (steps[None, :] < steps[:, None]).astype(BF)
    place = mm(earlier, live.astype(BF))
    place = jnp.where(live > 0.5, place, -1.0).astype(jnp.int32)
    slot_hot = place.T[:, None, :] == jnp.arange(capacity, dtype=jnp.int32)[None, :, None]
    slot_low = slot_hot.astype(BF).reshape(slot_count, TOK_DEV)

    slab = NEAR * CORES * 2
    slab_index = (near_index * CORES + core_index) * 2 + seq_index
    out_order = jnp.array([0, 2, 1, 3, 4, 6, 5, 7], jnp.int32)
    in_order = jnp.array([0, 1, 4, 5, 2, 3, 6, 7], jnp.int32)
    place_far = far_stack(far_all(place.T.astype(BF), far_count))
    place_slab = jnp.take(
        place_far, far_index * slab + lax.bitwise_xor(out_order, slab_index), axis=1
    ).astype(jnp.int32)
    chunk_slots = []
    for step in range(far_count):
        found = lax.dynamic_index_in_dim(
            place_slab, lax.rem(far_index + far_count - step, far_count), 0, keepdims=False
        )
        found = found[:, None, :] == jnp.arange(capacity, dtype=jnp.int32)[None, :, None]
        chunk_slots.append(found.astype(BF).reshape(slab * capacity, TOK_DEV))
    chunk_steps = jnp.arange(far_count, dtype=jnp.int32)
    source_ids = (
        lax.rem(far_index + far_count - chunk_steps, far_count)[:, None] * slab
        + lax.bitwise_xor(in_order, slab_index)[None, :]
    ).reshape(device_count)
    device_ids = jnp.arange(device_count, dtype=jnp.int32)
    found_at = jnp.sum(
        jnp.where(source_ids[None, :] == device_ids[:, None], device_ids[None, :], 0), axis=1
    )

    def to_blocks(rows):
        return rows.reshape(4, 2, rows.shape[0] // slab, rows.shape[1])


    router_size = qkv_rows * experts_all
    small_size = router_size + gain_rows
    mask_size = capacity * experts_all
    small_rows = -(-(small_size + mask_size) // (8 * LANES)) * 8
    small = jnp.broadcast_to(
        jnp.concatenate([w_router.reshape(router_size), norm_gains]), (device_count, small_size)
    )
    slot_mask = mm(slot_low, chosen.astype(BF)).astype(BF).reshape(device_count, mask_size)
    small = jnp.concatenate([slot_mask, small], axis=1)
    small = jnp.pad(small, ((0, 0), (0, small_rows * LANES - small_size - mask_size)))
    small_all = exchange(small.reshape(device_count, small_rows, LANES), ALL_AXES).reshape(
        device_count, small_rows * LANES
    )
    mask_back = jnp.take(small_all[:, :mask_size], source_ids, axis=0).reshape(
        far_count, slab * capacity, experts_all
    )
    small_all = small_all[:, mask_size : mask_size + small_size]
    router_full = small_all[:, :router_size].reshape(D, experts_all)
    gains_float = small_all[:, router_size:].reshape(-1).astype(F32)
    gain_attn = gains_float[:D]
    gain_ffn = gains_float[D : 2 * D]
    gain_query = gains_float[2 * D : 2 * D + HEAD_DIM]
    gain_key = gains_float[2 * D + HEAD_DIM :]

    cot_pair = jnp.concatenate(pair_order(cotangent, swap(cotangent, SEQ_AXIS), SEQ_AXIS), axis=0)
    cot_low = mm(hot_half, cot_pair).astype(BF)
    cot_rows = cot_low.astype(F32)
    qkv_own = far_stack(qkv_far)
    cot_low, qkv_own = tie(cot_low, qkv_own)
    qkv_own = qkv_own.reshape(far_count * NEAR, half_rows, width)
    qkv_mine = jnp.stack(pair_order(qkv_own, swap(qkv_own, CORE_AXIS), CORE_AXIS), axis=1).reshape(
        D, width
    )

    out_slabs = far_stack(far_all(w_out, far_count)).reshape(
        KV_HEADS, far_count // KV_HEADS * out_rows, D
    )
    far_part = far_count // KV_HEADS
    cot_low, out_slabs = tie(cot_low, out_slabs)
    cot_far = far_all(cot_low, far_count)
    out_own = quad_swap(out_slabs).reshape(NEAR * 2, far_part, out_rows, D)
    out_own = out_own.transpose(1, 0, 2, 3).reshape(far_part * NEAR, 2 * out_rows, D)
    out_mine = jnp.stack(pair_order(out_own, swap(out_own, CORE_AXIS), CORE_AXIS), axis=1).reshape(
        qcols, D
    )

    x_both = lax.dot_general(
        dealt_hot, tokens_both, (((2,), (1,)), ((0,), (0,))), preferred_element_type=F32
    )
    x_rows = lax.dynamic_slice(
        x_both, (near_index, seq_index * TOK_DEV, 0), (1, TOK_DEV, D)
    )[0]
    normed_low = rms_norm(x_both.reshape(2 * ROW, D), gain_attn).astype(BF)
    projected = mm(normed_low, qkv_mine)
    cosine, sine_part = tables(pos_both.reshape(2 * ROW), HEAD_DIM)
    shared = (
        jnp.concatenate([cosine, cosine], axis=1),
        jnp.concatenate([-sine_part, sine_part], axis=1),
        gain_query[None],
        gain_key[None],
        deal_both[:, :, None],
        (deal_both - pos_both)[:, :, None],
        deal_both[:, None, :],
    )
    mixed_low = attend(projected, shared, per_group)
    out_partial = mm(mixed_low, out_mine).astype(BF)
    residual = x_rows + quad_sum(out_partial.reshape(4, TOK_DEV, D))

    normed_two, ffn_back = jax.vjp(rms_norm, residual, gain_ffn)
    ffn_in = normed_two.astype(BF)
    logits = mm(ffn_in, router_full)
    logits = jnp.where(chosen > 0.5, logits, -1e30)
    gate_probs = jax.nn.softmax(logits, axis=-1)
    gate_probs = jnp.where(chosen > 0.5, gate_probs, 0.0)

    expert_weight = w_expert[0]
    expert_here = far_index * slab + slab_index
    in_rows, gu_grads, grad_rows, actives, slot_dots, in_grads, partials = ([] for _ in range(7))
    far_rows = [ffn_in]
    for step in range(1, far_count):
        far_rows.append(far_next(far_rows[-1], far_count))

    def gather(step, source):
        return mm(chunk_slots[step], jnp.concatenate([source, cot_far[step]], axis=1)).astype(BF)

    sent = gather(0, ffn_in)

    def combine(step):
        back = slab_back(in_grads[step].reshape(2, 4, capacity, 2 * D)).reshape(slab * capacity, 2 * D)
        if step + 1 < far_count:
            back, actives[step + 1] = tie(back, actives[step + 1])
        return mm_tn(chunk_slots[step], back)

    for step in range(far_count):
        arrived = slab_out(to_blocks(sent)).reshape(slab * capacity, 2 * D)
        in_chunk, cot_chunk = arrived[:, :D], arrived[:, D:]
        if step + 1 < far_count:
            source = far_rows[step + 1]
            if step > 0:
                source, gu_grads[step - 1] = tie(source, gu_grads[step - 1])
            sent = gather(step + 1, source)
        mask = mask_back[step]
        slot_logits = jnp.where(mask > 0.5, mm(in_chunk, router_full), -1e30)
        slot_probs = jnp.where(mask > 0.5, jax.nn.softmax(slot_logits, axis=-1), 0.0)
        gate_slot = jnp.sum(
            jnp.where(expert_ids == expert_here, slot_probs, 0.0), axis=1, keepdims=True
        )
        gate_up = mm(in_chunk, expert_weight[:, : 2 * FF])
        gate_pre = gate_up[:, :FF]
        up_pre = gate_up[:, FF:]
        sig_gate = jax.nn.sigmoid(gate_pre)
        silu_val = gate_pre * sig_gate
        active = (silu_val * up_pre).astype(BF)
        expert_out = mm_nt(active, expert_weight[:, 2 * FF :]).astype(BF)
        cot_float = cot_chunk.astype(F32)
        slot_dots.append(jnp.sum(cot_float * expert_out.astype(F32), axis=1))
        gated_out = (gate_slot * expert_out.astype(F32)).astype(BF)
        grad_chunk = (gate_slot * cot_float).astype(BF)
        act_grad = mm(grad_chunk, expert_weight[:, 2 * FF :])
        silu_slope = sig_gate * (1.0 + gate_pre * (1.0 - sig_gate))
        gu_grad = jnp.concatenate(
            [act_grad * up_pre * silu_slope, act_grad * silu_val], axis=1
        ).astype(BF)
        in_grad = mm_nt(gu_grad, expert_weight[:, : 2 * FF]).astype(BF)
        in_grads.append(jnp.concatenate([in_grad, gated_out], axis=1))
        in_rows.append(in_chunk)
        gu_grads.append(gu_grad)
        grad_rows.append(grad_chunk)
        actives.append(active)
        if step > 0:
            partials.append(combine(step - 1))
    partials.append(combine(far_count - 1))
    from_experts = partials[0][:, :D]
    for step in range(1, far_count):
        from_experts = from_experts + far_shift(
            partials[step][:, :D].astype(BF), -step, far_count
        ).astype(F32)
    out_parts = [part[:, D:] for part in partials]
    from_experts, *out_parts = tie(from_experts, *out_parts)
    out_sum = out_parts[0]
    for step in range(1, far_count):
        out_sum = out_sum + far_shift(out_parts[step].astype(BF), -step, far_count).astype(F32)
    dot_sent = jnp.take(jnp.stack(slot_dots).reshape(device_count, capacity), found_at, axis=0)
    dot_back = exchange(dot_sent[:, None, :], ALL_AXES).reshape(experts_all, capacity)

    gate_grad = jnp.sum(jnp.where(slot_hot, dot_back[:, :, None], 0.0), axis=1).T
    mean_term = jnp.sum(gate_probs * gate_grad, axis=1, keepdims=True)
    logit_grad = (gate_probs * (gate_grad - mean_term)).astype(BF)
    router_grad = mm_tn(ffn_in, logit_grad)
    ffn_in_grad = from_experts + mm_nt(logit_grad, router_full)
    resid_part, gain_ffn_grad = ffn_back(ffn_in_grad)
    resid_low = (cot_rows + resid_part).astype(BF)

    in_rows[0], resid_low = tie(in_rows[0], resid_low)
    grad_expert = expert_grads(in_rows, gu_grads, grad_rows, actives)[None]

    resid_both, grad_expert = tie(quad_gather(resid_low), grad_expert)
    resid_both = resid_both.reshape(2 * ROW, D)

    def core_sum(values):
        own, other = pair_order(values[:, 0], values[:, 1], CORE_AXIS)
        return own.astype(F32) + swap(other, CORE_AXIS).astype(F32)

    out_grad = mm_tn(mixed_low, resid_both).astype(BF)
    resid_both, out_grad = tie(resid_both, out_grad)
    mixed_grad = mm_nt(resid_both, out_mine).astype(BF)
    out_grad = core_sum(out_grad.reshape(far_part * NEAR, CORES, 2 * out_rows, D))
    mixed_grad, out_grad = tie(mixed_grad, out_grad)
    out_grad = (
        out_grad.astype(BF)
        .reshape(far_part, NEAR * 2, out_rows, D)
        .transpose(1, 0, 2, 3)
        .reshape(NEAR * 2, far_part * out_rows, D)
    )
    out_grad = quad_swap(out_grad).reshape(far_count, out_rows, D)
    query_grad, key_grad, value_grad, query_gain_grad, key_gain_grad = attend_back(
        projected, shared, mixed_grad, per_group
    )
    query_grad, out_grad, out_sum = tie(query_grad, out_grad, out_sum)
    out_share = far_sum(out_grad, far_count)
    proj_grad = jnp.concatenate([query_grad, key_grad, value_grad], axis=1)
    final_rows = (residual + out_sum).astype(BF)
    final_pair = jnp.concatenate(
        pair_order(final_rows, swap(final_rows, SEQ_AXIS), SEQ_AXIS), axis=0
    )
    layer_out = mm_tn(back_half, final_pair).astype(BF)

    back_grad = lax.dot_general(
        dealt_hot,
        proj_grad.reshape(2, ROW, width),
        (((1,), (1,)), ((0,), (0,))),
        preferred_element_type=F32,
    ).astype(BF).reshape(2 * ROW, width)
    qkv_grad = mm_tn(normed_low, proj_grad).astype(BF)
    back_grad, qkv_grad = tie(back_grad, qkv_grad)
    normed_partial = mm_nt(back_grad, qkv_mine).astype(BF)
    normed_grad = quad_sum(normed_partial.reshape(4, TOK_DEV, D))
    _, attn_back = jax.vjp(rms_norm, tokens.astype(F32), gain_attn)
    input_part, gain_attn_grad = attn_back(normed_grad)
    resid_group = lax.dynamic_slice_in_dim(resid_both, near_index * ROW, ROW, axis=0)
    grad_tokens = (mm_tn(back_half, resid_group) + input_part).astype(BF)

    qkv_grad = core_sum(qkv_grad.reshape(far_count * NEAR, CORES, half_rows, width))
    qkv_grad = far_sum(qkv_grad.astype(BF).reshape(far_count, core_rows, width), far_count)
    qkv_grad = quad_swap(qkv_grad.astype(BF).reshape(KV_HEADS, qkv_rows, width))
    qkv_grad = qkv_grad.transpose(1, 0, 2).astype(F32)
    qkv_share = jnp.concatenate(
        [
            qkv_grad[:, :, :qcols].reshape(qkv_rows, QDIM),
            qkv_grad[:, :, qcols : qcols + HEAD_DIM].reshape(qkv_rows, KVDIM),
            qkv_grad[:, :, qcols + HEAD_DIM :].reshape(qkv_rows, KVDIM),
        ],
        axis=1,
    )

    gains_grad = jnp.concatenate(
        [gain_attn_grad, gain_ffn_grad, query_gain_grad[0], key_gain_grad[0]]
    )
    share_rows = -(-small_size // (8 * LANES)) * 8
    small_grad = jnp.concatenate(
        [router_grad.reshape(device_count, router_size), gains_grad.reshape(device_count, gain_rows)],
        axis=1,
    )
    small_grad = jnp.pad(small_grad, ((0, 0), (0, share_rows * LANES - small_size)))
    small_share = jnp.sum(
        exchange(small_grad.reshape(device_count, share_rows, LANES), ALL_AXES), axis=0
    ).reshape(share_rows * LANES)
    router_share = small_share[:router_size].reshape(qkv_rows, experts_all)
    gains_share = small_share[router_size:small_size]
    return (layer_out, grad_tokens, qkv_share, out_share, router_share, gains_share, grad_expert)


def solution(mesh):
    shape = dict(mesh.shape)
    inner = Mesh(
        mesh.devices.reshape(shape["dp"] // (NEAR * CORES), NEAR, CORES, shape["seq"]), ALL_AXES
    )
    rows = P(ALL_AXES, None)
    in_specs = (
        rows,
        rows,
        rows,
        rows,
        rows,
        P(ALL_AXES),
        P(ALL_AXES, None, None),
        P(DP_AXES, None),
        P(DP_AXES, None),
        P(DP_AXES, None, None),
    )
    out_specs = (rows, rows, rows, rows, rows, P(ALL_AXES), P(ALL_AXES, None, None))
    return jax.shard_map(shards, mesh=inner, in_specs=in_specs, out_specs=out_specs, check_vma=False)
```

```python
import functools

import jax
import jax.numpy as jnp
from jax import lax
from jax.experimental import pallas as pl
from jax.experimental.pallas import tpu as pltpu
from jax.sharding import Mesh
from jax.sharding import PartitionSpec as P

D = 2048
HEADS = 32
KV_HEADS = 4
HEAD_DIM = 128
FF = 768
TOPK = 8
NSEG = 4
TOK_DEV = 128
ROW = 256
QDIM = 4096
KVDIM = 512
NEAR = 2
CORES = 2
LANES = 128

EPS = 1e-06
THETA = 1000000.0
BF = jnp.bfloat16
F32 = jnp.float32

FAR_AXIS = "far"
NEAR_AXIS = "near"
CORE_AXIS = "core"
SEQ_AXIS = "seq"
SLAB_AXES = (NEAR_AXIS, CORE_AXIS, SEQ_AXIS)
HEAD_AXES = (NEAR_AXIS, SEQ_AXIS)
ALL_AXES = (FAR_AXIS, NEAR_AXIS, CORE_AXIS, SEQ_AXIS)
DP_AXES = (FAR_AXIS, NEAR_AXIS, CORE_AXIS)


def rms_norm(values, scales):
    return values * lax.rsqrt(jnp.mean(values * values, axis=-1, keepdims=True) + EPS) * scales


def rotary(values, cosine, sine_part):
    half_width = values.shape[-1] // 2
    front_part = values[..., :half_width]
    back_part = values[..., half_width:]
    cos_wide = cosine[..., None, :]
    sin_wide = sine_part[..., None, :]
    return jnp.concatenate(
        [
            front_part * cos_wide - back_part * sin_wide,
            back_part * cos_wide + front_part * sin_wide,
        ],
        axis=-1,
    )


def tables(positions, head_width):
    half_width = head_width // 2
    inverse = THETA ** (-(jnp.arange(half_width, dtype=F32) * 2.0 / head_width))
    angles = positions.astype(F32)[..., None] * inverse
    return (jnp.cos(angles), jnp.sin(angles))


def dot(left, right, dims):
    return lax.dot_general(left, right, (dims, ((), ())), preferred_element_type=F32)


def mm(left, right):
    return dot(left, right, ((1,), (0,)))


def mm_nt(left, right):
    return dot(left, right, ((1,), (1,)))


def mm_tn(left, right):
    return dot(left, right, ((0,), (0,)))


def swap(value, axis):
    return lax.ppermute(value, axis, [(0, 1), (1, 0)])


def pair_order(own, other, axis):
    first = lax.axis_index(axis) == 0
    return (jnp.where(first, own, other), jnp.where(first, other, own))


def exchange(value, axes):
    return lax.all_to_all(value, axes, split_axis=0, concat_axis=0, tiled=True)


def quad_index():
    return lax.axis_index(NEAR_AXIS) * 2 + lax.axis_index(SEQ_AXIS)


def quad_send(parts, step):
    block = lax.dynamic_index_in_dim(parts, lax.bitwise_xor(quad_index(), step), 0, keepdims=False)
    return lax.ppermute(block, HEAD_AXES, [(i, i ^ step) for i in range(4)])


def quad_order(found):
    low = pair_order(found[0], found[1], SEQ_AXIS)
    high = pair_order(found[2], found[3], SEQ_AXIS)
    rows = [pair_order(low[k], high[k], NEAR_AXIS) for k in range(2)]
    return jnp.stack([rows[0][0], rows[1][0], rows[0][1], rows[1][1]])


def quad_gather(value):
    found = [value] + [
        lax.ppermute(value, HEAD_AXES, [(i, i ^ step) for i in range(4)]) for step in range(1, 4)
    ]
    return quad_order(found)


def quad_parts(parts):
    own = lax.dynamic_index_in_dim(parts, quad_index(), 0, keepdims=False)
    return [own] + [quad_send(parts, step) for step in range(1, 4)]


def quad_swap(parts):
    return quad_order(quad_parts(parts))


def quad_sum(parts):
    total = lax.dynamic_index_in_dim(parts, quad_index(), 0, keepdims=False).astype(F32)
    for step in range(1, 4):
        total = total + quad_send(parts, step).astype(F32)
    return total


def far_sum(parts, count):
    total = parts[0].astype(F32)
    if count != 4:
        for step in range(1, count):
            total = total + far_shift(parts[step].astype(BF), -step, count).astype(F32)
        return total
    relay = far_shift(parts[2].astype(BF), -1, count).astype(F32)
    direct = far_shift(parts[3].astype(BF), 1, count).astype(F32)
    relay = far_shift((parts[1].astype(F32) + relay).astype(BF), -1, count)
    return total + direct + relay.astype(F32)


def far_parts(values, count):
    here = lax.axis_index(FAR_AXIS)
    return [
        lax.dynamic_index_in_dim(values, lax.rem(here + count - step, count), 0, keepdims=False)
        for step in range(count)
    ]


def far_all(value, count, first=None):
    ahead = count // 2
    found = [value] + [None] * (count - 1)
    found[1] = far_shift(value, 1, count)
    if count > 2:
        found[count - 1] = far_shift(value, -1, count)
    for step in range(2, ahead + 1):
        found[step] = far_shift(found[step - 1], 1, count)
    for step in range(count - 2, ahead, -1):
        found[step] = far_shift(found[step + 1], -1, count)
    return found


def far_stack(found):
    count = len(found)
    here = lax.axis_index(FAR_AXIS)
    zeros = (0,) * found[0].ndim
    full = jnp.zeros((count,) + found[0].shape, found[0].dtype)
    for step, chunk in enumerate(found):
        full = lax.dynamic_update_slice(full, chunk[None], (lax.rem(here + count - step, count),) + zeros)
    return full


def tie(*values):
    return lax.optimization_barrier(values)


def far_shift(value, step, count):
    return lax.ppermute(value, FAR_AXIS, [(i, (i + step) % count) for i in range(count)])


def far_next(value, count):
    return lax.ppermute(value, FAR_AXIS, [(i, (i + 1) % count) for i in range(count)])


def quad_xor(value, step):
    return lax.ppermute(value, HEAD_AXES, [(i, i ^ step) for i in range(4)])


def slab_out(blocks):
    got = [blocks[0]] + [quad_xor(blocks[step], step) for step in range(1, 4)]
    keep = quad_order([part[0] for part in got])
    other = swap(quad_order([part[1] for part in got]), CORE_AXIS)
    first, second = pair_order(keep, other, CORE_AXIS)
    shape = (NEAR, 2) + keep.shape[1:]
    return jnp.stack([first.reshape(shape), second.reshape(shape)], axis=1)


def expert_kernel(
    here_ref, in_ref, cot_ref, mask_ref, router_ref, gate_ref, up_ref, down_ref,
    gate_grad_ref, up_grad_ref, active_ref, grad_ref, in_grad_ref, gated_ref, dot_ref,
    out_total, in_total, gate_slot,
):
    block = pl.program_id(0)

    @pl.when(block == 0)
    def _():
        chosen = mask_ref[...].astype(F32) > 0.5
        logits = jnp.where(chosen, mm(in_ref[...], router_ref[...]), -1e30)
        exped = jnp.where(chosen, jnp.exp(logits - jnp.max(logits, axis=-1, keepdims=True)), 0.0)
        total = jnp.sum(exped, axis=-1, keepdims=True)
        mine = lax.broadcasted_iota(jnp.int32, exped.shape, 1) == here_ref[0]
        picked = jnp.sum(jnp.where(mine, exped, 0.0), axis=-1, keepdims=True)
        gate = picked / jnp.where(total > 0.0, total, 1.0)
        gate_slot[...] = jnp.broadcast_to(gate, gate_slot.shape)
        grad_ref[...] = (gate * cot_ref[...].astype(F32)).astype(BF)
        out_total[...] = jnp.zeros_like(out_total)
        in_total[...] = jnp.zeros_like(in_total)

    gate_pre = mm(in_ref[...], gate_ref[...])
    up_pre = mm(in_ref[...], up_ref[...])
    act_grad = mm(grad_ref[...], down_ref[...])
    sig_gate = jax.nn.sigmoid(gate_pre)
    silu_val = gate_pre * sig_gate
    active = (silu_val * up_pre).astype(BF)
    silu_slope = sig_gate * (1.0 + gate_pre * (1.0 - sig_gate))
    gate_grad = (act_grad * up_pre * silu_slope).astype(BF)
    up_grad = (act_grad * silu_val).astype(BF)
    active_ref[...] = active
    gate_grad_ref[...] = gate_grad
    up_grad_ref[...] = up_grad
    out_total[...] += mm_nt(active, down_ref[...])
    in_total[...] += mm_nt(gate_grad, gate_ref[...]) + mm_nt(up_grad, up_ref[...])

    @pl.when(block == pl.num_programs(0) - 1)
    def _():
        out = out_total[...].astype(BF).astype(F32)
        dot_ref[...] = jnp.sum(cot_ref[...].astype(F32) * out, axis=-1, keepdims=True)
        gated_ref[...] = (gate_slot[:, :1] * out).astype(BF)
        in_grad_ref[...] = in_total[...].astype(BF)


def expert_chunk(here, in_chunk, cot_chunk, mask, router, weight):
    rows = in_chunk.shape[0]
    tile = 256
    steps = FF // tile
    whole = pl.BlockSpec((rows, D), lambda j, h: (0, 0))
    piece = pl.BlockSpec((rows, tile), lambda j, h: (0, j))
    low = jax.ShapeDtypeStruct((rows, FF), BF)
    wide = jax.ShapeDtypeStruct((rows, D), BF)
    return pl.pallas_call(
        expert_kernel,
        grid_spec=pltpu.PrefetchScalarGridSpec(
            num_scalar_prefetch=1,
            grid=(steps,),
            in_specs=[
                whole,
                whole,
                pl.BlockSpec(mask.shape, lambda j, h: (0, 0)),
                pl.BlockSpec(router.shape, lambda j, h: (0, 0)),
                pl.BlockSpec((D, tile), lambda j, h: (0, j)),
                pl.BlockSpec((D, tile), lambda j, h: (0, steps + j)),
                pl.BlockSpec((D, tile), lambda j, h: (0, 2 * steps + j)),
            ],
            out_specs=[
                piece, piece, piece, whole, whole, whole,
                pl.BlockSpec((rows, 1), lambda j, h: (0, 0)),
            ],
            scratch_shapes=[
                pltpu.VMEM((rows, D), F32),
                pltpu.VMEM((rows, D), F32),
                pltpu.VMEM((rows, LANES), F32),
            ],
        ),
        out_shape=[low, low, low, wide, wide, wide, jax.ShapeDtypeStruct((rows, 1), F32)],
        compiler_params=pltpu.CompilerParams(vmem_limit_bytes=40 << 20),
        cost_estimate=pl.CostEstimate(flops=1 << 20, bytes_accessed=1 << 20, transcendentals=0),
        name="expert_chunk",
    )(here, in_chunk, cot_chunk, mask, router, weight, weight, weight)


def expert_grad_kernel(count, *refs):
    lists = [refs[k * count : (k + 1) * count] for k in range(5)]
    out_ref = refs[5 * count]
    column = pl.program_id(1)

    def total(lefts, rights):
        found = mm_tn(lefts[0][...], rights[0][...])
        for left, right in zip(lefts[1:], rights[1:]):
            found = found + mm_tn(left[...], right[...])
        out_ref[...] = found

    for place, (left, right) in enumerate(((0, 2), (0, 3), (1, 4))):
        pl.when(column == place)(functools.partial(total, lists[left], lists[right]))


def expert_grads(in_rows, grad_rows, gate_grads, up_grads, actives):
    count = len(in_rows)
    rows = in_rows[0].shape[0]
    tile = 512
    tall = pl.BlockSpec((rows, tile), lambda i, j: (0, i))
    whole = pl.BlockSpec((rows, FF), lambda i, j: (0, 0))
    return pl.pallas_call(
        functools.partial(expert_grad_kernel, count),
        grid=(D // tile, 3),
        in_specs=[tall] * (2 * count) + [whole] * (3 * count),
        out_specs=pl.BlockSpec((tile, FF), lambda i, j: (i, j)),
        out_shape=jax.ShapeDtypeStruct((D, 3 * FF), F32),
        compiler_params=pltpu.CompilerParams(vmem_limit_bytes=48 << 20),
        cost_estimate=pl.CostEstimate(flops=1 << 20, bytes_accessed=1 << 20, transcendentals=0),
        name="expert_grads",
    )(*in_rows, *grad_rows, *gate_grads, *up_grads, *actives)


def head_normed(raw, gain_ref):
    scale = lax.rsqrt(jnp.mean(raw * raw, axis=-1, keepdims=True) + EPS)
    normal = raw * scale
    return (normal, scale, normal * gain_ref[...])


def turned(values, cos_ref, sin_ref):
    return values * cos_ref[...] + pltpu.roll(values, HEAD_DIM // 2, 1) * sin_ref[...]


def turned_back(values, cos_ref, sin_ref):
    return values * cos_ref[...] + pltpu.roll(values * sin_ref[...], HEAD_DIM // 2, 1)


def head_probs(query, key, row_ref, start_ref, key_row_ref):
    scores = mm_nt(query, key) * HEAD_DIM ** (-0.5)
    allowed = (key_row_ref[0] <= row_ref[0]) & (key_row_ref[0] >= start_ref[0])
    scores = jnp.where(allowed, scores, -1e30)
    exped = jnp.exp(scores - jnp.max(scores, axis=-1, keepdims=True))
    return exped / jnp.sum(exped, axis=-1, keepdims=True)


def attend_kernel(
    query_ref, key_ref, value_ref, cos_ref, sin_ref, qgain_ref, kgain_ref,
    row_ref, start_ref, key_row_ref, mixed_ref, key_low, value_low,
):
    @pl.when(pl.program_id(1) == 0)
    def _():
        key_low[...] = turned(head_normed(key_ref[...], kgain_ref)[2], cos_ref, sin_ref).astype(BF)
        value_low[...] = value_ref[...].astype(BF)

    query = turned(head_normed(query_ref[...], qgain_ref)[2], cos_ref, sin_ref).astype(BF)
    probs = head_probs(query, key_low[...], row_ref, start_ref, key_row_ref)
    mixed_ref[...] = mm(probs.astype(BF), value_low[...]).astype(BF)


def attend_back_kernel(
    query_ref, key_ref, value_ref, cos_ref, sin_ref, qgain_ref, kgain_ref,
    row_ref, start_ref, key_row_ref, grad_ref,
    query_out, key_out, value_out, qgain_out, kgain_out,
    key_low, value_low, key_total, value_total,
):
    group, head = pl.program_id(0), pl.program_id(1)
    score_scale = HEAD_DIM ** (-0.5)

    @pl.when((group == 0) & (head == 0))
    def _():
        qgain_out[...] = jnp.zeros_like(qgain_out)
        kgain_out[...] = jnp.zeros_like(kgain_out)

    @pl.when(head == 0)
    def _():
        key_low[...] = turned(head_normed(key_ref[...], kgain_ref)[2], cos_ref, sin_ref).astype(BF)
        value_low[...] = value_ref[...].astype(BF)
        key_total[...] = jnp.zeros_like(key_total)
        value_total[...] = jnp.zeros_like(value_total)

    def raw_grad(grad, normal, scale, gain_ref, gain_out):
        grad = turned_back(grad, cos_ref, sin_ref)
        gain_out[...] += jnp.sum(grad * normal, axis=0, keepdims=True)
        grad = grad * gain_ref[...]
        return scale * (grad - normal * jnp.mean(normal * grad, axis=-1, keepdims=True))

    normal, scale, gained = head_normed(query_ref[...], qgain_ref)
    query = turned(gained, cos_ref, sin_ref).astype(BF)
    probs = head_probs(query, key_low[...], row_ref, start_ref, key_row_ref)
    grad = grad_ref[...]
    value_total[...] += mm_tn(probs.astype(BF), grad)
    prob_grad = mm_nt(grad, value_low[...])
    score_grad = (probs * (prob_grad - jnp.sum(probs * prob_grad, axis=-1, keepdims=True))).astype(BF)
    key_total[...] += mm_tn(score_grad, query) * score_scale
    query_grad = mm(score_grad, key_low[...]) * score_scale
    query_out[...] = raw_grad(query_grad, normal, scale, qgain_ref, qgain_out).astype(BF)

    @pl.when(head == pl.num_programs(1) - 1)
    def _():
        key_normal, key_scale, _ = head_normed(key_ref[...], kgain_ref)
        key_out[...] = raw_grad(key_total[...], key_normal, key_scale, kgain_ref, kgain_out).astype(BF)
        value_out[...] = value_total[...].astype(BF)


def attend_specs(heads):
    head = pl.BlockSpec((ROW, HEAD_DIM), lambda b, h: (b, h))
    whole = pl.BlockSpec((ROW, HEAD_DIM), lambda b, h: (b, 0))
    gain = pl.BlockSpec((1, HEAD_DIM), lambda b, h: (0, 0))
    column = pl.BlockSpec((1, ROW, 1), lambda b, h: (b, 0, 0))
    specs = [
        head,
        pl.BlockSpec((ROW, HEAD_DIM), lambda b, h: (b, heads)),
        pl.BlockSpec((ROW, HEAD_DIM), lambda b, h: (b, heads + 1)),
        whole, whole, gain, gain, column, column,
        pl.BlockSpec((1, 1, ROW), lambda b, h: (b, 0, 0)),
    ]
    return (specs, head, whole, gain)


def attend(projected, shared, heads):
    specs, head, _, _ = attend_specs(heads)
    rows = projected.shape[0]
    return pl.pallas_call(
        attend_kernel,
        grid=(rows // ROW, heads),
        in_specs=specs,
        out_specs=head,
        out_shape=jax.ShapeDtypeStruct((rows, heads * HEAD_DIM), BF),
        scratch_shapes=[pltpu.VMEM((ROW, HEAD_DIM), BF)] * 2,
        cost_estimate=pl.CostEstimate(flops=1 << 20, bytes_accessed=1 << 20, transcendentals=0),
        name="attend",
    )(projected, projected, projected, *shared)


def attend_back(projected, shared, grad, heads):
    specs, head, whole, gain = attend_specs(heads)
    rows = projected.shape[0]
    return pl.pallas_call(
        attend_back_kernel,
        grid=(rows // ROW, heads),
        in_specs=specs + [head],
        out_specs=[head, whole, whole, gain, gain],
        out_shape=[
            jax.ShapeDtypeStruct((rows, heads * HEAD_DIM), BF),
            jax.ShapeDtypeStruct((rows, HEAD_DIM), BF),
            jax.ShapeDtypeStruct((rows, HEAD_DIM), BF),
            jax.ShapeDtypeStruct((1, HEAD_DIM), F32),
            jax.ShapeDtypeStruct((1, HEAD_DIM), F32),
        ],
        scratch_shapes=[pltpu.VMEM((ROW, HEAD_DIM), BF)] * 2 + [pltpu.VMEM((ROW, HEAD_DIM), F32)] * 2,
        cost_estimate=pl.CostEstimate(flops=1 << 20, bytes_accessed=1 << 20, transcendentals=0),
        name="attend_back",
    )(projected, projected, projected, *shared, grad)


def shards(tokens, cotangent, w_qkv, w_out, w_router, norm_gains, w_expert, lengths, deal, routes):
    far_count = lax.axis_size(FAR_AXIS)
    device_count = far_count * NEAR * CORES * 2
    experts_all = w_router.shape[1]
    capacity = TOK_DEV * TOPK // experts_all
    slot_count = experts_all * capacity
    seq_index = lax.axis_index(SEQ_AXIS)
    near_index = lax.axis_index(NEAR_AXIS)
    far_index = lax.axis_index(FAR_AXIS)
    core_index = lax.axis_index(CORE_AXIS)
    per_group = HEADS // KV_HEADS
    qcols = per_group * HEAD_DIM
    width = qcols + 2 * HEAD_DIM
    qkv_rows = w_qkv.shape[0]
    out_rows = w_out.shape[0]
    gain_rows = norm_gains.shape[0]
    score_scale = HEAD_DIM ** (-0.5)

    wide = jnp.concatenate(
        [
            w_qkv[:, :QDIM].reshape(qkv_rows, KV_HEADS, qcols),
            w_qkv[:, QDIM : QDIM + KVDIM].reshape(qkv_rows, KV_HEADS, HEAD_DIM),
            w_qkv[:, QDIM + KVDIM :].reshape(qkv_rows, KV_HEADS, HEAD_DIM),
        ],
        axis=2,
    ).transpose(1, 0, 2)
    core_rows = KV_HEADS * qkv_rows
    half_rows = 2 * qkv_rows
    wide_found = quad_parts(wide)
    tokens, *wide_found = tie(tokens, *wide_found)
    qkv_far = far_all(quad_order(wide_found).reshape(core_rows, width), far_count)

    tokens_both = quad_gather(tokens).reshape(2, ROW, D)
    table = jnp.concatenate([deal, jnp.pad(lengths, ((0, 0), (0, LANES - NSEG)))], axis=1)
    table_both = jnp.concatenate(pair_order(table, swap(table, NEAR_AXIS), NEAR_AXIS), axis=0)
    deal_both = table_both[:, :ROW]
    ends = jnp.cumsum(table_both[:, ROW : ROW + NSEG], axis=1)
    starts = ends - table_both[:, ROW : ROW + NSEG]
    seg_both = jnp.sum((deal_both[:, :, None] >= ends[:, None, :]).astype(jnp.int32), axis=2)
    picked = seg_both[:, :, None] == jnp.arange(NSEG, dtype=jnp.int32)[None, None, :]
    pos_both = deal_both - jnp.sum(jnp.where(picked, starts[:, None, :], 0), axis=2)
    dealt_hot = (deal_both[:, :, None] == jnp.arange(ROW, dtype=jnp.int32)[None, None, :]).astype(BF)
    hot_mine = lax.dynamic_index_in_dim(dealt_hot, near_index, 0, keepdims=False)
    hot_half = lax.dynamic_slice_in_dim(hot_mine, seq_index * TOK_DEV, TOK_DEV, axis=0)
    back_half = lax.dynamic_slice_in_dim(hot_mine, seq_index * TOK_DEV, TOK_DEV, axis=1)
    seg_mine = lax.dynamic_slice_in_dim(
        lax.dynamic_index_in_dim(seg_both, near_index, 0, keepdims=False), seq_index * TOK_DEV, TOK_DEV
    )

    expert_ids = jnp.arange(experts_all, dtype=jnp.int32)
    chosen_rows = jnp.sum(
        (routes[0][:, :, None] == expert_ids[None, None, :]).astype(jnp.int32), axis=1
    ).astype(BF)
    chosen = mm(hot_half, chosen_rows)
    live = jnp.where((seg_mine != NSEG - 1)[:, None], chosen, 0.0)
    steps = jnp.arange(TOK_DEV, dtype=jnp.int32)
    earlier = (steps[None, :] < steps[:, None]).astype(BF)
    place = mm(earlier, live.astype(BF))
    place = jnp.where(live > 0.5, place, -1.0).astype(jnp.int32)
    slot_hot = place.T[:, None, :] == jnp.arange(capacity, dtype=jnp.int32)[None, :, None]
    slot_low = slot_hot.astype(BF).reshape(slot_count, TOK_DEV)

    slab = NEAR * CORES * 2
    slab_index = (near_index * CORES + core_index) * 2 + seq_index
    slab_ids = jnp.arange(slab, dtype=jnp.int32)
    out_order = jnp.array([0, 2, 1, 3, 4, 6, 5, 7], jnp.int32)
    place_far = far_stack(far_all(place.T.astype(BF), far_count))

    def slots_of(places, step):
        found = lax.dynamic_index_in_dim(
            places, lax.rem(far_index + far_count - step, far_count), 0, keepdims=False
        )
        found = found[:, None, :] == jnp.arange(capacity, dtype=jnp.int32)[None, :, None]
        return found.astype(BF).reshape(slab * capacity, TOK_DEV)

    place_slab = lax.dynamic_slice_in_dim(place_far, far_index * slab, slab, axis=1).astype(jnp.int32)
    turned_ids = lax.bitwise_xor(out_order, slab_index)
    place_turned = jnp.sum(
        jnp.where(
            (turned_ids[:, None] == slab_ids[None, :])[None, :, :, None], place_slab[:, None], 0
        ),
        axis=2,
    )
    chunk_slots = [slots_of(place_slab, step) for step in range(far_count)]
    send_slots = [slots_of(place_turned, step) for step in range(far_count)]
    chunk_steps = jnp.arange(far_count, dtype=jnp.int32)
    source_ids = (
        lax.rem(far_index + far_count - chunk_steps, far_count)[:, None] * slab + slab_ids[None, :]
    ).reshape(device_count)
    device_ids = jnp.arange(device_count, dtype=jnp.int32)
    found_at = jnp.sum(
        jnp.where(source_ids[None, :] == device_ids[:, None], device_ids[None, :], 0), axis=1
    )

    def to_blocks(rows):
        return rows.reshape(4, 2, rows.shape[0] // slab, rows.shape[1])


    router_size = qkv_rows * experts_all
    small_size = router_size + gain_rows
    mask_size = capacity * experts_all
    small_rows = -(-(small_size + mask_size) // (8 * LANES)) * 8
    small = jnp.broadcast_to(
        jnp.concatenate([w_router.reshape(router_size), norm_gains]), (device_count, small_size)
    )
    slot_mask = mm(slot_low, chosen.astype(BF)).astype(BF).reshape(device_count, mask_size)
    small = jnp.concatenate([slot_mask, small], axis=1)
    small = jnp.pad(small, ((0, 0), (0, small_rows * LANES - small_size - mask_size)))
    small_all = exchange(small.reshape(device_count, small_rows, LANES), ALL_AXES).reshape(
        device_count, small_rows * LANES
    )
    mask_back = jnp.take(small_all[:, :mask_size], source_ids, axis=0).reshape(
        far_count, slab * capacity, experts_all
    )
    small_all = small_all[:, mask_size : mask_size + small_size]
    router_full = small_all[:, :router_size].reshape(D, experts_all)
    gains_float = small_all[:, router_size:].reshape(-1).astype(F32)
    gain_attn = gains_float[:D]
    gain_ffn = gains_float[D : 2 * D]
    gain_query = gains_float[2 * D : 2 * D + HEAD_DIM]
    gain_key = gains_float[2 * D + HEAD_DIM :]

    cot_pair = jnp.concatenate(pair_order(cotangent, swap(cotangent, SEQ_AXIS), SEQ_AXIS), axis=0)
    cot_low = mm(hot_half, cot_pair).astype(BF)
    cot_rows = cot_low.astype(F32)
    cot_low, qkv_far[2] = tie(cot_low, qkv_far[2])
    cot_sent = mm(slot_low, cot_low).astype(BF).reshape(device_count, capacity, D)
    cot_back = [exchange(cot_sent[:, :, : D // 2], ALL_AXES), exchange(cot_sent[:, :, D // 2 :], ALL_AXES)]
    qkv_own = far_stack(qkv_far).reshape(far_count * NEAR, half_rows, width)
    qkv_mine = jnp.stack(pair_order(qkv_own, swap(qkv_own, CORE_AXIS), CORE_AXIS), axis=1).reshape(
        D, width
    )

    out_slabs = far_stack(far_all(w_out, far_count)).reshape(
        KV_HEADS, far_count // KV_HEADS * out_rows, D
    )
    far_part = far_count // KV_HEADS
    x_both = lax.dot_general(
        dealt_hot, tokens_both, (((2,), (1,)), ((0,), (0,))), preferred_element_type=F32
    )
    x_rows = lax.dynamic_slice(
        x_both, (near_index, seq_index * TOK_DEV, 0), (1, TOK_DEV, D)
    )[0]
    normed_low = rms_norm(x_both.reshape(2 * ROW, D), gain_attn).astype(BF)
    projected = mm(normed_low, qkv_mine)
    cosine, sine_part = tables(pos_both.reshape(2 * ROW), HEAD_DIM)
    shared = (
        jnp.concatenate([cosine, cosine], axis=1),
        jnp.concatenate([-sine_part, sine_part], axis=1),
        gain_query[None],
        gain_key[None],
        deal_both[:, :, None],
        (deal_both - pos_both)[:, :, None],
        deal_both[:, None, :],
    )
    mixed_low = attend(projected, shared, per_group)
    out_found = quad_parts(out_slabs)
    mixed_low, cot_back[0], *out_found = tie(mixed_low, cot_back[0], *out_found)
    out_own = quad_order(out_found).reshape(NEAR * 2, far_part, out_rows, D)
    out_own = out_own.transpose(1, 0, 2, 3).reshape(far_part * NEAR, 2 * out_rows, D)
    out_mine = jnp.stack(pair_order(out_own, swap(out_own, CORE_AXIS), CORE_AXIS), axis=1).reshape(
        qcols, D
    )

    out_partial = mm(mixed_low, out_mine).astype(BF)
    residual = x_rows + quad_sum(out_partial.reshape(4, TOK_DEV, D))

    normed_two, ffn_back = jax.vjp(rms_norm, residual, gain_ffn)
    ffn_in = normed_two.astype(BF)
    logits = mm(ffn_in, router_full)
    logits = jnp.where(chosen > 0.5, logits, -1e30)
    gate_probs = jax.nn.softmax(logits, axis=-1)
    gate_probs = jnp.where(chosen > 0.5, gate_probs, 0.0)

    expert_weight = w_expert[0]
    expert_here = far_index * slab + slab_index
    in_rows, gate_grads, up_grads, grad_rows, actives, slot_dots, gated_outs, in_grads, partials = (
        [] for _ in range(9)
    )
    here = expert_here.reshape(1)
    far_rows = [ffn_in]
    for step in range(1, far_count):
        far_rows.append(far_next(far_rows[-1], far_count))

    def gather(step, source):
        return mm(send_slots[step], source).astype(BF)

    sent = gather(0, ffn_in)

    def combine(step):
        back = exchange(in_grads[step].reshape(slab, capacity, D), SLAB_AXES)
        back = back.reshape(slab * capacity, D)
        if step + 1 < far_count:
            back, actives[step + 1] = tie(back, actives[step + 1])
        else:
            back, slot_dots[0] = tie(back, slot_dots[0])
        return mm_tn(chunk_slots[step], back)

    ffn_in, cot_back[1] = tie(ffn_in, cot_back[1])
    cot_chunks = far_parts(
        jnp.concatenate(cot_back, axis=2).reshape(far_count, slab * capacity, D), far_count
    )
    for step in range(far_count):
        in_chunk = slab_out(to_blocks(sent)).reshape(slab * capacity, D)
        cot_chunk = cot_chunks[step]
        if step + 1 < far_count:
            source = far_rows[step + 1]
            if step > 0:
                source, up_grads[step - 1] = tie(source, up_grads[step - 1])
            sent = gather(step + 1, source)
        gate_grad, up_grad, active, grad_chunk, in_grad, gated_out, slot_dot = expert_chunk(
            here, in_chunk, cot_chunk, mask_back[step], router_full, expert_weight
        )
        in_rows.append(in_chunk)
        gate_grads.append(gate_grad)
        up_grads.append(up_grad)
        actives.append(active)
        grad_rows.append(grad_chunk)
        in_grads.append(in_grad)
        gated_outs.append(gated_out.reshape(slab, capacity, D))
        slot_dots.append(slot_dot[:, 0])
        if step > 0:
            partials.append(combine(step - 1))
    partials.append(combine(far_count - 1))
    dot_sent = jnp.take(jnp.stack(slot_dots).reshape(device_count, capacity), found_at, axis=0)
    dot_back = exchange(dot_sent[:, None, :], ALL_AXES).reshape(experts_all, capacity)
    from_experts = partials[0]
    for step in range(1, far_count):
        from_experts = from_experts + far_shift(partials[step].astype(BF), -step, far_count).astype(F32)

    gate_grad = jnp.sum(jnp.where(slot_hot, dot_back[:, :, None], 0.0), axis=1).T
    mean_term = jnp.sum(gate_probs * gate_grad, axis=1, keepdims=True)
    logit_grad = (gate_probs * (gate_grad - mean_term)).astype(BF)
    router_grad = mm_tn(ffn_in, logit_grad)
    ffn_in_grad = from_experts + mm_nt(logit_grad, router_full)
    resid_part, gain_ffn_grad = ffn_back(ffn_in_grad)
    resid_low = (cot_rows + resid_part).astype(BF)

    gated_sent = far_stack(gated_outs).reshape(device_count, capacity, D)
    gated_sent, resid_low = tie(gated_sent, resid_low)
    returned = [
        exchange(gated_sent[:, :, : D // 2], ALL_AXES).reshape(slot_count, D // 2),
        exchange(gated_sent[:, :, D // 2 :], ALL_AXES).reshape(slot_count, D // 2),
    ]
    in_rows[0], resid_low = tie(in_rows[0], resid_low)
    grad_expert = expert_grads(in_rows, grad_rows, gate_grads, up_grads, actives)[None]

    resid_both, grad_expert = tie(quad_gather(resid_low), grad_expert)
    resid_both = resid_both.reshape(2 * ROW, D)

    def core_sum(values):
        own, other = pair_order(values[:, 0], values[:, 1], CORE_AXIS)
        return own.astype(F32) + swap(other, CORE_AXIS).astype(F32)

    out_grad = mm_tn(mixed_low, resid_both).astype(BF)
    resid_both, out_grad = tie(resid_both, out_grad)
    mixed_grad = mm_nt(resid_both, out_mine).astype(BF)
    out_grad = core_sum(out_grad.reshape(far_part * NEAR, CORES, 2 * out_rows, D))
    mixed_grad, out_grad, returned[0] = tie(mixed_grad, out_grad, returned[0])
    out_grad = (
        out_grad.astype(BF)
        .reshape(far_part, NEAR * 2, out_rows, D)
        .transpose(1, 0, 2, 3)
        .reshape(NEAR * 2, far_part * out_rows, D)
    )
    out_grad = quad_swap(out_grad).reshape(far_count, out_rows, D)
    query_grad, key_grad, value_grad, query_gain_grad, key_gain_grad = attend_back(
        projected, shared, mixed_grad, per_group
    )
    query_grad, out_grad, returned[1] = tie(query_grad, out_grad, returned[1])
    out_share = far_sum(far_parts(out_grad, far_count), far_count)
    proj_grad = jnp.concatenate([query_grad, key_grad, value_grad], axis=1)
    final_rows = jnp.concatenate(
        [
            (residual[:, : D // 2] + mm_tn(slot_low, returned[0])).astype(BF),
            (residual[:, D // 2 :] + mm_tn(slot_low, returned[1])).astype(BF),
        ],
        axis=1,
    )
    final_pair = jnp.concatenate(
        pair_order(final_rows, swap(final_rows, SEQ_AXIS), SEQ_AXIS), axis=0
    )
    layer_out = mm_tn(back_half, final_pair).astype(BF)

    back_grad = lax.dot_general(
        dealt_hot,
        proj_grad.reshape(2, ROW, width),
        (((1,), (1,)), ((0,), (0,))),
        preferred_element_type=F32,
    ).astype(BF).reshape(2 * ROW, width)
    qkv_grad = mm_tn(normed_low, proj_grad).astype(BF)
    back_grad, qkv_grad = tie(back_grad, qkv_grad)
    normed_partial = mm_nt(back_grad, qkv_mine).astype(BF)
    normed_grad = quad_sum(normed_partial.reshape(4, TOK_DEV, D))
    _, attn_back = jax.vjp(rms_norm, tokens.astype(F32), gain_attn)
    input_part, gain_attn_grad = attn_back(normed_grad)
    resid_group = lax.dynamic_slice_in_dim(resid_both, near_index * ROW, ROW, axis=0)
    grad_tokens = (mm_tn(back_half, resid_group) + input_part).astype(BF)

    qkv_grad = core_sum(qkv_grad.reshape(far_count * NEAR, CORES, half_rows, width))
    qkv_grad = far_sum(
        far_parts(qkv_grad.astype(BF).reshape(far_count, core_rows, width), far_count), far_count
    )
    qkv_grad = quad_swap(qkv_grad.astype(BF).reshape(KV_HEADS, qkv_rows, width))
    qkv_grad = qkv_grad.transpose(1, 0, 2).astype(F32)
    qkv_share = jnp.concatenate(
        [
            qkv_grad[:, :, :qcols].reshape(qkv_rows, QDIM),
            qkv_grad[:, :, qcols : qcols + HEAD_DIM].reshape(qkv_rows, KVDIM),
            qkv_grad[:, :, qcols + HEAD_DIM :].reshape(qkv_rows, KVDIM),
        ],
        axis=1,
    )

    gains_grad = jnp.concatenate(
        [gain_attn_grad, gain_ffn_grad, query_gain_grad[0], key_gain_grad[0]]
    )
    share_rows = -(-small_size // (8 * LANES)) * 8
    small_grad = jnp.concatenate(
        [router_grad.reshape(device_count, router_size), gains_grad.reshape(device_count, gain_rows)],
        axis=1,
    )
    small_grad = jnp.pad(small_grad, ((0, 0), (0, share_rows * LANES - small_size)))
    small_share = jnp.sum(
        exchange(small_grad.reshape(device_count, share_rows, LANES), ALL_AXES), axis=0
    ).reshape(share_rows * LANES)
    router_share = small_share[:router_size].reshape(qkv_rows, experts_all)
    gains_share = small_share[router_size:small_size]
    return (layer_out, grad_tokens, qkv_share, out_share, router_share, gains_share, grad_expert)


def solution(mesh):
    shape = dict(mesh.shape)
    inner = Mesh(
        mesh.devices.reshape(shape["dp"] // (NEAR * CORES), NEAR, CORES, shape["seq"]), ALL_AXES
    )
    rows = P(ALL_AXES, None)
    in_specs = (
        rows,
        rows,
        rows,
        rows,
        rows,
        P(ALL_AXES),
        P(ALL_AXES, None, None),
        P(DP_AXES, None),
        P(DP_AXES, None),
        P(DP_AXES, None, None),
    )
    out_specs = (rows, rows, rows, rows, rows, P(ALL_AXES), P(ALL_AXES, None, None))
    return jax.shard_map(shards, mesh=inner, in_specs=in_specs, out_specs=out_specs, check_vma=False)
```

```python
import functools

import jax
import jax.numpy as jnp
from jax import lax
from jax.experimental import pallas as pl
from jax.experimental.pallas import tpu as pltpu
from jax.sharding import Mesh
from jax.sharding import PartitionSpec as P

D = 2048
HEADS = 32
KV_HEADS = 4
HEAD_DIM = 128
FF = 768
TOPK = 8
NSEG = 4
TOK_DEV = 128
ROW = 256
QDIM = 4096
KVDIM = 512
NEAR = 2
CORES = 2
LANES = 128

EPS = 1e-06
THETA = 1000000.0
BF = jnp.bfloat16
F32 = jnp.float32

FAR_AXIS = "far"
NEAR_AXIS = "near"
CORE_AXIS = "core"
SEQ_AXIS = "seq"
SLAB_AXES = (NEAR_AXIS, CORE_AXIS, SEQ_AXIS)
HEAD_AXES = (NEAR_AXIS, SEQ_AXIS)
ALL_AXES = (FAR_AXIS, NEAR_AXIS, CORE_AXIS, SEQ_AXIS)
DP_AXES = (FAR_AXIS, NEAR_AXIS, CORE_AXIS)


def rms_norm(values, scales):
    return values * lax.rsqrt(jnp.mean(values * values, axis=-1, keepdims=True) + EPS) * scales


def rotary(values, cosine, sine_part):
    half_width = values.shape[-1] // 2
    front_part = values[..., :half_width]
    back_part = values[..., half_width:]
    cos_wide = cosine[..., None, :]
    sin_wide = sine_part[..., None, :]
    return jnp.concatenate(
        [
            front_part * cos_wide - back_part * sin_wide,
            back_part * cos_wide + front_part * sin_wide,
        ],
        axis=-1,
    )


def tables(positions, head_width):
    half_width = head_width // 2
    inverse = THETA ** (-(jnp.arange(half_width, dtype=F32) * 2.0 / head_width))
    angles = positions.astype(F32)[..., None] * inverse
    return (jnp.cos(angles), jnp.sin(angles))


def dot(left, right, dims):
    return lax.dot_general(left, right, (dims, ((), ())), preferred_element_type=F32)


def mm(left, right):
    return dot(left, right, ((1,), (0,)))


def mm_nt(left, right):
    return dot(left, right, ((1,), (1,)))


def mm_tn(left, right):
    return dot(left, right, ((0,), (0,)))


def swap(value, axis):
    return lax.ppermute(value, axis, [(0, 1), (1, 0)])


def pair_order(own, other, axis):
    first = lax.axis_index(axis) == 0
    return (jnp.where(first, own, other), jnp.where(first, other, own))


def exchange(value, axes):
    return lax.all_to_all(value, axes, split_axis=0, concat_axis=0, tiled=True)


def quad_index():
    return lax.axis_index(NEAR_AXIS) * 2 + lax.axis_index(SEQ_AXIS)


def quad_send(parts, step):
    block = lax.dynamic_index_in_dim(parts, lax.bitwise_xor(quad_index(), step), 0, keepdims=False)
    return lax.ppermute(block, HEAD_AXES, [(i, i ^ step) for i in range(4)])


def quad_order(found):
    low = pair_order(found[0], found[1], SEQ_AXIS)
    high = pair_order(found[2], found[3], SEQ_AXIS)
    rows = [pair_order(low[k], high[k], NEAR_AXIS) for k in range(2)]
    return jnp.stack([rows[0][0], rows[1][0], rows[0][1], rows[1][1]])


def quad_gather(value):
    found = [value] + [
        lax.ppermute(value, HEAD_AXES, [(i, i ^ step) for i in range(4)]) for step in range(1, 4)
    ]
    return quad_order(found)


def quad_parts(parts):
    own = lax.dynamic_index_in_dim(parts, quad_index(), 0, keepdims=False)
    return [own] + [quad_send(parts, step) for step in range(1, 4)]


def quad_swap(parts):
    return quad_order(quad_parts(parts))


def quad_sum(parts):
    total = lax.dynamic_index_in_dim(parts, quad_index(), 0, keepdims=False).astype(F32)
    for step in range(1, 4):
        total = total + quad_send(parts, step).astype(F32)
    return total


def far_sum(parts, count):
    total = parts[0].astype(F32)
    if count != 4:
        for step in range(1, count):
            total = total + far_shift(parts[step].astype(BF), -step, count).astype(F32)
        return total
    relay = far_shift(parts[2].astype(BF), -1, count).astype(F32)
    direct = far_shift(parts[3].astype(BF), 1, count).astype(F32)
    relay = far_shift((parts[1].astype(F32) + relay).astype(BF), -1, count)
    return total + direct + relay.astype(F32)


def far_parts(values, count):
    here = lax.axis_index(FAR_AXIS)
    return [
        lax.dynamic_index_in_dim(values, lax.rem(here + count - step, count), 0, keepdims=False)
        for step in range(count)
    ]


def far_all(value, count, first=None):
    ahead = count // 2
    found = [value] + [None] * (count - 1)
    found[1] = far_shift(value, 1, count)
    if count > 2:
        found[count - 1] = far_shift(value, -1, count)
    for step in range(2, ahead + 1):
        found[step] = far_shift(found[step - 1], 1, count)
    for step in range(count - 2, ahead, -1):
        found[step] = far_shift(found[step + 1], -1, count)
    return found


def far_stack(found):
    count = len(found)
    here = lax.axis_index(FAR_AXIS)
    zeros = (0,) * found[0].ndim
    full = jnp.zeros((count,) + found[0].shape, found[0].dtype)
    for step, chunk in enumerate(found):
        full = lax.dynamic_update_slice(full, chunk[None], (lax.rem(here + count - step, count),) + zeros)
    return full


def tie(*values):
    return lax.optimization_barrier(values)


def far_shift(value, step, count):
    return lax.ppermute(value, FAR_AXIS, [(i, (i + step) % count) for i in range(count)])


def far_next(value, count):
    return lax.ppermute(value, FAR_AXIS, [(i, (i + 1) % count) for i in range(count)])


def quad_xor(value, step):
    return lax.ppermute(value, HEAD_AXES, [(i, i ^ step) for i in range(4)])


def slab_send(blocks):
    return [blocks[0]] + [quad_xor(blocks[step], step) for step in range(1, 4)]


def slab_take(got):
    keep = quad_order([part[0] for part in got])
    other = swap(quad_order([part[1] for part in got]), CORE_AXIS)
    first, second = pair_order(keep, other, CORE_AXIS)
    shape = (NEAR, 2) + keep.shape[1:]
    return jnp.stack([first.reshape(shape), second.reshape(shape)], axis=1)


def slab_return(rows):
    keep, give = pair_order(rows[:, 0], rows[:, 1], CORE_AXIS)
    both = jnp.stack([keep, swap(give, CORE_AXIS)], axis=2)
    return quad_parts(both.reshape((4, 2) + rows.shape[3:]))


def expert_kernel(
    here_ref, in_ref, cot_ref, mask_ref, router_ref, gate_ref, up_ref, down_ref,
    gate_grad_ref, up_grad_ref, active_ref, grad_ref, in_grad_ref, gated_ref, dot_ref,
    out_total, in_total, gate_slot,
):
    block = pl.program_id(0)

    @pl.when(block == 0)
    def _():
        chosen = mask_ref[...].astype(F32) > 0.5
        logits = jnp.where(chosen, mm(in_ref[...], router_ref[...]), -1e30)
        exped = jnp.where(chosen, jnp.exp(logits - jnp.max(logits, axis=-1, keepdims=True)), 0.0)
        total = jnp.sum(exped, axis=-1, keepdims=True)
        mine = lax.broadcasted_iota(jnp.int32, exped.shape, 1) == here_ref[0]
        picked = jnp.sum(jnp.where(mine, exped, 0.0), axis=-1, keepdims=True)
        gate = picked / jnp.where(total > 0.0, total, 1.0)
        gate_slot[...] = jnp.broadcast_to(gate, gate_slot.shape)
        grad_ref[...] = (gate * cot_ref[...].astype(F32)).astype(BF)
        out_total[...] = jnp.zeros_like(out_total)
        in_total[...] = jnp.zeros_like(in_total)

    gate_pre = mm(in_ref[...], gate_ref[...])
    up_pre = mm(in_ref[...], up_ref[...])
    act_grad = mm(grad_ref[...], down_ref[...])
    sig_gate = jax.nn.sigmoid(gate_pre)
    silu_val = gate_pre * sig_gate
    active = (silu_val * up_pre).astype(BF)
    silu_slope = sig_gate * (1.0 + gate_pre * (1.0 - sig_gate))
    gate_grad = (act_grad * up_pre * silu_slope).astype(BF)
    up_grad = (act_grad * silu_val).astype(BF)
    active_ref[...] = active
    gate_grad_ref[...] = gate_grad
    up_grad_ref[...] = up_grad
    out_total[...] += mm_nt(active, down_ref[...])
    in_total[...] += mm_nt(gate_grad, gate_ref[...]) + mm_nt(up_grad, up_ref[...])

    @pl.when(block == pl.num_programs(0) - 1)
    def _():
        out = out_total[...].astype(BF).astype(F32)
        dot_ref[...] = jnp.sum(cot_ref[...].astype(F32) * out, axis=-1, keepdims=True)
        gated_ref[...] = (gate_slot[:, :1] * out).astype(BF)
        in_grad_ref[...] = in_total[...].astype(BF)


def expert_chunk(here, in_chunk, cot_chunk, mask, router, weight):
    rows = in_chunk.shape[0]
    tile = 256
    steps = FF // tile
    whole = pl.BlockSpec((rows, D), lambda j, h: (0, 0))
    piece = pl.BlockSpec((rows, tile), lambda j, h: (0, j))
    low = jax.ShapeDtypeStruct((rows, FF), BF)
    wide = jax.ShapeDtypeStruct((rows, D), BF)
    return pl.pallas_call(
        expert_kernel,
        grid_spec=pltpu.PrefetchScalarGridSpec(
            num_scalar_prefetch=1,
            grid=(steps,),
            in_specs=[
                whole,
                whole,
                pl.BlockSpec(mask.shape, lambda j, h: (0, 0)),
                pl.BlockSpec(router.shape, lambda j, h: (0, 0)),
                pl.BlockSpec((D, tile), lambda j, h: (0, j)),
                pl.BlockSpec((D, tile), lambda j, h: (0, steps + j)),
                pl.BlockSpec((D, tile), lambda j, h: (0, 2 * steps + j)),
            ],
            out_specs=[
                piece, piece, piece, whole, whole, whole,
                pl.BlockSpec((rows, 1), lambda j, h: (0, 0)),
            ],
            scratch_shapes=[
                pltpu.VMEM((rows, D), F32),
                pltpu.VMEM((rows, D), F32),
                pltpu.VMEM((rows, LANES), F32),
            ],
        ),
        out_shape=[low, low, low, wide, wide, wide, jax.ShapeDtypeStruct((rows, 1), F32)],
        compiler_params=pltpu.CompilerParams(vmem_limit_bytes=40 << 20),
        cost_estimate=pl.CostEstimate(flops=1 << 20, bytes_accessed=1 << 20, transcendentals=0),
        name="expert_chunk",
    )(here, in_chunk, cot_chunk, mask, router, weight, weight, weight)


def expert_grad_kernel(count, *refs):
    lists = [refs[k * count : (k + 1) * count] for k in range(5)]
    out_ref = refs[5 * count]
    column = pl.program_id(1)

    def total(lefts, rights):
        found = mm_tn(lefts[0][...], rights[0][...])
        for left, right in zip(lefts[1:], rights[1:]):
            found = found + mm_tn(left[...], right[...])
        out_ref[...] = found

    for place, (left, right) in enumerate(((0, 2), (0, 3), (1, 4))):
        pl.when(column == place)(functools.partial(total, lists[left], lists[right]))


def expert_grads(in_rows, grad_rows, gate_grads, up_grads, actives):
    count = len(in_rows)
    rows = in_rows[0].shape[0]
    tile = 512
    tall = pl.BlockSpec((rows, tile), lambda i, j: (0, i))
    whole = pl.BlockSpec((rows, FF), lambda i, j: (0, 0))
    return pl.pallas_call(
        functools.partial(expert_grad_kernel, count),
        grid=(D // tile, 3),
        in_specs=[tall] * (2 * count) + [whole] * (3 * count),
        out_specs=pl.BlockSpec((tile, FF), lambda i, j: (i, j)),
        out_shape=jax.ShapeDtypeStruct((D, 3 * FF), F32),
        compiler_params=pltpu.CompilerParams(vmem_limit_bytes=48 << 20),
        cost_estimate=pl.CostEstimate(flops=1 << 20, bytes_accessed=1 << 20, transcendentals=0),
        name="expert_grads",
    )(*in_rows, *grad_rows, *gate_grads, *up_grads, *actives)


def head_normed(raw, gain_ref):
    scale = lax.rsqrt(jnp.mean(raw * raw, axis=-1, keepdims=True) + EPS)
    normal = raw * scale
    return (normal, scale, normal * gain_ref[...])


def turned(values, cos_ref, sin_ref):
    return values * cos_ref[...] + pltpu.roll(values, HEAD_DIM // 2, 1) * sin_ref[...]


def turned_back(values, cos_ref, sin_ref):
    return values * cos_ref[...] + pltpu.roll(values * sin_ref[...], HEAD_DIM // 2, 1)


def head_probs(query, key, row_ref, start_ref, key_row_ref):
    scores = mm_nt(query, key) * HEAD_DIM ** (-0.5)
    allowed = (key_row_ref[0] <= row_ref[0]) & (key_row_ref[0] >= start_ref[0])
    scores = jnp.where(allowed, scores, -1e30)
    exped = jnp.exp(scores - jnp.max(scores, axis=-1, keepdims=True))
    return exped / jnp.sum(exped, axis=-1, keepdims=True)


def attend_kernel(
    query_ref, key_ref, value_ref, cos_ref, sin_ref, qgain_ref, kgain_ref,
    row_ref, start_ref, key_row_ref, mixed_ref, key_low, value_low,
):
    @pl.when(pl.program_id(1) == 0)
    def _():
        key_low[...] = turned(head_normed(key_ref[...], kgain_ref)[2], cos_ref, sin_ref).astype(BF)
        value_low[...] = value_ref[...].astype(BF)

    query = turned(head_normed(query_ref[...], qgain_ref)[2], cos_ref, sin_ref).astype(BF)
    probs = head_probs(query, key_low[...], row_ref, start_ref, key_row_ref)
    mixed_ref[...] = mm(probs.astype(BF), value_low[...]).astype(BF)


def attend_back_kernel(
    query_ref, key_ref, value_ref, cos_ref, sin_ref, qgain_ref, kgain_ref,
    row_ref, start_ref, key_row_ref, grad_ref,
    query_out, key_out, value_out, qgain_out, kgain_out,
    key_low, value_low, key_total, value_total,
):
    group, head = pl.program_id(0), pl.program_id(1)
    score_scale = HEAD_DIM ** (-0.5)

    @pl.when((group == 0) & (head == 0))
    def _():
        qgain_out[...] = jnp.zeros_like(qgain_out)
        kgain_out[...] = jnp.zeros_like(kgain_out)

    @pl.when(head == 0)
    def _():
        key_low[...] = turned(head_normed(key_ref[...], kgain_ref)[2], cos_ref, sin_ref).astype(BF)
        value_low[...] = value_ref[...].astype(BF)
        key_total[...] = jnp.zeros_like(key_total)
        value_total[...] = jnp.zeros_like(value_total)

    def raw_grad(grad, normal, scale, gain_ref, gain_out):
        grad = turned_back(grad, cos_ref, sin_ref)
        gain_out[...] += jnp.sum(grad * normal, axis=0, keepdims=True)
        grad = grad * gain_ref[...]
        return scale * (grad - normal * jnp.mean(normal * grad, axis=-1, keepdims=True))

    normal, scale, gained = head_normed(query_ref[...], qgain_ref)
    query = turned(gained, cos_ref, sin_ref).astype(BF)
    probs = head_probs(query, key_low[...], row_ref, start_ref, key_row_ref)
    grad = grad_ref[...]
    value_total[...] += mm_tn(probs.astype(BF), grad)
    prob_grad = mm_nt(grad, value_low[...])
    score_grad = (probs * (prob_grad - jnp.sum(probs * prob_grad, axis=-1, keepdims=True))).astype(BF)
    key_total[...] += mm_tn(score_grad, query) * score_scale
    query_grad = mm(score_grad, key_low[...]) * score_scale
    query_out[...] = raw_grad(query_grad, normal, scale, qgain_ref, qgain_out).astype(BF)

    @pl.when(head == pl.num_programs(1) - 1)
    def _():
        key_normal, key_scale, _ = head_normed(key_ref[...], kgain_ref)
        key_out[...] = raw_grad(key_total[...], key_normal, key_scale, kgain_ref, kgain_out).astype(BF)
        value_out[...] = value_total[...].astype(BF)


def attend_specs(heads):
    head = pl.BlockSpec((ROW, HEAD_DIM), lambda b, h: (b, h))
    whole = pl.BlockSpec((ROW, HEAD_DIM), lambda b, h: (b, 0))
    gain = pl.BlockSpec((1, HEAD_DIM), lambda b, h: (0, 0))
    column = pl.BlockSpec((1, ROW, 1), lambda b, h: (b, 0, 0))
    specs = [
        head,
        pl.BlockSpec((ROW, HEAD_DIM), lambda b, h: (b, heads)),
        pl.BlockSpec((ROW, HEAD_DIM), lambda b, h: (b, heads + 1)),
        whole, whole, gain, gain, column, column,
        pl.BlockSpec((1, 1, ROW), lambda b, h: (b, 0, 0)),
    ]
    return (specs, head, whole, gain)


def attend(projected, shared, heads):
    specs, head, _, _ = attend_specs(heads)
    rows = projected.shape[0]
    return pl.pallas_call(
        attend_kernel,
        grid=(rows // ROW, heads),
        in_specs=specs,
        out_specs=head,
        out_shape=jax.ShapeDtypeStruct((rows, heads * HEAD_DIM), BF),
        scratch_shapes=[pltpu.VMEM((ROW, HEAD_DIM), BF)] * 2,
        cost_estimate=pl.CostEstimate(flops=1 << 20, bytes_accessed=1 << 20, transcendentals=0),
        name="attend",
    )(projected, projected, projected, *shared)


def attend_back(projected, shared, grad, heads):
    specs, head, whole, gain = attend_specs(heads)
    rows = projected.shape[0]
    return pl.pallas_call(
        attend_back_kernel,
        grid=(rows // ROW, heads),
        in_specs=specs + [head],
        out_specs=[head, whole, whole, gain, gain],
        out_shape=[
            jax.ShapeDtypeStruct((rows, heads * HEAD_DIM), BF),
            jax.ShapeDtypeStruct((rows, HEAD_DIM), BF),
            jax.ShapeDtypeStruct((rows, HEAD_DIM), BF),
            jax.ShapeDtypeStruct((1, HEAD_DIM), F32),
            jax.ShapeDtypeStruct((1, HEAD_DIM), F32),
        ],
        scratch_shapes=[pltpu.VMEM((ROW, HEAD_DIM), BF)] * 2 + [pltpu.VMEM((ROW, HEAD_DIM), F32)] * 2,
        cost_estimate=pl.CostEstimate(flops=1 << 20, bytes_accessed=1 << 20, transcendentals=0),
        name="attend_back",
    )(projected, projected, projected, *shared, grad)


def shards(tokens, cotangent, w_qkv, w_out, w_router, norm_gains, w_expert, lengths, deal, routes):
    far_count = lax.axis_size(FAR_AXIS)
    device_count = far_count * NEAR * CORES * 2
    experts_all = w_router.shape[1]
    capacity = TOK_DEV * TOPK // experts_all
    slot_count = experts_all * capacity
    seq_index = lax.axis_index(SEQ_AXIS)
    near_index = lax.axis_index(NEAR_AXIS)
    far_index = lax.axis_index(FAR_AXIS)
    core_index = lax.axis_index(CORE_AXIS)
    per_group = HEADS // KV_HEADS
    qcols = per_group * HEAD_DIM
    width = qcols + 2 * HEAD_DIM
    qkv_rows = w_qkv.shape[0]
    out_rows = w_out.shape[0]
    gain_rows = norm_gains.shape[0]
    score_scale = HEAD_DIM ** (-0.5)

    wide = jnp.concatenate(
        [
            w_qkv[:, :QDIM].reshape(qkv_rows, KV_HEADS, qcols),
            w_qkv[:, QDIM : QDIM + KVDIM].reshape(qkv_rows, KV_HEADS, HEAD_DIM),
            w_qkv[:, QDIM + KVDIM :].reshape(qkv_rows, KV_HEADS, HEAD_DIM),
        ],
        axis=2,
    ).transpose(1, 0, 2)
    core_rows = KV_HEADS * qkv_rows
    half_rows = 2 * qkv_rows
    wide_found = quad_parts(wide)
    tokens, *wide_found = tie(tokens, *wide_found)
    qkv_far = far_all(quad_order(wide_found).reshape(core_rows, width), far_count)

    tokens_both = quad_gather(tokens).reshape(2, ROW, D)
    table = jnp.concatenate([deal, jnp.pad(lengths, ((0, 0), (0, LANES - NSEG)))], axis=1)
    table_both = jnp.concatenate(pair_order(table, swap(table, NEAR_AXIS), NEAR_AXIS), axis=0)
    deal_both = table_both[:, :ROW]
    ends = jnp.cumsum(table_both[:, ROW : ROW + NSEG], axis=1)
    starts = ends - table_both[:, ROW : ROW + NSEG]
    seg_both = jnp.sum((deal_both[:, :, None] >= ends[:, None, :]).astype(jnp.int32), axis=2)
    picked = seg_both[:, :, None] == jnp.arange(NSEG, dtype=jnp.int32)[None, None, :]
    pos_both = deal_both - jnp.sum(jnp.where(picked, starts[:, None, :], 0), axis=2)
    dealt_hot = (deal_both[:, :, None] == jnp.arange(ROW, dtype=jnp.int32)[None, None, :]).astype(BF)
    hot_mine = lax.dynamic_index_in_dim(dealt_hot, near_index, 0, keepdims=False)
    hot_half = lax.dynamic_slice_in_dim(hot_mine, seq_index * TOK_DEV, TOK_DEV, axis=0)
    back_half = lax.dynamic_slice_in_dim(hot_mine, seq_index * TOK_DEV, TOK_DEV, axis=1)
    seg_mine = lax.dynamic_slice_in_dim(
        lax.dynamic_index_in_dim(seg_both, near_index, 0, keepdims=False), seq_index * TOK_DEV, TOK_DEV
    )

    expert_ids = jnp.arange(experts_all, dtype=jnp.int32)
    chosen_rows = jnp.sum(
        (routes[0][:, :, None] == expert_ids[None, None, :]).astype(jnp.int32), axis=1
    ).astype(BF)
    chosen = mm(hot_half, chosen_rows)
    live = jnp.where((seg_mine != NSEG - 1)[:, None], chosen, 0.0)
    steps = jnp.arange(TOK_DEV, dtype=jnp.int32)
    earlier = (steps[None, :] < steps[:, None]).astype(BF)
    place = mm(earlier, live.astype(BF))
    place = jnp.where(live > 0.5, place, -1.0).astype(jnp.int32)
    slot_hot = place.T[:, None, :] == jnp.arange(capacity, dtype=jnp.int32)[None, :, None]
    slot_low = slot_hot.astype(BF).reshape(slot_count, TOK_DEV)

    slab = NEAR * CORES * 2
    slab_index = (near_index * CORES + core_index) * 2 + seq_index
    slab_ids = jnp.arange(slab, dtype=jnp.int32)
    out_order = jnp.array([0, 2, 1, 3, 4, 6, 5, 7], jnp.int32)
    place_far = far_stack(far_all(place.T.astype(BF), far_count))

    def slots_of(places, step):
        found = lax.dynamic_index_in_dim(
            places, lax.rem(far_index + far_count - step, far_count), 0, keepdims=False
        )
        found = found[:, None, :] == jnp.arange(capacity, dtype=jnp.int32)[None, :, None]
        return found.astype(BF).reshape(slab * capacity, TOK_DEV)

    place_slab = lax.dynamic_slice_in_dim(place_far, far_index * slab, slab, axis=1).astype(jnp.int32)
    turned_ids = lax.bitwise_xor(out_order, slab_index)
    place_turned = jnp.sum(
        jnp.where(
            (turned_ids[:, None] == slab_ids[None, :])[None, :, :, None], place_slab[:, None], 0
        ),
        axis=2,
    )
    chunk_slots = [slots_of(place_slab, step) for step in range(far_count)]
    send_slots = [slots_of(place_turned, step) for step in range(far_count)]
    chunk_steps = jnp.arange(far_count, dtype=jnp.int32)
    source_ids = (
        lax.rem(far_index + far_count - chunk_steps, far_count)[:, None] * slab + slab_ids[None, :]
    ).reshape(device_count)
    device_ids = jnp.arange(device_count, dtype=jnp.int32)
    found_at = jnp.sum(
        jnp.where(source_ids[None, :] == device_ids[:, None], device_ids[None, :], 0), axis=1
    )

    def to_blocks(rows):
        return rows.reshape(4, 2, rows.shape[0] // slab, rows.shape[1])


    router_size = qkv_rows * experts_all
    small_size = router_size + gain_rows
    mask_size = capacity * experts_all
    small_rows = -(-(small_size + mask_size) // (8 * LANES)) * 8
    small = jnp.broadcast_to(
        jnp.concatenate([w_router.reshape(router_size), norm_gains]), (device_count, small_size)
    )
    slot_mask = mm(slot_low, chosen.astype(BF)).astype(BF).reshape(device_count, mask_size)
    small = jnp.concatenate([slot_mask, small], axis=1)
    small = jnp.pad(small, ((0, 0), (0, small_rows * LANES - small_size - mask_size)))
    small_all = exchange(small.reshape(device_count, small_rows, LANES), ALL_AXES).reshape(
        device_count, small_rows * LANES
    )
    mask_back = jnp.take(small_all[:, :mask_size], source_ids, axis=0).reshape(
        far_count, slab * capacity, experts_all
    )
    small_all = small_all[:, mask_size : mask_size + small_size]
    router_full = small_all[:, :router_size].reshape(D, experts_all)
    gains_float = small_all[:, router_size:].reshape(-1).astype(F32)
    gain_attn = gains_float[:D]
    gain_ffn = gains_float[D : 2 * D]
    gain_query = gains_float[2 * D : 2 * D + HEAD_DIM]
    gain_key = gains_float[2 * D + HEAD_DIM :]

    cot_pair = jnp.concatenate(pair_order(cotangent, swap(cotangent, SEQ_AXIS), SEQ_AXIS), axis=0)
    cot_low = mm(hot_half, cot_pair).astype(BF)
    cot_rows = cot_low.astype(F32)
    cot_low, qkv_far[2] = tie(cot_low, qkv_far[2])
    cot_sent = mm(slot_low, cot_low).astype(BF).reshape(device_count, capacity, D)
    cot_back = [exchange(cot_sent[:, :, : D // 2], ALL_AXES), exchange(cot_sent[:, :, D // 2 :], ALL_AXES)]
    qkv_own = far_stack(qkv_far).reshape(far_count * NEAR, half_rows, width)
    qkv_mine = jnp.stack(pair_order(qkv_own, swap(qkv_own, CORE_AXIS), CORE_AXIS), axis=1).reshape(
        D, width
    )

    out_slabs = far_stack(far_all(w_out, far_count)).reshape(
        KV_HEADS, far_count // KV_HEADS * out_rows, D
    )
    far_part = far_count // KV_HEADS
    x_both = lax.dot_general(
        dealt_hot, tokens_both, (((2,), (1,)), ((0,), (0,))), preferred_element_type=F32
    )
    x_rows = lax.dynamic_slice(
        x_both, (near_index, seq_index * TOK_DEV, 0), (1, TOK_DEV, D)
    )[0]
    normed_low = rms_norm(x_both.reshape(2 * ROW, D), gain_attn).astype(BF)
    projected = mm(normed_low, qkv_mine)
    cosine, sine_part = tables(pos_both.reshape(2 * ROW), HEAD_DIM)
    shared = (
        jnp.concatenate([cosine, cosine], axis=1),
        jnp.concatenate([-sine_part, sine_part], axis=1),
        gain_query[None],
        gain_key[None],
        deal_both[:, :, None],
        (deal_both - pos_both)[:, :, None],
        deal_both[:, None, :],
    )
    mixed_low = attend(projected, shared, per_group)
    out_found = quad_parts(out_slabs)
    mixed_low, cot_back[0], *out_found = tie(mixed_low, cot_back[0], *out_found)
    out_own = quad_order(out_found).reshape(NEAR * 2, far_part, out_rows, D)
    out_own = out_own.transpose(1, 0, 2, 3).reshape(far_part * NEAR, 2 * out_rows, D)
    out_mine = jnp.stack(pair_order(out_own, swap(out_own, CORE_AXIS), CORE_AXIS), axis=1).reshape(
        qcols, D
    )

    out_partial = mm(mixed_low, out_mine).astype(BF)
    residual = x_rows + quad_sum(out_partial.reshape(4, TOK_DEV, D))

    normed_two, ffn_back = jax.vjp(rms_norm, residual, gain_ffn)
    ffn_in = normed_two.astype(BF)
    logits = mm(ffn_in, router_full)
    logits = jnp.where(chosen > 0.5, logits, -1e30)
    gate_probs = jax.nn.softmax(logits, axis=-1)
    gate_probs = jnp.where(chosen > 0.5, gate_probs, 0.0)

    expert_weight = w_expert[0]
    expert_here = far_index * slab + slab_index
    in_rows, gate_grads, up_grads, grad_rows, actives, in_grads = ([] for _ in range(6))
    slot_dots, gated_outs = [None] * far_count, [None] * far_count
    arrived = []
    here = expert_here.reshape(1)
    order = list(range(far_count))
    far_rows = [ffn_in]
    for step in range(1, far_count):
        with jax.named_scope('rows_far%d' % step):
            far_rows.append(far_shift(far_rows[-1], 1, far_count))

    def gather(step, source):
        return mm(send_slots[step], source).astype(BF)

    sent = gather(0, ffn_in)

    def send_back(step):
        return slab_return(in_grads[step].reshape(NEAR, CORES, 2, capacity, D))

    def combine(step, found):
        back = jnp.concatenate(found, axis=0).reshape(slab * capacity, D)
        return mm_tn(send_slots[step], back).astype(BF if step else F32)

    ffn_in, cot_back[1] = tie(ffn_in, cot_back[1])
    cot_chunks = far_parts(
        jnp.concatenate(cot_back, axis=2).reshape(far_count, slab * capacity, D), far_count
    )
    pending = []
    for turn, step in enumerate(order):
        with jax.named_scope("rows_out%d" % turn):
            got = slab_send(to_blocks(sent))
        if turn + 1 < far_count:
            source = far_rows[order[turn + 1]]
            if turn > 0:
                source, up_grads[turn - 1] = tie(source, up_grads[turn - 1])
            sent = gather(order[turn + 1], source)
        if turn > 0:
            gate_grads[turn - 1], *got = tie(gate_grads[turn - 1], *got)
        with jax.named_scope("rows_core%d" % turn):
            in_chunk = slab_take(got).reshape(slab * capacity, D)
        if turn > 2:
            in_chunk, *pending = tie(in_chunk, *pending)
            partial = combine(order[turn - 2], pending)
            in_chunk, partial = tie(in_chunk, partial)
            with jax.named_scope("partial_far%d" % (turn - 2)):
                arrived.append(far_shift(partial, -order[turn - 2], far_count))
        gate_grad, up_grad, active, grad_chunk, in_grad, gated_out, slot_dot = expert_chunk(
            here, in_chunk, cot_chunks[step], mask_back[step], router_full, expert_weight
        )
        if turn > 2:
            gate_grad, arrived[-1] = tie(gate_grad, arrived[-1])
        in_rows.append(in_chunk)
        gate_grads.append(gate_grad)
        up_grads.append(up_grad)
        actives.append(active)
        grad_rows.append(grad_chunk)
        in_grads.append(in_grad)
        gated_outs[step] = gated_out.reshape(slab, capacity, D)
        slot_dots[step] = slot_dot[:, 0]
        if turn > 1:
            with jax.named_scope("rows_back%d" % (turn - 1)):
                pending = send_back(turn - 1)
    partial = None
    for turn in range(max(1, far_count - 2), far_count):
        if turn == far_count - 1:
            with jax.named_scope("rows_back%d" % turn):
                pending = send_back(turn)
        else:
            up_grads[-1], *pending = tie(up_grads[-1], *pending)
        partial = combine(order[turn], pending)
        if turn == far_count - 2:
            partial, in_grads[0] = tie(partial, in_grads[0])
        with jax.named_scope("partial_far%d" % turn):
            arrived.append(far_shift(partial, -order[turn], far_count))
    slot_dots[0], partial = tie(slot_dots[0], partial)
    with jax.named_scope("rows_back0"):
        from_experts = combine(0, send_back(0))
    for part in arrived:
        from_experts = from_experts + part.astype(F32)
    dot_sent = jnp.take(jnp.stack(slot_dots).reshape(device_count, capacity), found_at, axis=0)
    dot_back = exchange(dot_sent[:, None, :], ALL_AXES).reshape(experts_all, capacity)

    gate_grad = jnp.sum(jnp.where(slot_hot, dot_back[:, :, None], 0.0), axis=1).T
    mean_term = jnp.sum(gate_probs * gate_grad, axis=1, keepdims=True)
    logit_grad = (gate_probs * (gate_grad - mean_term)).astype(BF)
    router_grad = mm_tn(ffn_in, logit_grad)
    ffn_in_grad = from_experts + mm_nt(logit_grad, router_full)
    resid_part, gain_ffn_grad = ffn_back(ffn_in_grad)
    resid_low = (cot_rows + resid_part).astype(BF)

    in_rows[0], resid_low = tie(in_rows[0], resid_low)
    grad_expert = expert_grads(in_rows, grad_rows, gate_grads, up_grads, actives)[None]

    resid_both, grad_expert = tie(quad_gather(resid_low), grad_expert)
    returned = []
    for half in range(2):
        gated = far_stack([part[:, :, half * D // 2 : (half + 1) * D // 2] for part in gated_outs])
        gated, resid_both = tie(gated, resid_both)
        gated = exchange(gated.reshape(device_count, capacity, D // 2), ALL_AXES)
        returned.append(gated.reshape(slot_count, D // 2))
    resid_both = resid_both.reshape(2 * ROW, D)

    def core_sum(values):
        own, other = pair_order(values[:, 0], values[:, 1], CORE_AXIS)
        return own.astype(F32) + swap(other, CORE_AXIS).astype(F32)

    out_grad = mm_tn(mixed_low, resid_both).astype(BF)
    resid_both, out_grad = tie(resid_both, out_grad)
    mixed_grad = mm_nt(resid_both, out_mine).astype(BF)
    out_grad = core_sum(out_grad.reshape(far_part * NEAR, CORES, 2 * out_rows, D)).astype(BF)
    mixed_grad, out_grad = tie(mixed_grad, out_grad)
    out_grad = (
        out_grad
        .reshape(far_part, NEAR * 2, out_rows, D)
        .transpose(1, 0, 2, 3)
        .reshape(NEAR * 2, far_part * out_rows, D)
    )
    out_grad = quad_swap(out_grad).reshape(far_count, out_rows, D)
    query_grad, key_grad, value_grad, query_gain_grad, key_gain_grad = attend_back(
        projected, shared, mixed_grad, per_group
    )
    query_grad, returned[0] = tie(query_grad, returned[0])
    proj_grad = jnp.concatenate([query_grad, key_grad, value_grad], axis=1)

    back_grad = lax.dot_general(
        dealt_hot,
        proj_grad.reshape(2, ROW, width),
        (((1,), (1,)), ((0,), (0,))),
        preferred_element_type=F32,
    ).astype(BF).reshape(2 * ROW, width)
    qkv_grad = mm_tn(normed_low, proj_grad).astype(BF)
    back_grad, qkv_grad = tie(back_grad, qkv_grad)
    normed_partial = mm_nt(back_grad, qkv_mine).astype(BF)
    qkv_grad = core_sum(qkv_grad.reshape(far_count * NEAR, CORES, half_rows, width)).astype(BF)
    normed_partial, qkv_grad, out_grad = tie(normed_partial, qkv_grad, out_grad)
    qkv_grad = far_sum(far_parts(qkv_grad.reshape(far_count, core_rows, width), far_count), far_count)
    out_share = far_sum(far_parts(out_grad, far_count), far_count)
    normed_grad = quad_sum(normed_partial.reshape(4, TOK_DEV, D))
    normed_grad, returned[1] = tie(normed_grad, returned[1])
    final_rows = jnp.concatenate(
        [
            (residual[:, : D // 2] + mm_tn(slot_low, returned[0])).astype(BF),
            (residual[:, D // 2 :] + mm_tn(slot_low, returned[1])).astype(BF),
        ],
        axis=1,
    )
    final_pair = jnp.concatenate(
        pair_order(final_rows, swap(final_rows, SEQ_AXIS), SEQ_AXIS), axis=0
    )
    layer_out = mm_tn(back_half, final_pair).astype(BF)
    _, attn_back = jax.vjp(rms_norm, tokens.astype(F32), gain_attn)
    input_part, gain_attn_grad = attn_back(normed_grad)
    resid_group = lax.dynamic_slice_in_dim(resid_both, near_index * ROW, ROW, axis=0)
    grad_tokens = (mm_tn(back_half, resid_group) + input_part).astype(BF)

    qkv_grad = quad_swap(qkv_grad.astype(BF).reshape(KV_HEADS, qkv_rows, width))
    qkv_grad = qkv_grad.transpose(1, 0, 2).astype(F32)
    qkv_share = jnp.concatenate(
        [
            qkv_grad[:, :, :qcols].reshape(qkv_rows, QDIM),
            qkv_grad[:, :, qcols : qcols + HEAD_DIM].reshape(qkv_rows, KVDIM),
            qkv_grad[:, :, qcols + HEAD_DIM :].reshape(qkv_rows, KVDIM),
        ],
        axis=1,
    )

    gains_grad = jnp.concatenate(
        [gain_attn_grad, gain_ffn_grad, query_gain_grad[0], key_gain_grad[0]]
    )
    share_rows = -(-small_size // (8 * LANES)) * 8
    small_grad = jnp.concatenate(
        [router_grad.reshape(device_count, router_size), gains_grad.reshape(device_count, gain_rows)],
        axis=1,
    )
    small_grad = jnp.pad(small_grad, ((0, 0), (0, share_rows * LANES - small_size)))
    small_share = jnp.sum(
        exchange(small_grad.reshape(device_count, share_rows, LANES), ALL_AXES), axis=0
    ).reshape(share_rows * LANES)
    router_share = small_share[:router_size].reshape(qkv_rows, experts_all)
    gains_share = small_share[router_size:small_size]
    return (layer_out, grad_tokens, qkv_share, out_share, router_share, gains_share, grad_expert)


def solution(mesh):
    shape = dict(mesh.shape)
    inner = Mesh(
        mesh.devices.reshape(shape["dp"] // (NEAR * CORES), NEAR, CORES, shape["seq"]), ALL_AXES
    )
    rows = P(ALL_AXES, None)
    in_specs = (
        rows,
        rows,
        rows,
        rows,
        rows,
        P(ALL_AXES),
        P(ALL_AXES, None, None),
        P(DP_AXES, None),
        P(DP_AXES, None),
        P(DP_AXES, None, None),
    )
    out_specs = (rows, rows, rows, rows, rows, P(ALL_AXES), P(ALL_AXES, None, None))
    return jax.shard_map(shards, mesh=inner, in_specs=in_specs, out_specs=out_specs, check_vma=False)
```

```python
import functools

import jax
import jax.numpy as jnp
from jax import lax
from jax.experimental import pallas as pl
from jax.experimental.pallas import tpu as pltpu
from jax.sharding import Mesh
from jax.sharding import PartitionSpec as P

D = 2048
HEADS = 32
KV_HEADS = 4
HEAD_DIM = 128
FF = 768
TOPK = 8
NSEG = 4
TOK_DEV = 128
ROW = 256
QDIM = 4096
KVDIM = 512
NEAR = 2
CORES = 2
LANES = 128

EPS = 1e-06
THETA = 1000000.0
BF = jnp.bfloat16
F32 = jnp.float32

FAR_AXIS = "far"
NEAR_AXIS = "near"
CORE_AXIS = "core"
SEQ_AXIS = "seq"
SLAB_AXES = (NEAR_AXIS, CORE_AXIS, SEQ_AXIS)
HEAD_AXES = (NEAR_AXIS, SEQ_AXIS)
ALL_AXES = (FAR_AXIS, NEAR_AXIS, CORE_AXIS, SEQ_AXIS)
DP_AXES = (FAR_AXIS, NEAR_AXIS, CORE_AXIS)


def rms_norm(values, scales):
    return values * lax.rsqrt(jnp.mean(values * values, axis=-1, keepdims=True) + EPS) * scales


def rotary(values, cosine, sine_part):
    half_width = values.shape[-1] // 2
    front_part = values[..., :half_width]
    back_part = values[..., half_width:]
    cos_wide = cosine[..., None, :]
    sin_wide = sine_part[..., None, :]
    return jnp.concatenate(
        [
            front_part * cos_wide - back_part * sin_wide,
            back_part * cos_wide + front_part * sin_wide,
        ],
        axis=-1,
    )


def tables(positions, head_width):
    half_width = head_width // 2
    inverse = THETA ** (-(jnp.arange(half_width, dtype=F32) * 2.0 / head_width))
    angles = positions.astype(F32)[..., None] * inverse
    return (jnp.cos(angles), jnp.sin(angles))


def dot(left, right, dims):
    return lax.dot_general(left, right, (dims, ((), ())), preferred_element_type=F32)


def mm(left, right):
    return dot(left, right, ((1,), (0,)))


def mm_nt(left, right):
    return dot(left, right, ((1,), (1,)))


def mm_tn(left, right):
    return dot(left, right, ((0,), (0,)))


def swap(value, axis):
    return lax.ppermute(value, axis, [(0, 1), (1, 0)])


def pair_order(own, other, axis):
    first = lax.axis_index(axis) == 0
    return (jnp.where(first, own, other), jnp.where(first, other, own))


def exchange(value, axes):
    return lax.all_to_all(value, axes, split_axis=0, concat_axis=0, tiled=True)


def quad_index():
    return lax.axis_index(NEAR_AXIS) * 2 + lax.axis_index(SEQ_AXIS)


def quad_send(parts, step):
    block = lax.dynamic_index_in_dim(parts, lax.bitwise_xor(quad_index(), step), 0, keepdims=False)
    return lax.ppermute(block, HEAD_AXES, [(i, i ^ step) for i in range(4)])


def quad_order(found):
    low = pair_order(found[0], found[1], SEQ_AXIS)
    high = pair_order(found[2], found[3], SEQ_AXIS)
    rows = [pair_order(low[k], high[k], NEAR_AXIS) for k in range(2)]
    return jnp.stack([rows[0][0], rows[1][0], rows[0][1], rows[1][1]])


def quad_gather(value):
    found = [value] + [
        lax.ppermute(value, HEAD_AXES, [(i, i ^ step) for i in range(4)]) for step in range(1, 4)
    ]
    return quad_order(found)


def quad_parts(parts):
    own = lax.dynamic_index_in_dim(parts, quad_index(), 0, keepdims=False)
    return [own] + [quad_send(parts, step) for step in range(1, 4)]


def quad_swap(parts):
    return quad_order(quad_parts(parts))


def quad_sum(parts):
    total = lax.dynamic_index_in_dim(parts, quad_index(), 0, keepdims=False).astype(F32)
    for step in range(1, 4):
        total = total + quad_send(parts, step).astype(F32)
    return total


def far_begin(parts, count):
    if count != 4:
        return [far_shift(parts[step].astype(BF), -step, count) for step in range(1, count)]
    return [far_shift(parts[2].astype(BF), -1, count), far_shift(parts[3].astype(BF), 1, count)]


def far_end(parts, found, count):
    total = parts[0].astype(F32)
    if count != 4:
        for part in found:
            total = total + part.astype(F32)
        return total
    relay = (parts[1].astype(F32) + found[0].astype(F32)).astype(BF)
    return total + found[1].astype(F32) + far_shift(relay, -1, count).astype(F32)


def far_parts(values, count):
    here = lax.axis_index(FAR_AXIS)
    return [
        lax.dynamic_index_in_dim(values, lax.rem(here + count - step, count), 0, keepdims=False)
        for step in range(count)
    ]


def far_all(value, count, first=None):
    ahead = count // 2
    found = [value] + [None] * (count - 1)
    found[1] = far_shift(value, 1, count)
    if count > 2:
        found[count - 1] = far_shift(value, -1, count)
    for step in range(2, ahead + 1):
        found[step] = far_shift(found[step - 1], 1, count)
    for step in range(count - 2, ahead, -1):
        found[step] = far_shift(found[step + 1], -1, count)
    return found


def far_stack(found):
    count = len(found)
    here = lax.axis_index(FAR_AXIS)
    zeros = (0,) * found[0].ndim
    full = jnp.zeros((count,) + found[0].shape, found[0].dtype)
    for step, chunk in enumerate(found):
        full = lax.dynamic_update_slice(full, chunk[None], (lax.rem(here + count - step, count),) + zeros)
    return full


def tie(*values):
    return lax.optimization_barrier(values)


def far_shift(value, step, count):
    return lax.ppermute(value, FAR_AXIS, [(i, (i + step) % count) for i in range(count)])


def far_next(value, count):
    return lax.ppermute(value, FAR_AXIS, [(i, (i + 1) % count) for i in range(count)])


def quad_xor(value, step):
    return lax.ppermute(value, HEAD_AXES, [(i, i ^ step) for i in range(4)])


def slab_send(blocks):
    return [blocks[0]] + [quad_xor(blocks[step], step) for step in range(1, 4)]


def slab_take(got):
    keep = quad_order([part[0] for part in got])
    other = swap(quad_order([part[1] for part in got]), CORE_AXIS)
    first, second = pair_order(keep, other, CORE_AXIS)
    shape = (NEAR, 2) + keep.shape[1:]
    return jnp.stack([first.reshape(shape), second.reshape(shape)], axis=1)


def slab_return(rows):
    keep, give = pair_order(rows[:, 0], rows[:, 1], CORE_AXIS)
    both = jnp.stack([keep, swap(give, CORE_AXIS)], axis=2)
    return quad_parts(both.reshape((4, 2) + rows.shape[3:]))


def expert_kernel(
    here_ref, in_ref, cot_ref, mask_ref, router_ref, gate_ref, up_ref, down_ref,
    gate_grad_ref, up_grad_ref, active_ref, grad_ref, in_grad_ref, gated_ref, dot_ref,
    out_total, in_total, gate_slot,
):
    block = pl.program_id(0)

    @pl.when(block == 0)
    def _():
        chosen = mask_ref[...].astype(F32) > 0.5
        logits = jnp.where(chosen, mm(in_ref[...], router_ref[...]), -1e30)
        exped = jnp.where(chosen, jnp.exp(logits - jnp.max(logits, axis=-1, keepdims=True)), 0.0)
        total = jnp.sum(exped, axis=-1, keepdims=True)
        mine = lax.broadcasted_iota(jnp.int32, exped.shape, 1) == here_ref[0]
        picked = jnp.sum(jnp.where(mine, exped, 0.0), axis=-1, keepdims=True)
        gate = picked / jnp.where(total > 0.0, total, 1.0)
        gate_slot[...] = jnp.broadcast_to(gate, gate_slot.shape)
        grad_ref[...] = (gate * cot_ref[...].astype(F32)).astype(BF)
        out_total[...] = jnp.zeros_like(out_total)
        in_total[...] = jnp.zeros_like(in_total)

    gate_pre = mm(in_ref[...], gate_ref[...])
    up_pre = mm(in_ref[...], up_ref[...])
    act_grad = mm(grad_ref[...], down_ref[...])
    sig_gate = jax.nn.sigmoid(gate_pre)
    silu_val = gate_pre * sig_gate
    active = (silu_val * up_pre).astype(BF)
    silu_slope = sig_gate * (1.0 + gate_pre * (1.0 - sig_gate))
    gate_grad = (act_grad * up_pre * silu_slope).astype(BF)
    up_grad = (act_grad * silu_val).astype(BF)
    active_ref[...] = active
    gate_grad_ref[...] = gate_grad
    up_grad_ref[...] = up_grad
    out_total[...] += mm_nt(active, down_ref[...])
    in_total[...] += mm_nt(gate_grad, gate_ref[...]) + mm_nt(up_grad, up_ref[...])

    @pl.when(block == pl.num_programs(0) - 1)
    def _():
        out = out_total[...].astype(BF).astype(F32)
        dot_ref[...] = jnp.sum(cot_ref[...].astype(F32) * out, axis=-1, keepdims=True)
        gated_ref[...] = (gate_slot[:, :1] * out).astype(BF)
        in_grad_ref[...] = in_total[...].astype(BF)


def expert_chunk(here, in_chunk, cot_chunk, mask, router, weight):
    rows = in_chunk.shape[0]
    tile = 256
    steps = FF // tile
    whole = pl.BlockSpec((rows, D), lambda j, h: (0, 0))
    piece = pl.BlockSpec((rows, tile), lambda j, h: (0, j))
    low = jax.ShapeDtypeStruct((rows, FF), BF)
    wide = jax.ShapeDtypeStruct((rows, D), BF)
    return pl.pallas_call(
        expert_kernel,
        grid_spec=pltpu.PrefetchScalarGridSpec(
            num_scalar_prefetch=1,
            grid=(steps,),
            in_specs=[
                whole,
                whole,
                pl.BlockSpec(mask.shape, lambda j, h: (0, 0)),
                pl.BlockSpec(router.shape, lambda j, h: (0, 0)),
                pl.BlockSpec((D, tile), lambda j, h: (0, j)),
                pl.BlockSpec((D, tile), lambda j, h: (0, steps + j)),
                pl.BlockSpec((D, tile), lambda j, h: (0, 2 * steps + j)),
            ],
            out_specs=[
                piece, piece, piece, whole, whole, whole,
                pl.BlockSpec((rows, 1), lambda j, h: (0, 0)),
            ],
            scratch_shapes=[
                pltpu.VMEM((rows, D), F32),
                pltpu.VMEM((rows, D), F32),
                pltpu.VMEM((rows, LANES), F32),
            ],
        ),
        out_shape=[low, low, low, wide, wide, wide, jax.ShapeDtypeStruct((rows, 1), F32)],
        compiler_params=pltpu.CompilerParams(vmem_limit_bytes=40 << 20),
        cost_estimate=pl.CostEstimate(flops=1 << 20, bytes_accessed=1 << 20, transcendentals=0),
        name="expert_chunk",
    )(here, in_chunk, cot_chunk, mask, router, weight, weight, weight)


def expert_grad_kernel(count, *refs):
    lists = [refs[k * count : (k + 1) * count] for k in range(5)]
    out_ref = refs[5 * count]
    column = pl.program_id(1)

    def total(lefts, rights):
        found = mm_tn(lefts[0][...], rights[0][...])
        for left, right in zip(lefts[1:], rights[1:]):
            found = found + mm_tn(left[...], right[...])
        out_ref[...] = found

    for place, (left, right) in enumerate(((0, 2), (0, 3), (1, 4))):
        pl.when(column == place)(functools.partial(total, lists[left], lists[right]))


def expert_grads(in_rows, grad_rows, gate_grads, up_grads, actives):
    count = len(in_rows)
    rows = in_rows[0].shape[0]
    tile = 512
    tall = pl.BlockSpec((rows, tile), lambda i, j: (0, i))
    whole = pl.BlockSpec((rows, FF), lambda i, j: (0, 0))
    return pl.pallas_call(
        functools.partial(expert_grad_kernel, count),
        grid=(D // tile, 3),
        in_specs=[tall] * (2 * count) + [whole] * (3 * count),
        out_specs=pl.BlockSpec((tile, FF), lambda i, j: (i, j)),
        out_shape=jax.ShapeDtypeStruct((D, 3 * FF), F32),
        compiler_params=pltpu.CompilerParams(vmem_limit_bytes=48 << 20),
        cost_estimate=pl.CostEstimate(flops=1 << 20, bytes_accessed=1 << 20, transcendentals=0),
        name="expert_grads",
    )(*in_rows, *grad_rows, *gate_grads, *up_grads, *actives)


def head_normed(raw, gain_ref):
    scale = lax.rsqrt(jnp.mean(raw * raw, axis=-1, keepdims=True) + EPS)
    normal = raw * scale
    return (normal, scale, normal * gain_ref[...])


def turned(values, cos_ref, sin_ref):
    return values * cos_ref[...] + pltpu.roll(values, HEAD_DIM // 2, 1) * sin_ref[...]


def turned_back(values, cos_ref, sin_ref):
    return values * cos_ref[...] + pltpu.roll(values * sin_ref[...], HEAD_DIM // 2, 1)


def head_probs(query, key, row_ref, start_ref, key_row_ref):
    scores = mm_nt(query, key) * HEAD_DIM ** (-0.5)
    allowed = (key_row_ref[0] <= row_ref[0]) & (key_row_ref[0] >= start_ref[0])
    scores = jnp.where(allowed, scores, -1e30)
    exped = jnp.exp(scores - jnp.max(scores, axis=-1, keepdims=True))
    return exped / jnp.sum(exped, axis=-1, keepdims=True)


def attend_kernel(
    query_ref, key_ref, value_ref, cos_ref, sin_ref, qgain_ref, kgain_ref,
    row_ref, start_ref, key_row_ref, mixed_ref, key_low, value_low,
):
    @pl.when(pl.program_id(1) == 0)
    def _():
        key_low[...] = turned(head_normed(key_ref[...], kgain_ref)[2], cos_ref, sin_ref).astype(BF)
        value_low[...] = value_ref[...].astype(BF)

    query = turned(head_normed(query_ref[...], qgain_ref)[2], cos_ref, sin_ref).astype(BF)
    probs = head_probs(query, key_low[...], row_ref, start_ref, key_row_ref)
    mixed_ref[...] = mm(probs.astype(BF), value_low[...]).astype(BF)


def attend_back_kernel(
    query_ref, key_ref, value_ref, cos_ref, sin_ref, qgain_ref, kgain_ref,
    row_ref, start_ref, key_row_ref, grad_ref,
    query_out, key_out, value_out, qgain_out, kgain_out,
    key_low, value_low, key_total, value_total,
):
    group, head = pl.program_id(0), pl.program_id(1)
    score_scale = HEAD_DIM ** (-0.5)

    @pl.when((group == 0) & (head == 0))
    def _():
        qgain_out[...] = jnp.zeros_like(qgain_out)
        kgain_out[...] = jnp.zeros_like(kgain_out)

    @pl.when(head == 0)
    def _():
        key_low[...] = turned(head_normed(key_ref[...], kgain_ref)[2], cos_ref, sin_ref).astype(BF)
        value_low[...] = value_ref[...].astype(BF)
        key_total[...] = jnp.zeros_like(key_total)
        value_total[...] = jnp.zeros_like(value_total)

    def raw_grad(grad, normal, scale, gain_ref, gain_out):
        grad = turned_back(grad, cos_ref, sin_ref)
        gain_out[...] += jnp.sum(grad * normal, axis=0, keepdims=True)
        grad = grad * gain_ref[...]
        return scale * (grad - normal * jnp.mean(normal * grad, axis=-1, keepdims=True))

    normal, scale, gained = head_normed(query_ref[...], qgain_ref)
    query = turned(gained, cos_ref, sin_ref).astype(BF)
    probs = head_probs(query, key_low[...], row_ref, start_ref, key_row_ref)
    grad = grad_ref[...]
    value_total[...] += mm_tn(probs.astype(BF), grad)
    prob_grad = mm_nt(grad, value_low[...])
    score_grad = (probs * (prob_grad - jnp.sum(probs * prob_grad, axis=-1, keepdims=True))).astype(BF)
    key_total[...] += mm_tn(score_grad, query) * score_scale
    query_grad = mm(score_grad, key_low[...]) * score_scale
    query_out[...] = raw_grad(query_grad, normal, scale, qgain_ref, qgain_out).astype(BF)

    @pl.when(head == pl.num_programs(1) - 1)
    def _():
        key_normal, key_scale, _ = head_normed(key_ref[...], kgain_ref)
        key_out[...] = raw_grad(key_total[...], key_normal, key_scale, kgain_ref, kgain_out).astype(BF)
        value_out[...] = value_total[...].astype(BF)


def attend_specs(heads):
    head = pl.BlockSpec((ROW, HEAD_DIM), lambda b, h: (b, h))
    whole = pl.BlockSpec((ROW, HEAD_DIM), lambda b, h: (b, 0))
    gain = pl.BlockSpec((1, HEAD_DIM), lambda b, h: (0, 0))
    column = pl.BlockSpec((1, ROW, 1), lambda b, h: (b, 0, 0))
    specs = [
        head,
        pl.BlockSpec((ROW, HEAD_DIM), lambda b, h: (b, heads)),
        pl.BlockSpec((ROW, HEAD_DIM), lambda b, h: (b, heads + 1)),
        whole, whole, gain, gain, column, column,
        pl.BlockSpec((1, 1, ROW), lambda b, h: (b, 0, 0)),
    ]
    return (specs, head, whole, gain)


def attend(projected, shared, heads):
    specs, head, _, _ = attend_specs(heads)
    rows = projected.shape[0]
    return pl.pallas_call(
        attend_kernel,
        grid=(rows // ROW, heads),
        in_specs=specs,
        out_specs=head,
        out_shape=jax.ShapeDtypeStruct((rows, heads * HEAD_DIM), BF),
        scratch_shapes=[pltpu.VMEM((ROW, HEAD_DIM), BF)] * 2,
        cost_estimate=pl.CostEstimate(flops=1 << 20, bytes_accessed=1 << 20, transcendentals=0),
        name="attend",
    )(projected, projected, projected, *shared)


def attend_back(projected, shared, grad, heads):
    specs, head, whole, gain = attend_specs(heads)
    rows = projected.shape[0]
    return pl.pallas_call(
        attend_back_kernel,
        grid=(rows // ROW, heads),
        in_specs=specs + [head],
        out_specs=[head, whole, whole, gain, gain],
        out_shape=[
            jax.ShapeDtypeStruct((rows, heads * HEAD_DIM), BF),
            jax.ShapeDtypeStruct((rows, HEAD_DIM), BF),
            jax.ShapeDtypeStruct((rows, HEAD_DIM), BF),
            jax.ShapeDtypeStruct((1, HEAD_DIM), F32),
            jax.ShapeDtypeStruct((1, HEAD_DIM), F32),
        ],
        scratch_shapes=[pltpu.VMEM((ROW, HEAD_DIM), BF)] * 2 + [pltpu.VMEM((ROW, HEAD_DIM), F32)] * 2,
        cost_estimate=pl.CostEstimate(flops=1 << 20, bytes_accessed=1 << 20, transcendentals=0),
        name="attend_back",
    )(projected, projected, projected, *shared, grad)


def shards(tokens, cotangent, w_qkv, w_out, w_router, norm_gains, w_expert, lengths, deal, routes):
    far_count = lax.axis_size(FAR_AXIS)
    device_count = far_count * NEAR * CORES * 2
    experts_all = w_router.shape[1]
    capacity = TOK_DEV * TOPK // experts_all
    slot_count = experts_all * capacity
    seq_index = lax.axis_index(SEQ_AXIS)
    near_index = lax.axis_index(NEAR_AXIS)
    far_index = lax.axis_index(FAR_AXIS)
    core_index = lax.axis_index(CORE_AXIS)
    per_group = HEADS // KV_HEADS
    qcols = per_group * HEAD_DIM
    width = qcols + 2 * HEAD_DIM
    qkv_rows = w_qkv.shape[0]
    out_rows = w_out.shape[0]
    gain_rows = norm_gains.shape[0]
    score_scale = HEAD_DIM ** (-0.5)

    wide = jnp.concatenate(
        [
            w_qkv[:, :QDIM].reshape(qkv_rows, KV_HEADS, qcols),
            w_qkv[:, QDIM : QDIM + KVDIM].reshape(qkv_rows, KV_HEADS, HEAD_DIM),
            w_qkv[:, QDIM + KVDIM :].reshape(qkv_rows, KV_HEADS, HEAD_DIM),
        ],
        axis=2,
    ).transpose(1, 0, 2)
    core_rows = KV_HEADS * qkv_rows
    half_rows = 2 * qkv_rows
    wide_found = quad_parts(wide)
    tokens, *wide_found = tie(tokens, *wide_found)
    qkv_far = far_all(quad_order(wide_found).reshape(core_rows, width), far_count)

    tokens_both = quad_gather(tokens).reshape(2, ROW, D)
    table = jnp.concatenate([deal, jnp.pad(lengths, ((0, 0), (0, LANES - NSEG)))], axis=1)
    table_both = jnp.concatenate(pair_order(table, swap(table, NEAR_AXIS), NEAR_AXIS), axis=0)
    deal_both = table_both[:, :ROW]
    ends = jnp.cumsum(table_both[:, ROW : ROW + NSEG], axis=1)
    starts = ends - table_both[:, ROW : ROW + NSEG]
    seg_both = jnp.sum((deal_both[:, :, None] >= ends[:, None, :]).astype(jnp.int32), axis=2)
    picked = seg_both[:, :, None] == jnp.arange(NSEG, dtype=jnp.int32)[None, None, :]
    pos_both = deal_both - jnp.sum(jnp.where(picked, starts[:, None, :], 0), axis=2)
    dealt_hot = (deal_both[:, :, None] == jnp.arange(ROW, dtype=jnp.int32)[None, None, :]).astype(BF)
    hot_mine = lax.dynamic_index_in_dim(dealt_hot, near_index, 0, keepdims=False)
    hot_half = lax.dynamic_slice_in_dim(hot_mine, seq_index * TOK_DEV, TOK_DEV, axis=0)
    back_half = lax.dynamic_slice_in_dim(hot_mine, seq_index * TOK_DEV, TOK_DEV, axis=1)
    seg_mine = lax.dynamic_slice_in_dim(
        lax.dynamic_index_in_dim(seg_both, near_index, 0, keepdims=False), seq_index * TOK_DEV, TOK_DEV
    )

    expert_ids = jnp.arange(experts_all, dtype=jnp.int32)
    chosen_rows = jnp.sum(
        (routes[0][:, :, None] == expert_ids[None, None, :]).astype(jnp.int32), axis=1
    ).astype(BF)
    chosen = mm(hot_half, chosen_rows)
    live = jnp.where((seg_mine != NSEG - 1)[:, None], chosen, 0.0)
    steps = jnp.arange(TOK_DEV, dtype=jnp.int32)
    earlier = (steps[None, :] < steps[:, None]).astype(BF)
    place = mm(earlier, live.astype(BF))
    place = jnp.where(live > 0.5, place, -1.0).astype(jnp.int32)
    slot_hot = place.T[:, None, :] == jnp.arange(capacity, dtype=jnp.int32)[None, :, None]
    slot_low = slot_hot.astype(BF).reshape(slot_count, TOK_DEV)

    slab = NEAR * CORES * 2
    slab_index = (near_index * CORES + core_index) * 2 + seq_index
    slab_ids = jnp.arange(slab, dtype=jnp.int32)
    out_order = jnp.array([0, 2, 1, 3, 4, 6, 5, 7], jnp.int32)
    place_far = far_stack(far_all(place.T.astype(BF), far_count))

    def slots_of(places, step):
        found = lax.dynamic_index_in_dim(
            places, lax.rem(far_index + far_count - step, far_count), 0, keepdims=False
        )
        found = found[:, None, :] == jnp.arange(capacity, dtype=jnp.int32)[None, :, None]
        return found.astype(BF).reshape(slab * capacity, TOK_DEV)

    place_slab = lax.dynamic_slice_in_dim(place_far, far_index * slab, slab, axis=1).astype(jnp.int32)
    turned_ids = lax.bitwise_xor(out_order, slab_index)
    place_turned = jnp.sum(
        jnp.where(
            (turned_ids[:, None] == slab_ids[None, :])[None, :, :, None], place_slab[:, None], 0
        ),
        axis=2,
    )
    chunk_slots = [slots_of(place_slab, step) for step in range(far_count)]
    send_slots = [slots_of(place_turned, step) for step in range(far_count)]
    chunk_steps = jnp.arange(far_count, dtype=jnp.int32)
    source_ids = (
        lax.rem(far_index + far_count - chunk_steps, far_count)[:, None] * slab + slab_ids[None, :]
    ).reshape(device_count)
    device_ids = jnp.arange(device_count, dtype=jnp.int32)
    found_at = jnp.sum(
        jnp.where(source_ids[None, :] == device_ids[:, None], device_ids[None, :], 0), axis=1
    )

    def to_blocks(rows):
        return rows.reshape(4, 2, rows.shape[0] // slab, rows.shape[1])


    router_size = qkv_rows * experts_all
    small_size = router_size + gain_rows
    mask_size = capacity * experts_all
    small_rows = -(-(small_size + mask_size) // (8 * LANES)) * 8
    small = jnp.broadcast_to(
        jnp.concatenate([w_router.reshape(router_size), norm_gains]), (device_count, small_size)
    )
    slot_mask = mm(slot_low, chosen.astype(BF)).astype(BF).reshape(device_count, mask_size)
    small = jnp.concatenate([slot_mask, small], axis=1)
    small = jnp.pad(small, ((0, 0), (0, small_rows * LANES - small_size - mask_size)))
    small_all = exchange(small.reshape(device_count, small_rows, LANES), ALL_AXES).reshape(
        device_count, small_rows * LANES
    )
    mask_back = jnp.take(small_all[:, :mask_size], source_ids, axis=0).reshape(
        far_count, slab * capacity, experts_all
    )
    small_all = small_all[:, mask_size : mask_size + small_size]
    router_full = small_all[:, :router_size].reshape(D, experts_all)
    gains_float = small_all[:, router_size:].reshape(-1).astype(F32)
    gain_attn = gains_float[:D]
    gain_ffn = gains_float[D : 2 * D]
    gain_query = gains_float[2 * D : 2 * D + HEAD_DIM]
    gain_key = gains_float[2 * D + HEAD_DIM :]

    cot_pair = jnp.concatenate(pair_order(cotangent, swap(cotangent, SEQ_AXIS), SEQ_AXIS), axis=0)
    cot_low = mm(hot_half, cot_pair).astype(BF)
    cot_rows = cot_low.astype(F32)
    cot_sent = [
        mm(slot_low, half).astype(BF).reshape(device_count, capacity, D // 2)
        for half in (cot_low[:, : D // 2], cot_low[:, D // 2 :])
    ]
    qkv_own = far_stack(qkv_far).reshape(far_count * NEAR, half_rows, width)
    qkv_mine = jnp.stack(pair_order(qkv_own, swap(qkv_own, CORE_AXIS), CORE_AXIS), axis=1).reshape(
        D, width
    )

    out_slabs = far_stack(far_all(w_out, far_count)).reshape(
        KV_HEADS, far_count // KV_HEADS * out_rows, D
    )
    far_part = far_count // KV_HEADS
    x_both = lax.dot_general(
        dealt_hot, tokens_both, (((2,), (1,)), ((0,), (0,))), preferred_element_type=F32
    )
    x_rows = lax.dynamic_slice(
        x_both, (near_index, seq_index * TOK_DEV, 0), (1, TOK_DEV, D)
    )[0]
    normed_low = rms_norm(x_both.reshape(2 * ROW, D), gain_attn).astype(BF)
    projected, *cot_sent = tie(mm(normed_low, qkv_mine), *cot_sent)
    cot_back = [exchange(half, ALL_AXES) for half in cot_sent]
    cosine, sine_part = tables(pos_both.reshape(2 * ROW), HEAD_DIM)
    shared = (
        jnp.concatenate([cosine, cosine], axis=1),
        jnp.concatenate([-sine_part, sine_part], axis=1),
        gain_query[None],
        gain_key[None],
        deal_both[:, :, None],
        (deal_both - pos_both)[:, :, None],
        deal_both[:, None, :],
    )
    mixed_low = attend(projected, shared, per_group)
    out_found = quad_parts(out_slabs)
    mixed_low, *out_found = tie(mixed_low, *out_found)
    out_own = quad_order(out_found).reshape(NEAR * 2, far_part, out_rows, D)
    out_own = out_own.transpose(1, 0, 2, 3).reshape(far_part * NEAR, 2 * out_rows, D)
    out_mine = jnp.stack(pair_order(out_own, swap(out_own, CORE_AXIS), CORE_AXIS), axis=1).reshape(
        qcols, D
    )

    out_partial = mm(mixed_low, out_mine).astype(BF)
    out_partial, cot_back[0] = tie(out_partial, cot_back[0])
    residual = x_rows + quad_sum(out_partial.reshape(4, TOK_DEV, D))

    normed_two, ffn_back = jax.vjp(rms_norm, residual, gain_ffn)
    ffn_in = normed_two.astype(BF)
    logits = mm(ffn_in, router_full)
    logits = jnp.where(chosen > 0.5, logits, -1e30)
    gate_probs = jax.nn.softmax(logits, axis=-1)
    gate_probs = jnp.where(chosen > 0.5, gate_probs, 0.0)

    expert_weight = w_expert[0]
    expert_here = far_index * slab + slab_index
    in_rows, gate_grads, up_grads, grad_rows, actives, in_grads = ([] for _ in range(6))
    slot_dots, gated_outs = [None] * far_count, [None] * far_count
    arrived = []
    here = expert_here.reshape(1)
    order = list(range(far_count))
    far_rows = [ffn_in]
    for step in range(1, far_count):
        with jax.named_scope('rows_far%d' % step):
            far_rows.append(far_shift(far_rows[-1], 1, far_count))

    def gather(step, source):
        return mm(send_slots[step], source).astype(BF)

    sent = gather(0, ffn_in)

    def send_back(step):
        return slab_return(in_grads[step].reshape(NEAR, CORES, 2, capacity, D))

    def combine(step, found):
        back = jnp.concatenate(found, axis=0).reshape(slab * capacity, D)
        return mm_tn(send_slots[step], back).astype(BF if step else F32)

    ffn_in, cot_back[1] = tie(ffn_in, cot_back[1])
    cot_chunks = far_parts(
        jnp.concatenate(cot_back, axis=2).reshape(far_count, slab * capacity, D), far_count
    )
    pending = []
    for turn, step in enumerate(order):
        with jax.named_scope("rows_out%d" % turn):
            got = slab_send(to_blocks(sent))
        if turn + 1 < far_count:
            source = far_rows[order[turn + 1]]
            if turn > 0:
                source, up_grads[turn - 1] = tie(source, up_grads[turn - 1])
            sent = gather(order[turn + 1], source)
        if turn > 0:
            gate_grads[turn - 1], *got = tie(gate_grads[turn - 1], *got)
        with jax.named_scope("rows_core%d" % turn):
            in_chunk = slab_take(got).reshape(slab * capacity, D)
        if turn > 2:
            in_chunk, *pending = tie(in_chunk, *pending)
            partial = combine(order[turn - 2], pending)
            in_chunk, partial = tie(in_chunk, partial)
            with jax.named_scope("partial_far%d" % (turn - 2)):
                arrived.append(far_shift(partial, -order[turn - 2], far_count))
        gate_grad, up_grad, active, grad_chunk, in_grad, gated_out, slot_dot = expert_chunk(
            here, in_chunk, cot_chunks[step], mask_back[step], router_full, expert_weight
        )
        if turn > 2:
            gate_grad, arrived[-1] = tie(gate_grad, arrived[-1])
        in_rows.append(in_chunk)
        gate_grads.append(gate_grad)
        up_grads.append(up_grad)
        actives.append(active)
        grad_rows.append(grad_chunk)
        in_grads.append(in_grad)
        gated_outs[step] = gated_out.reshape(slab, capacity, D)
        slot_dots[step] = slot_dot[:, 0]
        if turn > 1:
            with jax.named_scope("rows_back%d" % (turn - 1)):
                pending = send_back(turn - 1)
    partial = None
    for turn in range(max(1, far_count - 2), far_count):
        if turn == far_count - 1:
            with jax.named_scope("rows_back%d" % turn):
                pending = send_back(turn)
        else:
            up_grads[-1], *pending = tie(up_grads[-1], *pending)
        partial = combine(order[turn], pending)
        if turn == far_count - 2:
            partial, in_grads[0] = tie(partial, in_grads[0])
        with jax.named_scope("partial_far%d" % turn):
            arrived.append(far_shift(partial, -order[turn], far_count))
    slot_dots[0], partial = tie(slot_dots[0], partial)
    with jax.named_scope("rows_back0"):
        from_experts = combine(0, send_back(0))
    for part in arrived:
        from_experts = from_experts + part.astype(F32)
    dot_sent = jnp.take(jnp.stack(slot_dots).reshape(device_count, capacity), found_at, axis=0)
    dot_back = exchange(dot_sent[:, None, :], ALL_AXES).reshape(experts_all, capacity)

    gate_grad = jnp.sum(jnp.where(slot_hot, dot_back[:, :, None], 0.0), axis=1).T
    mean_term = jnp.sum(gate_probs * gate_grad, axis=1, keepdims=True)
    logit_grad = (gate_probs * (gate_grad - mean_term)).astype(BF)
    router_grad = mm_tn(ffn_in, logit_grad)
    ffn_in_grad = from_experts + mm_nt(logit_grad, router_full)
    resid_part, gain_ffn_grad = ffn_back(ffn_in_grad)
    resid_low = (cot_rows + resid_part).astype(BF)

    in_rows[0], resid_low = tie(in_rows[0], resid_low)
    grad_expert = expert_grads(in_rows, grad_rows, gate_grads, up_grads, actives)[None]

    resid_both, grad_expert = tie(quad_gather(resid_low), grad_expert)
    resid_both = resid_both.reshape(2 * ROW, D)

    def core_sum(values):
        own, other = pair_order(values[:, 0], values[:, 1], CORE_AXIS)
        return own.astype(F32) + swap(other, CORE_AXIS).astype(F32)

    out_grad = mm_tn(mixed_low, resid_both).astype(BF)
    resid_both, out_grad = tie(resid_both, out_grad)
    mixed_grad = mm_nt(resid_both, out_mine).astype(BF)
    out_grad = core_sum(out_grad.reshape(far_part * NEAR, CORES, 2 * out_rows, D)).astype(BF)
    mixed_grad, out_grad = tie(mixed_grad, out_grad)
    out_grad = (
        out_grad
        .reshape(far_part, NEAR * 2, out_rows, D)
        .transpose(1, 0, 2, 3)
        .reshape(NEAR * 2, far_part * out_rows, D)
    )
    out_grad = quad_swap(out_grad).reshape(far_count, out_rows, D)
    query_grad, key_grad, value_grad, query_gain_grad, key_gain_grad = attend_back(
        projected, shared, mixed_grad, per_group
    )
    query_grad, out_grad = tie(query_grad, out_grad)
    out_sent = far_parts(out_grad, far_count)
    out_found = far_begin(out_sent, far_count)
    gated, query_grad = tie(jnp.stack(gated_outs, axis=1), query_grad)
    gated = exchange(gated, SLAB_AXES)
    out_parts = [
        mm_tn(hot, gated[:, step].reshape(slab * capacity, D)).astype(BF if step else F32)
        for step, hot in enumerate(chunk_slots)
    ]
    out_sum = far_end(out_parts, far_begin(out_parts, far_count), far_count)
    proj_grad = jnp.concatenate([query_grad, key_grad, value_grad], axis=1)

    back_grad = lax.dot_general(
        dealt_hot,
        proj_grad.reshape(2, ROW, width),
        (((1,), (1,)), ((0,), (0,))),
        preferred_element_type=F32,
    ).astype(BF).reshape(2 * ROW, width)
    qkv_grad = mm_tn(normed_low, proj_grad).astype(BF)
    back_grad, qkv_grad = tie(back_grad, qkv_grad)
    normed_partial = mm_nt(back_grad, qkv_mine).astype(BF)
    qkv_grad = core_sum(qkv_grad.reshape(far_count * NEAR, CORES, half_rows, width)).astype(BF)
    normed_partial, qkv_grad, *out_found = tie(normed_partial, qkv_grad, *out_found)
    qkv_parts = far_parts(qkv_grad.reshape(far_count, core_rows, width), far_count)
    qkv_found = far_begin(qkv_parts, far_count)
    out_share = far_end(out_sent, out_found, far_count)
    qkv_grad = far_end(qkv_parts, qkv_found, far_count)
    normed_grad = quad_sum(normed_partial.reshape(4, TOK_DEV, D))
    normed_grad, out_sum = tie(normed_grad, out_sum)
    final_rows = (residual + out_sum).astype(BF)
    final_pair = jnp.concatenate(
        pair_order(final_rows, swap(final_rows, SEQ_AXIS), SEQ_AXIS), axis=0
    )
    layer_out = mm_tn(back_half, final_pair).astype(BF)
    _, attn_back = jax.vjp(rms_norm, tokens.astype(F32), gain_attn)
    input_part, gain_attn_grad = attn_back(normed_grad)
    resid_group = lax.dynamic_slice_in_dim(resid_both, near_index * ROW, ROW, axis=0)
    grad_tokens = (mm_tn(back_half, resid_group) + input_part).astype(BF)

    qkv_grad = quad_swap(qkv_grad.astype(BF).reshape(KV_HEADS, qkv_rows, width))
    qkv_grad = qkv_grad.transpose(1, 0, 2).astype(F32)
    qkv_share = jnp.concatenate(
        [
            qkv_grad[:, :, :qcols].reshape(qkv_rows, QDIM),
            qkv_grad[:, :, qcols : qcols + HEAD_DIM].reshape(qkv_rows, KVDIM),
            qkv_grad[:, :, qcols + HEAD_DIM :].reshape(qkv_rows, KVDIM),
        ],
        axis=1,
    )

    gains_grad = jnp.concatenate(
        [gain_attn_grad, gain_ffn_grad, query_gain_grad[0], key_gain_grad[0]]
    )
    share_rows = -(-small_size // (8 * LANES)) * 8
    small_grad = jnp.concatenate(
        [router_grad.reshape(device_count, router_size), gains_grad.reshape(device_count, gain_rows)],
        axis=1,
    )
    small_grad = jnp.pad(small_grad, ((0, 0), (0, share_rows * LANES - small_size)))
    small_share = jnp.sum(
        exchange(small_grad.reshape(device_count, share_rows, LANES), ALL_AXES), axis=0
    ).reshape(share_rows * LANES)
    router_share = small_share[:router_size].reshape(qkv_rows, experts_all)
    gains_share = small_share[router_size:small_size]
    return (layer_out, grad_tokens, qkv_share, out_share, router_share, gains_share, grad_expert)


def solution(mesh):
    shape = dict(mesh.shape)
    inner = Mesh(
        mesh.devices.reshape(shape["dp"] // (NEAR * CORES), NEAR, CORES, shape["seq"]), ALL_AXES
    )
    rows = P(ALL_AXES, None)
    in_specs = (
        rows,
        rows,
        rows,
        rows,
        rows,
        P(ALL_AXES),
        P(ALL_AXES, None, None),
        P(DP_AXES, None),
        P(DP_AXES, None),
        P(DP_AXES, None, None),
    )
    out_specs = (rows, rows, rows, rows, rows, P(ALL_AXES), P(ALL_AXES, None, None))
    return jax.shard_map(shards, mesh=inner, in_specs=in_specs, out_specs=out_specs, check_vma=False)
```

```python
import functools

import jax
import jax.numpy as jnp
from jax import lax
from jax.experimental import pallas as pl
from jax.experimental.pallas import tpu as pltpu
from jax.sharding import Mesh
from jax.sharding import PartitionSpec as P

D = 2048
HEADS = 32
KV_HEADS = 4
HEAD_DIM = 128
FF = 768
TOPK = 8
NSEG = 4
TOK_DEV = 128
ROW = 256
QDIM = 4096
KVDIM = 512
NEAR = 2
CORES = 2
SLAB = NEAR * CORES * 2
LANES = 128

EPS = 1e-06
THETA = 1000000.0
BF = jnp.bfloat16
F32 = jnp.float32

FAR_AXIS = "far"
NEAR_AXIS = "near"
CORE_AXIS = "core"
SEQ_AXIS = "seq"
SLAB_AXES = (NEAR_AXIS, CORE_AXIS, SEQ_AXIS)
HEAD_AXES = (NEAR_AXIS, SEQ_AXIS)
ALL_AXES = (FAR_AXIS, NEAR_AXIS, CORE_AXIS, SEQ_AXIS)
DP_AXES = (FAR_AXIS, NEAR_AXIS, CORE_AXIS)


def rms_norm(values, scales):
    return values * lax.rsqrt(jnp.mean(values * values, axis=-1, keepdims=True) + EPS) * scales


def rotary(values, cosine, sine_part):
    half_width = values.shape[-1] // 2
    front_part = values[..., :half_width]
    back_part = values[..., half_width:]
    cos_wide = cosine[..., None, :]
    sin_wide = sine_part[..., None, :]
    return jnp.concatenate(
        [
            front_part * cos_wide - back_part * sin_wide,
            back_part * cos_wide + front_part * sin_wide,
        ],
        axis=-1,
    )


def tables(positions, head_width):
    half_width = head_width // 2
    inverse = THETA ** (-(jnp.arange(half_width, dtype=F32) * 2.0 / head_width))
    angles = positions.astype(F32)[..., None] * inverse
    return (jnp.cos(angles), jnp.sin(angles))


def dot(left, right, dims):
    return lax.dot_general(left, right, (dims, ((), ())), preferred_element_type=F32)


def mm(left, right):
    return dot(left, right, ((1,), (0,)))


def mm_nt(left, right):
    return dot(left, right, ((1,), (1,)))


def mm_tn(left, right):
    return dot(left, right, ((0,), (0,)))


def swap(value, axis):
    return lax.ppermute(value, axis, [(0, 1), (1, 0)])


def pair_order(own, other, axis):
    first = lax.axis_index(axis) == 0
    return (jnp.where(first, own, other), jnp.where(first, other, own))


def exchange(value, axes):
    return lax.all_to_all(value, axes, split_axis=0, concat_axis=0, tiled=True)


def quad_index():
    return lax.axis_index(NEAR_AXIS) * 2 + lax.axis_index(SEQ_AXIS)


def quad_send(parts, step):
    block = lax.dynamic_index_in_dim(parts, lax.bitwise_xor(quad_index(), step), 0, keepdims=False)
    return lax.ppermute(block, HEAD_AXES, [(i, i ^ step) for i in range(4)])


def quad_order(found):
    low = pair_order(found[0], found[1], SEQ_AXIS)
    high = pair_order(found[2], found[3], SEQ_AXIS)
    rows = [pair_order(low[k], high[k], NEAR_AXIS) for k in range(2)]
    return jnp.stack([rows[0][0], rows[1][0], rows[0][1], rows[1][1]])


def quad_gather(value):
    found = [value] + [
        lax.ppermute(value, HEAD_AXES, [(i, i ^ step) for i in range(4)]) for step in range(1, 4)
    ]
    return quad_order(found)


def quad_parts(parts):
    own = lax.dynamic_index_in_dim(parts, quad_index(), 0, keepdims=False)
    return [own] + [quad_send(parts, step) for step in range(1, 4)]


def quad_swap(parts):
    return quad_order(quad_parts(parts))


def sum_parts(parts):
    total = parts[0].astype(F32)
    for part in parts[1:]:
        total = total + part.astype(F32)
    return total


def far_begin(parts, count):
    if count != 4:
        return [far_shift(parts[step].astype(BF), -step, count) for step in range(1, count)]
    return [far_shift(parts[2].astype(BF), -1, count), far_shift(parts[3].astype(BF), 1, count)]


def far_end(parts, found, count):
    total = parts[0].astype(F32)
    if count != 4:
        for part in found:
            total = total + part.astype(F32)
        return total
    relay = (parts[1].astype(F32) + found[0].astype(F32)).astype(BF)
    return total + found[1].astype(F32) + far_shift(relay, -1, count).astype(F32)


def far_parts(values, count):
    here = lax.axis_index(FAR_AXIS)
    return [
        lax.dynamic_index_in_dim(values, lax.rem(here + count - step, count), 0, keepdims=False)
        for step in range(count)
    ]


def far_all(value, count, first=None):
    ahead = count // 2
    found = [value] + [None] * (count - 1)
    found[1] = far_shift(value, 1, count)
    if count > 2:
        found[count - 1] = far_shift(value, -1, count)
    for step in range(2, ahead + 1):
        found[step] = far_shift(found[step - 1], 1, count)
    for step in range(count - 2, ahead, -1):
        found[step] = far_shift(found[step + 1], -1, count)
    return found


def far_stack(found):
    count = len(found)
    here = lax.axis_index(FAR_AXIS)
    zeros = (0,) * found[0].ndim
    full = jnp.zeros((count,) + found[0].shape, found[0].dtype)
    for step, chunk in enumerate(found):
        full = lax.dynamic_update_slice(full, chunk[None], (lax.rem(here + count - step, count),) + zeros)
    return full


def tie(*values):
    return lax.optimization_barrier(values)


def far_shift(value, step, count):
    return lax.ppermute(value, FAR_AXIS, [(i, (i + step) % count) for i in range(count)])


def far_next(value, count):
    return lax.ppermute(value, FAR_AXIS, [(i, (i + 1) % count) for i in range(count)])


def quad_xor(value, step):
    return lax.ppermute(value, HEAD_AXES, [(i, i ^ step) for i in range(4)])


def slab_send(blocks):
    return [blocks[0]] + [quad_xor(blocks[step], step) for step in range(1, 4)]


def slab_take(got):
    keep = quad_order([part[0] for part in got])
    other = swap(quad_order([part[1] for part in got]), CORE_AXIS)
    first, second = pair_order(keep, other, CORE_AXIS)
    shape = (NEAR, 2) + keep.shape[1:]
    return jnp.stack([first.reshape(shape), second.reshape(shape)], axis=1)


def slab_return(rows):
    keep, give = pair_order(rows[:, 0], rows[:, 1], CORE_AXIS)
    both = jnp.stack([keep, swap(give, CORE_AXIS)], axis=2)
    return quad_parts(both.reshape((4, 2) + rows.shape[3:]))


def expert_kernel(
    here_ref, in_ref, cot_ref, mask_ref, router_ref, gate_ref, up_ref, down_ref,
    gate_grad_ref, up_grad_ref, active_ref, grad_ref, in_grad_ref, gated_ref,
    out_total, in_total, gate_slot,
):
    block = pl.program_id(0)

    @pl.when(block == 0)
    def _():
        chosen = mask_ref[...].astype(F32) > 0.5
        logits = jnp.where(chosen, mm(in_ref[...], router_ref[...]), -1e30)
        exped = jnp.where(chosen, jnp.exp(logits - jnp.max(logits, axis=-1, keepdims=True)), 0.0)
        total = jnp.sum(exped, axis=-1, keepdims=True)
        mine = lax.broadcasted_iota(jnp.int32, exped.shape, 1) == here_ref[0]
        picked = jnp.sum(jnp.where(mine, exped, 0.0), axis=-1, keepdims=True)
        gate = picked / jnp.where(total > 0.0, total, 1.0)
        gate_slot[...] = jnp.broadcast_to(gate, gate_slot.shape)
        grad_ref[...] = (gate * cot_ref[...].astype(F32)).astype(BF)
        out_total[...] = jnp.zeros_like(out_total)
        in_total[...] = jnp.zeros_like(in_total)

    gate_pre = mm(in_ref[...], gate_ref[...])
    up_pre = mm(in_ref[...], up_ref[...])
    act_grad = mm(grad_ref[...], down_ref[...])
    sig_gate = jax.nn.sigmoid(gate_pre)
    silu_val = gate_pre * sig_gate
    active = (silu_val * up_pre).astype(BF)
    silu_slope = sig_gate * (1.0 + gate_pre * (1.0 - sig_gate))
    gate_grad = (act_grad * up_pre * silu_slope).astype(BF)
    up_grad = (act_grad * silu_val).astype(BF)
    active_ref[...] = active
    gate_grad_ref[...] = gate_grad
    up_grad_ref[...] = up_grad
    out_total[...] += mm_nt(active, down_ref[...])
    in_total[...] += mm_nt(gate_grad, gate_ref[...]) + mm_nt(up_grad, up_ref[...])

    @pl.when(block == pl.num_programs(0) - 1)
    def _():
        out = out_total[...].astype(BF).astype(F32)
        gated_ref[...] = (gate_slot[:, :1] * out).astype(BF)
        in_grad_ref[:, :D] = in_total[...].astype(BF)
        found = jnp.sum(cot_ref[...].astype(F32) * out, axis=-1, keepdims=True)
        high = found.astype(BF).astype(F32)
        lane = lax.broadcasted_iota(jnp.int32, (in_grad_ref.shape[0], in_grad_ref.shape[1] - D), 1)
        lane = lane - here_ref[1]
        parts = jnp.where(lane == 0, high, jnp.where(lane == SLAB, found - high, 0.0))
        in_grad_ref[:, D:] = parts.astype(BF)


def expert_chunk(here, in_chunk, cot_chunk, mask, router, weight, back_width):
    rows = in_chunk.shape[0]
    tile = 256
    steps = FF // tile
    whole = pl.BlockSpec((rows, D), lambda j, h: (0, 0))
    piece = pl.BlockSpec((rows, tile), lambda j, h: (0, j))
    low = jax.ShapeDtypeStruct((rows, FF), BF)
    wide = jax.ShapeDtypeStruct((rows, D), BF)
    return pl.pallas_call(
        expert_kernel,
        grid_spec=pltpu.PrefetchScalarGridSpec(
            num_scalar_prefetch=1,
            grid=(steps,),
            in_specs=[
                whole,
                whole,
                pl.BlockSpec(mask.shape, lambda j, h: (0, 0)),
                pl.BlockSpec(router.shape, lambda j, h: (0, 0)),
                pl.BlockSpec((D, tile), lambda j, h: (0, j)),
                pl.BlockSpec((D, tile), lambda j, h: (0, steps + j)),
                pl.BlockSpec((D, tile), lambda j, h: (0, 2 * steps + j)),
            ],
            out_specs=[
                piece, piece, piece, whole,
                pl.BlockSpec((rows, back_width), lambda j, h: (0, 0)),
                whole,
            ],
            scratch_shapes=[
                pltpu.VMEM((rows, D), F32),
                pltpu.VMEM((rows, D), F32),
                pltpu.VMEM((rows, LANES), F32),
            ],
        ),
        out_shape=[low, low, low, wide, jax.ShapeDtypeStruct((rows, back_width), BF), wide],
        compiler_params=pltpu.CompilerParams(vmem_limit_bytes=40 << 20),
        cost_estimate=pl.CostEstimate(flops=1 << 20, bytes_accessed=1 << 20, transcendentals=0),
        name="expert_chunk",
    )(here, in_chunk, cot_chunk, mask, router, weight, weight, weight)


def expert_grad_kernel(count, *refs):
    lists = [refs[k * count : (k + 1) * count] for k in range(5)]
    out_ref = refs[5 * count]
    column = pl.program_id(1)

    def total(lefts, rights):
        found = mm_tn(lefts[0][...], rights[0][...])
        for left, right in zip(lefts[1:], rights[1:]):
            found = found + mm_tn(left[...], right[...])
        out_ref[...] = found

    for place, (left, right) in enumerate(((0, 2), (0, 3), (1, 4))):
        pl.when(column == place)(functools.partial(total, lists[left], lists[right]))


def expert_grads(in_rows, grad_rows, gate_grads, up_grads, actives):
    count = len(in_rows)
    rows = in_rows[0].shape[0]
    tile = 512
    tall = pl.BlockSpec((rows, tile), lambda i, j: (0, i))
    whole = pl.BlockSpec((rows, FF), lambda i, j: (0, 0))
    return pl.pallas_call(
        functools.partial(expert_grad_kernel, count),
        grid=(D // tile, 3),
        in_specs=[tall] * (2 * count) + [whole] * (3 * count),
        out_specs=pl.BlockSpec((tile, FF), lambda i, j: (i, j)),
        out_shape=jax.ShapeDtypeStruct((D, 3 * FF), F32),
        compiler_params=pltpu.CompilerParams(vmem_limit_bytes=48 << 20),
        cost_estimate=pl.CostEstimate(flops=1 << 20, bytes_accessed=1 << 20, transcendentals=0),
        name="expert_grads",
    )(*in_rows, *grad_rows, *gate_grads, *up_grads, *actives)


def head_normed(raw, gain_ref):
    scale = lax.rsqrt(jnp.mean(raw * raw, axis=-1, keepdims=True) + EPS)
    normal = raw * scale
    return (normal, scale, normal * gain_ref[...])


def turned(values, cos_ref, sin_ref):
    return values * cos_ref[...] + pltpu.roll(values, HEAD_DIM // 2, 1) * sin_ref[...]


def turned_back(values, cos_ref, sin_ref):
    return values * cos_ref[...] + pltpu.roll(values * sin_ref[...], HEAD_DIM // 2, 1)


def head_probs(query, key, row_ref, start_ref, key_row_ref):
    scores = mm_nt(query, key) * HEAD_DIM ** (-0.5)
    allowed = (key_row_ref[0] <= row_ref[0]) & (key_row_ref[0] >= start_ref[0])
    scores = jnp.where(allowed, scores, -1e30)
    exped = jnp.exp(scores - jnp.max(scores, axis=-1, keepdims=True))
    return exped / jnp.sum(exped, axis=-1, keepdims=True)


def attend_kernel(
    query_ref, key_ref, value_ref, cos_ref, sin_ref, qgain_ref, kgain_ref,
    row_ref, start_ref, key_row_ref, mixed_ref, key_low, value_low,
):
    @pl.when(pl.program_id(1) == 0)
    def _():
        key_low[...] = turned(head_normed(key_ref[...], kgain_ref)[2], cos_ref, sin_ref).astype(BF)
        value_low[...] = value_ref[...].astype(BF)

    query = turned(head_normed(query_ref[...], qgain_ref)[2], cos_ref, sin_ref).astype(BF)
    probs = head_probs(query, key_low[...], row_ref, start_ref, key_row_ref)
    mixed_ref[...] = mm(probs.astype(BF), value_low[...]).astype(BF)


def attend_back_kernel(
    query_ref, key_ref, value_ref, cos_ref, sin_ref, qgain_ref, kgain_ref,
    row_ref, start_ref, key_row_ref, grad_ref,
    query_out, key_out, value_out, qgain_out, kgain_out,
    key_low, value_low, key_total, value_total,
):
    group, head = pl.program_id(0), pl.program_id(1)
    score_scale = HEAD_DIM ** (-0.5)

    @pl.when((group == 0) & (head == 0))
    def _():
        qgain_out[...] = jnp.zeros_like(qgain_out)
        kgain_out[...] = jnp.zeros_like(kgain_out)

    @pl.when(head == 0)
    def _():
        key_low[...] = turned(head_normed(key_ref[...], kgain_ref)[2], cos_ref, sin_ref).astype(BF)
        value_low[...] = value_ref[...].astype(BF)
        key_total[...] = jnp.zeros_like(key_total)
        value_total[...] = jnp.zeros_like(value_total)

    def raw_grad(grad, normal, scale, gain_ref, gain_out):
        grad = turned_back(grad, cos_ref, sin_ref)
        gain_out[...] += jnp.sum(grad * normal, axis=0, keepdims=True)
        grad = grad * gain_ref[...]
        return scale * (grad - normal * jnp.mean(normal * grad, axis=-1, keepdims=True))

    normal, scale, gained = head_normed(query_ref[...], qgain_ref)
    query = turned(gained, cos_ref, sin_ref).astype(BF)
    probs = head_probs(query, key_low[...], row_ref, start_ref, key_row_ref)
    grad = grad_ref[...]
    value_total[...] += mm_tn(probs.astype(BF), grad)
    prob_grad = mm_nt(grad, value_low[...])
    score_grad = (probs * (prob_grad - jnp.sum(probs * prob_grad, axis=-1, keepdims=True))).astype(BF)
    key_total[...] += mm_tn(score_grad, query) * score_scale
    query_grad = mm(score_grad, key_low[...]) * score_scale
    query_out[...] = raw_grad(query_grad, normal, scale, qgain_ref, qgain_out).astype(BF)

    @pl.when(head == pl.num_programs(1) - 1)
    def _():
        key_normal, key_scale, _ = head_normed(key_ref[...], kgain_ref)
        key_out[...] = raw_grad(key_total[...], key_normal, key_scale, kgain_ref, kgain_out).astype(BF)
        value_out[...] = value_total[...].astype(BF)


def attend_specs(heads):
    head = pl.BlockSpec((ROW, HEAD_DIM), lambda b, h: (b, h))
    whole = pl.BlockSpec((ROW, HEAD_DIM), lambda b, h: (b, 0))
    gain = pl.BlockSpec((1, HEAD_DIM), lambda b, h: (0, 0))
    column = pl.BlockSpec((1, ROW, 1), lambda b, h: (b, 0, 0))
    specs = [
        head,
        pl.BlockSpec((ROW, HEAD_DIM), lambda b, h: (b, heads)),
        pl.BlockSpec((ROW, HEAD_DIM), lambda b, h: (b, heads + 1)),
        whole, whole, gain, gain, column, column,
        pl.BlockSpec((1, 1, ROW), lambda b, h: (b, 0, 0)),
    ]
    return (specs, head, whole, gain)


def attend(projected, shared, heads):
    specs, head, _, _ = attend_specs(heads)
    rows = projected.shape[0]
    return pl.pallas_call(
        attend_kernel,
        grid=(rows // ROW, heads),
        in_specs=specs,
        out_specs=head,
        out_shape=jax.ShapeDtypeStruct((rows, heads * HEAD_DIM), BF),
        scratch_shapes=[pltpu.VMEM((ROW, HEAD_DIM), BF)] * 2,
        cost_estimate=pl.CostEstimate(flops=1 << 20, bytes_accessed=1 << 20, transcendentals=0),
        name="attend",
    )(projected, projected, projected, *shared)


def attend_back(projected, shared, grad, heads):
    specs, head, whole, gain = attend_specs(heads)
    rows = projected.shape[0]
    return pl.pallas_call(
        attend_back_kernel,
        grid=(rows // ROW, heads),
        in_specs=specs + [head],
        out_specs=[head, whole, whole, gain, gain],
        out_shape=[
            jax.ShapeDtypeStruct((rows, heads * HEAD_DIM), BF),
            jax.ShapeDtypeStruct((rows, HEAD_DIM), BF),
            jax.ShapeDtypeStruct((rows, HEAD_DIM), BF),
            jax.ShapeDtypeStruct((1, HEAD_DIM), F32),
            jax.ShapeDtypeStruct((1, HEAD_DIM), F32),
        ],
        scratch_shapes=[pltpu.VMEM((ROW, HEAD_DIM), BF)] * 2 + [pltpu.VMEM((ROW, HEAD_DIM), F32)] * 2,
        cost_estimate=pl.CostEstimate(flops=1 << 20, bytes_accessed=1 << 20, transcendentals=0),
        name="attend_back",
    )(projected, projected, projected, *shared, grad)


def shards(tokens, cotangent, w_qkv, w_out, w_router, norm_gains, w_expert, lengths, deal, routes):
    far_count = lax.axis_size(FAR_AXIS)
    device_count = far_count * NEAR * CORES * 2
    experts_all = w_router.shape[1]
    capacity = TOK_DEV * TOPK // experts_all
    slot_count = experts_all * capacity
    seq_index = lax.axis_index(SEQ_AXIS)
    near_index = lax.axis_index(NEAR_AXIS)
    far_index = lax.axis_index(FAR_AXIS)
    core_index = lax.axis_index(CORE_AXIS)
    per_group = HEADS // KV_HEADS
    qcols = per_group * HEAD_DIM
    width = qcols + 2 * HEAD_DIM
    qkv_rows = w_qkv.shape[0]
    out_rows = w_out.shape[0]
    gain_rows = norm_gains.shape[0]
    score_scale = HEAD_DIM ** (-0.5)

    wide = jnp.concatenate(
        [
            w_qkv[:, :QDIM].reshape(qkv_rows, KV_HEADS, qcols),
            w_qkv[:, QDIM : QDIM + KVDIM].reshape(qkv_rows, KV_HEADS, HEAD_DIM),
            w_qkv[:, QDIM + KVDIM :].reshape(qkv_rows, KV_HEADS, HEAD_DIM),
        ],
        axis=2,
    ).transpose(1, 0, 2)
    core_rows = KV_HEADS * qkv_rows
    half_rows = 2 * qkv_rows
    wide_found = quad_parts(wide)
    tokens, *wide_found = tie(tokens, *wide_found)
    qkv_far = far_all(quad_order(wide_found).reshape(core_rows, width), far_count)

    tokens_both = quad_gather(tokens).reshape(2, ROW, D)
    table = jnp.concatenate([deal, jnp.pad(lengths, ((0, 0), (0, LANES - NSEG)))], axis=1)
    table_both = jnp.concatenate(pair_order(table, swap(table, NEAR_AXIS), NEAR_AXIS), axis=0)
    deal_both = table_both[:, :ROW]
    ends = jnp.cumsum(table_both[:, ROW : ROW + NSEG], axis=1)
    starts = ends - table_both[:, ROW : ROW + NSEG]
    seg_both = jnp.sum((deal_both[:, :, None] >= ends[:, None, :]).astype(jnp.int32), axis=2)
    picked = seg_both[:, :, None] == jnp.arange(NSEG, dtype=jnp.int32)[None, None, :]
    pos_both = deal_both - jnp.sum(jnp.where(picked, starts[:, None, :], 0), axis=2)
    dealt_hot = (deal_both[:, :, None] == jnp.arange(ROW, dtype=jnp.int32)[None, None, :]).astype(BF)
    hot_mine = lax.dynamic_index_in_dim(dealt_hot, near_index, 0, keepdims=False)
    hot_half = lax.dynamic_slice_in_dim(hot_mine, seq_index * TOK_DEV, TOK_DEV, axis=0)
    back_half = lax.dynamic_slice_in_dim(hot_mine, seq_index * TOK_DEV, TOK_DEV, axis=1)
    seg_mine = lax.dynamic_slice_in_dim(
        lax.dynamic_index_in_dim(seg_both, near_index, 0, keepdims=False), seq_index * TOK_DEV, TOK_DEV
    )

    expert_ids = jnp.arange(experts_all, dtype=jnp.int32)
    chosen_rows = jnp.sum(
        (routes[0][:, :, None] == expert_ids[None, None, :]).astype(jnp.int32), axis=1
    ).astype(BF)
    chosen = mm(hot_half, chosen_rows)
    live = jnp.where((seg_mine != NSEG - 1)[:, None], chosen, 0.0)
    steps = jnp.arange(TOK_DEV, dtype=jnp.int32)
    earlier = (steps[None, :] < steps[:, None]).astype(BF)
    place = mm(earlier, live.astype(BF))
    place = jnp.where(live > 0.5, place, -1.0).astype(jnp.int32)
    slot_hot = place.T[:, None, :] == jnp.arange(capacity, dtype=jnp.int32)[None, :, None]
    slot_low = slot_hot.astype(BF).reshape(slot_count, TOK_DEV)

    slab = NEAR * CORES * 2
    slab_index = (near_index * CORES + core_index) * 2 + seq_index
    slab_ids = jnp.arange(slab, dtype=jnp.int32)
    out_order = jnp.array([0, 2, 1, 3, 4, 6, 5, 7], jnp.int32)
    place_far = far_stack(far_all(place.T.astype(BF), far_count))

    def slots_of(places, step):
        found = lax.dynamic_index_in_dim(
            places, lax.rem(far_index + far_count - step, far_count), 0, keepdims=False
        )
        found = found[:, None, :] == jnp.arange(capacity, dtype=jnp.int32)[None, :, None]
        return found.astype(BF).reshape(slab * capacity, TOK_DEV)

    place_slab = lax.dynamic_slice_in_dim(place_far, far_index * slab, slab, axis=1).astype(jnp.int32)
    turned_ids = lax.bitwise_xor(out_order, slab_index)
    place_turned = jnp.sum(
        jnp.where(
            (turned_ids[:, None] == slab_ids[None, :])[None, :, :, None], place_slab[:, None], 0
        ),
        axis=2,
    )
    chunk_slots = [slots_of(place_slab, step) for step in range(far_count)]
    send_slots = [slots_of(place_turned, step) for step in range(far_count)]
    chunk_steps = jnp.arange(far_count, dtype=jnp.int32)
    source_ids = (
        lax.rem(far_index + far_count - chunk_steps, far_count)[:, None] * slab + slab_ids[None, :]
    ).reshape(device_count)
    def to_blocks(rows):
        return rows.reshape(4, 2, rows.shape[0] // slab, rows.shape[1])


    router_size = qkv_rows * experts_all
    small_size = router_size + gain_rows
    mask_size = capacity * experts_all
    small_rows = -(-(small_size + mask_size) // (8 * LANES)) * 8
    small = jnp.broadcast_to(
        jnp.concatenate([w_router.reshape(router_size), norm_gains]), (device_count, small_size)
    )
    slot_mask = mm(slot_low, chosen.astype(BF)).astype(BF).reshape(device_count, mask_size)
    small = jnp.concatenate([slot_mask, small], axis=1)
    small = jnp.pad(small, ((0, 0), (0, small_rows * LANES - small_size - mask_size)))
    small_all = exchange(small.reshape(device_count, small_rows, LANES), ALL_AXES).reshape(
        device_count, small_rows * LANES
    )
    mask_back = jnp.take(small_all[:, :mask_size], source_ids, axis=0).reshape(
        far_count, slab * capacity, experts_all
    )
    small_all = small_all[:, mask_size : mask_size + small_size]
    router_full = small_all[:, :router_size].reshape(D, experts_all)
    gains_float = small_all[:, router_size:].reshape(-1).astype(F32)
    gain_attn = gains_float[:D]
    gain_ffn = gains_float[D : 2 * D]
    gain_query = gains_float[2 * D : 2 * D + HEAD_DIM]
    gain_key = gains_float[2 * D + HEAD_DIM :]

    cot_pair = jnp.concatenate(pair_order(cotangent, swap(cotangent, SEQ_AXIS), SEQ_AXIS), axis=0)
    cot_low = mm(hot_half, cot_pair).astype(BF)
    cot_rows = cot_low.astype(F32)
    cot_sent = [
        mm(slot_low, half).astype(BF).reshape(device_count, capacity, D // 2)
        for half in (cot_low[:, : D // 2], cot_low[:, D // 2 :])
    ]
    qkv_own = far_stack(qkv_far).reshape(far_count * NEAR, half_rows, width)
    qkv_mine = jnp.stack(pair_order(qkv_own, swap(qkv_own, CORE_AXIS), CORE_AXIS), axis=1).reshape(
        D, width
    )

    out_slabs = far_stack(far_all(w_out, far_count)).reshape(
        KV_HEADS, far_count // KV_HEADS * out_rows, D
    )
    far_part = far_count // KV_HEADS
    x_both = lax.dot_general(
        dealt_hot, tokens_both, (((2,), (1,)), ((0,), (0,))), preferred_element_type=F32
    )
    x_rows = lax.dynamic_slice(
        x_both, (near_index, seq_index * TOK_DEV, 0), (1, TOK_DEV, D)
    )[0]
    normed_low = rms_norm(x_both.reshape(2 * ROW, D), gain_attn).astype(BF)
    projected, *cot_sent = tie(mm(normed_low, qkv_mine), *cot_sent)
    cot_back = [exchange(half, ALL_AXES) for half in cot_sent]
    cosine, sine_part = tables(pos_both.reshape(2 * ROW), HEAD_DIM)
    shared = (
        jnp.concatenate([cosine, cosine], axis=1),
        jnp.concatenate([-sine_part, sine_part], axis=1),
        gain_query[None],
        gain_key[None],
        deal_both[:, :, None],
        (deal_both - pos_both)[:, :, None],
        deal_both[:, None, :],
    )
    mixed_low = attend(projected, shared, per_group)
    out_found = quad_parts(out_slabs)
    mixed_low, *out_found = tie(mixed_low, *out_found)
    out_own = quad_order(out_found).reshape(NEAR * 2, far_part, out_rows, D)
    out_own = out_own.transpose(1, 0, 2, 3).reshape(far_part * NEAR, 2 * out_rows, D)
    out_mine = jnp.stack(pair_order(out_own, swap(out_own, CORE_AXIS), CORE_AXIS), axis=1).reshape(
        qcols, D
    )

    out_partial = mm(mixed_low, out_mine).astype(BF)
    out_partial, cot_back[0] = tie(out_partial, cot_back[0])
    residual = x_rows + sum_parts(quad_parts(out_partial.reshape(4, TOK_DEV, D)))

    normed_two, ffn_back = jax.vjp(rms_norm, residual, gain_ffn)
    ffn_in = normed_two.astype(BF)
    logits = mm(ffn_in, router_full)
    logits = jnp.where(chosen > 0.5, logits, -1e30)
    gate_probs = jax.nn.softmax(logits, axis=-1)
    gate_probs = jnp.where(chosen > 0.5, gate_probs, 0.0)

    expert_weight = w_expert[0]
    expert_here = far_index * slab + slab_index
    in_rows, gate_grads, up_grads, grad_rows, actives, in_grads = ([] for _ in range(6))
    gated_outs = [None] * far_count
    here = jnp.stack([expert_here, far_index * 2 * SLAB + slab_index])
    back_width = D + -(-far_count * 2 * SLAB // LANES) * LANES
    far_rows = [ffn_in]
    for step in range(1, far_count):
        with jax.named_scope('rows_far%d' % step):
            far_rows.append(far_shift(far_rows[-1], 1, far_count))

    def gather(step, source):
        return mm(send_slots[step], source).astype(BF)

    sent = gather(0, ffn_in)

    def send_back(step):
        return slab_return(in_grads[step].reshape(NEAR, CORES, 2, capacity, back_width))

    def combine(step, found):
        back = jnp.concatenate(found, axis=0).reshape(slab * capacity, back_width)
        return mm_tn(send_slots[step], back).astype(BF if step else F32)

    ffn_in, cot_back[1] = tie(ffn_in, cot_back[1])
    cot_chunks = far_parts(
        jnp.concatenate(cot_back, axis=2).reshape(far_count, slab * capacity, D), far_count
    )
    pending, parts = {}, [None] * far_count
    for turn in range(far_count):
        with jax.named_scope("rows_out%d" % turn):
            got = slab_send(to_blocks(sent))
        if turn + 1 < far_count:
            source = far_rows[turn + 1]
            if turn > 0:
                source, up_grads[turn - 1] = tie(source, up_grads[turn - 1])
            sent = gather(turn + 1, source)
        if turn > 0:
            gate_grads[turn - 1], *got = tie(gate_grads[turn - 1], *got)
        with jax.named_scope("rows_core%d" % turn):
            in_chunk = slab_take(got).reshape(slab * capacity, D)
        gate_grad, up_grad, active, grad_chunk, in_grad, gated_out = expert_chunk(
            here, in_chunk, cot_chunks[turn], mask_back[turn], router_full, expert_weight, back_width
        )
        in_rows.append(in_chunk)
        gate_grads.append(gate_grad)
        up_grads.append(up_grad)
        actives.append(active)
        grad_rows.append(grad_chunk)
        in_grads.append(in_grad)
        gated_outs[turn] = gated_out.reshape(slab, capacity, D)
        if 0 < turn < far_count - 1:
            with jax.named_scope("rows_back%d" % turn):
                pending[turn] = send_back(turn)
    up_grads[-1], *pending[1] = tie(up_grads[-1], *pending[1])
    for turn in range(1, far_count - 1):
        parts[turn] = combine(turn, pending[turn])
        if turn + 1 in pending:
            parts[turn], *pending[turn + 1] = tie(parts[turn], *pending[turn + 1])
    last = far_count - 1
    with jax.named_scope("rows_back%d" % last):
        parts[last] = combine(last, send_back(last))
    parts[max(last - 1, 0)], in_grads[0] = tie(parts[max(last - 1, 0)], in_grads[0])
    with jax.named_scope("partial_far"):
        part_found = far_begin(parts, far_count)
    with jax.named_scope("rows_back0"):
        parts[0] = combine(0, send_back(0))
    with jax.named_scope("partial_far"):
        total = far_end(parts, part_found, far_count)
    from_experts = total[:, :D]

    lanes = jnp.arange(back_width - D, dtype=jnp.int32)
    lanes = lanes // (2 * SLAB) * SLAB + lanes % SLAB
    spread = (lanes[:, None] == expert_ids[None, :]).astype(BF)
    gate_grad = mm(total[:, D:].astype(BF), spread)
    mean_term = jnp.sum(gate_probs * gate_grad, axis=1, keepdims=True)
    logit_grad = (gate_probs * (gate_grad - mean_term)).astype(BF)
    router_grad = mm_tn(ffn_in, logit_grad)
    ffn_in_grad = from_experts + mm_nt(logit_grad, router_full)
    resid_part, gain_ffn_grad = ffn_back(ffn_in_grad)
    resid_low = (cot_rows + resid_part).astype(BF)

    in_rows[0], resid_low = tie(in_rows[0], resid_low)
    grad_expert = expert_grads(in_rows, grad_rows, gate_grads, up_grads, actives)[None]

    resid_both, grad_expert = tie(quad_gather(resid_low), grad_expert)
    resid_both = resid_both.reshape(2 * ROW, D)

    def core_sum(values):
        own, other = pair_order(values[:, 0], values[:, 1], CORE_AXIS)
        return own.astype(F32) + swap(other, CORE_AXIS).astype(F32)

    out_grad = mm_tn(mixed_low, resid_both).astype(BF)
    resid_both, out_grad = tie(resid_both, out_grad)
    mixed_grad = mm_nt(resid_both, out_mine).astype(BF)
    out_grad = core_sum(out_grad.reshape(far_part * NEAR, CORES, 2 * out_rows, D)).astype(BF)
    mixed_grad, out_grad = tie(mixed_grad, out_grad)
    out_grad = (
        out_grad
        .reshape(far_part, NEAR * 2, out_rows, D)
        .transpose(1, 0, 2, 3)
        .reshape(NEAR * 2, far_part * out_rows, D)
    )
    out_grad = quad_swap(out_grad).reshape(far_count, out_rows, D)
    query_grad, key_grad, value_grad, query_gain_grad, key_gain_grad = attend_back(
        projected, shared, mixed_grad, per_group
    )
    query_grad, out_grad = tie(query_grad, out_grad)
    out_sent = far_parts(out_grad, far_count)
    out_found = far_begin(out_sent, far_count)
    gated, query_grad = tie(jnp.stack(gated_outs, axis=1), query_grad)
    gated = exchange(gated, SLAB_AXES)
    out_parts = [
        mm_tn(hot, gated[:, step].reshape(slab * capacity, D)).astype(BF if step else F32)
        for step, hot in enumerate(chunk_slots)
    ]
    out_sum = far_end(out_parts, far_begin(out_parts, far_count), far_count)
    proj_grad = jnp.concatenate([query_grad, key_grad, value_grad], axis=1)

    back_grad = lax.dot_general(
        dealt_hot,
        proj_grad.reshape(2, ROW, width),
        (((1,), (1,)), ((0,), (0,))),
        preferred_element_type=F32,
    ).astype(BF).reshape(2 * ROW, width)
    qkv_grad = mm_tn(normed_low, proj_grad).astype(BF)
    back_grad, qkv_grad = tie(back_grad, qkv_grad)
    normed_partial = mm_nt(back_grad, qkv_mine).astype(BF)
    qkv_grad = core_sum(qkv_grad.reshape(far_count * NEAR, CORES, half_rows, width)).astype(BF)
    normed_partial, qkv_grad, *out_found = tie(normed_partial, qkv_grad, *out_found)
    qkv_parts = far_parts(qkv_grad.reshape(far_count, core_rows, width), far_count)
    qkv_found = far_begin(qkv_parts, far_count)
    out_share = far_end(out_sent, out_found, far_count)
    qkv_grad = far_end(qkv_parts, qkv_found, far_count)
    normed_found = quad_parts(normed_partial.reshape(4, TOK_DEV, D))
    qkv_grad, *normed_found = tie(qkv_grad, *normed_found)
    normed_grad = sum_parts(normed_found)
    normed_grad, out_sum = tie(normed_grad, out_sum)
    final_rows = (residual + out_sum).astype(BF)
    final_pair = jnp.concatenate(
        pair_order(final_rows, swap(final_rows, SEQ_AXIS), SEQ_AXIS), axis=0
    )
    layer_out = mm_tn(back_half, final_pair).astype(BF)
    _, attn_back = jax.vjp(rms_norm, tokens.astype(F32), gain_attn)
    input_part, gain_attn_grad = attn_back(normed_grad)
    resid_group = lax.dynamic_slice_in_dim(resid_both, near_index * ROW, ROW, axis=0)
    grad_tokens = (mm_tn(back_half, resid_group) + input_part).astype(BF)

    qkv_grad = quad_swap(qkv_grad.astype(BF).reshape(KV_HEADS, qkv_rows, width))
    qkv_grad = qkv_grad.transpose(1, 0, 2).astype(F32)
    qkv_share = jnp.concatenate(
        [
            qkv_grad[:, :, :qcols].reshape(qkv_rows, QDIM),
            qkv_grad[:, :, qcols : qcols + HEAD_DIM].reshape(qkv_rows, KVDIM),
            qkv_grad[:, :, qcols + HEAD_DIM :].reshape(qkv_rows, KVDIM),
        ],
        axis=1,
    )

    gains_grad = jnp.concatenate(
        [gain_attn_grad, gain_ffn_grad, query_gain_grad[0], key_gain_grad[0]]
    )
    share_rows = -(-small_size // (8 * LANES)) * 8
    small_grad = jnp.concatenate(
        [router_grad.reshape(device_count, router_size), gains_grad.reshape(device_count, gain_rows)],
        axis=1,
    )
    small_grad = jnp.pad(small_grad, ((0, 0), (0, share_rows * LANES - small_size)))
    small_share = jnp.sum(
        exchange(small_grad.reshape(device_count, share_rows, LANES), ALL_AXES), axis=0
    ).reshape(share_rows * LANES)
    router_share = small_share[:router_size].reshape(qkv_rows, experts_all)
    gains_share = small_share[router_size:small_size]
    return (layer_out, grad_tokens, qkv_share, out_share, router_share, gains_share, grad_expert)


def solution(mesh):
    shape = dict(mesh.shape)
    inner = Mesh(
        mesh.devices.reshape(shape["dp"] // (NEAR * CORES), NEAR, CORES, shape["seq"]), ALL_AXES
    )
    rows = P(ALL_AXES, None)
    in_specs = (
        rows,
        rows,
        rows,
        rows,
        rows,
        P(ALL_AXES),
        P(ALL_AXES, None, None),
        P(DP_AXES, None),
        P(DP_AXES, None),
        P(DP_AXES, None, None),
    )
    out_specs = (rows, rows, rows, rows, rows, P(ALL_AXES), P(ALL_AXES, None, None))
    return jax.shard_map(shards, mesh=inner, in_specs=in_specs, out_specs=out_specs, check_vma=False)
```

```python
import functools

import jax
import jax.numpy as jnp
from jax import lax
from jax.experimental import pallas as pl
from jax.experimental.pallas import tpu as pltpu
from jax.sharding import Mesh
from jax.sharding import PartitionSpec as P

D = 2048
HEADS = 32
KV_HEADS = 4
HEAD_DIM = 128
FF = 768
TOPK = 8
NSEG = 4
TOK_DEV = 128
ROW = 256
QDIM = 4096
KVDIM = 512
NEAR = 2
CORES = 2
SLAB = NEAR * CORES * 2
COT_CUT = 1280
HEADS_STEP = 4
LANES = 128

EPS = 1e-06
THETA = 1000000.0
BF = jnp.bfloat16
F32 = jnp.float32

FAR_AXIS = "far"
NEAR_AXIS = "near"
CORE_AXIS = "core"
SEQ_AXIS = "seq"
SLAB_AXES = (NEAR_AXIS, CORE_AXIS, SEQ_AXIS)
HEAD_AXES = (NEAR_AXIS, SEQ_AXIS)
ALL_AXES = (FAR_AXIS, NEAR_AXIS, CORE_AXIS, SEQ_AXIS)
DP_AXES = (FAR_AXIS, NEAR_AXIS, CORE_AXIS)


def rms_norm(values, scales):
    return values * lax.rsqrt(jnp.mean(values * values, axis=-1, keepdims=True) + EPS) * scales


def rotary(values, cosine, sine_part):
    half_width = values.shape[-1] // 2
    front_part = values[..., :half_width]
    back_part = values[..., half_width:]
    cos_wide = cosine[..., None, :]
    sin_wide = sine_part[..., None, :]
    return jnp.concatenate(
        [
            front_part * cos_wide - back_part * sin_wide,
            back_part * cos_wide + front_part * sin_wide,
        ],
        axis=-1,
    )


def tables(positions, head_width):
    half_width = head_width // 2
    inverse = THETA ** (-(jnp.arange(half_width, dtype=F32) * 2.0 / head_width))
    angles = positions.astype(F32)[..., None] * inverse
    return (jnp.cos(angles), jnp.sin(angles))


def dot(left, right, dims):
    return lax.dot_general(left, right, (dims, ((), ())), preferred_element_type=F32)


def mm(left, right):
    return dot(left, right, ((1,), (0,)))


def mm_nt(left, right):
    return dot(left, right, ((1,), (1,)))


def mm_tn(left, right):
    return dot(left, right, ((0,), (0,)))


def swap(value, axis):
    return lax.ppermute(value, axis, [(0, 1), (1, 0)])


def pair_order(own, other, axis):
    first = lax.axis_index(axis) == 0
    return (jnp.where(first, own, other), jnp.where(first, other, own))


def exchange(value, axes):
    return lax.all_to_all(value, axes, split_axis=0, concat_axis=0, tiled=True)


def quad_index():
    return lax.axis_index(NEAR_AXIS) * 2 + lax.axis_index(SEQ_AXIS)


def quad_send(parts, step):
    block = lax.dynamic_index_in_dim(parts, lax.bitwise_xor(quad_index(), step), 0, keepdims=False)
    return lax.ppermute(block, HEAD_AXES, [(i, i ^ step) for i in range(4)])


def quad_order(found):
    low = pair_order(found[0], found[1], SEQ_AXIS)
    high = pair_order(found[2], found[3], SEQ_AXIS)
    rows = [pair_order(low[k], high[k], NEAR_AXIS) for k in range(2)]
    return jnp.stack([rows[0][0], rows[1][0], rows[0][1], rows[1][1]])


def quad_gather(value):
    found = [value] + [
        lax.ppermute(value, HEAD_AXES, [(i, i ^ step) for i in range(4)]) for step in range(1, 4)
    ]
    return quad_order(found)


def quad_parts(parts):
    own = lax.dynamic_index_in_dim(parts, quad_index(), 0, keepdims=False)
    return [own] + [quad_send(parts, step) for step in range(1, 4)]


def quad_swap(parts):
    return quad_order(quad_parts(parts))


def sum_parts(parts):
    total = parts[0].astype(F32)
    for part in parts[1:]:
        total = total + part.astype(F32)
    return total


def far_begin(parts, count):
    if count != 4:
        return [far_shift(parts[step].astype(BF), -step, count) for step in range(1, count)]
    return [far_shift(parts[2].astype(BF), -1, count), far_shift(parts[3].astype(BF), 1, count)]


def far_end(parts, found, count):
    total = parts[0].astype(F32)
    if count != 4:
        for part in found:
            total = total + part.astype(F32)
        return total
    relay = (parts[1].astype(F32) + found[0].astype(F32)).astype(BF)
    return total + found[1].astype(F32) + far_shift(relay, -1, count).astype(F32)


def far_parts(values, count):
    here = lax.axis_index(FAR_AXIS)
    return [
        lax.dynamic_index_in_dim(values, lax.rem(here + count - step, count), 0, keepdims=False)
        for step in range(count)
    ]


def far_all(value, count, first=None):
    ahead = count // 2
    found = [value] + [None] * (count - 1)
    found[1] = far_shift(value, 1, count)
    if count > 2:
        found[count - 1] = far_shift(value, -1, count)
    for step in range(2, ahead + 1):
        found[step] = far_shift(found[step - 1], 1, count)
    for step in range(count - 2, ahead, -1):
        found[step] = far_shift(found[step + 1], -1, count)
    return found


def far_stack(found):
    count = len(found)
    here = lax.axis_index(FAR_AXIS)
    zeros = (0,) * found[0].ndim
    full = jnp.zeros((count,) + found[0].shape, found[0].dtype)
    for step, chunk in enumerate(found):
        full = lax.dynamic_update_slice(full, chunk[None], (lax.rem(here + count - step, count),) + zeros)
    return full


def tie(*values):
    return lax.optimization_barrier(values)


def far_shift(value, step, count):
    return lax.ppermute(value, FAR_AXIS, [(i, (i + step) % count) for i in range(count)])


def far_next(value, count):
    return lax.ppermute(value, FAR_AXIS, [(i, (i + 1) % count) for i in range(count)])


def quad_xor(value, step):
    return lax.ppermute(value, HEAD_AXES, [(i, i ^ step) for i in range(4)])


def slab_send(blocks):
    return [blocks[0]] + [quad_xor(blocks[step], step) for step in range(1, 4)]


def slab_take(got):
    keep = quad_order([part[0] for part in got])
    other = swap(quad_order([part[1] for part in got]), CORE_AXIS)
    first, second = pair_order(keep, other, CORE_AXIS)
    shape = (NEAR, 2) + keep.shape[1:]
    return jnp.stack([first.reshape(shape), second.reshape(shape)], axis=1)


def slab_return(rows):
    keep, give = pair_order(rows[:, 0], rows[:, 1], CORE_AXIS)
    both = jnp.stack([keep, swap(give, CORE_AXIS)], axis=2)
    return quad_parts(both.reshape((4, 2) + rows.shape[3:]))


def expert_kernel(
    here_ref, in_ref, cot_ref, mask_ref, router_ref, gate_ref, up_ref, down_ref,
    gate_grad_ref, up_grad_ref, active_ref, grad_ref, in_grad_ref, gated_ref,
    out_total, in_total, gate_slot,
):
    block = pl.program_id(0)

    @pl.when(block == 0)
    def _():
        chosen = mask_ref[...].astype(F32) > 0.5
        logits = jnp.where(chosen, mm(in_ref[...], router_ref[...]), -1e30)
        exped = jnp.where(chosen, jnp.exp(logits - jnp.max(logits, axis=-1, keepdims=True)), 0.0)
        total = jnp.sum(exped, axis=-1, keepdims=True)
        mine = lax.broadcasted_iota(jnp.int32, exped.shape, 1) == here_ref[0]
        picked = jnp.sum(jnp.where(mine, exped, 0.0), axis=-1, keepdims=True)
        gate = picked / jnp.where(total > 0.0, total, 1.0)
        gate_slot[...] = jnp.broadcast_to(gate, gate_slot.shape)
        grad_ref[...] = (gate * cot_ref[...].astype(F32)).astype(BF)
        out_total[...] = jnp.zeros_like(out_total)
        in_total[...] = jnp.zeros_like(in_total)

    gate_pre = mm(in_ref[...], gate_ref[...])
    up_pre = mm(in_ref[...], up_ref[...])
    act_grad = mm(grad_ref[...], down_ref[...])
    sig_gate = jax.nn.sigmoid(gate_pre)
    silu_val = gate_pre * sig_gate
    active = (silu_val * up_pre).astype(BF)
    silu_slope = sig_gate * (1.0 + gate_pre * (1.0 - sig_gate))
    gate_grad = (act_grad * up_pre * silu_slope).astype(BF)
    up_grad = (act_grad * silu_val).astype(BF)
    active_ref[...] = active
    gate_grad_ref[...] = gate_grad
    up_grad_ref[...] = up_grad
    out_total[...] += mm_nt(active, down_ref[...])
    in_total[...] += mm_nt(gate_grad, gate_ref[...]) + mm_nt(up_grad, up_ref[...])

    @pl.when(block == pl.num_programs(0) - 1)
    def _():
        out = out_total[...].astype(BF).astype(F32)
        gated_ref[...] = (gate_slot[:, :1] * out).astype(BF)
        in_grad_ref[:, :D] = in_total[...].astype(BF)
        found = jnp.sum(cot_ref[...].astype(F32) * out, axis=-1, keepdims=True)
        high = found.astype(BF).astype(F32)
        lane = lax.broadcasted_iota(jnp.int32, (in_grad_ref.shape[0], in_grad_ref.shape[1] - D), 1)
        lane = lane - here_ref[1]
        parts = jnp.where(lane == 0, high, jnp.where(lane == SLAB, found - high, 0.0))
        in_grad_ref[:, D:] = parts.astype(BF)


def expert_chunk(here, in_chunk, cot_chunk, mask, router, weight, back_width):
    rows = in_chunk.shape[0]
    tile = 256
    steps = FF // tile
    whole = pl.BlockSpec((rows, D), lambda j, h: (0, 0))
    piece = pl.BlockSpec((rows, tile), lambda j, h: (0, j))
    low = jax.ShapeDtypeStruct((rows, FF), BF)
    wide = jax.ShapeDtypeStruct((rows, D), BF)
    return pl.pallas_call(
        expert_kernel,
        grid_spec=pltpu.PrefetchScalarGridSpec(
            num_scalar_prefetch=1,
            grid=(steps,),
            in_specs=[
                whole,
                whole,
                pl.BlockSpec(mask.shape, lambda j, h: (0, 0)),
                pl.BlockSpec(router.shape, lambda j, h: (0, 0)),
                pl.BlockSpec((D, tile), lambda j, h: (0, j)),
                pl.BlockSpec((D, tile), lambda j, h: (0, steps + j)),
                pl.BlockSpec((D, tile), lambda j, h: (0, 2 * steps + j)),
            ],
            out_specs=[
                piece, piece, piece, whole,
                pl.BlockSpec((rows, back_width), lambda j, h: (0, 0)),
                whole,
            ],
            scratch_shapes=[
                pltpu.VMEM((rows, D), F32),
                pltpu.VMEM((rows, D), F32),
                pltpu.VMEM((rows, LANES), F32),
            ],
        ),
        out_shape=[low, low, low, wide, jax.ShapeDtypeStruct((rows, back_width), BF), wide],
        compiler_params=pltpu.CompilerParams(vmem_limit_bytes=40 << 20),
        cost_estimate=pl.CostEstimate(flops=1 << 20, bytes_accessed=1 << 20, transcendentals=0),
        name="expert_chunk",
    )(here, in_chunk, cot_chunk, mask, router, weight, weight, weight)


def expert_grad_kernel(count, *refs):
    lists = [refs[k * count : (k + 1) * count] for k in range(5)]
    out_ref = refs[5 * count]
    column = pl.program_id(1)

    def total(lefts, rights):
        found = mm_tn(lefts[0][...], rights[0][...])
        for left, right in zip(lefts[1:], rights[1:]):
            found = found + mm_tn(left[...], right[...])
        out_ref[...] = found

    for place, (left, right) in enumerate(((0, 2), (0, 3), (1, 4))):
        pl.when(column == place)(functools.partial(total, lists[left], lists[right]))


def expert_grads(in_rows, grad_rows, gate_grads, up_grads, actives):
    count = len(in_rows)
    rows = in_rows[0].shape[0]
    tile = 512
    tall = pl.BlockSpec((rows, tile), lambda i, j: (0, i))
    whole = pl.BlockSpec((rows, FF), lambda i, j: (0, 0))
    return pl.pallas_call(
        functools.partial(expert_grad_kernel, count),
        grid=(D // tile, 3),
        in_specs=[tall] * (2 * count) + [whole] * (3 * count),
        out_specs=pl.BlockSpec((tile, FF), lambda i, j: (i, j)),
        out_shape=jax.ShapeDtypeStruct((D, 3 * FF), F32),
        compiler_params=pltpu.CompilerParams(vmem_limit_bytes=48 << 20),
        cost_estimate=pl.CostEstimate(flops=1 << 20, bytes_accessed=1 << 20, transcendentals=0),
        name="expert_grads",
    )(*in_rows, *grad_rows, *gate_grads, *up_grads, *actives)


def head_normed(raw, gain_ref):
    scale = lax.rsqrt(jnp.mean(raw * raw, axis=-1, keepdims=True) + EPS)
    normal = raw * scale
    return (normal, scale, normal * gain_ref[...])


def turned(values, cos_ref, sin_ref):
    return values * cos_ref[...] + pltpu.roll(values, HEAD_DIM // 2, 1) * sin_ref[...]


def turned_back(values, cos_ref, sin_ref):
    return values * cos_ref[...] + pltpu.roll(values * sin_ref[...], HEAD_DIM // 2, 1)


def head_probs(query, key, row_ref, start_ref, key_row_ref):
    scores = mm_nt(query, key) * HEAD_DIM ** (-0.5)
    allowed = (key_row_ref[0] <= row_ref[0]) & (key_row_ref[0] >= start_ref[0])
    scores = jnp.where(allowed, scores, -1e30)
    exped = jnp.exp(scores - jnp.max(scores, axis=-1, keepdims=True))
    return exped / jnp.sum(exped, axis=-1, keepdims=True)


def attend_kernel(
    query_ref, key_ref, value_ref, cos_ref, sin_ref, qgain_ref, kgain_ref,
    row_ref, start_ref, key_row_ref, mixed_ref, key_low, value_low,
):
    @pl.when(pl.program_id(1) == 0)
    def _():
        key_low[...] = turned(head_normed(key_ref[...], kgain_ref)[2], cos_ref, sin_ref).astype(BF)
        value_low[...] = value_ref[...].astype(BF)

    for part in range(HEADS_STEP):
        lanes = pl.ds(part * HEAD_DIM, HEAD_DIM)
        query = turned(head_normed(query_ref[:, lanes], qgain_ref)[2], cos_ref, sin_ref).astype(BF)
        probs = head_probs(query, key_low[...], row_ref, start_ref, key_row_ref)
        mixed_ref[:, lanes] = mm(probs.astype(BF), value_low[...]).astype(BF)


def attend_back_kernel(
    query_ref, key_ref, value_ref, cos_ref, sin_ref, qgain_ref, kgain_ref,
    row_ref, start_ref, key_row_ref, grad_ref,
    query_out, key_out, value_out, qgain_out, kgain_out,
    key_low, value_low, key_total, value_total,
):
    group, head = pl.program_id(0), pl.program_id(1)
    score_scale = HEAD_DIM ** (-0.5)

    @pl.when((group == 0) & (head == 0))
    def _():
        qgain_out[...] = jnp.zeros_like(qgain_out)
        kgain_out[...] = jnp.zeros_like(kgain_out)

    @pl.when(head == 0)
    def _():
        key_low[...] = turned(head_normed(key_ref[...], kgain_ref)[2], cos_ref, sin_ref).astype(BF)
        value_low[...] = value_ref[...].astype(BF)
        key_total[...] = jnp.zeros_like(key_total)
        value_total[...] = jnp.zeros_like(value_total)

    def raw_grad(grad, normal, scale, gain_ref, gain_out):
        grad = turned_back(grad, cos_ref, sin_ref)
        gain_out[...] += jnp.sum(grad * normal, axis=0, keepdims=True)
        grad = grad * gain_ref[...]
        return scale * (grad - normal * jnp.mean(normal * grad, axis=-1, keepdims=True))

    for part in range(HEADS_STEP):
        lanes = pl.ds(part * HEAD_DIM, HEAD_DIM)
        normal, scale, gained = head_normed(query_ref[:, lanes], qgain_ref)
        query = turned(gained, cos_ref, sin_ref).astype(BF)
        probs = head_probs(query, key_low[...], row_ref, start_ref, key_row_ref)
        grad = grad_ref[:, lanes]
        value_total[...] += mm_tn(probs.astype(BF), grad)
        prob_grad = mm_nt(grad, value_low[...])
        score_grad = (
            probs * (prob_grad - jnp.sum(probs * prob_grad, axis=-1, keepdims=True))
        ).astype(BF)
        key_total[...] += mm_tn(score_grad, query) * score_scale
        query_grad = mm(score_grad, key_low[...]) * score_scale
        query_out[:, lanes] = raw_grad(query_grad, normal, scale, qgain_ref, qgain_out).astype(BF)

    @pl.when(head == pl.num_programs(1) - 1)
    def _():
        key_normal, key_scale, _ = head_normed(key_ref[...], kgain_ref)
        key_out[...] = raw_grad(key_total[...], key_normal, key_scale, kgain_ref, kgain_out).astype(BF)
        value_out[...] = value_total[...].astype(BF)


def attend_specs(heads):
    head = pl.BlockSpec((ROW, HEADS_STEP * HEAD_DIM), lambda b, h: (b, h))
    whole = pl.BlockSpec((ROW, HEAD_DIM), lambda b, h: (b, 0))
    gain = pl.BlockSpec((1, HEAD_DIM), lambda b, h: (0, 0))
    column = pl.BlockSpec((1, ROW, 1), lambda b, h: (b, 0, 0))
    specs = [
        head,
        pl.BlockSpec((ROW, HEAD_DIM), lambda b, h: (b, heads)),
        pl.BlockSpec((ROW, HEAD_DIM), lambda b, h: (b, heads + 1)),
        whole, whole, gain, gain, column, column,
        pl.BlockSpec((1, 1, ROW), lambda b, h: (b, 0, 0)),
    ]
    return (specs, head, whole, gain)


def attend(projected, shared, heads):
    specs, head, _, _ = attend_specs(heads)
    rows = projected.shape[0]
    return pl.pallas_call(
        attend_kernel,
        grid=(rows // ROW, heads // HEADS_STEP),
        in_specs=specs,
        out_specs=head,
        out_shape=jax.ShapeDtypeStruct((rows, heads * HEAD_DIM), BF),
        scratch_shapes=[pltpu.VMEM((ROW, HEAD_DIM), BF)] * 2,
        cost_estimate=pl.CostEstimate(flops=1 << 20, bytes_accessed=1 << 20, transcendentals=0),
        name="attend",
    )(projected, projected, projected, *shared)


def attend_back(projected, shared, grad, heads):
    specs, head, whole, gain = attend_specs(heads)
    rows = projected.shape[0]
    return pl.pallas_call(
        attend_back_kernel,
        grid=(rows // ROW, heads // HEADS_STEP),
        in_specs=specs + [head],
        out_specs=[head, whole, whole, gain, gain],
        out_shape=[
            jax.ShapeDtypeStruct((rows, heads * HEAD_DIM), BF),
            jax.ShapeDtypeStruct((rows, HEAD_DIM), BF),
            jax.ShapeDtypeStruct((rows, HEAD_DIM), BF),
            jax.ShapeDtypeStruct((1, HEAD_DIM), F32),
            jax.ShapeDtypeStruct((1, HEAD_DIM), F32),
        ],
        scratch_shapes=[pltpu.VMEM((ROW, HEAD_DIM), BF)] * 2 + [pltpu.VMEM((ROW, HEAD_DIM), F32)] * 2,
        cost_estimate=pl.CostEstimate(flops=1 << 20, bytes_accessed=1 << 20, transcendentals=0),
        name="attend_back",
    )(projected, projected, projected, *shared, grad)


def shards(tokens, cotangent, w_qkv, w_out, w_router, norm_gains, w_expert, lengths, deal, routes):
    far_count = lax.axis_size(FAR_AXIS)
    device_count = far_count * NEAR * CORES * 2
    experts_all = w_router.shape[1]
    capacity = TOK_DEV * TOPK // experts_all
    slot_count = experts_all * capacity
    seq_index = lax.axis_index(SEQ_AXIS)
    near_index = lax.axis_index(NEAR_AXIS)
    far_index = lax.axis_index(FAR_AXIS)
    core_index = lax.axis_index(CORE_AXIS)
    per_group = HEADS // KV_HEADS
    qcols = per_group * HEAD_DIM
    width = qcols + 2 * HEAD_DIM
    qkv_rows = w_qkv.shape[0]
    out_rows = w_out.shape[0]
    gain_rows = norm_gains.shape[0]
    score_scale = HEAD_DIM ** (-0.5)

    wide = jnp.concatenate(
        [
            w_qkv[:, :QDIM].reshape(qkv_rows, KV_HEADS, qcols),
            w_qkv[:, QDIM : QDIM + KVDIM].reshape(qkv_rows, KV_HEADS, HEAD_DIM),
            w_qkv[:, QDIM + KVDIM :].reshape(qkv_rows, KV_HEADS, HEAD_DIM),
        ],
        axis=2,
    ).transpose(1, 0, 2)
    core_rows = KV_HEADS * qkv_rows
    half_rows = 2 * qkv_rows
    wide_found = quad_parts(wide)
    tokens, *wide_found = tie(tokens, *wide_found)
    qkv_far = far_all(quad_order(wide_found).reshape(core_rows, width), far_count)

    tokens_both = quad_gather(tokens).reshape(2, ROW, D)
    table = jnp.concatenate([deal, jnp.pad(lengths, ((0, 0), (0, LANES - NSEG)))], axis=1)
    table_both = jnp.concatenate(pair_order(table, swap(table, NEAR_AXIS), NEAR_AXIS), axis=0)
    deal_both = table_both[:, :ROW]
    ends = jnp.cumsum(table_both[:, ROW : ROW + NSEG], axis=1)
    starts = ends - table_both[:, ROW : ROW + NSEG]
    seg_both = jnp.sum((deal_both[:, :, None] >= ends[:, None, :]).astype(jnp.int32), axis=2)
    picked = seg_both[:, :, None] == jnp.arange(NSEG, dtype=jnp.int32)[None, None, :]
    pos_both = deal_both - jnp.sum(jnp.where(picked, starts[:, None, :], 0), axis=2)
    dealt_hot = (deal_both[:, :, None] == jnp.arange(ROW, dtype=jnp.int32)[None, None, :]).astype(BF)
    hot_mine = lax.dynamic_index_in_dim(dealt_hot, near_index, 0, keepdims=False)
    hot_half = lax.dynamic_slice_in_dim(hot_mine, seq_index * TOK_DEV, TOK_DEV, axis=0)
    back_half = lax.dynamic_slice_in_dim(hot_mine, seq_index * TOK_DEV, TOK_DEV, axis=1)
    seg_mine = lax.dynamic_slice_in_dim(
        lax.dynamic_index_in_dim(seg_both, near_index, 0, keepdims=False), seq_index * TOK_DEV, TOK_DEV
    )

    expert_ids = jnp.arange(experts_all, dtype=jnp.int32)
    chosen_rows = jnp.sum(
        (routes[0][:, :, None] == expert_ids[None, None, :]).astype(jnp.int32), axis=1
    ).astype(BF)
    chosen = mm(hot_half, chosen_rows)
    live = jnp.where((seg_mine != NSEG - 1)[:, None], chosen, 0.0)
    steps = jnp.arange(TOK_DEV, dtype=jnp.int32)
    earlier = (steps[None, :] < steps[:, None]).astype(BF)
    place = mm(earlier, live.astype(BF))
    place = jnp.where(live > 0.5, place, -1.0).astype(jnp.int32)
    slot_hot = place.T[:, None, :] == jnp.arange(capacity, dtype=jnp.int32)[None, :, None]
    slot_low = slot_hot.astype(BF).reshape(slot_count, TOK_DEV)

    slab = NEAR * CORES * 2
    slab_index = (near_index * CORES + core_index) * 2 + seq_index
    slab_ids = jnp.arange(slab, dtype=jnp.int32)
    out_order = jnp.array([0, 2, 1, 3, 4, 6, 5, 7], jnp.int32)
    place_far = far_stack(far_all(place.T.astype(BF), far_count))

    def slots_of(places, step):
        found = lax.dynamic_index_in_dim(
            places, lax.rem(far_index + far_count - step, far_count), 0, keepdims=False
        )
        found = found[:, None, :] == jnp.arange(capacity, dtype=jnp.int32)[None, :, None]
        return found.astype(BF).reshape(slab * capacity, TOK_DEV)

    place_slab = lax.dynamic_slice_in_dim(place_far, far_index * slab, slab, axis=1).astype(jnp.int32)
    turned_ids = lax.bitwise_xor(out_order, slab_index)
    place_turned = jnp.sum(
        jnp.where(
            (turned_ids[:, None] == slab_ids[None, :])[None, :, :, None], place_slab[:, None], 0
        ),
        axis=2,
    )
    chunk_slots = [slots_of(place_slab, step) for step in range(far_count)]
    send_slots = [slots_of(place_turned, step) for step in range(far_count)]
    chunk_steps = jnp.arange(far_count, dtype=jnp.int32)
    source_ids = (
        lax.rem(far_index + far_count - chunk_steps, far_count)[:, None] * slab + slab_ids[None, :]
    ).reshape(device_count)
    def to_blocks(rows):
        return rows.reshape(4, 2, rows.shape[0] // slab, rows.shape[1])


    router_size = qkv_rows * experts_all
    small_size = router_size + gain_rows
    mask_size = capacity * experts_all
    small_rows = -(-(small_size + mask_size) // (8 * LANES)) * 8
    small = jnp.broadcast_to(
        jnp.concatenate([w_router.reshape(router_size), norm_gains]), (device_count, small_size)
    )
    slot_mask = mm(slot_low, chosen.astype(BF)).astype(BF).reshape(device_count, mask_size)
    small = jnp.concatenate([slot_mask, small], axis=1)
    small = jnp.pad(small, ((0, 0), (0, small_rows * LANES - small_size - mask_size)))
    small_all = exchange(small.reshape(device_count, small_rows, LANES), ALL_AXES).reshape(
        device_count, small_rows * LANES
    )
    mask_back = jnp.take(small_all[:, :mask_size], source_ids, axis=0).reshape(
        far_count, slab * capacity, experts_all
    )
    small_all = small_all[:, mask_size : mask_size + small_size]
    router_full = small_all[:, :router_size].reshape(D, experts_all)
    gains_float = small_all[:, router_size:].reshape(-1).astype(F32)
    gain_attn = gains_float[:D]
    gain_ffn = gains_float[D : 2 * D]
    gain_query = gains_float[2 * D : 2 * D + HEAD_DIM]
    gain_key = gains_float[2 * D + HEAD_DIM :]

    cot_pair = jnp.concatenate(pair_order(cotangent, swap(cotangent, SEQ_AXIS), SEQ_AXIS), axis=0)
    cot_low = mm(hot_half, cot_pair).astype(BF)
    cot_rows = cot_low.astype(F32)
    cot_sent = [
        mm(slot_low, part).astype(BF).reshape(device_count, capacity, part.shape[1])
        for part in (cot_low[:, :COT_CUT], cot_low[:, COT_CUT:])
    ]
    qkv_own = far_stack(qkv_far).reshape(far_count * NEAR, half_rows, width)
    qkv_mine = jnp.stack(pair_order(qkv_own, swap(qkv_own, CORE_AXIS), CORE_AXIS), axis=1).reshape(
        D, width
    )

    out_slabs = far_stack(far_all(w_out, far_count)).reshape(
        KV_HEADS, far_count // KV_HEADS * out_rows, D
    )
    far_part = far_count // KV_HEADS
    x_both = lax.dot_general(
        dealt_hot, tokens_both, (((2,), (1,)), ((0,), (0,))), preferred_element_type=F32
    )
    x_rows = lax.dynamic_slice(
        x_both, (near_index, seq_index * TOK_DEV, 0), (1, TOK_DEV, D)
    )[0]
    normed_low = rms_norm(x_both.reshape(2 * ROW, D), gain_attn).astype(BF)
    projected, *cot_sent = tie(mm(normed_low, qkv_mine), *cot_sent)
    cot_back = [exchange(half, ALL_AXES) for half in cot_sent]
    cosine, sine_part = tables(pos_both.reshape(2 * ROW), HEAD_DIM)
    shared = (
        jnp.concatenate([cosine, cosine], axis=1),
        jnp.concatenate([-sine_part, sine_part], axis=1),
        gain_query[None],
        gain_key[None],
        deal_both[:, :, None],
        (deal_both - pos_both)[:, :, None],
        deal_both[:, None, :],
    )
    mixed_low = attend(projected, shared, per_group)
    out_found = quad_parts(out_slabs)
    mixed_low, *out_found = tie(mixed_low, *out_found)
    out_own = quad_order(out_found).reshape(NEAR * 2, far_part, out_rows, D)
    out_own = out_own.transpose(1, 0, 2, 3).reshape(far_part * NEAR, 2 * out_rows, D)
    out_mine = jnp.stack(pair_order(out_own, swap(out_own, CORE_AXIS), CORE_AXIS), axis=1).reshape(
        qcols, D
    )

    out_partial = mm(mixed_low, out_mine).astype(BF)
    out_partial, cot_back[0] = tie(out_partial, cot_back[0])
    residual = x_rows + sum_parts(quad_parts(out_partial.reshape(4, TOK_DEV, D)))

    normed_two, ffn_back = jax.vjp(rms_norm, residual, gain_ffn)
    ffn_in = normed_two.astype(BF)
    logits = mm(ffn_in, router_full)
    logits = jnp.where(chosen > 0.5, logits, -1e30)
    gate_probs = jax.nn.softmax(logits, axis=-1)
    gate_probs = jnp.where(chosen > 0.5, gate_probs, 0.0)

    expert_weight = w_expert[0]
    expert_here = far_index * slab + slab_index
    in_rows, gate_grads, up_grads, grad_rows, actives, in_grads = ([] for _ in range(6))
    gated_outs = [None] * far_count
    here = jnp.stack([expert_here, far_index * 2 * SLAB + slab_index])
    back_width = D + -(-far_count * 2 * SLAB // LANES) * LANES
    far_rows = [ffn_in]
    for step in range(1, far_count):
        with jax.named_scope('rows_far%d' % step):
            far_rows.append(far_shift(far_rows[-1], 1, far_count))

    def gather(step, source):
        return mm(send_slots[step], source).astype(BF)

    sent = gather(0, ffn_in)

    def send_back(step):
        return slab_return(in_grads[step].reshape(NEAR, CORES, 2, capacity, back_width))

    def combine(step, found):
        back = jnp.concatenate(found, axis=0).reshape(slab * capacity, back_width)
        return mm_tn(send_slots[step], back).astype(BF if step else F32)

    ffn_in, cot_back[1] = tie(ffn_in, cot_back[1])
    cot_chunks = far_parts(
        jnp.concatenate(cot_back, axis=2).reshape(far_count, slab * capacity, D), far_count
    )
    pending, parts = {}, [None] * far_count
    for turn in range(far_count):
        with jax.named_scope("rows_out%d" % turn):
            got = slab_send(to_blocks(sent))
        if turn + 1 < far_count:
            source = far_rows[turn + 1]
            if turn > 0:
                source, up_grads[turn - 1] = tie(source, up_grads[turn - 1])
            sent = gather(turn + 1, source)
        if turn > 0:
            gate_grads[turn - 1], *got = tie(gate_grads[turn - 1], *got)
        with jax.named_scope("rows_core%d" % turn):
            in_chunk = slab_take(got).reshape(slab * capacity, D)
        gate_grad, up_grad, active, grad_chunk, in_grad, gated_out = expert_chunk(
            here, in_chunk, cot_chunks[turn], mask_back[turn], router_full, expert_weight, back_width
        )
        in_rows.append(in_chunk)
        gate_grads.append(gate_grad)
        up_grads.append(up_grad)
        actives.append(active)
        grad_rows.append(grad_chunk)
        in_grads.append(in_grad)
        gated_outs[turn] = gated_out.reshape(slab, capacity, D)
        if 0 < turn < far_count - 1:
            with jax.named_scope("rows_back%d" % turn):
                pending[turn] = send_back(turn)
    up_grads[-1], *pending[1] = tie(up_grads[-1], *pending[1])
    for turn in range(1, far_count - 1):
        parts[turn] = combine(turn, pending[turn])
        if turn + 1 in pending:
            parts[turn], *pending[turn + 1] = tie(parts[turn], *pending[turn + 1])
    last = far_count - 1
    with jax.named_scope("rows_back%d" % last):
        parts[last] = combine(last, send_back(last))
    parts[max(last - 1, 0)], in_grads[0] = tie(parts[max(last - 1, 0)], in_grads[0])
    with jax.named_scope("partial_far"):
        part_found = far_begin(parts, far_count)
    with jax.named_scope("rows_back0"):
        parts[0] = combine(0, send_back(0))
    with jax.named_scope("partial_far"):
        total = far_end(parts, part_found, far_count)
    from_experts = total[:, :D]

    lanes = jnp.arange(back_width - D, dtype=jnp.int32)
    lanes = lanes // (2 * SLAB) * SLAB + lanes % SLAB
    spread = (lanes[:, None] == expert_ids[None, :]).astype(BF)
    gate_grad = mm(total[:, D:].astype(BF), spread)
    mean_term = jnp.sum(gate_probs * gate_grad, axis=1, keepdims=True)
    logit_grad = (gate_probs * (gate_grad - mean_term)).astype(BF)
    router_grad = mm_tn(ffn_in, logit_grad)
    ffn_in_grad = from_experts + mm_nt(logit_grad, router_full)
    resid_part, gain_ffn_grad = ffn_back(ffn_in_grad)
    resid_low = (cot_rows + resid_part).astype(BF)

    in_rows[0], resid_low = tie(in_rows[0], resid_low)
    grad_expert = expert_grads(in_rows, grad_rows, gate_grads, up_grads, actives)[None]

    resid_both, grad_expert = tie(quad_gather(resid_low), grad_expert)
    resid_both = resid_both.reshape(2 * ROW, D)

    def core_sum(values):
        own, other = pair_order(values[:, 0], values[:, 1], CORE_AXIS)
        return own.astype(F32) + swap(other, CORE_AXIS).astype(F32)

    out_grad = mm_tn(mixed_low, resid_both).astype(BF)
    resid_both, out_grad = tie(resid_both, out_grad)
    mixed_grad = mm_nt(resid_both, out_mine).astype(BF)
    out_grad = core_sum(out_grad.reshape(far_part * NEAR, CORES, 2 * out_rows, D)).astype(BF)
    mixed_grad, out_grad = tie(mixed_grad, out_grad)
    out_grad = (
        out_grad
        .reshape(far_part, NEAR * 2, out_rows, D)
        .transpose(1, 0, 2, 3)
        .reshape(NEAR * 2, far_part * out_rows, D)
    )
    out_grad = quad_swap(out_grad).reshape(far_count, out_rows, D)
    query_grad, key_grad, value_grad, query_gain_grad, key_gain_grad = attend_back(
        projected, shared, mixed_grad, per_group
    )
    query_grad, out_grad = tie(query_grad, out_grad)
    out_sent = far_parts(out_grad, far_count)
    out_found = far_begin(out_sent, far_count)
    gated, query_grad = tie(jnp.stack(gated_outs, axis=1), query_grad)
    gated = exchange(gated, SLAB_AXES)
    out_parts = [
        mm_tn(hot, gated[:, step].reshape(slab * capacity, D)).astype(BF if step else F32)
        for step, hot in enumerate(chunk_slots)
    ]
    out_sum = far_end(out_parts, far_begin(out_parts, far_count), far_count)
    proj_grad = jnp.concatenate([query_grad, key_grad, value_grad], axis=1)

    back_grad = lax.dot_general(
        dealt_hot,
        proj_grad.reshape(2, ROW, width),
        (((1,), (1,)), ((0,), (0,))),
        preferred_element_type=F32,
    ).astype(BF).reshape(2 * ROW, width)
    qkv_grad = mm_tn(normed_low, proj_grad).astype(BF)
    back_grad, qkv_grad = tie(back_grad, qkv_grad)
    normed_partial = mm_nt(back_grad, qkv_mine).astype(BF)
    qkv_grad = core_sum(qkv_grad.reshape(far_count * NEAR, CORES, half_rows, width)).astype(BF)
    normed_partial, qkv_grad, *out_found = tie(normed_partial, qkv_grad, *out_found)
    qkv_parts = far_parts(qkv_grad.reshape(far_count, core_rows, width), far_count)
    qkv_found = far_begin(qkv_parts, far_count)
    out_share = far_end(out_sent, out_found, far_count)
    qkv_grad = far_end(qkv_parts, qkv_found, far_count)
    normed_found = quad_parts(normed_partial.reshape(4, TOK_DEV, D))
    qkv_grad, *normed_found = tie(qkv_grad, *normed_found)
    normed_grad = sum_parts(normed_found)
    normed_grad, out_sum = tie(normed_grad, out_sum)
    final_rows = (residual + out_sum).astype(BF)
    final_pair = jnp.concatenate(
        pair_order(final_rows, swap(final_rows, SEQ_AXIS), SEQ_AXIS), axis=0
    )
    layer_out = mm_tn(back_half, final_pair).astype(BF)
    _, attn_back = jax.vjp(rms_norm, tokens.astype(F32), gain_attn)
    input_part, gain_attn_grad = attn_back(normed_grad)
    resid_group = lax.dynamic_slice_in_dim(resid_both, near_index * ROW, ROW, axis=0)
    grad_tokens = (mm_tn(back_half, resid_group) + input_part).astype(BF)

    qkv_grad = quad_swap(qkv_grad.astype(BF).reshape(KV_HEADS, qkv_rows, width))
    qkv_grad = qkv_grad.transpose(1, 0, 2).astype(F32)
    qkv_share = jnp.concatenate(
        [
            qkv_grad[:, :, :qcols].reshape(qkv_rows, QDIM),
            qkv_grad[:, :, qcols : qcols + HEAD_DIM].reshape(qkv_rows, KVDIM),
            qkv_grad[:, :, qcols + HEAD_DIM :].reshape(qkv_rows, KVDIM),
        ],
        axis=1,
    )

    gains_grad = jnp.concatenate(
        [gain_attn_grad, gain_ffn_grad, query_gain_grad[0], key_gain_grad[0]]
    )
    share_rows = -(-small_size // (8 * LANES)) * 8
    small_grad = jnp.concatenate(
        [router_grad.reshape(device_count, router_size), gains_grad.reshape(device_count, gain_rows)],
        axis=1,
    )
    small_grad = jnp.pad(small_grad, ((0, 0), (0, share_rows * LANES - small_size)))
    small_share = jnp.sum(
        exchange(small_grad.reshape(device_count, share_rows, LANES), ALL_AXES), axis=0
    ).reshape(share_rows * LANES)
    router_share = small_share[:router_size].reshape(qkv_rows, experts_all)
    gains_share = small_share[router_size:small_size]
    return (layer_out, grad_tokens, qkv_share, out_share, router_share, gains_share, grad_expert)


def solution(mesh):
    shape = dict(mesh.shape)
    inner = Mesh(
        mesh.devices.reshape(shape["dp"] // (NEAR * CORES), NEAR, CORES, shape["seq"]), ALL_AXES
    )
    rows = P(ALL_AXES, None)
    in_specs = (
        rows,
        rows,
        rows,
        rows,
        rows,
        P(ALL_AXES),
        P(ALL_AXES, None, None),
        P(DP_AXES, None),
        P(DP_AXES, None),
        P(DP_AXES, None, None),
    )
    out_specs = (rows, rows, rows, rows, rows, P(ALL_AXES), P(ALL_AXES, None, None))
    return jax.shard_map(shards, mesh=inner, in_specs=in_specs, out_specs=out_specs, check_vma=False)
```

```python
import functools

import jax
import jax.numpy as jnp
from jax import lax
from jax.experimental import pallas as pl
from jax.experimental.pallas import tpu as pltpu
from jax.sharding import Mesh
from jax.sharding import PartitionSpec as P

D = 2048
HEADS = 32
KV_HEADS = 4
HEAD_DIM = 128
FF = 768
TOPK = 8
NSEG = 4
TOK_DEV = 128
ROW = 256
QDIM = 4096
KVDIM = 512
NEAR = 2
CORES = 2
SLAB = NEAR * CORES * 2
COT_CUT = 1280
HEADS_STEP = 4
LANES = 128

EPS = 1e-06
THETA = 1000000.0
BF = jnp.bfloat16
F32 = jnp.float32

FAR_AXIS = "far"
NEAR_AXIS = "near"
CORE_AXIS = "core"
SEQ_AXIS = "seq"
SLAB_AXES = (NEAR_AXIS, CORE_AXIS, SEQ_AXIS)
HEAD_AXES = (NEAR_AXIS, SEQ_AXIS)
ALL_AXES = (FAR_AXIS, NEAR_AXIS, CORE_AXIS, SEQ_AXIS)
DP_AXES = (FAR_AXIS, NEAR_AXIS, CORE_AXIS)


def rms_norm(values, scales):
    return values * lax.rsqrt(jnp.mean(values * values, axis=-1, keepdims=True) + EPS) * scales


def rotary(values, cosine, sine_part):
    half_width = values.shape[-1] // 2
    front_part = values[..., :half_width]
    back_part = values[..., half_width:]
    cos_wide = cosine[..., None, :]
    sin_wide = sine_part[..., None, :]
    return jnp.concatenate(
        [
            front_part * cos_wide - back_part * sin_wide,
            back_part * cos_wide + front_part * sin_wide,
        ],
        axis=-1,
    )


def tables(positions, head_width):
    half_width = head_width // 2
    inverse = THETA ** (-(jnp.arange(half_width, dtype=F32) * 2.0 / head_width))
    angles = positions.astype(F32)[..., None] * inverse
    return (jnp.cos(angles), jnp.sin(angles))


def dot(left, right, dims):
    return lax.dot_general(left, right, (dims, ((), ())), preferred_element_type=F32)


def mm(left, right):
    return dot(left, right, ((1,), (0,)))


def mm_nt(left, right):
    return dot(left, right, ((1,), (1,)))


def mm_tn(left, right):
    return dot(left, right, ((0,), (0,)))


def swap(value, axis):
    return lax.ppermute(value, axis, [(0, 1), (1, 0)])


def pair_order(own, other, axis):
    first = lax.axis_index(axis) == 0
    return (jnp.where(first, own, other), jnp.where(first, other, own))


def exchange(value, axes):
    return lax.all_to_all(value, axes, split_axis=0, concat_axis=0, tiled=True)


def quad_index():
    return lax.axis_index(NEAR_AXIS) * 2 + lax.axis_index(SEQ_AXIS)


def quad_send(parts, step):
    block = lax.dynamic_index_in_dim(parts, lax.bitwise_xor(quad_index(), step), 0, keepdims=False)
    return lax.ppermute(block, HEAD_AXES, [(i, i ^ step) for i in range(4)])


def quad_order(found):
    low = pair_order(found[0], found[1], SEQ_AXIS)
    high = pair_order(found[2], found[3], SEQ_AXIS)
    rows = [pair_order(low[k], high[k], NEAR_AXIS) for k in range(2)]
    return jnp.stack([rows[0][0], rows[1][0], rows[0][1], rows[1][1]])


def quad_gather(value):
    found = [value] + [
        lax.ppermute(value, HEAD_AXES, [(i, i ^ step) for i in range(4)]) for step in range(1, 4)
    ]
    return quad_order(found)


def quad_parts(parts):
    own = lax.dynamic_index_in_dim(parts, quad_index(), 0, keepdims=False)
    return [own] + [quad_send(parts, step) for step in range(1, 4)]


def quad_swap(parts):
    return quad_order(quad_parts(parts))


def sum_parts(parts):
    total = parts[0].astype(F32)
    for part in parts[1:]:
        total = total + part.astype(F32)
    return total


def far_begin(parts, count):
    if count != 4:
        return [far_shift(parts[step].astype(BF), -step, count) for step in range(1, count)]
    return [far_shift(parts[2].astype(BF), -1, count), far_shift(parts[3].astype(BF), 1, count)]


def far_end(parts, found, count):
    total = parts[0].astype(F32)
    if count != 4:
        for part in found:
            total = total + part.astype(F32)
        return total
    relay = (parts[1].astype(F32) + found[0].astype(F32)).astype(BF)
    return total + found[1].astype(F32) + far_shift(relay, -1, count).astype(F32)


def far_parts(values, count):
    here = lax.axis_index(FAR_AXIS)
    return [
        lax.dynamic_index_in_dim(values, lax.rem(here + count - step, count), 0, keepdims=False)
        for step in range(count)
    ]


def far_all(value, count, first=None):
    ahead = count // 2
    found = [value] + [None] * (count - 1)
    found[1] = far_shift(value, 1, count)
    if count > 2:
        found[count - 1] = far_shift(value, -1, count)
    for step in range(2, ahead + 1):
        found[step] = far_shift(found[step - 1], 1, count)
    for step in range(count - 2, ahead, -1):
        found[step] = far_shift(found[step + 1], -1, count)
    return found


def far_stack(found):
    count = len(found)
    here = lax.axis_index(FAR_AXIS)
    zeros = (0,) * found[0].ndim
    full = jnp.zeros((count,) + found[0].shape, found[0].dtype)
    for step, chunk in enumerate(found):
        full = lax.dynamic_update_slice(full, chunk[None], (lax.rem(here + count - step, count),) + zeros)
    return full


def tie(*values):
    return lax.optimization_barrier(values)


def far_shift(value, step, count):
    return lax.ppermute(value, FAR_AXIS, [(i, (i + step) % count) for i in range(count)])


def far_next(value, count):
    return lax.ppermute(value, FAR_AXIS, [(i, (i + 1) % count) for i in range(count)])


def quad_xor(value, step):
    return lax.ppermute(value, HEAD_AXES, [(i, i ^ step) for i in range(4)])


def slab_send(blocks):
    return [blocks[0]] + [quad_xor(blocks[step], step) for step in range(1, 4)]


def slab_take(got):
    keep = quad_order([part[0] for part in got])
    other = swap(quad_order([part[1] for part in got]), CORE_AXIS)
    first, second = pair_order(keep, other, CORE_AXIS)
    shape = (NEAR, 2) + keep.shape[1:]
    return jnp.stack([first.reshape(shape), second.reshape(shape)], axis=1)


def slab_return(rows):
    keep, give = pair_order(rows[:, 0], rows[:, 1], CORE_AXIS)
    both = jnp.stack([keep, swap(give, CORE_AXIS)], axis=2)
    return quad_parts(both.reshape((4, 2) + rows.shape[3:]))


def expert_kernel(
    here_ref, in_ref, cot_ref, mask_ref, router_ref, gate_ref, up_ref, down_ref,
    gate_grad_ref, up_grad_ref, active_ref, grad_ref, in_grad_ref, gated_ref,
    out_total, in_total, gate_slot,
):
    block = pl.program_id(0)

    @pl.when(block == 0)
    def _():
        chosen = mask_ref[...].astype(F32) > 0.5
        logits = jnp.where(chosen, mm(in_ref[...], router_ref[...]), -1e30)
        exped = jnp.where(chosen, jnp.exp(logits - jnp.max(logits, axis=-1, keepdims=True)), 0.0)
        total = jnp.sum(exped, axis=-1, keepdims=True)
        mine = lax.broadcasted_iota(jnp.int32, exped.shape, 1) == here_ref[0]
        picked = jnp.sum(jnp.where(mine, exped, 0.0), axis=-1, keepdims=True)
        gate = picked / jnp.where(total > 0.0, total, 1.0)
        gate_slot[...] = jnp.broadcast_to(gate, gate_slot.shape)
        grad_ref[...] = (gate * cot_ref[...].astype(F32)).astype(BF)
        out_total[...] = jnp.zeros_like(out_total)
        in_total[...] = jnp.zeros_like(in_total)

    gate_pre = mm(in_ref[...], gate_ref[...])
    up_pre = mm(in_ref[...], up_ref[...])
    act_grad = mm(grad_ref[...], down_ref[...])
    sig_gate = jax.nn.sigmoid(gate_pre)
    silu_val = gate_pre * sig_gate
    active = (silu_val * up_pre).astype(BF)
    silu_slope = sig_gate * (1.0 + gate_pre * (1.0 - sig_gate))
    gate_grad = (act_grad * up_pre * silu_slope).astype(BF)
    up_grad = (act_grad * silu_val).astype(BF)
    active_ref[...] = active
    gate_grad_ref[...] = gate_grad
    up_grad_ref[...] = up_grad
    out_total[...] += mm_nt(active, down_ref[...])
    in_total[...] += mm_nt(gate_grad, gate_ref[...]) + mm_nt(up_grad, up_ref[...])

    @pl.when(block == pl.num_programs(0) - 1)
    def _():
        out = out_total[...].astype(BF).astype(F32)
        gated_ref[...] = (gate_slot[:, :1] * out).astype(BF)
        in_grad_ref[:, :D] = in_total[...].astype(BF)
        found = jnp.sum(cot_ref[...].astype(F32) * out, axis=-1, keepdims=True)
        high = found.astype(BF).astype(F32)
        lane = lax.broadcasted_iota(jnp.int32, (in_grad_ref.shape[0], in_grad_ref.shape[1] - D), 1)
        lane = lane - here_ref[1]
        parts = jnp.where(lane == 0, high, jnp.where(lane == SLAB, found - high, 0.0))
        in_grad_ref[:, D:] = parts.astype(BF)


def expert_chunk(here, in_chunk, cot_chunk, mask, router, weight, back_width):
    rows = in_chunk.shape[0]
    tile = 256
    steps = FF // tile
    whole = pl.BlockSpec((rows, D), lambda j, h: (0, 0))
    piece = pl.BlockSpec((rows, tile), lambda j, h: (0, j))
    low = jax.ShapeDtypeStruct((rows, FF), BF)
    wide = jax.ShapeDtypeStruct((rows, D), BF)
    return pl.pallas_call(
        expert_kernel,
        grid_spec=pltpu.PrefetchScalarGridSpec(
            num_scalar_prefetch=1,
            grid=(steps,),
            in_specs=[
                whole,
                whole,
                pl.BlockSpec(mask.shape, lambda j, h: (0, 0)),
                pl.BlockSpec(router.shape, lambda j, h: (0, 0)),
                pl.BlockSpec((D, tile), lambda j, h: (0, j)),
                pl.BlockSpec((D, tile), lambda j, h: (0, steps + j)),
                pl.BlockSpec((D, tile), lambda j, h: (0, 2 * steps + j)),
            ],
            out_specs=[
                piece, piece, piece, whole,
                pl.BlockSpec((rows, back_width), lambda j, h: (0, 0)),
                whole,
            ],
            scratch_shapes=[
                pltpu.VMEM((rows, D), F32),
                pltpu.VMEM((rows, D), F32),
                pltpu.VMEM((rows, LANES), F32),
            ],
        ),
        out_shape=[low, low, low, wide, jax.ShapeDtypeStruct((rows, back_width), BF), wide],
        compiler_params=pltpu.CompilerParams(vmem_limit_bytes=40 << 20),
        cost_estimate=pl.CostEstimate(flops=1 << 20, bytes_accessed=1 << 20, transcendentals=0),
        name="expert_chunk",
    )(here, in_chunk, cot_chunk, mask, router, weight, weight, weight)


def expert_grad_kernel(count, *refs):
    lists = [refs[k * count : (k + 1) * count] for k in range(5)]
    out_ref = refs[5 * count]
    column = pl.program_id(1)

    def total(lefts, rights):
        found = mm_tn(lefts[0][...], rights[0][...])
        for left, right in zip(lefts[1:], rights[1:]):
            found = found + mm_tn(left[...], right[...])
        out_ref[...] = found

    for place, (left, right) in enumerate(((0, 2), (0, 3), (1, 4))):
        pl.when(column == place)(functools.partial(total, lists[left], lists[right]))


def expert_grads(in_rows, grad_rows, gate_grads, up_grads, actives):
    count = len(in_rows)
    rows = in_rows[0].shape[0]
    tile = 512
    tall = pl.BlockSpec((rows, tile), lambda i, j: (0, i))
    whole = pl.BlockSpec((rows, FF), lambda i, j: (0, 0))
    return pl.pallas_call(
        functools.partial(expert_grad_kernel, count),
        grid=(D // tile, 3),
        in_specs=[tall] * (2 * count) + [whole] * (3 * count),
        out_specs=pl.BlockSpec((tile, FF), lambda i, j: (i, j)),
        out_shape=jax.ShapeDtypeStruct((D, 3 * FF), F32),
        compiler_params=pltpu.CompilerParams(vmem_limit_bytes=48 << 20),
        cost_estimate=pl.CostEstimate(flops=1 << 20, bytes_accessed=1 << 20, transcendentals=0),
        name="expert_grads",
    )(*in_rows, *grad_rows, *gate_grads, *up_grads, *actives)


def head_normed(raw, gain_ref):
    scale = lax.rsqrt(jnp.mean(raw * raw, axis=-1, keepdims=True) + EPS)
    normal = raw * scale
    return (normal, scale, normal * gain_ref[...])


def turned(values, cos_ref, sin_ref):
    return values * cos_ref[...] + pltpu.roll(values, HEAD_DIM // 2, 1) * sin_ref[...]


def turned_back(values, cos_ref, sin_ref):
    return values * cos_ref[...] + pltpu.roll(values * sin_ref[...], HEAD_DIM // 2, 1)


def head_probs(query, key, row_ref, start_ref, key_row_ref):
    scores = mm_nt(query, key) * HEAD_DIM ** (-0.5)
    allowed = (key_row_ref[0] <= row_ref[0]) & (key_row_ref[0] >= start_ref[0])
    scores = jnp.where(allowed, scores, -1e30)
    exped = jnp.exp(scores - jnp.max(scores, axis=-1, keepdims=True))
    return exped / jnp.sum(exped, axis=-1, keepdims=True)


def attend_kernel(
    query_ref, key_ref, value_ref, cos_ref, sin_ref, qgain_ref, kgain_ref,
    row_ref, start_ref, key_row_ref, mixed_ref, key_low, value_low,
):
    @pl.when(pl.program_id(1) == 0)
    def _():
        key_low[...] = turned(head_normed(key_ref[...], kgain_ref)[2], cos_ref, sin_ref).astype(BF)
        value_low[...] = value_ref[...].astype(BF)

    for part in range(HEADS_STEP):
        lanes = pl.ds(part * HEAD_DIM, HEAD_DIM)
        query = turned(head_normed(query_ref[:, lanes], qgain_ref)[2], cos_ref, sin_ref).astype(BF)
        probs = head_probs(query, key_low[...], row_ref, start_ref, key_row_ref)
        mixed_ref[:, lanes] = mm(probs.astype(BF), value_low[...]).astype(BF)


def attend_back_kernel(
    query_ref, key_ref, value_ref, cos_ref, sin_ref, qgain_ref, kgain_ref,
    row_ref, start_ref, key_row_ref, grad_ref,
    query_out, key_out, value_out, qgain_out, kgain_out,
    key_low, value_low, key_total, value_total,
):
    group, head = pl.program_id(0), pl.program_id(1)
    score_scale = HEAD_DIM ** (-0.5)

    @pl.when((group == 0) & (head == 0))
    def _():
        qgain_out[...] = jnp.zeros_like(qgain_out)
        kgain_out[...] = jnp.zeros_like(kgain_out)

    @pl.when(head == 0)
    def _():
        key_low[...] = turned(head_normed(key_ref[...], kgain_ref)[2], cos_ref, sin_ref).astype(BF)
        value_low[...] = value_ref[...].astype(BF)
        key_total[...] = jnp.zeros_like(key_total)
        value_total[...] = jnp.zeros_like(value_total)

    def raw_grad(grad, normal, scale, gain_ref, gain_out):
        grad = turned_back(grad, cos_ref, sin_ref)
        gain_out[...] += jnp.sum(grad * normal, axis=0, keepdims=True)
        grad = grad * gain_ref[...]
        return scale * (grad - normal * jnp.mean(normal * grad, axis=-1, keepdims=True))

    for part in range(HEADS_STEP):
        lanes = pl.ds(part * HEAD_DIM, HEAD_DIM)
        normal, scale, gained = head_normed(query_ref[:, lanes], qgain_ref)
        query = turned(gained, cos_ref, sin_ref).astype(BF)
        probs = head_probs(query, key_low[...], row_ref, start_ref, key_row_ref)
        grad = grad_ref[:, lanes]
        value_total[...] += mm_tn(probs.astype(BF), grad)
        prob_grad = mm_nt(grad, value_low[...])
        score_grad = (
            probs * (prob_grad - jnp.sum(probs * prob_grad, axis=-1, keepdims=True))
        ).astype(BF)
        key_total[...] += mm_tn(score_grad, query) * score_scale
        query_grad = mm(score_grad, key_low[...]) * score_scale
        query_out[:, lanes] = raw_grad(query_grad, normal, scale, qgain_ref, qgain_out).astype(BF)

    @pl.when(head == pl.num_programs(1) - 1)
    def _():
        key_normal, key_scale, _ = head_normed(key_ref[...], kgain_ref)
        key_out[...] = raw_grad(key_total[...], key_normal, key_scale, kgain_ref, kgain_out).astype(BF)
        value_out[...] = value_total[...].astype(BF)


def attend_specs(heads):
    head = pl.BlockSpec((ROW, HEADS_STEP * HEAD_DIM), lambda b, h: (b, h))
    whole = pl.BlockSpec((ROW, HEAD_DIM), lambda b, h: (b, 0))
    gain = pl.BlockSpec((1, HEAD_DIM), lambda b, h: (0, 0))
    column = pl.BlockSpec((1, ROW, 1), lambda b, h: (b, 0, 0))
    specs = [
        head,
        pl.BlockSpec((ROW, HEAD_DIM), lambda b, h: (b, heads)),
        pl.BlockSpec((ROW, HEAD_DIM), lambda b, h: (b, heads + 1)),
        whole, whole, gain, gain, column, column,
        pl.BlockSpec((1, 1, ROW), lambda b, h: (b, 0, 0)),
    ]
    return (specs, head, whole, gain)


def attend(projected, shared, heads):
    specs, head, _, _ = attend_specs(heads)
    rows = projected.shape[0]
    return pl.pallas_call(
        attend_kernel,
        grid=(rows // ROW, heads // HEADS_STEP),
        in_specs=specs,
        out_specs=head,
        out_shape=jax.ShapeDtypeStruct((rows, heads * HEAD_DIM), BF),
        scratch_shapes=[pltpu.VMEM((ROW, HEAD_DIM), BF)] * 2,
        cost_estimate=pl.CostEstimate(flops=1 << 20, bytes_accessed=1 << 20, transcendentals=0),
        name="attend",
    )(projected, projected, projected, *shared)


def attend_back(projected, shared, grad, heads):
    specs, head, whole, gain = attend_specs(heads)
    rows = projected.shape[0]
    return pl.pallas_call(
        attend_back_kernel,
        grid=(rows // ROW, heads // HEADS_STEP),
        in_specs=specs + [head],
        out_specs=[head, whole, whole, gain, gain],
        out_shape=[
            jax.ShapeDtypeStruct((rows, heads * HEAD_DIM), BF),
            jax.ShapeDtypeStruct((rows, HEAD_DIM), BF),
            jax.ShapeDtypeStruct((rows, HEAD_DIM), BF),
            jax.ShapeDtypeStruct((1, HEAD_DIM), F32),
            jax.ShapeDtypeStruct((1, HEAD_DIM), F32),
        ],
        scratch_shapes=[pltpu.VMEM((ROW, HEAD_DIM), BF)] * 2 + [pltpu.VMEM((ROW, HEAD_DIM), F32)] * 2,
        cost_estimate=pl.CostEstimate(flops=1 << 20, bytes_accessed=1 << 20, transcendentals=0),
        name="attend_back",
    )(projected, projected, projected, *shared, grad)


def shards(tokens, cotangent, w_qkv, w_out, w_router, norm_gains, w_expert, lengths, deal, routes):
    far_count = lax.axis_size(FAR_AXIS)
    device_count = far_count * NEAR * CORES * 2
    experts_all = w_router.shape[1]
    capacity = TOK_DEV * TOPK // experts_all
    slot_count = experts_all * capacity
    seq_index = lax.axis_index(SEQ_AXIS)
    near_index = lax.axis_index(NEAR_AXIS)
    far_index = lax.axis_index(FAR_AXIS)
    core_index = lax.axis_index(CORE_AXIS)
    per_group = HEADS // KV_HEADS
    qcols = per_group * HEAD_DIM
    width = qcols + 2 * HEAD_DIM
    qkv_rows = w_qkv.shape[0]
    out_rows = w_out.shape[0]
    gain_rows = norm_gains.shape[0]
    score_scale = HEAD_DIM ** (-0.5)

    wide = jnp.concatenate(
        [
            w_qkv[:, :QDIM].reshape(qkv_rows, KV_HEADS, qcols),
            w_qkv[:, QDIM : QDIM + KVDIM].reshape(qkv_rows, KV_HEADS, HEAD_DIM),
            w_qkv[:, QDIM + KVDIM :].reshape(qkv_rows, KV_HEADS, HEAD_DIM),
        ],
        axis=2,
    ).transpose(1, 0, 2)
    core_rows = KV_HEADS * qkv_rows
    half_rows = 2 * qkv_rows
    wide_found = quad_parts(wide)
    tokens, *wide_found = tie(tokens, *wide_found)
    qkv_far = far_all(quad_order(wide_found).reshape(core_rows, width), far_count)

    tokens_both = quad_gather(tokens).reshape(2, ROW, D)
    table = jnp.concatenate([deal, jnp.pad(lengths, ((0, 0), (0, LANES - NSEG)))], axis=1)
    table_both = jnp.concatenate(pair_order(table, swap(table, NEAR_AXIS), NEAR_AXIS), axis=0)
    deal_both = table_both[:, :ROW]
    ends = jnp.cumsum(table_both[:, ROW : ROW + NSEG], axis=1)
    starts = ends - table_both[:, ROW : ROW + NSEG]
    seg_both = jnp.sum((deal_both[:, :, None] >= ends[:, None, :]).astype(jnp.int32), axis=2)
    picked = seg_both[:, :, None] == jnp.arange(NSEG, dtype=jnp.int32)[None, None, :]
    pos_both = deal_both - jnp.sum(jnp.where(picked, starts[:, None, :], 0), axis=2)
    dealt_hot = (deal_both[:, :, None] == jnp.arange(ROW, dtype=jnp.int32)[None, None, :]).astype(BF)
    hot_mine = lax.dynamic_index_in_dim(dealt_hot, near_index, 0, keepdims=False)
    hot_half = lax.dynamic_slice_in_dim(hot_mine, seq_index * TOK_DEV, TOK_DEV, axis=0)
    back_half = lax.dynamic_slice_in_dim(hot_mine, seq_index * TOK_DEV, TOK_DEV, axis=1)
    seg_mine = lax.dynamic_slice_in_dim(
        lax.dynamic_index_in_dim(seg_both, near_index, 0, keepdims=False), seq_index * TOK_DEV, TOK_DEV
    )

    expert_ids = jnp.arange(experts_all, dtype=jnp.int32)
    chosen_rows = jnp.sum(
        (routes[0][:, :, None] == expert_ids[None, None, :]).astype(jnp.int32), axis=1
    ).astype(BF)
    chosen = mm(hot_half, chosen_rows)
    live = jnp.where((seg_mine != NSEG - 1)[:, None], chosen, 0.0)
    steps = jnp.arange(TOK_DEV, dtype=jnp.int32)
    earlier = (steps[None, :] < steps[:, None]).astype(BF)
    place = mm(earlier, live.astype(BF))
    place = jnp.where(live > 0.5, place, -1.0).astype(jnp.int32)
    slot_hot = place.T[:, None, :] == jnp.arange(capacity, dtype=jnp.int32)[None, :, None]
    slot_low = slot_hot.astype(BF).reshape(slot_count, TOK_DEV)

    slab = NEAR * CORES * 2
    slab_index = (near_index * CORES + core_index) * 2 + seq_index
    slab_ids = jnp.arange(slab, dtype=jnp.int32)
    out_order = jnp.array([0, 2, 1, 3, 4, 6, 5, 7], jnp.int32)
    place_far = far_stack(far_all(place.T.astype(BF), far_count))

    def slots_of(places, step):
        found = lax.dynamic_index_in_dim(
            places, lax.rem(far_index + far_count - step, far_count), 0, keepdims=False
        )
        found = found[:, None, :] == jnp.arange(capacity, dtype=jnp.int32)[None, :, None]
        return found.astype(BF).reshape(slab * capacity, TOK_DEV)

    place_slab = lax.dynamic_slice_in_dim(place_far, far_index * slab, slab, axis=1).astype(jnp.int32)
    turned_ids = lax.bitwise_xor(out_order, slab_index)
    place_turned = jnp.sum(
        jnp.where(
            (turned_ids[:, None] == slab_ids[None, :])[None, :, :, None], place_slab[:, None], 0
        ),
        axis=2,
    )
    chunk_slots = [slots_of(place_slab, step) for step in range(far_count)]
    send_slots = [slots_of(place_turned, step) for step in range(far_count)]
    chunk_steps = jnp.arange(far_count, dtype=jnp.int32)
    source_ids = (
        lax.rem(far_index + far_count - chunk_steps, far_count)[:, None] * slab + slab_ids[None, :]
    ).reshape(device_count)
    def to_blocks(rows):
        return rows.reshape(4, 2, rows.shape[0] // slab, rows.shape[1])


    router_size = qkv_rows * experts_all
    small_size = router_size + gain_rows
    mask_size = capacity * experts_all
    small_rows = -(-(small_size + mask_size) // (8 * LANES)) * 8
    small = jnp.broadcast_to(
        jnp.concatenate([w_router.reshape(router_size), norm_gains]), (device_count, small_size)
    )
    slot_mask = mm(slot_low, chosen.astype(BF)).astype(BF).reshape(device_count, mask_size)
    small = jnp.concatenate([slot_mask, small], axis=1)
    small = jnp.pad(small, ((0, 0), (0, small_rows * LANES - small_size - mask_size)))
    small_all = exchange(small.reshape(device_count, small_rows, LANES), ALL_AXES).reshape(
        device_count, small_rows * LANES
    )
    mask_back = jnp.take(small_all[:, :mask_size], source_ids, axis=0).reshape(
        far_count, slab * capacity, experts_all
    )
    small_all = small_all[:, mask_size : mask_size + small_size]
    router_full = small_all[:, :router_size].reshape(D, experts_all)
    gains_float = small_all[:, router_size:].reshape(-1).astype(F32)
    gain_attn = gains_float[:D]
    gain_ffn = gains_float[D : 2 * D]
    gain_query = gains_float[2 * D : 2 * D + HEAD_DIM]
    gain_key = gains_float[2 * D + HEAD_DIM :]

    cot_pair = jnp.concatenate(pair_order(cotangent, swap(cotangent, SEQ_AXIS), SEQ_AXIS), axis=0)
    cot_low = mm(hot_half, cot_pair).astype(BF)
    cot_rows = cot_low.astype(F32)
    cot_sent = [
        mm(slot_low, part).astype(BF).reshape(device_count, capacity, part.shape[1])
        for part in (cot_low[:, :COT_CUT], cot_low[:, COT_CUT:])
    ]
    qkv_own = far_stack(qkv_far).reshape(far_count * NEAR, half_rows, width)
    qkv_mine = jnp.stack(pair_order(qkv_own, swap(qkv_own, CORE_AXIS), CORE_AXIS), axis=1).reshape(
        D, width
    )

    out_slabs = far_stack(far_all(w_out, far_count)).reshape(
        KV_HEADS, far_count // KV_HEADS * out_rows, D
    )
    far_part = far_count // KV_HEADS
    x_both = lax.dot_general(
        dealt_hot, tokens_both, (((2,), (1,)), ((0,), (0,))), preferred_element_type=F32
    )
    x_rows = lax.dynamic_slice(
        x_both, (near_index, seq_index * TOK_DEV, 0), (1, TOK_DEV, D)
    )[0]
    normed_low = rms_norm(x_both.reshape(2 * ROW, D), gain_attn).astype(BF)
    projected, *cot_sent = tie(mm(normed_low, qkv_mine), *cot_sent)
    cot_back = [exchange(half, ALL_AXES) for half in cot_sent]
    cosine, sine_part = tables(pos_both.reshape(2 * ROW), HEAD_DIM)
    shared = (
        jnp.concatenate([cosine, cosine], axis=1),
        jnp.concatenate([-sine_part, sine_part], axis=1),
        gain_query[None],
        gain_key[None],
        deal_both[:, :, None],
        (deal_both - pos_both)[:, :, None],
        deal_both[:, None, :],
    )
    mixed_low = attend(projected, shared, per_group)
    out_found = quad_parts(out_slabs)
    mixed_low, *out_found = tie(mixed_low, *out_found)
    out_own = quad_order(out_found).reshape(NEAR * 2, far_part, out_rows, D)
    out_own = out_own.transpose(1, 0, 2, 3).reshape(far_part * NEAR, 2 * out_rows, D)
    out_mine = jnp.stack(pair_order(out_own, swap(out_own, CORE_AXIS), CORE_AXIS), axis=1).reshape(
        qcols, D
    )

    out_partial = mm(mixed_low, out_mine).astype(BF)
    out_partial, cot_back[0] = tie(out_partial, cot_back[0])
    residual = x_rows + sum_parts(quad_parts(out_partial.reshape(4, TOK_DEV, D)))

    normed_two, ffn_back = jax.vjp(rms_norm, residual, gain_ffn)
    ffn_in = normed_two.astype(BF)
    logits = mm(ffn_in, router_full)
    logits = jnp.where(chosen > 0.5, logits, -1e30)
    gate_probs = jax.nn.softmax(logits, axis=-1)
    gate_probs = jnp.where(chosen > 0.5, gate_probs, 0.0)

    expert_weight = w_expert[0]
    expert_here = far_index * slab + slab_index
    in_rows, gate_grads, up_grads, grad_rows, actives, in_grads = ([] for _ in range(6))
    gated_outs = [None] * far_count
    here = jnp.stack([expert_here, far_index * 2 * SLAB + slab_index])
    back_width = D + -(-far_count * 2 * SLAB // LANES) * LANES
    far_rows = [ffn_in]
    for step in range(1, far_count):
        with jax.named_scope('rows_far%d' % step):
            far_rows.append(far_shift(far_rows[-1], 1, far_count))

    def gather(step, source):
        return mm(send_slots[step], source).astype(BF)

    sent = gather(0, ffn_in)

    def send_back(step):
        return slab_return(in_grads[step].reshape(NEAR, CORES, 2, capacity, back_width))

    def combine(step, found):
        back = jnp.concatenate(found, axis=0).reshape(slab * capacity, back_width)
        return mm_tn(send_slots[step], back).astype(BF if step else F32)

    ffn_in, cot_back[1] = tie(ffn_in, cot_back[1])
    cot_chunks = far_parts(
        jnp.concatenate(cot_back, axis=2).reshape(far_count, slab * capacity, D), far_count
    )
    pending, parts = {}, [None] * far_count
    for turn in range(far_count):
        with jax.named_scope("rows_out%d" % turn):
            got = slab_send(to_blocks(sent))
        if turn + 1 < far_count:
            source = far_rows[turn + 1]
            if turn > 0:
                source, up_grads[turn - 1] = tie(source, up_grads[turn - 1])
            sent = gather(turn + 1, source)
        if turn > 0:
            gate_grads[turn - 1], *got = tie(gate_grads[turn - 1], *got)
        with jax.named_scope("rows_core%d" % turn):
            in_chunk = slab_take(got).reshape(slab * capacity, D)
        gate_grad, up_grad, active, grad_chunk, in_grad, gated_out = expert_chunk(
            here, in_chunk, cot_chunks[turn], mask_back[turn], router_full, expert_weight, back_width
        )
        in_rows.append(in_chunk)
        gate_grads.append(gate_grad)
        up_grads.append(up_grad)
        actives.append(active)
        grad_rows.append(grad_chunk)
        in_grads.append(in_grad)
        gated_outs[turn] = gated_out.reshape(slab, capacity, D)
        if 0 < turn < far_count - 1:
            with jax.named_scope("rows_back%d" % turn):
                pending[turn] = send_back(turn)
    up_grads[-1], *pending[1] = tie(up_grads[-1], *pending[1])
    for turn in range(1, far_count - 1):
        parts[turn] = combine(turn, pending[turn])
        if turn + 1 in pending:
            parts[turn], *pending[turn + 1] = tie(parts[turn], *pending[turn + 1])
    last = far_count - 1
    with jax.named_scope("rows_back%d" % last):
        parts[last] = combine(last, send_back(last))
    parts[max(last - 1, 0)], in_grads[0] = tie(parts[max(last - 1, 0)], in_grads[0])
    with jax.named_scope("partial_far"):
        part_found = far_begin(parts, far_count)
    with jax.named_scope("rows_back0"):
        parts[0] = combine(0, send_back(0))
    with jax.named_scope("partial_far"):
        total = far_end(parts, part_found, far_count)
    from_experts = total[:, :D]

    lanes = jnp.arange(back_width - D, dtype=jnp.int32)
    lanes = lanes // (2 * SLAB) * SLAB + lanes % SLAB
    spread = (lanes[:, None] == expert_ids[None, :]).astype(BF)
    gate_grad = mm(total[:, D:].astype(BF), spread)
    mean_term = jnp.sum(gate_probs * gate_grad, axis=1, keepdims=True)
    logit_grad = (gate_probs * (gate_grad - mean_term)).astype(BF)
    ffn_in_grad = from_experts + mm_nt(logit_grad, router_full)
    resid_part, gain_ffn_grad = ffn_back(ffn_in_grad)
    resid_low = (cot_rows + resid_part).astype(BF)

    in_rows[0], resid_low = tie(in_rows[0], resid_low)
    grad_expert = expert_grads(in_rows, grad_rows, gate_grads, up_grads, actives)[None]

    resid_both, grad_expert = tie(quad_gather(resid_low), grad_expert)
    resid_both = resid_both.reshape(2 * ROW, D)

    def core_sum(values):
        own, other = pair_order(values[:, 0], values[:, 1], CORE_AXIS)
        return own.astype(F32) + swap(other, CORE_AXIS).astype(F32)

    out_grad = mm_tn(mixed_low, resid_both).astype(BF)
    resid_both, out_grad = tie(resid_both, out_grad)
    mixed_grad = mm_nt(resid_both, out_mine).astype(BF)
    out_grad = core_sum(out_grad.reshape(far_part * NEAR, CORES, 2 * out_rows, D)).astype(BF)
    mixed_grad, out_grad = tie(mixed_grad, out_grad)
    out_grad = (
        out_grad
        .reshape(far_part, NEAR * 2, out_rows, D)
        .transpose(1, 0, 2, 3)
        .reshape(NEAR * 2, far_part * out_rows, D)
    )
    out_grad = quad_swap(out_grad).reshape(far_count, out_rows, D)
    query_grad, key_grad, value_grad, query_gain_grad, key_gain_grad = attend_back(
        projected, shared, mixed_grad, per_group
    )
    query_grad, out_grad = tie(query_grad, out_grad)
    out_sent = far_parts(out_grad, far_count)
    out_found = far_begin(out_sent, far_count)
    gated, query_grad = tie(jnp.stack(gated_outs, axis=1), query_grad)
    gated = exchange(gated, SLAB_AXES)
    out_parts = [
        mm_tn(hot, gated[:, step].reshape(slab * capacity, D)).astype(BF if step else F32)
        for step, hot in enumerate(chunk_slots)
    ]
    out_sum = far_end(out_parts, far_begin(out_parts, far_count), far_count)
    proj_grad = jnp.concatenate([query_grad, key_grad, value_grad], axis=1)

    back_grad = lax.dot_general(
        dealt_hot,
        proj_grad.reshape(2, ROW, width),
        (((1,), (1,)), ((0,), (0,))),
        preferred_element_type=F32,
    ).astype(BF).reshape(2 * ROW, width)
    qkv_grad = mm_tn(normed_low, proj_grad).astype(BF)
    back_grad, qkv_grad = tie(back_grad, qkv_grad)
    normed_partial = mm_nt(back_grad, qkv_mine).astype(BF)
    qkv_grad = core_sum(qkv_grad.reshape(far_count * NEAR, CORES, half_rows, width)).astype(BF)
    normed_partial, qkv_grad, *out_found = tie(normed_partial, qkv_grad, *out_found)
    qkv_parts = far_parts(qkv_grad.reshape(far_count, core_rows, width), far_count)
    qkv_found = far_begin(qkv_parts, far_count)
    out_share = far_end(out_sent, out_found, far_count)
    qkv_grad = far_end(qkv_parts, qkv_found, far_count)
    normed_found = quad_parts(normed_partial.reshape(4, TOK_DEV, D))
    qkv_grad, *normed_found = tie(qkv_grad, *normed_found)
    normed_grad, logit_late = tie(sum_parts(normed_found), logit_grad)
    router_grad = mm_tn(ffn_in, logit_late)
    normed_grad, out_sum = tie(normed_grad, out_sum)
    final_rows = (residual + out_sum).astype(BF)
    final_pair = jnp.concatenate(
        pair_order(final_rows, swap(final_rows, SEQ_AXIS), SEQ_AXIS), axis=0
    )
    layer_out = mm_tn(back_half, final_pair).astype(BF)
    _, attn_back = jax.vjp(rms_norm, tokens.astype(F32), gain_attn)
    input_part, gain_attn_grad = attn_back(normed_grad)
    resid_group = lax.dynamic_slice_in_dim(resid_both, near_index * ROW, ROW, axis=0)
    grad_tokens = (mm_tn(back_half, resid_group) + input_part).astype(BF)

    qkv_grad = quad_swap(qkv_grad.astype(BF).reshape(KV_HEADS, qkv_rows, width))
    qkv_grad = qkv_grad.transpose(1, 0, 2).astype(F32)
    qkv_share = jnp.concatenate(
        [
            qkv_grad[:, :, :qcols].reshape(qkv_rows, QDIM),
            qkv_grad[:, :, qcols : qcols + HEAD_DIM].reshape(qkv_rows, KVDIM),
            qkv_grad[:, :, qcols + HEAD_DIM :].reshape(qkv_rows, KVDIM),
        ],
        axis=1,
    )

    gains_grad = jnp.concatenate(
        [gain_attn_grad, gain_ffn_grad, query_gain_grad[0], key_gain_grad[0]]
    )
    share_rows = -(-small_size // (8 * LANES)) * 8
    small_grad = jnp.concatenate(
        [router_grad.reshape(device_count, router_size), gains_grad.reshape(device_count, gain_rows)],
        axis=1,
    )
    small_grad = jnp.pad(small_grad, ((0, 0), (0, share_rows * LANES - small_size)))
    small_share = jnp.sum(
        exchange(small_grad.reshape(device_count, share_rows, LANES), ALL_AXES), axis=0
    ).reshape(share_rows * LANES)
    router_share = small_share[:router_size].reshape(qkv_rows, experts_all)
    gains_share = small_share[router_size:small_size]
    return (layer_out, grad_tokens, qkv_share, out_share, router_share, gains_share, grad_expert)


def solution(mesh):
    shape = dict(mesh.shape)
    inner = Mesh(
        mesh.devices.reshape(shape["dp"] // (NEAR * CORES), NEAR, CORES, shape["seq"]), ALL_AXES
    )
    rows = P(ALL_AXES, None)
    in_specs = (
        rows,
        rows,
        rows,
        rows,
        rows,
        P(ALL_AXES),
        P(ALL_AXES, None, None),
        P(DP_AXES, None),
        P(DP_AXES, None),
        P(DP_AXES, None, None),
    )
    out_specs = (rows, rows, rows, rows, rows, P(ALL_AXES), P(ALL_AXES, None, None))
    return jax.shard_map(shards, mesh=inner, in_specs=in_specs, out_specs=out_specs, check_vma=False)
```

```python
import functools

import jax
import jax.numpy as jnp
from jax import lax
from jax.experimental import pallas as pl
from jax.experimental.pallas import tpu as pltpu
from jax.sharding import Mesh
from jax.sharding import PartitionSpec as P

D = 2048
HEADS = 32
KV_HEADS = 4
HEAD_DIM = 128
FF = 768
TOPK = 8
NSEG = 4
TOK_DEV = 128
ROW = 256
QDIM = 4096
KVDIM = 512
NEAR = 2
CORES = 2
SLAB = NEAR * CORES * 2
COT_CUT = 1152
HEADS_STEP = 4
LANES = 128

EPS = 1e-06
THETA = 1000000.0
BF = jnp.bfloat16
F32 = jnp.float32

FAR_AXIS = "far"
NEAR_AXIS = "near"
CORE_AXIS = "core"
SEQ_AXIS = "seq"
SLAB_AXES = (NEAR_AXIS, CORE_AXIS, SEQ_AXIS)
HEAD_AXES = (NEAR_AXIS, SEQ_AXIS)
ALL_AXES = (FAR_AXIS, NEAR_AXIS, CORE_AXIS, SEQ_AXIS)
DP_AXES = (FAR_AXIS, NEAR_AXIS, CORE_AXIS)


def rms_norm(values, scales):
    return values * lax.rsqrt(jnp.mean(values * values, axis=-1, keepdims=True) + EPS) * scales


def rotary(values, cosine, sine_part):
    half_width = values.shape[-1] // 2
    front_part = values[..., :half_width]
    back_part = values[..., half_width:]
    cos_wide = cosine[..., None, :]
    sin_wide = sine_part[..., None, :]
    return jnp.concatenate(
        [
            front_part * cos_wide - back_part * sin_wide,
            back_part * cos_wide + front_part * sin_wide,
        ],
        axis=-1,
    )


def tables(positions, head_width):
    half_width = head_width // 2
    inverse = THETA ** (-(jnp.arange(half_width, dtype=F32) * 2.0 / head_width))
    angles = positions.astype(F32)[..., None] * inverse
    return (jnp.cos(angles), jnp.sin(angles))


def dot(left, right, dims):
    return lax.dot_general(left, right, (dims, ((), ())), preferred_element_type=F32)


def mm(left, right):
    return dot(left, right, ((1,), (0,)))


def mm_nt(left, right):
    return dot(left, right, ((1,), (1,)))


def mm_tn(left, right):
    return dot(left, right, ((0,), (0,)))


def swap(value, axis):
    return lax.ppermute(value, axis, [(0, 1), (1, 0)])


def pair_order(own, other, axis):
    first = lax.axis_index(axis) == 0
    return (jnp.where(first, own, other), jnp.where(first, other, own))


def exchange(value, axes):
    return lax.all_to_all(value, axes, split_axis=0, concat_axis=0, tiled=True)


def quad_index():
    return lax.axis_index(NEAR_AXIS) * 2 + lax.axis_index(SEQ_AXIS)


def quad_send(parts, step):
    block = lax.dynamic_index_in_dim(parts, lax.bitwise_xor(quad_index(), step), 0, keepdims=False)
    return lax.ppermute(block, HEAD_AXES, [(i, i ^ step) for i in range(4)])


def quad_order(found):
    low = pair_order(found[0], found[1], SEQ_AXIS)
    high = pair_order(found[2], found[3], SEQ_AXIS)
    rows = [pair_order(low[k], high[k], NEAR_AXIS) for k in range(2)]
    return jnp.stack([rows[0][0], rows[1][0], rows[0][1], rows[1][1]])


def quad_gather(value):
    found = [value] + [
        lax.ppermute(value, HEAD_AXES, [(i, i ^ step) for i in range(4)]) for step in range(1, 4)
    ]
    return quad_order(found)


def quad_parts(parts):
    own = lax.dynamic_index_in_dim(parts, quad_index(), 0, keepdims=False)
    return [own] + [quad_send(parts, step) for step in range(1, 4)]


def quad_swap(parts):
    return quad_order(quad_parts(parts))


def sum_parts(parts):
    total = parts[0].astype(F32)
    for part in parts[1:]:
        total = total + part.astype(F32)
    return total


def far_begin(parts, count):
    if count != 4:
        return [far_shift(parts[step].astype(BF), -step, count) for step in range(1, count)]
    return [far_shift(parts[2].astype(BF), -1, count), far_shift(parts[3].astype(BF), 1, count)]


def far_end(parts, found, count):
    total = parts[0].astype(F32)
    if count != 4:
        for part in found:
            total = total + part.astype(F32)
        return total
    relay = (parts[1].astype(F32) + found[0].astype(F32)).astype(BF)
    return total + found[1].astype(F32) + far_shift(relay, -1, count).astype(F32)


def far_parts(values, count):
    here = lax.axis_index(FAR_AXIS)
    return [
        lax.dynamic_index_in_dim(values, lax.rem(here + count - step, count), 0, keepdims=False)
        for step in range(count)
    ]


def far_all(value, count, first=None):
    ahead = count // 2
    found = [value] + [None] * (count - 1)
    found[1] = far_shift(value, 1, count)
    if count > 2:
        found[count - 1] = far_shift(value, -1, count)
    for step in range(2, ahead + 1):
        found[step] = far_shift(found[step - 1], 1, count)
    for step in range(count - 2, ahead, -1):
        found[step] = far_shift(found[step + 1], -1, count)
    return found


def far_stack(found):
    count = len(found)
    here = lax.axis_index(FAR_AXIS)
    zeros = (0,) * found[0].ndim
    full = jnp.zeros((count,) + found[0].shape, found[0].dtype)
    for step, chunk in enumerate(found):
        full = lax.dynamic_update_slice(full, chunk[None], (lax.rem(here + count - step, count),) + zeros)
    return full


def tie(*values):
    return lax.optimization_barrier(values)


def far_shift(value, step, count):
    return lax.ppermute(value, FAR_AXIS, [(i, (i + step) % count) for i in range(count)])


def far_next(value, count):
    return lax.ppermute(value, FAR_AXIS, [(i, (i + 1) % count) for i in range(count)])


def quad_xor(value, step):
    return lax.ppermute(value, HEAD_AXES, [(i, i ^ step) for i in range(4)])


def slab_send(blocks):
    return [blocks[0]] + [quad_xor(blocks[step], step) for step in range(1, 4)]


def slab_take(got):
    keep = quad_order([part[0] for part in got])
    other = swap(quad_order([part[1] for part in got]), CORE_AXIS)
    first, second = pair_order(keep, other, CORE_AXIS)
    shape = (NEAR, 2) + keep.shape[1:]
    return jnp.stack([first.reshape(shape), second.reshape(shape)], axis=1)


def slab_return(rows):
    keep, give = pair_order(rows[:, 0], rows[:, 1], CORE_AXIS)
    both = jnp.stack([keep, swap(give, CORE_AXIS)], axis=2)
    return quad_parts(both.reshape((4, 2) + rows.shape[3:]))


def expert_kernel(
    here_ref, in_ref, cot_ref, mask_ref, router_ref, gate_ref, up_ref, down_ref,
    gate_grad_ref, up_grad_ref, active_ref, grad_ref, in_grad_ref, gated_ref,
    out_total, in_total, gate_slot,
):
    block = pl.program_id(0)

    @pl.when(block == 0)
    def _():
        chosen = mask_ref[...].astype(F32) > 0.5
        logits = jnp.where(chosen, mm(in_ref[...], router_ref[...]), -1e30)
        exped = jnp.where(chosen, jnp.exp(logits - jnp.max(logits, axis=-1, keepdims=True)), 0.0)
        total = jnp.sum(exped, axis=-1, keepdims=True)
        mine = lax.broadcasted_iota(jnp.int32, exped.shape, 1) == here_ref[0]
        picked = jnp.sum(jnp.where(mine, exped, 0.0), axis=-1, keepdims=True)
        gate = picked / jnp.where(total > 0.0, total, 1.0)
        gate_slot[...] = jnp.broadcast_to(gate, gate_slot.shape)
        grad_ref[...] = (gate * cot_ref[...].astype(F32)).astype(BF)
        out_total[...] = jnp.zeros_like(out_total)
        in_total[...] = jnp.zeros_like(in_total)

    gate_pre = mm(in_ref[...], gate_ref[...])
    up_pre = mm(in_ref[...], up_ref[...])
    act_grad = mm(grad_ref[...], down_ref[...])
    sig_gate = jax.nn.sigmoid(gate_pre)
    silu_val = gate_pre * sig_gate
    active = (silu_val * up_pre).astype(BF)
    silu_slope = sig_gate * (1.0 + gate_pre * (1.0 - sig_gate))
    gate_grad = (act_grad * up_pre * silu_slope).astype(BF)
    up_grad = (act_grad * silu_val).astype(BF)
    active_ref[...] = active
    gate_grad_ref[...] = gate_grad
    up_grad_ref[...] = up_grad
    out_total[...] += mm_nt(active, down_ref[...])
    in_total[...] += mm_nt(gate_grad, gate_ref[...]) + mm_nt(up_grad, up_ref[...])

    @pl.when(block == pl.num_programs(0) - 1)
    def _():
        out = out_total[...].astype(BF).astype(F32)
        gated_ref[...] = (gate_slot[:, :1] * out).astype(BF)
        in_grad_ref[:, :D] = in_total[...].astype(BF)
        found = jnp.sum(cot_ref[...].astype(F32) * out, axis=-1, keepdims=True)
        high = found.astype(BF).astype(F32)
        lane = lax.broadcasted_iota(jnp.int32, (in_grad_ref.shape[0], in_grad_ref.shape[1] - D), 1)
        lane = lane - here_ref[1]
        parts = jnp.where(lane == 0, high, jnp.where(lane == SLAB, found - high, 0.0))
        in_grad_ref[:, D:] = parts.astype(BF)


def expert_chunk(here, in_chunk, cot_chunk, mask, router, weight, back_width):
    rows = in_chunk.shape[0]
    tile = 256
    steps = FF // tile
    whole = pl.BlockSpec((rows, D), lambda j, h: (0, 0))
    piece = pl.BlockSpec((rows, tile), lambda j, h: (0, j))
    low = jax.ShapeDtypeStruct((rows, FF), BF)
    wide = jax.ShapeDtypeStruct((rows, D), BF)
    return pl.pallas_call(
        expert_kernel,
        grid_spec=pltpu.PrefetchScalarGridSpec(
            num_scalar_prefetch=1,
            grid=(steps,),
            in_specs=[
                whole,
                whole,
                pl.BlockSpec(mask.shape, lambda j, h: (0, 0)),
                pl.BlockSpec(router.shape, lambda j, h: (0, 0)),
                pl.BlockSpec((D, tile), lambda j, h: (0, j)),
                pl.BlockSpec((D, tile), lambda j, h: (0, steps + j)),
                pl.BlockSpec((D, tile), lambda j, h: (0, 2 * steps + j)),
            ],
            out_specs=[
                piece, piece, piece, whole,
                pl.BlockSpec((rows, back_width), lambda j, h: (0, 0)),
                whole,
            ],
            scratch_shapes=[
                pltpu.VMEM((rows, D), F32),
                pltpu.VMEM((rows, D), F32),
                pltpu.VMEM((rows, LANES), F32),
            ],
        ),
        out_shape=[low, low, low, wide, jax.ShapeDtypeStruct((rows, back_width), BF), wide],
        compiler_params=pltpu.CompilerParams(vmem_limit_bytes=40 << 20),
        cost_estimate=pl.CostEstimate(flops=1 << 20, bytes_accessed=1 << 20, transcendentals=0),
        name="expert_chunk",
    )(here, in_chunk, cot_chunk, mask, router, weight, weight, weight)


def expert_grad_kernel(count, *refs):
    lists = [refs[k * count : (k + 1) * count] for k in range(5)]
    out_ref = refs[5 * count]
    column = pl.program_id(1)

    def total(lefts, rights):
        found = mm_tn(lefts[0][...], rights[0][...])
        for left, right in zip(lefts[1:], rights[1:]):
            found = found + mm_tn(left[...], right[...])
        out_ref[...] = found

    for place, (left, right) in enumerate(((0, 2), (0, 3), (1, 4))):
        pl.when(column == place)(functools.partial(total, lists[left], lists[right]))


def expert_grads(in_rows, grad_rows, gate_grads, up_grads, actives):
    count = len(in_rows)
    rows = in_rows[0].shape[0]
    tile = 512
    tall = pl.BlockSpec((rows, tile), lambda i, j: (0, i))
    whole = pl.BlockSpec((rows, FF), lambda i, j: (0, 0))
    return pl.pallas_call(
        functools.partial(expert_grad_kernel, count),
        grid=(D // tile, 3),
        in_specs=[tall] * (2 * count) + [whole] * (3 * count),
        out_specs=pl.BlockSpec((tile, FF), lambda i, j: (i, j)),
        out_shape=jax.ShapeDtypeStruct((D, 3 * FF), F32),
        compiler_params=pltpu.CompilerParams(vmem_limit_bytes=48 << 20),
        cost_estimate=pl.CostEstimate(flops=1 << 20, bytes_accessed=1 << 20, transcendentals=0),
        name="expert_grads",
    )(*in_rows, *grad_rows, *gate_grads, *up_grads, *actives)


def head_normed(raw, gain_ref):
    scale = lax.rsqrt(jnp.mean(raw * raw, axis=-1, keepdims=True) + EPS)
    normal = raw * scale
    return (normal, scale, normal * gain_ref[...])


def turned(values, cos_ref, sin_ref):
    return values * cos_ref[...] + pltpu.roll(values, HEAD_DIM // 2, 1) * sin_ref[...]


def turned_back(values, cos_ref, sin_ref):
    return values * cos_ref[...] + pltpu.roll(values * sin_ref[...], HEAD_DIM // 2, 1)


def head_probs(query, key, row_ref, start_ref, key_row_ref):
    scores = mm_nt(query, key) * HEAD_DIM ** (-0.5)
    allowed = (key_row_ref[0] <= row_ref[0]) & (key_row_ref[0] >= start_ref[0])
    scores = jnp.where(allowed, scores, -1e30)
    exped = jnp.exp(scores - jnp.max(scores, axis=-1, keepdims=True))
    return exped / jnp.sum(exped, axis=-1, keepdims=True)


def attend_kernel(
    query_ref, key_ref, value_ref, cos_ref, sin_ref, qgain_ref, kgain_ref,
    row_ref, start_ref, key_row_ref, mixed_ref, key_low, value_low,
):
    @pl.when(pl.program_id(1) == 0)
    def _():
        key_low[...] = turned(head_normed(key_ref[...], kgain_ref)[2], cos_ref, sin_ref).astype(BF)
        value_low[...] = value_ref[...].astype(BF)

    for part in range(HEADS_STEP):
        lanes = pl.ds(part * HEAD_DIM, HEAD_DIM)
        query = turned(head_normed(query_ref[:, lanes], qgain_ref)[2], cos_ref, sin_ref).astype(BF)
        probs = head_probs(query, key_low[...], row_ref, start_ref, key_row_ref)
        mixed_ref[:, lanes] = mm(probs.astype(BF), value_low[...]).astype(BF)


def attend_back_kernel(
    query_ref, key_ref, value_ref, cos_ref, sin_ref, qgain_ref, kgain_ref,
    row_ref, start_ref, key_row_ref, grad_ref,
    query_out, key_out, value_out, qgain_out, kgain_out,
    key_low, value_low, key_total, value_total,
):
    group, head = pl.program_id(0), pl.program_id(1)
    score_scale = HEAD_DIM ** (-0.5)

    @pl.when((group == 0) & (head == 0))
    def _():
        qgain_out[...] = jnp.zeros_like(qgain_out)
        kgain_out[...] = jnp.zeros_like(kgain_out)

    @pl.when(head == 0)
    def _():
        key_low[...] = turned(head_normed(key_ref[...], kgain_ref)[2], cos_ref, sin_ref).astype(BF)
        value_low[...] = value_ref[...].astype(BF)
        key_total[...] = jnp.zeros_like(key_total)
        value_total[...] = jnp.zeros_like(value_total)

    def raw_grad(grad, normal, scale, gain_ref, gain_out):
        grad = turned_back(grad, cos_ref, sin_ref)
        gain_out[...] += jnp.sum(grad * normal, axis=0, keepdims=True)
        grad = grad * gain_ref[...]
        return scale * (grad - normal * jnp.mean(normal * grad, axis=-1, keepdims=True))

    for part in range(HEADS_STEP):
        lanes = pl.ds(part * HEAD_DIM, HEAD_DIM)
        normal, scale, gained = head_normed(query_ref[:, lanes], qgain_ref)
        query = turned(gained, cos_ref, sin_ref).astype(BF)
        probs = head_probs(query, key_low[...], row_ref, start_ref, key_row_ref)
        grad = grad_ref[:, lanes]
        value_total[...] += mm_tn(probs.astype(BF), grad)
        prob_grad = mm_nt(grad, value_low[...])
        score_grad = (
            probs * (prob_grad - jnp.sum(probs * prob_grad, axis=-1, keepdims=True))
        ).astype(BF)
        key_total[...] += mm_tn(score_grad, query) * score_scale
        query_grad = mm(score_grad, key_low[...]) * score_scale
        query_out[:, lanes] = raw_grad(query_grad, normal, scale, qgain_ref, qgain_out).astype(BF)

    @pl.when(head == pl.num_programs(1) - 1)
    def _():
        key_normal, key_scale, _ = head_normed(key_ref[...], kgain_ref)
        key_out[...] = raw_grad(key_total[...], key_normal, key_scale, kgain_ref, kgain_out).astype(BF)
        value_out[...] = value_total[...].astype(BF)


def attend_specs(heads):
    head = pl.BlockSpec((ROW, HEADS_STEP * HEAD_DIM), lambda b, h: (b, h))
    whole = pl.BlockSpec((ROW, HEAD_DIM), lambda b, h: (b, 0))
    gain = pl.BlockSpec((1, HEAD_DIM), lambda b, h: (0, 0))
    column = pl.BlockSpec((1, ROW, 1), lambda b, h: (b, 0, 0))
    specs = [
        head,
        pl.BlockSpec((ROW, HEAD_DIM), lambda b, h: (b, heads)),
        pl.BlockSpec((ROW, HEAD_DIM), lambda b, h: (b, heads + 1)),
        whole, whole, gain, gain, column, column,
        pl.BlockSpec((1, 1, ROW), lambda b, h: (b, 0, 0)),
    ]
    return (specs, head, whole, gain)


def attend(projected, shared, heads):
    specs, head, _, _ = attend_specs(heads)
    rows = projected.shape[0]
    return pl.pallas_call(
        attend_kernel,
        grid=(rows // ROW, heads // HEADS_STEP),
        in_specs=specs,
        out_specs=head,
        out_shape=jax.ShapeDtypeStruct((rows, heads * HEAD_DIM), BF),
        scratch_shapes=[pltpu.VMEM((ROW, HEAD_DIM), BF)] * 2,
        cost_estimate=pl.CostEstimate(flops=1 << 20, bytes_accessed=1 << 20, transcendentals=0),
        name="attend",
    )(projected, projected, projected, *shared)


def attend_back(projected, shared, grad, heads):
    specs, head, whole, gain = attend_specs(heads)
    rows = projected.shape[0]
    return pl.pallas_call(
        attend_back_kernel,
        grid=(rows // ROW, heads // HEADS_STEP),
        in_specs=specs + [head],
        out_specs=[head, whole, whole, gain, gain],
        out_shape=[
            jax.ShapeDtypeStruct((rows, heads * HEAD_DIM), BF),
            jax.ShapeDtypeStruct((rows, HEAD_DIM), BF),
            jax.ShapeDtypeStruct((rows, HEAD_DIM), BF),
            jax.ShapeDtypeStruct((1, HEAD_DIM), F32),
            jax.ShapeDtypeStruct((1, HEAD_DIM), F32),
        ],
        scratch_shapes=[pltpu.VMEM((ROW, HEAD_DIM), BF)] * 2 + [pltpu.VMEM((ROW, HEAD_DIM), F32)] * 2,
        cost_estimate=pl.CostEstimate(flops=1 << 20, bytes_accessed=1 << 20, transcendentals=0),
        name="attend_back",
    )(projected, projected, projected, *shared, grad)


def shards(tokens, cotangent, w_qkv, w_out, w_router, norm_gains, w_expert, lengths, deal, routes):
    far_count = lax.axis_size(FAR_AXIS)
    device_count = far_count * NEAR * CORES * 2
    experts_all = w_router.shape[1]
    capacity = TOK_DEV * TOPK // experts_all
    slot_count = experts_all * capacity
    seq_index = lax.axis_index(SEQ_AXIS)
    near_index = lax.axis_index(NEAR_AXIS)
    far_index = lax.axis_index(FAR_AXIS)
    core_index = lax.axis_index(CORE_AXIS)
    per_group = HEADS // KV_HEADS
    qcols = per_group * HEAD_DIM
    width = qcols + 2 * HEAD_DIM
    qkv_rows = w_qkv.shape[0]
    out_rows = w_out.shape[0]
    gain_rows = norm_gains.shape[0]
    score_scale = HEAD_DIM ** (-0.5)

    wide = jnp.concatenate(
        [
            w_qkv[:, :QDIM].reshape(qkv_rows, KV_HEADS, qcols),
            w_qkv[:, QDIM : QDIM + KVDIM].reshape(qkv_rows, KV_HEADS, HEAD_DIM),
            w_qkv[:, QDIM + KVDIM :].reshape(qkv_rows, KV_HEADS, HEAD_DIM),
        ],
        axis=2,
    ).transpose(1, 0, 2)
    core_rows = KV_HEADS * qkv_rows
    half_rows = 2 * qkv_rows
    wide_found = quad_parts(wide)
    tokens, *wide_found = tie(tokens, *wide_found)
    qkv_far = far_all(quad_order(wide_found).reshape(core_rows, width), far_count)

    tokens_both = quad_gather(tokens).reshape(2, ROW, D)
    table = jnp.concatenate([deal, jnp.pad(lengths, ((0, 0), (0, LANES - NSEG)))], axis=1)
    table_both = jnp.concatenate(pair_order(table, swap(table, NEAR_AXIS), NEAR_AXIS), axis=0)
    deal_both = table_both[:, :ROW]
    ends = jnp.cumsum(table_both[:, ROW : ROW + NSEG], axis=1)
    starts = ends - table_both[:, ROW : ROW + NSEG]
    seg_both = jnp.sum((deal_both[:, :, None] >= ends[:, None, :]).astype(jnp.int32), axis=2)
    picked = seg_both[:, :, None] == jnp.arange(NSEG, dtype=jnp.int32)[None, None, :]
    pos_both = deal_both - jnp.sum(jnp.where(picked, starts[:, None, :], 0), axis=2)
    dealt_hot = (deal_both[:, :, None] == jnp.arange(ROW, dtype=jnp.int32)[None, None, :]).astype(BF)
    hot_mine = lax.dynamic_index_in_dim(dealt_hot, near_index, 0, keepdims=False)
    hot_half = lax.dynamic_slice_in_dim(hot_mine, seq_index * TOK_DEV, TOK_DEV, axis=0)
    back_half = lax.dynamic_slice_in_dim(hot_mine, seq_index * TOK_DEV, TOK_DEV, axis=1)
    seg_mine = lax.dynamic_slice_in_dim(
        lax.dynamic_index_in_dim(seg_both, near_index, 0, keepdims=False), seq_index * TOK_DEV, TOK_DEV
    )

    expert_ids = jnp.arange(experts_all, dtype=jnp.int32)
    chosen_rows = jnp.sum(
        (routes[0][:, :, None] == expert_ids[None, None, :]).astype(jnp.int32), axis=1
    ).astype(BF)
    chosen = mm(hot_half, chosen_rows)
    live = jnp.where((seg_mine != NSEG - 1)[:, None], chosen, 0.0)
    steps = jnp.arange(TOK_DEV, dtype=jnp.int32)
    earlier = (steps[None, :] < steps[:, None]).astype(BF)
    place = mm(earlier, live.astype(BF))
    place = jnp.where(live > 0.5, place, -1.0).astype(jnp.int32)
    slot_hot = place.T[:, None, :] == jnp.arange(capacity, dtype=jnp.int32)[None, :, None]
    slot_low = slot_hot.astype(BF).reshape(slot_count, TOK_DEV)

    slab = NEAR * CORES * 2
    slab_index = (near_index * CORES + core_index) * 2 + seq_index
    slab_ids = jnp.arange(slab, dtype=jnp.int32)
    out_order = jnp.array([0, 2, 1, 3, 4, 6, 5, 7], jnp.int32)
    place_far = far_stack(far_all(place.T.astype(BF), far_count))

    def slots_of(places, step):
        found = lax.dynamic_index_in_dim(
            places, lax.rem(far_index + far_count - step, far_count), 0, keepdims=False
        )
        found = found[:, None, :] == jnp.arange(capacity, dtype=jnp.int32)[None, :, None]
        return found.astype(BF).reshape(slab * capacity, TOK_DEV)

    place_slab = lax.dynamic_slice_in_dim(place_far, far_index * slab, slab, axis=1).astype(jnp.int32)
    turned_ids = lax.bitwise_xor(out_order, slab_index)
    place_turned = jnp.sum(
        jnp.where(
            (turned_ids[:, None] == slab_ids[None, :])[None, :, :, None], place_slab[:, None], 0
        ),
        axis=2,
    )
    chunk_slots = [slots_of(place_slab, step) for step in range(far_count)]
    send_slots = [slots_of(place_turned, step) for step in range(far_count)]
    chunk_steps = jnp.arange(far_count, dtype=jnp.int32)
    source_ids = (
        lax.rem(far_index + far_count - chunk_steps, far_count)[:, None] * slab + slab_ids[None, :]
    ).reshape(device_count)
    def to_blocks(rows):
        return rows.reshape(4, 2, rows.shape[0] // slab, rows.shape[1])


    router_size = qkv_rows * experts_all
    small_size = router_size + gain_rows
    mask_size = capacity * experts_all
    small_rows = -(-(small_size + mask_size) // (8 * LANES)) * 8
    small = jnp.broadcast_to(
        jnp.concatenate([w_router.reshape(router_size), norm_gains]), (device_count, small_size)
    )
    slot_mask = mm(slot_low, chosen.astype(BF)).astype(BF).reshape(device_count, mask_size)
    small = jnp.concatenate([slot_mask, small], axis=1)
    small = jnp.pad(small, ((0, 0), (0, small_rows * LANES - small_size - mask_size)))
    small_all = exchange(small.reshape(device_count, small_rows, LANES), ALL_AXES).reshape(
        device_count, small_rows * LANES
    )
    mask_back = jnp.take(small_all[:, :mask_size], source_ids, axis=0).reshape(
        far_count, slab * capacity, experts_all
    )
    small_all = small_all[:, mask_size : mask_size + small_size]
    router_full = small_all[:, :router_size].reshape(D, experts_all)
    gains_float = small_all[:, router_size:].reshape(-1).astype(F32)
    gain_attn = gains_float[:D]
    gain_ffn = gains_float[D : 2 * D]
    gain_query = gains_float[2 * D : 2 * D + HEAD_DIM]
    gain_key = gains_float[2 * D + HEAD_DIM :]

    cot_pair = jnp.concatenate(pair_order(cotangent, swap(cotangent, SEQ_AXIS), SEQ_AXIS), axis=0)
    cot_low = mm(hot_half, cot_pair).astype(BF)
    cot_rows = cot_low.astype(F32)
    cot_sent = [
        mm(slot_low, part).astype(BF).reshape(device_count, capacity, part.shape[1])
        for part in (cot_low[:, :COT_CUT], cot_low[:, COT_CUT:])
    ]
    qkv_own = far_stack(qkv_far).reshape(far_count * NEAR, half_rows, width)
    qkv_mine = jnp.stack(pair_order(qkv_own, swap(qkv_own, CORE_AXIS), CORE_AXIS), axis=1).reshape(
        D, width
    )

    out_slabs = far_stack(far_all(w_out, far_count)).reshape(
        KV_HEADS, far_count // KV_HEADS * out_rows, D
    )
    far_part = far_count // KV_HEADS
    x_both = lax.dot_general(
        dealt_hot, tokens_both, (((2,), (1,)), ((0,), (0,))), preferred_element_type=F32
    )
    x_rows = lax.dynamic_slice(
        x_both, (near_index, seq_index * TOK_DEV, 0), (1, TOK_DEV, D)
    )[0]
    normed_low = rms_norm(x_both.reshape(2 * ROW, D), gain_attn).astype(BF)
    projected, *cot_sent = tie(mm(normed_low, qkv_mine), *cot_sent)
    cot_back = [exchange(half, ALL_AXES) for half in cot_sent]
    cosine, sine_part = tables(pos_both.reshape(2 * ROW), HEAD_DIM)
    shared = (
        jnp.concatenate([cosine, cosine], axis=1),
        jnp.concatenate([-sine_part, sine_part], axis=1),
        gain_query[None],
        gain_key[None],
        deal_both[:, :, None],
        (deal_both - pos_both)[:, :, None],
        deal_both[:, None, :],
    )
    mixed_low = attend(projected, shared, per_group)
    out_found = quad_parts(out_slabs)
    mixed_low, *out_found = tie(mixed_low, *out_found)
    out_own = quad_order(out_found).reshape(NEAR * 2, far_part, out_rows, D)
    out_own = out_own.transpose(1, 0, 2, 3).reshape(far_part * NEAR, 2 * out_rows, D)
    out_mine = jnp.stack(pair_order(out_own, swap(out_own, CORE_AXIS), CORE_AXIS), axis=1).reshape(
        qcols, D
    )

    out_partial = mm(mixed_low, out_mine).astype(BF)
    out_partial, cot_back[0] = tie(out_partial, cot_back[0])
    residual = x_rows + sum_parts(quad_parts(out_partial.reshape(4, TOK_DEV, D)))

    normed_two, ffn_back = jax.vjp(rms_norm, residual, gain_ffn)
    ffn_in = normed_two.astype(BF)
    logits = mm(ffn_in, router_full)
    logits = jnp.where(chosen > 0.5, logits, -1e30)
    gate_probs = jax.nn.softmax(logits, axis=-1)
    gate_probs = jnp.where(chosen > 0.5, gate_probs, 0.0)

    expert_weight = w_expert[0]
    expert_here = far_index * slab + slab_index
    in_rows, gate_grads, up_grads, grad_rows, actives, in_grads = ([] for _ in range(6))
    gated_outs = [None] * far_count
    here = jnp.stack([expert_here, far_index * 2 * SLAB + slab_index])
    back_width = D + -(-far_count * 2 * SLAB // LANES) * LANES
    far_rows = [ffn_in]
    for step in range(1, far_count):
        with jax.named_scope('rows_far%d' % step):
            far_rows.append(far_shift(far_rows[-1], 1, far_count))

    def gather(step, source):
        return mm(send_slots[step], source).astype(BF)

    sent = gather(0, ffn_in)

    def send_back(step):
        return slab_return(in_grads[step].reshape(NEAR, CORES, 2, capacity, back_width))

    def combine(step, found):
        back = jnp.concatenate(found, axis=0).reshape(slab * capacity, back_width)
        return mm_tn(send_slots[step], back).astype(BF if step else F32)

    ffn_in, cot_back[1] = tie(ffn_in, cot_back[1])
    cot_chunks = far_parts(
        jnp.concatenate(cot_back, axis=2).reshape(far_count, slab * capacity, D), far_count
    )
    pending, parts = {}, [None] * far_count
    for turn in range(far_count):
        with jax.named_scope("rows_out%d" % turn):
            got = slab_send(to_blocks(sent))
        if turn + 1 < far_count:
            source = far_rows[turn + 1]
            if turn > 0:
                source, up_grads[turn - 1] = tie(source, up_grads[turn - 1])
            sent = gather(turn + 1, source)
        if turn > 0:
            gate_grads[turn - 1], *got = tie(gate_grads[turn - 1], *got)
        with jax.named_scope("rows_core%d" % turn):
            in_chunk = slab_take(got).reshape(slab * capacity, D)
        gate_grad, up_grad, active, grad_chunk, in_grad, gated_out = expert_chunk(
            here, in_chunk, cot_chunks[turn], mask_back[turn], router_full, expert_weight, back_width
        )
        in_rows.append(in_chunk)
        gate_grads.append(gate_grad)
        up_grads.append(up_grad)
        actives.append(active)
        grad_rows.append(grad_chunk)
        in_grads.append(in_grad)
        gated_outs[turn] = gated_out.reshape(slab, capacity, D)
        if 0 < turn < far_count - 1:
            with jax.named_scope("rows_back%d" % turn):
                pending[turn] = send_back(turn)
    up_grads[-1], *pending[1] = tie(up_grads[-1], *pending[1])
    for turn in range(1, far_count - 1):
        parts[turn] = combine(turn, pending[turn])
        if turn + 1 in pending:
            parts[turn], *pending[turn + 1] = tie(parts[turn], *pending[turn + 1])
    last = far_count - 1
    with jax.named_scope("rows_back%d" % last):
        parts[last] = combine(last, send_back(last))
    parts[max(last - 1, 0)], in_grads[0] = tie(parts[max(last - 1, 0)], in_grads[0])
    with jax.named_scope("partial_far"):
        part_found = far_begin(parts, far_count)
    with jax.named_scope("rows_back0"):
        parts[0] = combine(0, send_back(0))
    with jax.named_scope("partial_far"):
        total = far_end(parts, part_found, far_count)
    from_experts = total[:, :D]

    lanes = jnp.arange(back_width - D, dtype=jnp.int32)
    lanes = lanes // (2 * SLAB) * SLAB + lanes % SLAB
    spread = (lanes[:, None] == expert_ids[None, :]).astype(BF)
    gate_grad = mm(total[:, D:].astype(BF), spread)
    mean_term = jnp.sum(gate_probs * gate_grad, axis=1, keepdims=True)
    logit_grad = (gate_probs * (gate_grad - mean_term)).astype(BF)
    ffn_in_grad = from_experts + mm_nt(logit_grad, router_full)
    resid_part, gain_ffn_grad = ffn_back(ffn_in_grad)
    resid_low = (cot_rows + resid_part).astype(BF)

    in_rows[0], resid_low = tie(in_rows[0], resid_low)
    grad_expert = expert_grads(in_rows, grad_rows, gate_grads, up_grads, actives)[None]

    resid_both, grad_expert = tie(quad_gather(resid_low), grad_expert)
    resid_both = resid_both.reshape(2 * ROW, D)

    def core_sum(values):
        own, other = pair_order(values[:, 0], values[:, 1], CORE_AXIS)
        return own.astype(F32) + swap(other, CORE_AXIS).astype(F32)

    out_grad = mm_tn(mixed_low, resid_both).astype(BF)
    resid_both, out_grad = tie(resid_both, out_grad)
    mixed_grad = mm_nt(resid_both, out_mine).astype(BF)
    out_grad = core_sum(out_grad.reshape(far_part * NEAR, CORES, 2 * out_rows, D)).astype(BF)
    mixed_grad, out_grad = tie(mixed_grad, out_grad)
    out_grad = (
        out_grad
        .reshape(far_part, NEAR * 2, out_rows, D)
        .transpose(1, 0, 2, 3)
        .reshape(NEAR * 2, far_part * out_rows, D)
    )
    out_quad = quad_parts(out_grad)
    query_grad, key_grad, value_grad, query_gain_grad, key_gain_grad = attend_back(
        projected, shared, mixed_grad, per_group
    )
    query_grad, *out_quad = tie(query_grad, *out_quad)
    if far_part == 1:
        out_sent = []
        for step in range(far_count):
            at = lax.bitwise_xor(lax.rem(far_index + far_count - step, far_count), quad_index())
            low = jnp.where(at == 0, out_quad[0], out_quad[1])
            high = jnp.where(at == 2, out_quad[2], out_quad[3])
            out_sent.append(jnp.where(at < 2, low, high))
    else:
        out_sent = far_parts(quad_order(out_quad).reshape(far_count, out_rows, D), far_count)
    out_found = far_begin(out_sent, far_count)
    gated, query_grad = tie(jnp.stack(gated_outs, axis=1), query_grad)
    gated = exchange(gated, SLAB_AXES)
    out_parts = [
        mm_tn(hot, gated[:, step].reshape(slab * capacity, D)).astype(BF if step else F32)
        for step, hot in enumerate(chunk_slots)
    ]
    out_sum = far_end(out_parts, far_begin(out_parts, far_count), far_count)
    proj_grad = jnp.concatenate([query_grad, key_grad, value_grad], axis=1)

    back_grad = lax.dot_general(
        dealt_hot,
        proj_grad.reshape(2, ROW, width),
        (((1,), (1,)), ((0,), (0,))),
        preferred_element_type=F32,
    ).astype(BF).reshape(2 * ROW, width)
    qkv_grad = mm_tn(normed_low, proj_grad).astype(BF)
    back_grad, qkv_grad = tie(back_grad, qkv_grad)
    normed_partial = mm_nt(back_grad, qkv_mine).astype(BF)
    qkv_grad = core_sum(qkv_grad.reshape(far_count * NEAR, CORES, half_rows, width)).astype(BF)
    normed_partial, qkv_grad, *out_found = tie(normed_partial, qkv_grad, *out_found)
    qkv_parts = far_parts(qkv_grad.reshape(far_count, core_rows, width), far_count)
    qkv_found = far_begin(qkv_parts, far_count)
    out_share = far_end(out_sent, out_found, far_count)
    qkv_grad = far_end(qkv_parts, qkv_found, far_count)
    normed_found = quad_parts(normed_partial.reshape(4, TOK_DEV, D))
    qkv_grad, *normed_found = tie(qkv_grad, *normed_found)
    normed_grad, logit_late = tie(sum_parts(normed_found), logit_grad)
    router_grad = mm_tn(ffn_in, logit_late)
    normed_grad, out_sum = tie(normed_grad, out_sum)
    final_rows = (residual + out_sum).astype(BF)
    final_pair = jnp.concatenate(
        pair_order(final_rows, swap(final_rows, SEQ_AXIS), SEQ_AXIS), axis=0
    )
    layer_out = mm_tn(back_half, final_pair).astype(BF)
    _, attn_back = jax.vjp(rms_norm, tokens.astype(F32), gain_attn)
    input_part, gain_attn_grad = attn_back(normed_grad)
    resid_group = lax.dynamic_slice_in_dim(resid_both, near_index * ROW, ROW, axis=0)
    grad_tokens = (mm_tn(back_half, resid_group) + input_part).astype(BF)

    qkv_grad = quad_swap(qkv_grad.astype(BF).reshape(KV_HEADS, qkv_rows, width))
    qkv_grad = qkv_grad.transpose(1, 0, 2).astype(F32)
    qkv_share = jnp.concatenate(
        [
            qkv_grad[:, :, :qcols].reshape(qkv_rows, QDIM),
            qkv_grad[:, :, qcols : qcols + HEAD_DIM].reshape(qkv_rows, KVDIM),
            qkv_grad[:, :, qcols + HEAD_DIM :].reshape(qkv_rows, KVDIM),
        ],
        axis=1,
    )

    gains_grad = jnp.concatenate(
        [gain_attn_grad, gain_ffn_grad, query_gain_grad[0], key_gain_grad[0]]
    )
    share_rows = -(-small_size // (8 * LANES)) * 8
    small_grad = jnp.concatenate(
        [router_grad.reshape(device_count, router_size), gains_grad.reshape(device_count, gain_rows)],
        axis=1,
    )
    small_grad = jnp.pad(small_grad, ((0, 0), (0, share_rows * LANES - small_size)))
    small_share = jnp.sum(
        exchange(small_grad.reshape(device_count, share_rows, LANES), ALL_AXES), axis=0
    ).reshape(share_rows * LANES)
    router_share = small_share[:router_size].reshape(qkv_rows, experts_all)
    gains_share = small_share[router_size:small_size]
    return (layer_out, grad_tokens, qkv_share, out_share, router_share, gains_share, grad_expert)


def solution(mesh):
    shape = dict(mesh.shape)
    inner = Mesh(
        mesh.devices.reshape(shape["dp"] // (NEAR * CORES), NEAR, CORES, shape["seq"]), ALL_AXES
    )
    rows = P(ALL_AXES, None)
    in_specs = (
        rows,
        rows,
        rows,
        rows,
        rows,
        P(ALL_AXES),
        P(ALL_AXES, None, None),
        P(DP_AXES, None),
        P(DP_AXES, None),
        P(DP_AXES, None, None),
    )
    out_specs = (rows, rows, rows, rows, rows, P(ALL_AXES), P(ALL_AXES, None, None))
    return jax.shard_map(shards, mesh=inner, in_specs=in_specs, out_specs=out_specs, check_vma=False)
```

```python
import functools

import jax
import jax.numpy as jnp
from jax import lax
from jax.experimental import pallas as pl
from jax.experimental.pallas import tpu as pltpu
from jax.sharding import Mesh
from jax.sharding import PartitionSpec as P

D = 2048
HEADS = 32
KV_HEADS = 4
HEAD_DIM = 128
FF = 768
TOPK = 8
NSEG = 4
TOK_DEV = 128
ROW = 256
QDIM = 4096
KVDIM = 512
NEAR = 2
CORES = 2
SLAB = NEAR * CORES * 2
COT_CUT = 1152
HEADS_STEP = 4
LANES = 128

EPS = 1e-06
THETA = 1000000.0
BF = jnp.bfloat16
F32 = jnp.float32

FAR_AXIS = "far"
NEAR_AXIS = "near"
CORE_AXIS = "core"
SEQ_AXIS = "seq"
SLAB_AXES = (NEAR_AXIS, CORE_AXIS, SEQ_AXIS)
HEAD_AXES = (NEAR_AXIS, SEQ_AXIS)
ALL_AXES = (FAR_AXIS, NEAR_AXIS, CORE_AXIS, SEQ_AXIS)
DP_AXES = (FAR_AXIS, NEAR_AXIS, CORE_AXIS)


def rms_norm(values, scales):
    return values * lax.rsqrt(jnp.mean(values * values, axis=-1, keepdims=True) + EPS) * scales


def rotary(values, cosine, sine_part):
    half_width = values.shape[-1] // 2
    front_part = values[..., :half_width]
    back_part = values[..., half_width:]
    cos_wide = cosine[..., None, :]
    sin_wide = sine_part[..., None, :]
    return jnp.concatenate(
        [
            front_part * cos_wide - back_part * sin_wide,
            back_part * cos_wide + front_part * sin_wide,
        ],
        axis=-1,
    )


def tables(positions, head_width):
    half_width = head_width // 2
    inverse = THETA ** (-(jnp.arange(half_width, dtype=F32) * 2.0 / head_width))
    angles = positions.astype(F32)[..., None] * inverse
    return (jnp.cos(angles), jnp.sin(angles))


def dot(left, right, dims):
    return lax.dot_general(left, right, (dims, ((), ())), preferred_element_type=F32)


def mm(left, right):
    return dot(left, right, ((1,), (0,)))


def mm_nt(left, right):
    return dot(left, right, ((1,), (1,)))


def mm_tn(left, right):
    return dot(left, right, ((0,), (0,)))


def swap(value, axis):
    return lax.ppermute(value, axis, [(0, 1), (1, 0)])


def pair_order(own, other, axis):
    first = lax.axis_index(axis) == 0
    return (jnp.where(first, own, other), jnp.where(first, other, own))


def exchange(value, axes):
    return lax.all_to_all(value, axes, split_axis=0, concat_axis=0, tiled=True)


def quad_index():
    return lax.axis_index(NEAR_AXIS) * 2 + lax.axis_index(SEQ_AXIS)


def quad_send(parts, step):
    block = lax.dynamic_index_in_dim(parts, lax.bitwise_xor(quad_index(), step), 0, keepdims=False)
    return lax.ppermute(block, HEAD_AXES, [(i, i ^ step) for i in range(4)])


def quad_order(found):
    low = pair_order(found[0], found[1], SEQ_AXIS)
    high = pair_order(found[2], found[3], SEQ_AXIS)
    rows = [pair_order(low[k], high[k], NEAR_AXIS) for k in range(2)]
    return jnp.stack([rows[0][0], rows[1][0], rows[0][1], rows[1][1]])


def quad_gather(value):
    found = [value] + [
        lax.ppermute(value, HEAD_AXES, [(i, i ^ step) for i in range(4)]) for step in range(1, 4)
    ]
    return quad_order(found)


def quad_parts(parts):
    own = lax.dynamic_index_in_dim(parts, quad_index(), 0, keepdims=False)
    return [own] + [quad_send(parts, step) for step in range(1, 4)]


def quad_swap(parts):
    return quad_order(quad_parts(parts))


def sum_parts(parts):
    total = parts[0].astype(F32)
    for part in parts[1:]:
        total = total + part.astype(F32)
    return total


def far_begin(parts, count):
    if count != 4:
        return [far_shift(parts[step].astype(BF), -step, count) for step in range(1, count)]
    return [far_shift(parts[2].astype(BF), -1, count), far_shift(parts[3].astype(BF), 1, count)]


def far_end(parts, found, count):
    total = parts[0].astype(F32)
    if count != 4:
        for part in found:
            total = total + part.astype(F32)
        return total
    relay = (parts[1].astype(F32) + found[0].astype(F32)).astype(BF)
    return total + found[1].astype(F32) + far_shift(relay, -1, count).astype(F32)


def far_parts(values, count):
    here = lax.axis_index(FAR_AXIS)
    return [
        lax.dynamic_index_in_dim(values, lax.rem(here + count - step, count), 0, keepdims=False)
        for step in range(count)
    ]


def far_all(value, count, first=None):
    ahead = count // 2
    found = [value] + [None] * (count - 1)
    found[1] = far_shift(value, 1, count)
    if count > 2:
        found[count - 1] = far_shift(value, -1, count)
    for step in range(2, ahead + 1):
        found[step] = far_shift(found[step - 1], 1, count)
    for step in range(count - 2, ahead, -1):
        found[step] = far_shift(found[step + 1], -1, count)
    return found


def far_stack(found):
    count = len(found)
    here = lax.axis_index(FAR_AXIS)
    zeros = (0,) * found[0].ndim
    full = jnp.zeros((count,) + found[0].shape, found[0].dtype)
    for step, chunk in enumerate(found):
        full = lax.dynamic_update_slice(full, chunk[None], (lax.rem(here + count - step, count),) + zeros)
    return full


def tie(*values):
    return lax.optimization_barrier(values)


def far_shift(value, step, count):
    return lax.ppermute(value, FAR_AXIS, [(i, (i + step) % count) for i in range(count)])


def far_next(value, count):
    return lax.ppermute(value, FAR_AXIS, [(i, (i + 1) % count) for i in range(count)])


def quad_xor(value, step):
    return lax.ppermute(value, HEAD_AXES, [(i, i ^ step) for i in range(4)])


def slab_send(blocks):
    return [blocks[0]] + [quad_xor(blocks[step], step) for step in range(1, 4)]


def slab_take(got):
    keep = quad_order([part[0] for part in got])
    other = swap(quad_order([part[1] for part in got]), CORE_AXIS)
    first, second = pair_order(keep, other, CORE_AXIS)
    shape = (NEAR, 2) + keep.shape[1:]
    return jnp.stack([first.reshape(shape), second.reshape(shape)], axis=1)


def slab_return(rows):
    keep, give = pair_order(rows[:, 0], rows[:, 1], CORE_AXIS)
    both = jnp.stack([keep, swap(give, CORE_AXIS)], axis=2)
    return quad_parts(both.reshape((4, 2) + rows.shape[3:]))


def expert_kernel(
    here_ref, in_ref, cot_ref, mask_ref, router_ref, gate_ref, up_ref, down_ref,
    gate_grad_ref, up_grad_ref, active_ref, grad_ref, in_grad_ref, gated_ref,
    out_total, in_total, gate_slot,
):
    block = pl.program_id(0)

    @pl.when(block == 0)
    def _():
        chosen = mask_ref[...].astype(F32) > 0.5
        logits = jnp.where(chosen, mm(in_ref[...], router_ref[...]), -1e30)
        exped = jnp.where(chosen, jnp.exp(logits - jnp.max(logits, axis=-1, keepdims=True)), 0.0)
        total = jnp.sum(exped, axis=-1, keepdims=True)
        mine = lax.broadcasted_iota(jnp.int32, exped.shape, 1) == here_ref[0]
        picked = jnp.sum(jnp.where(mine, exped, 0.0), axis=-1, keepdims=True)
        gate = picked / jnp.where(total > 0.0, total, 1.0)
        gate_slot[...] = jnp.broadcast_to(gate, gate_slot.shape)
        grad_ref[...] = (gate * cot_ref[...].astype(F32)).astype(BF)
        out_total[...] = jnp.zeros_like(out_total)
        in_total[...] = jnp.zeros_like(in_total)

    gate_pre = mm(in_ref[...], gate_ref[...])
    up_pre = mm(in_ref[...], up_ref[...])
    act_grad = mm(grad_ref[...], down_ref[...])
    sig_gate = jax.nn.sigmoid(gate_pre)
    silu_val = gate_pre * sig_gate
    active = (silu_val * up_pre).astype(BF)
    silu_slope = sig_gate * (1.0 + gate_pre * (1.0 - sig_gate))
    gate_grad = (act_grad * up_pre * silu_slope).astype(BF)
    up_grad = (act_grad * silu_val).astype(BF)
    active_ref[...] = active
    gate_grad_ref[...] = gate_grad
    up_grad_ref[...] = up_grad
    out_total[...] += mm_nt(active, down_ref[...])
    in_total[...] += mm_nt(gate_grad, gate_ref[...]) + mm_nt(up_grad, up_ref[...])

    @pl.when(block == pl.num_programs(0) - 1)
    def _():
        out = out_total[...].astype(BF).astype(F32)
        gated_ref[...] = (gate_slot[:, :1] * out).astype(BF)
        in_grad_ref[:, :D] = in_total[...].astype(BF)
        found = jnp.sum(cot_ref[...].astype(F32) * out, axis=-1, keepdims=True)
        high = found.astype(BF).astype(F32)
        lane = lax.broadcasted_iota(jnp.int32, (in_grad_ref.shape[0], in_grad_ref.shape[1] - D), 1)
        lane = lane - here_ref[1]
        parts = jnp.where(lane == 0, high, jnp.where(lane == SLAB, found - high, 0.0))
        in_grad_ref[:, D:] = parts.astype(BF)


def expert_chunk(here, in_chunk, cot_chunk, mask, router, weight, back_width):
    rows = in_chunk.shape[0]
    tile = 256
    steps = FF // tile
    whole = pl.BlockSpec((rows, D), lambda j, h: (0, 0))
    piece = pl.BlockSpec((rows, tile), lambda j, h: (0, j))
    low = jax.ShapeDtypeStruct((rows, FF), BF)
    wide = jax.ShapeDtypeStruct((rows, D), BF)
    return pl.pallas_call(
        expert_kernel,
        grid_spec=pltpu.PrefetchScalarGridSpec(
            num_scalar_prefetch=1,
            grid=(steps,),
            in_specs=[
                whole,
                whole,
                pl.BlockSpec(mask.shape, lambda j, h: (0, 0)),
                pl.BlockSpec(router.shape, lambda j, h: (0, 0)),
                pl.BlockSpec((D, tile), lambda j, h: (0, j)),
                pl.BlockSpec((D, tile), lambda j, h: (0, steps + j)),
                pl.BlockSpec((D, tile), lambda j, h: (0, 2 * steps + j)),
            ],
            out_specs=[
                piece, piece, piece, whole,
                pl.BlockSpec((rows, back_width), lambda j, h: (0, 0)),
                whole,
            ],
            scratch_shapes=[
                pltpu.VMEM((rows, D), F32),
                pltpu.VMEM((rows, D), F32),
                pltpu.VMEM((rows, LANES), F32),
            ],
        ),
        out_shape=[low, low, low, wide, jax.ShapeDtypeStruct((rows, back_width), BF), wide],
        compiler_params=pltpu.CompilerParams(vmem_limit_bytes=40 << 20),
        cost_estimate=pl.CostEstimate(flops=1 << 20, bytes_accessed=1 << 20, transcendentals=0),
        name="expert_chunk",
    )(here, in_chunk, cot_chunk, mask, router, weight, weight, weight)


def expert_grad_kernel(count, *refs):
    lists = [refs[k * count : (k + 1) * count] for k in range(5)]
    out_ref = refs[5 * count]
    column = pl.program_id(1)

    def total(lefts, rights):
        found = mm_tn(lefts[0][...], rights[0][...])
        for left, right in zip(lefts[1:], rights[1:]):
            found = found + mm_tn(left[...], right[...])
        out_ref[...] = found

    for place, (left, right) in enumerate(((0, 2), (0, 3), (1, 4))):
        pl.when(column == place)(functools.partial(total, lists[left], lists[right]))


def expert_grads(in_rows, grad_rows, gate_grads, up_grads, actives):
    count = len(in_rows)
    rows = in_rows[0].shape[0]
    tile = 512
    tall = pl.BlockSpec((rows, tile), lambda i, j: (0, i))
    whole = pl.BlockSpec((rows, FF), lambda i, j: (0, 0))
    return pl.pallas_call(
        functools.partial(expert_grad_kernel, count),
        grid=(D // tile, 3),
        in_specs=[tall] * (2 * count) + [whole] * (3 * count),
        out_specs=pl.BlockSpec((tile, FF), lambda i, j: (i, j)),
        out_shape=jax.ShapeDtypeStruct((D, 3 * FF), F32),
        compiler_params=pltpu.CompilerParams(vmem_limit_bytes=48 << 20),
        cost_estimate=pl.CostEstimate(flops=1 << 20, bytes_accessed=1 << 20, transcendentals=0),
        name="expert_grads",
    )(*in_rows, *grad_rows, *gate_grads, *up_grads, *actives)


def head_normed(raw, gain_ref):
    scale = lax.rsqrt(jnp.mean(raw * raw, axis=-1, keepdims=True) + EPS)
    normal = raw * scale
    return (normal, scale, normal * gain_ref[...])


def turned(values, cos_ref, sin_ref):
    return values * cos_ref[...] + pltpu.roll(values, HEAD_DIM // 2, 1) * sin_ref[...]


def turned_back(values, cos_ref, sin_ref):
    return values * cos_ref[...] + pltpu.roll(values * sin_ref[...], HEAD_DIM // 2, 1)


def head_probs(query, key, row_ref, start_ref, key_row_ref):
    scores = mm_nt(query, key) * HEAD_DIM ** (-0.5)
    allowed = (key_row_ref[0] <= row_ref[0]) & (key_row_ref[0] >= start_ref[0])
    scores = jnp.where(allowed, scores, -1e30)
    exped = jnp.exp(scores - jnp.max(scores, axis=-1, keepdims=True))
    return exped * (1.0 / jnp.sum(exped, axis=-1, keepdims=True))


def attend_kernel(
    query_ref, key_ref, value_ref, cos_ref, sin_ref, qgain_ref, kgain_ref,
    row_ref, start_ref, key_row_ref, mixed_ref, key_low, value_low,
):
    @pl.when(pl.program_id(1) == 0)
    def _():
        key_low[...] = turned(head_normed(key_ref[...], kgain_ref)[2], cos_ref, sin_ref).astype(BF)
        value_low[...] = value_ref[...].astype(BF)

    for part in range(HEADS_STEP):
        lanes = pl.ds(part * HEAD_DIM, HEAD_DIM)
        query = turned(head_normed(query_ref[:, lanes], qgain_ref)[2], cos_ref, sin_ref).astype(BF)
        probs = head_probs(query, key_low[...], row_ref, start_ref, key_row_ref)
        mixed_ref[:, lanes] = mm(probs.astype(BF), value_low[...]).astype(BF)


def attend_back_kernel(
    query_ref, key_ref, value_ref, cos_ref, sin_ref, qgain_ref, kgain_ref,
    row_ref, start_ref, key_row_ref, grad_ref,
    query_out, key_out, value_out, qgain_out, kgain_out,
    key_low, value_low, key_total, value_total,
):
    group, head = pl.program_id(0), pl.program_id(1)
    score_scale = HEAD_DIM ** (-0.5)

    @pl.when((group == 0) & (head == 0))
    def _():
        qgain_out[...] = jnp.zeros_like(qgain_out)
        kgain_out[...] = jnp.zeros_like(kgain_out)

    @pl.when(head == 0)
    def _():
        key_low[...] = turned(head_normed(key_ref[...], kgain_ref)[2], cos_ref, sin_ref).astype(BF)
        value_low[...] = value_ref[...].astype(BF)
        key_total[...] = jnp.zeros_like(key_total)
        value_total[...] = jnp.zeros_like(value_total)

    def raw_grad(grad, normal, scale, gain_ref, gain_out):
        grad = turned_back(grad, cos_ref, sin_ref)
        gain_out[...] += jnp.sum(grad * normal, axis=0, keepdims=True)
        grad = grad * gain_ref[...]
        return scale * (grad - normal * jnp.mean(normal * grad, axis=-1, keepdims=True))

    for part in range(HEADS_STEP):
        lanes = pl.ds(part * HEAD_DIM, HEAD_DIM)
        normal, scale, gained = head_normed(query_ref[:, lanes], qgain_ref)
        query = turned(gained, cos_ref, sin_ref).astype(BF)
        probs = head_probs(query, key_low[...], row_ref, start_ref, key_row_ref)
        grad = grad_ref[:, lanes]
        value_total[...] += mm_tn(probs.astype(BF), grad)
        prob_grad = mm_nt(grad, value_low[...])
        score_grad = (
            probs * (prob_grad - jnp.sum(probs * prob_grad, axis=-1, keepdims=True))
        ).astype(BF)
        key_total[...] += mm_tn(score_grad, query)
        query_grad = mm(score_grad, key_low[...]) * score_scale
        query_out[:, lanes] = raw_grad(query_grad, normal, scale, qgain_ref, qgain_out).astype(BF)

    @pl.when(head == pl.num_programs(1) - 1)
    def _():
        key_normal, key_scale, _ = head_normed(key_ref[...], kgain_ref)
        key_out[...] = raw_grad(key_total[...] * score_scale, key_normal, key_scale, kgain_ref, kgain_out).astype(BF)
        value_out[...] = value_total[...].astype(BF)


def attend_specs(heads):
    head = pl.BlockSpec((ROW, HEADS_STEP * HEAD_DIM), lambda b, h: (b, h))
    whole = pl.BlockSpec((ROW, HEAD_DIM), lambda b, h: (b, 0))
    gain = pl.BlockSpec((1, HEAD_DIM), lambda b, h: (0, 0))
    column = pl.BlockSpec((1, ROW, 1), lambda b, h: (b, 0, 0))
    specs = [
        head,
        pl.BlockSpec((ROW, HEAD_DIM), lambda b, h: (b, heads)),
        pl.BlockSpec((ROW, HEAD_DIM), lambda b, h: (b, heads + 1)),
        whole, whole, gain, gain, column, column,
        pl.BlockSpec((1, 1, ROW), lambda b, h: (b, 0, 0)),
    ]
    return (specs, head, whole, gain)


def attend(projected, shared, heads):
    specs, head, _, _ = attend_specs(heads)
    rows = projected.shape[0]
    return pl.pallas_call(
        attend_kernel,
        grid=(rows // ROW, heads // HEADS_STEP),
        in_specs=specs,
        out_specs=head,
        out_shape=jax.ShapeDtypeStruct((rows, heads * HEAD_DIM), BF),
        scratch_shapes=[pltpu.VMEM((ROW, HEAD_DIM), BF)] * 2,
        cost_estimate=pl.CostEstimate(flops=1 << 20, bytes_accessed=1 << 20, transcendentals=0),
        name="attend",
    )(projected, projected, projected, *shared)


def attend_back(projected, shared, grad, heads):
    specs, head, whole, gain = attend_specs(heads)
    rows = projected.shape[0]
    return pl.pallas_call(
        attend_back_kernel,
        grid=(rows // ROW, heads // HEADS_STEP),
        in_specs=specs + [head],
        out_specs=[head, whole, whole, gain, gain],
        out_shape=[
            jax.ShapeDtypeStruct((rows, heads * HEAD_DIM), BF),
            jax.ShapeDtypeStruct((rows, HEAD_DIM), BF),
            jax.ShapeDtypeStruct((rows, HEAD_DIM), BF),
            jax.ShapeDtypeStruct((1, HEAD_DIM), F32),
            jax.ShapeDtypeStruct((1, HEAD_DIM), F32),
        ],
        scratch_shapes=[pltpu.VMEM((ROW, HEAD_DIM), BF)] * 2 + [pltpu.VMEM((ROW, HEAD_DIM), F32)] * 2,
        cost_estimate=pl.CostEstimate(flops=1 << 20, bytes_accessed=1 << 20, transcendentals=0),
        name="attend_back",
    )(projected, projected, projected, *shared, grad)


def shards(tokens, cotangent, w_qkv, w_out, w_router, norm_gains, w_expert, lengths, deal, routes):
    far_count = lax.axis_size(FAR_AXIS)
    device_count = far_count * NEAR * CORES * 2
    experts_all = w_router.shape[1]
    capacity = TOK_DEV * TOPK // experts_all
    slot_count = experts_all * capacity
    seq_index = lax.axis_index(SEQ_AXIS)
    near_index = lax.axis_index(NEAR_AXIS)
    far_index = lax.axis_index(FAR_AXIS)
    core_index = lax.axis_index(CORE_AXIS)
    per_group = HEADS // KV_HEADS
    qcols = per_group * HEAD_DIM
    width = qcols + 2 * HEAD_DIM
    qkv_rows = w_qkv.shape[0]
    out_rows = w_out.shape[0]
    gain_rows = norm_gains.shape[0]
    score_scale = HEAD_DIM ** (-0.5)

    wide = jnp.concatenate(
        [
            w_qkv[:, :QDIM].reshape(qkv_rows, KV_HEADS, qcols),
            w_qkv[:, QDIM : QDIM + KVDIM].reshape(qkv_rows, KV_HEADS, HEAD_DIM),
            w_qkv[:, QDIM + KVDIM :].reshape(qkv_rows, KV_HEADS, HEAD_DIM),
        ],
        axis=2,
    ).transpose(1, 0, 2)
    core_rows = KV_HEADS * qkv_rows
    half_rows = 2 * qkv_rows
    wide_found = quad_parts(wide)
    tokens, *wide_found = tie(tokens, *wide_found)
    qkv_far = far_all(quad_order(wide_found).reshape(core_rows, width), far_count)

    tokens_both = quad_gather(tokens).reshape(2, ROW, D)
    table = jnp.concatenate([deal, jnp.pad(lengths, ((0, 0), (0, LANES - NSEG)))], axis=1)
    table_both = jnp.concatenate(pair_order(table, swap(table, NEAR_AXIS), NEAR_AXIS), axis=0)
    deal_both = table_both[:, :ROW]
    ends = jnp.cumsum(table_both[:, ROW : ROW + NSEG], axis=1)
    starts = ends - table_both[:, ROW : ROW + NSEG]
    seg_both = jnp.sum((deal_both[:, :, None] >= ends[:, None, :]).astype(jnp.int32), axis=2)
    picked = seg_both[:, :, None] == jnp.arange(NSEG, dtype=jnp.int32)[None, None, :]
    pos_both = deal_both - jnp.sum(jnp.where(picked, starts[:, None, :], 0), axis=2)
    dealt_hot = (deal_both[:, :, None] == jnp.arange(ROW, dtype=jnp.int32)[None, None, :]).astype(BF)
    hot_mine = lax.dynamic_index_in_dim(dealt_hot, near_index, 0, keepdims=False)
    hot_half = lax.dynamic_slice_in_dim(hot_mine, seq_index * TOK_DEV, TOK_DEV, axis=0)
    back_half = lax.dynamic_slice_in_dim(hot_mine, seq_index * TOK_DEV, TOK_DEV, axis=1)
    seg_mine = lax.dynamic_slice_in_dim(
        lax.dynamic_index_in_dim(seg_both, near_index, 0, keepdims=False), seq_index * TOK_DEV, TOK_DEV
    )

    expert_ids = jnp.arange(experts_all, dtype=jnp.int32)
    chosen_rows = jnp.sum(
        (routes[0][:, :, None] == expert_ids[None, None, :]).astype(jnp.int32), axis=1
    ).astype(BF)
    chosen = mm(hot_half, chosen_rows)
    live = jnp.where((seg_mine != NSEG - 1)[:, None], chosen, 0.0)
    steps = jnp.arange(TOK_DEV, dtype=jnp.int32)
    earlier = (steps[None, :] < steps[:, None]).astype(BF)
    place = mm(earlier, live.astype(BF))
    place = jnp.where(live > 0.5, place, -1.0).astype(jnp.int32)
    slot_hot = place.T[:, None, :] == jnp.arange(capacity, dtype=jnp.int32)[None, :, None]
    slot_low = slot_hot.astype(BF).reshape(slot_count, TOK_DEV)

    slab = NEAR * CORES * 2
    slab_index = (near_index * CORES + core_index) * 2 + seq_index
    slab_ids = jnp.arange(slab, dtype=jnp.int32)
    out_order = jnp.array([0, 2, 1, 3, 4, 6, 5, 7], jnp.int32)
    place_far = far_stack(far_all(place.T.astype(BF), far_count))

    def slots_of(places, step):
        found = lax.dynamic_index_in_dim(
            places, lax.rem(far_index + far_count - step, far_count), 0, keepdims=False
        )
        found = found[:, None, :] == jnp.arange(capacity, dtype=jnp.int32)[None, :, None]
        return found.astype(BF).reshape(slab * capacity, TOK_DEV)

    place_slab = lax.dynamic_slice_in_dim(place_far, far_index * slab, slab, axis=1).astype(jnp.int32)
    turned_ids = lax.bitwise_xor(out_order, slab_index)
    place_turned = jnp.sum(
        jnp.where(
            (turned_ids[:, None] == slab_ids[None, :])[None, :, :, None], place_slab[:, None], 0
        ),
        axis=2,
    )
    chunk_slots = [slots_of(place_slab, step) for step in range(far_count)]
    send_slots = [slots_of(place_turned, step) for step in range(far_count)]
    chunk_steps = jnp.arange(far_count, dtype=jnp.int32)
    source_ids = (
        lax.rem(far_index + far_count - chunk_steps, far_count)[:, None] * slab + slab_ids[None, :]
    ).reshape(device_count)
    def to_blocks(rows):
        return rows.reshape(4, 2, rows.shape[0] // slab, rows.shape[1])


    router_size = qkv_rows * experts_all
    small_size = router_size + gain_rows
    mask_size = capacity * experts_all
    small_rows = -(-(small_size + mask_size) // (8 * LANES)) * 8
    small = jnp.broadcast_to(
        jnp.concatenate([w_router.reshape(router_size), norm_gains]), (device_count, small_size)
    )
    slot_mask = mm(slot_low, chosen.astype(BF)).astype(BF).reshape(device_count, mask_size)
    small = jnp.concatenate([slot_mask, small], axis=1)
    small = jnp.pad(small, ((0, 0), (0, small_rows * LANES - small_size - mask_size)))
    small_all = exchange(small.reshape(device_count, small_rows, LANES), ALL_AXES).reshape(
        device_count, small_rows * LANES
    )
    mask_back = jnp.take(small_all[:, :mask_size], source_ids, axis=0).reshape(
        far_count, slab * capacity, experts_all
    )
    small_all = small_all[:, mask_size : mask_size + small_size]
    router_full = small_all[:, :router_size].reshape(D, experts_all)
    gains_float = small_all[:, router_size:].reshape(-1).astype(F32)
    gain_attn = gains_float[:D]
    gain_ffn = gains_float[D : 2 * D]
    gain_query = gains_float[2 * D : 2 * D + HEAD_DIM]
    gain_key = gains_float[2 * D + HEAD_DIM :]

    cot_pair = jnp.concatenate(pair_order(cotangent, swap(cotangent, SEQ_AXIS), SEQ_AXIS), axis=0)
    cot_low = mm(hot_half, cot_pair).astype(BF)
    cot_rows = cot_low.astype(F32)
    cot_sent = [
        mm(slot_low, part).astype(BF).reshape(device_count, capacity, part.shape[1])
        for part in (cot_low[:, :COT_CUT], cot_low[:, COT_CUT:])
    ]
    qkv_own = far_stack(qkv_far).reshape(far_count * NEAR, half_rows, width)
    qkv_mine = jnp.stack(pair_order(qkv_own, swap(qkv_own, CORE_AXIS), CORE_AXIS), axis=1).reshape(
        D, width
    )

    out_slabs = far_stack(far_all(w_out, far_count)).reshape(
        KV_HEADS, far_count // KV_HEADS * out_rows, D
    )
    far_part = far_count // KV_HEADS
    x_both = lax.dot_general(
        dealt_hot, tokens_both, (((2,), (1,)), ((0,), (0,))), preferred_element_type=F32
    )
    x_rows = lax.dynamic_slice(
        x_both, (near_index, seq_index * TOK_DEV, 0), (1, TOK_DEV, D)
    )[0]
    normed_low = rms_norm(x_both.reshape(2 * ROW, D), gain_attn).astype(BF)
    projected, *cot_sent = tie(mm(normed_low, qkv_mine), *cot_sent)
    cot_back = [exchange(half, ALL_AXES) for half in cot_sent]
    cosine, sine_part = tables(pos_both.reshape(2 * ROW), HEAD_DIM)
    shared = (
        jnp.concatenate([cosine, cosine], axis=1),
        jnp.concatenate([-sine_part, sine_part], axis=1),
        gain_query[None],
        gain_key[None],
        deal_both[:, :, None],
        (deal_both - pos_both)[:, :, None],
        deal_both[:, None, :],
    )
    mixed_low = attend(projected, shared, per_group)
    out_found = quad_parts(out_slabs)
    mixed_low, *out_found = tie(mixed_low, *out_found)
    out_own = quad_order(out_found).reshape(NEAR * 2, far_part, out_rows, D)
    out_own = out_own.transpose(1, 0, 2, 3).reshape(far_part * NEAR, 2 * out_rows, D)
    out_mine = jnp.stack(pair_order(out_own, swap(out_own, CORE_AXIS), CORE_AXIS), axis=1).reshape(
        qcols, D
    )

    out_partial = mm(mixed_low, out_mine).astype(BF)
    out_partial, cot_back[0] = tie(out_partial, cot_back[0])
    residual = x_rows + sum_parts(quad_parts(out_partial.reshape(4, TOK_DEV, D)))

    normed_two, ffn_back = jax.vjp(rms_norm, residual, gain_ffn)
    ffn_in = normed_two.astype(BF)
    logits = mm(ffn_in, router_full)
    logits = jnp.where(chosen > 0.5, logits, -1e30)
    gate_probs = jax.nn.softmax(logits, axis=-1)
    gate_probs = jnp.where(chosen > 0.5, gate_probs, 0.0)

    expert_weight = w_expert[0]
    expert_here = far_index * slab + slab_index
    in_rows, gate_grads, up_grads, grad_rows, actives, in_grads = ([] for _ in range(6))
    gated_outs = [None] * far_count
    here = jnp.stack([expert_here, far_index * 2 * SLAB + slab_index])
    back_width = D + -(-far_count * 2 * SLAB // LANES) * LANES
    far_rows = [ffn_in]
    for step in range(1, far_count):
        with jax.named_scope('rows_far%d' % step):
            far_rows.append(far_shift(far_rows[-1], 1, far_count))

    def gather(step, source):
        return mm(send_slots[step], source).astype(BF)

    sent = gather(0, ffn_in)

    def send_back(step):
        return slab_return(in_grads[step].reshape(NEAR, CORES, 2, capacity, back_width))

    def combine(step, found):
        back = jnp.concatenate(found, axis=0).reshape(slab * capacity, back_width)
        return mm_tn(send_slots[step], back).astype(BF if step else F32)

    ffn_in, cot_back[1] = tie(ffn_in, cot_back[1])
    cot_chunks = far_parts(
        jnp.concatenate(cot_back, axis=2).reshape(far_count, slab * capacity, D), far_count
    )
    pending, parts = {}, [None] * far_count
    for turn in range(far_count):
        with jax.named_scope("rows_out%d" % turn):
            got = slab_send(to_blocks(sent))
        if turn + 1 < far_count:
            source = far_rows[turn + 1]
            if turn > 0:
                source, up_grads[turn - 1] = tie(source, up_grads[turn - 1])
            sent = gather(turn + 1, source)
        if turn > 0:
            gate_grads[turn - 1], *got = tie(gate_grads[turn - 1], *got)
        with jax.named_scope("rows_core%d" % turn):
            in_chunk = slab_take(got).reshape(slab * capacity, D)
        gate_grad, up_grad, active, grad_chunk, in_grad, gated_out = expert_chunk(
            here, in_chunk, cot_chunks[turn], mask_back[turn], router_full, expert_weight, back_width
        )
        in_rows.append(in_chunk)
        gate_grads.append(gate_grad)
        up_grads.append(up_grad)
        actives.append(active)
        grad_rows.append(grad_chunk)
        in_grads.append(in_grad)
        gated_outs[turn] = gated_out.reshape(slab, capacity, D)
        if 0 < turn < far_count - 1:
            with jax.named_scope("rows_back%d" % turn):
                pending[turn] = send_back(turn)
    up_grads[-1], *pending[1] = tie(up_grads[-1], *pending[1])
    for turn in range(1, far_count - 1):
        parts[turn] = combine(turn, pending[turn])
        if turn + 1 in pending:
            parts[turn], *pending[turn + 1] = tie(parts[turn], *pending[turn + 1])
    last = far_count - 1
    with jax.named_scope("rows_back%d" % last):
        parts[last] = combine(last, send_back(last))
    parts[max(last - 1, 0)], in_grads[0] = tie(parts[max(last - 1, 0)], in_grads[0])
    with jax.named_scope("partial_far"):
        part_found = far_begin(parts, far_count)
    with jax.named_scope("rows_back0"):
        parts[0] = combine(0, send_back(0))
    with jax.named_scope("partial_far"):
        total = far_end(parts, part_found, far_count)
    from_experts = total[:, :D]

    lanes = jnp.arange(back_width - D, dtype=jnp.int32)
    lanes = lanes // (2 * SLAB) * SLAB + lanes % SLAB
    spread = (lanes[:, None] == expert_ids[None, :]).astype(BF)
    gate_grad = mm(total[:, D:].astype(BF), spread)
    mean_term = jnp.sum(gate_probs * gate_grad, axis=1, keepdims=True)
    logit_grad = (gate_probs * (gate_grad - mean_term)).astype(BF)
    ffn_in_grad = from_experts + mm_nt(logit_grad, router_full)
    resid_part, gain_ffn_grad = ffn_back(ffn_in_grad)
    resid_low = (cot_rows + resid_part).astype(BF)

    in_rows[0], resid_low = tie(in_rows[0], resid_low)
    grad_expert = expert_grads(in_rows, grad_rows, gate_grads, up_grads, actives)[None]

    resid_both, grad_expert = tie(quad_gather(resid_low), grad_expert)
    resid_both = resid_both.reshape(2 * ROW, D)

    def core_sum(values):
        own, other = pair_order(values[:, 0], values[:, 1], CORE_AXIS)
        return own.astype(F32) + swap(other, CORE_AXIS).astype(F32)

    out_grad = mm_tn(mixed_low, resid_both).astype(BF)
    resid_both, out_grad = tie(resid_both, out_grad)
    mixed_grad = mm_nt(resid_both, out_mine).astype(BF)
    out_grad = core_sum(out_grad.reshape(far_part * NEAR, CORES, 2 * out_rows, D)).astype(BF)
    mixed_grad, out_grad = tie(mixed_grad, out_grad)
    out_grad = (
        out_grad
        .reshape(far_part, NEAR * 2, out_rows, D)
        .transpose(1, 0, 2, 3)
        .reshape(NEAR * 2, far_part * out_rows, D)
    )
    out_quad = quad_parts(out_grad)
    query_grad, key_grad, value_grad, query_gain_grad, key_gain_grad = attend_back(
        projected, shared, mixed_grad, per_group
    )
    query_grad, *out_quad = tie(query_grad, *out_quad)
    if far_part == 1:
        out_sent = []
        for step in range(far_count):
            at = lax.bitwise_xor(lax.rem(far_index + far_count - step, far_count), quad_index())
            low = jnp.where(at == 0, out_quad[0], out_quad[1])
            high = jnp.where(at == 2, out_quad[2], out_quad[3])
            out_sent.append(jnp.where(at < 2, low, high))
    else:
        out_sent = far_parts(quad_order(out_quad).reshape(far_count, out_rows, D), far_count)
    out_found = far_begin(out_sent, far_count)
    gated, query_grad = tie(jnp.stack(gated_outs, axis=1), query_grad)
    gated = exchange(gated, SLAB_AXES)
    out_parts = [
        mm_tn(hot, gated[:, step].reshape(slab * capacity, D)).astype(BF if step else F32)
        for step, hot in enumerate(chunk_slots)
    ]
    out_sum = far_end(out_parts, far_begin(out_parts, far_count), far_count)
    proj_grad = jnp.concatenate([query_grad, key_grad, value_grad], axis=1)

    back_grad = lax.dot_general(
        dealt_hot,
        proj_grad.reshape(2, ROW, width),
        (((1,), (1,)), ((0,), (0,))),
        preferred_element_type=F32,
    ).astype(BF).reshape(2 * ROW, width)
    qkv_grad = mm_tn(normed_low, proj_grad).astype(BF)
    back_grad, qkv_grad = tie(back_grad, qkv_grad)
    normed_partial = mm_nt(back_grad, qkv_mine).astype(BF)
    qkv_grad = core_sum(qkv_grad.reshape(far_count * NEAR, CORES, half_rows, width)).astype(BF)
    normed_partial, qkv_grad, *out_found = tie(normed_partial, qkv_grad, *out_found)
    qkv_parts = far_parts(qkv_grad.reshape(far_count, core_rows, width), far_count)
    qkv_found = far_begin(qkv_parts, far_count)
    out_share = far_end(out_sent, out_found, far_count)
    qkv_grad = far_end(qkv_parts, qkv_found, far_count)
    normed_found = quad_parts(normed_partial.reshape(4, TOK_DEV, D))
    qkv_grad, *normed_found = tie(qkv_grad, *normed_found)
    normed_grad, logit_late = tie(sum_parts(normed_found), logit_grad)
    router_grad = mm_tn(ffn_in, logit_late)
    normed_grad, out_sum = tie(normed_grad, out_sum)
    final_rows = (residual + out_sum).astype(BF)
    final_pair = jnp.concatenate(
        pair_order(final_rows, swap(final_rows, SEQ_AXIS), SEQ_AXIS), axis=0
    )
    layer_out = mm_tn(back_half, final_pair).astype(BF)
    _, attn_back = jax.vjp(rms_norm, tokens.astype(F32), gain_attn)
    input_part, gain_attn_grad = attn_back(normed_grad)
    resid_group = lax.dynamic_slice_in_dim(resid_both, near_index * ROW, ROW, axis=0)
    grad_tokens = (mm_tn(back_half, resid_group) + input_part).astype(BF)

    qkv_grad = quad_swap(qkv_grad.astype(BF).reshape(KV_HEADS, qkv_rows, width))
    qkv_grad = qkv_grad.transpose(1, 0, 2).astype(F32)
    qkv_share = jnp.concatenate(
        [
            qkv_grad[:, :, :qcols].reshape(qkv_rows, QDIM),
            qkv_grad[:, :, qcols : qcols + HEAD_DIM].reshape(qkv_rows, KVDIM),
            qkv_grad[:, :, qcols + HEAD_DIM :].reshape(qkv_rows, KVDIM),
        ],
        axis=1,
    )

    gains_grad = jnp.concatenate(
        [gain_attn_grad, gain_ffn_grad, query_gain_grad[0], key_gain_grad[0]]
    )
    share_rows = -(-small_size // (8 * LANES)) * 8
    small_grad = jnp.concatenate(
        [router_grad.reshape(device_count, router_size), gains_grad.reshape(device_count, gain_rows)],
        axis=1,
    )
    small_grad = jnp.pad(small_grad, ((0, 0), (0, share_rows * LANES - small_size)))
    small_share = jnp.sum(
        exchange(small_grad.reshape(device_count, share_rows, LANES), ALL_AXES), axis=0
    ).reshape(share_rows * LANES)
    router_share = small_share[:router_size].reshape(qkv_rows, experts_all)
    gains_share = small_share[router_size:small_size]
    return (layer_out, grad_tokens, qkv_share, out_share, router_share, gains_share, grad_expert)


def solution(mesh):
    shape = dict(mesh.shape)
    inner = Mesh(
        mesh.devices.reshape(shape["dp"] // (NEAR * CORES), NEAR, CORES, shape["seq"]), ALL_AXES
    )
    rows = P(ALL_AXES, None)
    in_specs = (
        rows,
        rows,
        rows,
        rows,
        rows,
        P(ALL_AXES),
        P(ALL_AXES, None, None),
        P(DP_AXES, None),
        P(DP_AXES, None),
        P(DP_AXES, None, None),
    )
    out_specs = (rows, rows, rows, rows, rows, P(ALL_AXES), P(ALL_AXES, None, None))
    return jax.shard_map(shards, mesh=inner, in_specs=in_specs, out_specs=out_specs, check_vma=False)
```
